32 devices in a mesh: dp: 16 (over z, y, core), mp: 2 (over x).
Axes of the slice: x: 2, y: 2, z: 4, core: 2. Of those that a mesh axis runs over, the one named last changes fastest.
Arguments:
- block_in: bfloat16 [16, 1024, 1024], P('dp', 'mp'), may hold values from -6 to 6
- lengths: int32 [16], P('dp'), may hold values from 102 to 1024, as said below
- input_weight: bfloat16 [3, 1024, 1024], P(None, None, 'mp'), may hold values from -0.1875 to 0.1875
- output_weight: bfloat16 [1024, 1024], P('mp'), may hold values from -1.5 to 1.5
- up_weight: bfloat16 [1024, 4096], P(None, 'mp'), may hold values from -0.1875 to 0.1875
- down_weight: bfloat16 [4096, 1024], P('mp'), may hold values from -0.09375 to 0.09375
- norm_gain: float32 [2, 1024], replicated, may hold values from 0.1 to 1.9
- norm_bias: float32 [2, 1024], replicated, may hold values from -3 to 3
- cotangent: bfloat16 [16, 1024, 1024], P('dp', 'mp'), may hold values from -6 to 6
Outputs:
- block_out: bfloat16 [16, 1024, 1024], P('dp', 'mp')
- grad_input: float32 [16, 1024, 1024], P('dp', 'mp')
- input_weight_grad: float32 [3, 1024, 1024], P(None, None, 'mp')
- output_weight_grad: float32 [1024, 1024], P('mp')
- up_weight_grad: float32 [1024, 4096], P(None, 'mp')
- down_weight_grad: float32 [4096, 1024], P('mp')
- gain_grad: float32 [2, 1024], replicated
- bias_grad: float32 [2, 1024], replicated
- denominator_stats: float32 [2], replicated
The draws below stay inside these ranges and needn't reach their ends.
Inputs may be any that keep to these rules, and one draw needn't show every extreme that they name: Positions 0 to lengths[c] - 1 of crop slot c hold pixels, the rest is padding; some crop fills its slot of 1024.
All inputs are finite; a program needn't handle non-finite values.
Results may differ from the reference program's by a relative error of at most 0.019.
Values may be sent and summed in bfloat16 or wider, within the bound.
A program may use at most 128 MiB of HBM per device.

```python
import jax
import jax.numpy as jnp
from jax import lax

D = 1024
H = 16
DH = 64
FF = 4096
HD = 1024
BLK = 512
SLOT = 1024
CROPS = 16
N_MP = 2


def draw_lengths(key, part):
    first_key, second_key = jax.random.split(key)
    level = jax.random.randint(first_key, (CROPS,), 0, 1024)
    cubed = level * level // 1024 * level // 1024
    shortfall = SLOT * 9 // 10 * cubed // 1024
    drawn = SLOT - shortfall
    chosen = jax.random.randint(second_key, (), 0, CROPS)
    return jnp.where(jnp.arange(CROPS) == chosen, SLOT, drawn).astype(jnp.int32)


def block_levels(key, dims, cuts, least, largest):
    loudness = 1.0
    for axis_at, shards_of in cuts:
        heights = jax.random.uniform(jax.random.fold_in(jax.random.fold_in(key, 6), axis_at), (shards_of,), jnp.float32, least / len(cuts), largest / len(cuts))
        loudness = loudness * jnp.repeat(jnp.exp(heights), dims[axis_at] // shards_of).reshape((-1,) + (1,) * (len(dims) - 1 - axis_at))
    return loudness


def gaussian(key, dims, scale, most, shards=(), dtype=jnp.bfloat16):
    values = scale * jax.random.normal(key, dims, jnp.float32)
    if shards:
        values = values * block_levels(key, dims, shards, -0.22, 0.18)
    return jnp.clip(values, -most, most).astype(dtype)


def setup_inputs(seed: int = 0) -> dict:
    streams_of = jax.random.split(jax.random.key(seed), 10)
    return {
        "block_in": gaussian(streams_of[0], (CROPS, SLOT, D), 1.0, 6.0, ((0, 16), (1, 2))),
        "lengths": draw_lengths(jax.random.fold_in(streams_of[9], 71), 0),
        "input_weight": gaussian(streams_of[2], (3, D, HD), D ** -0.5, 0.1875, ((2, 2),)),
        "output_weight": gaussian(streams_of[3], (HD, D), (max(1, HD * 16 // SLOT)) ** -0.5, 1.5, ((0, 2),)),
        "up_weight": gaussian(streams_of[4], (D, FF), D ** -0.5, 0.1875, ((1, 2),)),
        "down_weight": gaussian(streams_of[5], (FF, D), FF ** -0.5, 0.09375, ((0, 2),)),
        "norm_gain": jnp.clip(1.0 + 0.18 * jax.random.normal(streams_of[6], (2, D), jnp.float32), 0.1, 1.9),
        "norm_bias": gaussian(streams_of[7], (2, D), 0.5, 3.0, (), jnp.float32),
        "cotangent": gaussian(streams_of[8], (CROPS, SLOT, D), 1.0, 6.0, ((0, 16), (1, 2))),
    }


PRECISE = lax.Precision.HIGHEST
EPSILON = 1e-05

@jax.custom_vjp
def low(v):
    return lax.optimization_barrier(v.astype(jnp.bfloat16)).astype(jnp.float32)

@jax.custom_vjp
def low_back(v):
    return v

def low_keep(v):
    return (low(v), None)

def low_pass(kept, grad):
    return (grad,)

def back_keep(v):
    return (v, None)

def back_low(kept, grad):
    return (low(grad),)
low.defvjp(low_keep, low_pass)
low_back.defvjp(back_keep, back_low)

def feature(values):
    return jax.nn.elu(values) + 1.0

def normalise(inputs, gain_row, bias_row):
    centre = lax.optimization_barrier(jnp.mean(inputs, axis=-1, keepdims=True))
    centred = inputs - centre
    spread = lax.optimization_barrier(jnp.mean(centred * centred, axis=-1, keepdims=True))
    return centred * lax.rsqrt(spread + EPSILON) * gain_row + bias_row

def exclusive(stacked):
    running = jnp.cumsum(stacked, axis=0)
    return jnp.concatenate([jnp.zeros_like(running[:1]), running[:-1]], axis=0)

def linear_attention(query_map, key_map, values):
    block_shape = (SLOT // BLK, BLK, H, DH)
    block_q = query_map.reshape(block_shape)
    block_k = key_map.reshape(block_shape)
    block_v = values.reshape(block_shape)
    memory = exclusive(jnp.einsum('nihd,nihe->nhde', block_k, block_v, precision=PRECISE))
    key_total = exclusive(lax.optimization_barrier(jnp.sum(block_k, axis=1)))
    causal = jnp.tril(jnp.ones((BLK, BLK), jnp.float32))

    def one_block(block_item):
        query_b, key_b, value_b, memory_b, total_b = block_item
        scores = low_back(jnp.einsum('ihd,jhd->hij', query_b, key_b, precision=PRECISE)) * causal
        numerator = jnp.einsum('ihd,hde->ihe', query_b, memory_b, precision=PRECISE) + jnp.einsum('hij,jhd->ihd', low(scores), value_b, precision=PRECISE)
        denominator = jnp.einsum('ihd,hd->ih', query_b, total_b, precision=PRECISE) + lax.optimization_barrier(jnp.sum(scores, axis=-1)).T
        return (numerator / denominator[..., None], denominator)
    attended, denoms = lax.map(jax.checkpoint(one_block), (block_q, block_k, block_v, memory, key_total))
    return (attended.reshape(SLOT, H, DH), denoms.reshape(SLOT, H))

def crop_forward(inputs, input_weight, output_weight, up_weight, down_weight, norm_gain, norm_bias, valid_mask):
    local_width = HD // N_MP
    local_units = FF // N_MP
    first_norm = low(normalise(inputs, norm_gain[0], norm_bias[0]))
    first_copies = low_back(jnp.broadcast_to(first_norm, (N_MP, SLOT, D)))
    projected = jnp.einsum('grd,cdgk->rcgk', first_copies, input_weight.reshape(3, D, N_MP, local_width), precision=PRECISE).reshape(SLOT, 3, H, DH)
    query = low_back(projected[:, 0])
    key_raw = low_back(projected[:, 1])
    values = low(low_back(projected[:, 2]))
    query_map = low(feature(query))
    key_map = low(feature(key_raw) * valid_mask[:, None, None])
    attended, denoms = linear_attention(query_map, key_map, values)
    mixed = low_back(low(attended.reshape(SLOT, HD)))
    pieces = jnp.einsum('rgk,gkd->grd', mixed.reshape(SLOT, N_MP, local_width), output_weight.reshape(N_MP, local_width, D), precision=PRECISE)
    middle = inputs + low_back(lax.optimization_barrier(jnp.sum(low(pieces), axis=0)))
    second_norm = low(normalise(middle, norm_gain[1], norm_bias[1]))
    second_copies = low_back(jnp.broadcast_to(second_norm, (N_MP, SLOT, D)))
    hidden_in = low_back(jnp.einsum('grd,dgf->rgf', second_copies, up_weight.reshape(D, N_MP, local_units), precision=PRECISE).reshape(SLOT, FF))
    hidden = low(jax.nn.gelu(hidden_in, approximate=True))
    pieces = jnp.einsum('rgf,gfd->grd', hidden.reshape(SLOT, N_MP, local_units), down_weight.reshape(N_MP, local_units, D), precision=PRECISE)
    return (middle + lax.optimization_barrier(jnp.sum(low(pieces), axis=0)), denoms)

def reference(block_in, lengths, input_weight, output_weight, up_weight, down_weight, norm_gain, norm_bias, cotangent):
    weights = (input_weight.astype(jnp.float32), output_weight.astype(jnp.float32), up_weight.astype(jnp.float32), down_weight.astype(jnp.float32), norm_gain.astype(jnp.float32), norm_bias.astype(jnp.float32))

    def crop_step(running, crop_item):
        grad_sums, peak_value, den_total, counted = running
        inputs, grad_rows, length = crop_item
        valid_mask = (jnp.arange(SLOT) < length).astype(jnp.float32)

        def forward(inputs_in, *params):
            return crop_forward(inputs_in, *params, valid_mask)
        outputs, pullback, denoms = jax.vjp(forward, inputs.astype(jnp.float32), *weights, has_aux=True)
        gradients = pullback(grad_rows.astype(jnp.float32))
        kept_denoms = jnp.where(valid_mask[:, None] > 0, denoms, 0.0)
        running = (jax.tree.map(jnp.add, grad_sums, tuple(gradients[1:])), jnp.maximum(peak_value, jnp.max(kept_denoms)), den_total + jnp.sum(kept_denoms), counted + length.astype(jnp.float32) * H)
        return (running, (outputs.astype(jnp.bfloat16), gradients[0]))
    initial = (tuple((jnp.zeros(weight_item.shape, jnp.float32) for weight_item in weights)), jnp.zeros((), jnp.float32), jnp.zeros((), jnp.float32), jnp.zeros((), jnp.float32))
    running, (outputs, grad_input) = lax.scan(crop_step, initial, (block_in, cotangent, lengths))
    grad_sums, peak_value, den_total, counted = running
    scaling = DH * SLOT
    denominator_stats = jnp.stack([peak_value / scaling, den_total / counted / scaling])
    return (outputs, grad_input, grad_sums[0], grad_sums[1], grad_sums[2], grad_sums[3], grad_sums[4], grad_sums[5], denominator_stats)
```

```python
from functools import partial

import jax
import jax.numpy as jnp
from jax import lax
from jax.experimental import pallas as pl
from jax.experimental.pallas import tpu as pltpu
from jax.sharding import PartitionSpec as P

DH = 64
BLK = 512


EPSILON = 1e-05
PRECISE = lax.Precision.HIGHEST


def combined_all(part, axis, combine):
    gathered = jax.tree.map(lambda a: lax.all_gather(a, axis), part)

    def take(source):
        return jax.tree.map(lambda a: lax.dynamic_index_in_dim(a, source, 0, False), gathered)

    return lax.fori_loop(
        1, lax.axis_size(axis), lambda source, state: combine(state, take(source)), take(0)
    )


def feature(values):
    return jax.nn.elu(values) + 1.0


def feature_slope(values):
    return jnp.where(values > 0, 1.0, jnp.exp(values))


def normalise(inputs, gain_row, bias_row):
    centre = jnp.mean(inputs, axis=-1, keepdims=True)
    centred = inputs - centre
    spread = jnp.mean(centred * centred, axis=-1, keepdims=True)
    inverse = lax.rsqrt(spread + EPSILON)
    unit_rows = centred * inverse
    return (unit_rows * gain_row + bias_row, unit_rows, inverse)


def normalise_back(grad_rows, unit_rows, inverse, gain_row):
    scaled = grad_rows * gain_row
    centre = jnp.mean(scaled, axis=-1, keepdims=True)
    along = jnp.mean(scaled * unit_rows, axis=-1, keepdims=True)
    input_grad = inverse * (scaled - centre - unit_rows * along)
    return (input_grad, jnp.sum(grad_rows * unit_rows, axis=0), jnp.sum(grad_rows, axis=0))


def exclusive(stacked):
    running = jnp.cumsum(stacked, axis=0)
    return jnp.concatenate([jnp.zeros_like(running[:1]), running[:-1]], axis=0)


def later(stacked):
    return exclusive(stacked[::-1])[::-1]


def unchanged(carried):
    return carried


def causal_mask():
    return jnp.tril(jnp.ones((BLK, BLK), jnp.float32))


def attend_forward(query_map, key_map, values, crop_len):
    slot_len, head_count, depth = query_map.shape
    block_count = slot_len // BLK
    block_shape = (block_count, BLK, head_count, depth)
    block_q = query_map.reshape(block_shape)
    block_k = key_map.reshape(block_shape)
    block_v = values.reshape(block_shape)
    memory = exclusive(
        jnp.einsum("nihd,nihe->nhde", block_k, block_v, preferred_element_type=jnp.float32)
    )
    key_total = exclusive(jnp.sum(block_k.astype(jnp.float32), axis=1))
    causal = causal_mask()
    block_starts = jnp.arange(block_count, dtype=jnp.int32) * BLK

    def one_block(block_item):
        query_b, key_b, value_b, memory_b, total_b, start_b = block_item
        query_f = query_b.astype(jnp.float32)
        numerator = jnp.einsum("ihd,hde->ihe", query_f, memory_b, precision=PRECISE)
        denominator = jnp.einsum("ihd,hd->ih", query_f, total_b, precision=PRECISE)

        def inside(partial_sums):
            value_part, weight_part = partial_sums
            scores = (
                jnp.einsum("ihd,jhd->hij", query_b, key_b, preferred_element_type=jnp.float32)
                * causal
            )
            value_part = value_part + jnp.einsum(
                "hij,jhd->ihd",
                scores.astype(jnp.bfloat16),
                value_b,
                preferred_element_type=jnp.float32,
            )
            weight_part = weight_part + jnp.sum(scores, axis=-1).T
            return (value_part, weight_part)

        numerator, denominator = lax.cond(
            start_b < crop_len, inside, unchanged, (numerator, denominator)
        )
        return (numerator / denominator[..., None], denominator)

    attended, denoms = lax.map(
        one_block, (block_q, block_k, block_v, memory, key_total, block_starts)
    )
    return (
        attended.reshape(slot_len, head_count, depth),
        denoms.reshape(slot_len, head_count),
        memory,
        key_total,
    )


def attend_backward(
    grad_attn, attended, denoms, query_map, key_map, values, memory, key_total, crop_len
):
    slot_len, head_count, depth = query_map.shape
    block_count = slot_len // BLK
    block_shape = (block_count, BLK, head_count, depth)
    top_all = (grad_attn / denoms[..., None]).reshape(block_shape)
    bottom_all = (-jnp.sum(grad_attn * attended, axis=-1) / denoms).reshape(
        block_count, BLK, head_count
    )
    query_full = query_map.astype(jnp.float32).reshape(block_shape)
    memory_later = later(jnp.einsum("nihd,nihe->nhde", query_full, top_all, precision=PRECISE))
    total_later = later(jnp.einsum("nihd,nih->nhd", query_full, bottom_all, precision=PRECISE))
    causal = causal_mask()
    block_starts = jnp.arange(block_count, dtype=jnp.int32) * BLK

    def one_block(block_item):
        (
            query_b,
            key_b,
            value_b,
            memory_b,
            total_b,
            later_memory,
            later_total,
            top_grad,
            bottom_grad,
            start_b,
        ) = block_item
        value_f = value_b.astype(jnp.float32)
        key_f = key_b.astype(jnp.float32)
        query_sum = (
            jnp.einsum("ihe,hde->ihd", top_grad, memory_b, precision=PRECISE)
            + bottom_grad[..., None] * total_b[None]
        )
        key_sum = (
            jnp.einsum("jhe,hde->jhd", value_f, later_memory, precision=PRECISE) + later_total[None]
        )
        value_sum = jnp.einsum("jhd,hde->jhe", key_f, later_memory, precision=PRECISE)

        def inside(partial_grads):
            query_acc, key_acc, value_acc = partial_grads
            scores = (
                jnp.einsum("ihd,jhd->hij", query_b, key_b, preferred_element_type=jnp.float32)
                * causal
            )
            score_grad = (
                (
                    jnp.einsum("ihe,jhe->hij", top_grad, value_f, precision=PRECISE)
                    + bottom_grad.T[:, :, None]
                )
                * causal
            ).astype(jnp.bfloat16)
            query_acc = query_acc + jnp.einsum(
                "hij,jhd->ihd", score_grad, key_b, preferred_element_type=jnp.float32
            )
            key_acc = key_acc + jnp.einsum(
                "hij,ihd->jhd", score_grad, query_b, preferred_element_type=jnp.float32
            )
            rounded_scores = scores.astype(jnp.bfloat16).astype(jnp.float32)
            value_acc = value_acc + jnp.einsum(
                "hij,ihe->jhe", rounded_scores, top_grad, precision=PRECISE
            )
            return (query_acc, key_acc, value_acc)

        return lax.cond(start_b < crop_len, inside, unchanged, (query_sum, key_sum, value_sum))

    query_grad, key_grad, value_grad = lax.map(
        one_block,
        (
            query_map.reshape(block_shape),
            key_map.reshape(block_shape),
            values.reshape(block_shape),
            memory,
            key_total,
            memory_later,
            total_later,
            top_all,
            bottom_all,
            block_starts,
        ),
    )
    return (
        query_grad.reshape(slot_len, head_count, depth),
        key_grad.reshape(slot_len, head_count, depth),
        value_grad.reshape(slot_len, head_count, depth),
    )


def combine_stats(first_part, second_part):
    return (
        first_part[0] + second_part[0],
        first_part[1] + second_part[1],
        first_part[2] + second_part[2],
        first_part[3] + second_part[3],
        jnp.maximum(first_part[4], second_part[4]),
    )


def per_device(
    block_in,
    lengths,
    input_weight,
    output_weight,
    up_weight,
    down_weight,
    norm_gain,
    norm_bias,
    cotangent,
):
    group_count = lax.axis_size("mp")
    rows_here = block_in.shape[1]
    slot_len = rows_here * group_count
    local_width = output_weight.shape[0]
    head_count = local_width // DH
    crop_len = lengths[0]
    valid_mask = (jnp.arange(slot_len, dtype=jnp.int32) < crop_len).astype(jnp.float32)
    own_rows = block_in[0].astype(jnp.float32)
    first_norm, unit_one, inverse_one = normalise(own_rows, norm_gain[0], norm_bias[0])
    first_rows = lax.all_gather(first_norm.astype(jnp.bfloat16), "mp", axis=0, tiled=True)
    projected = jnp.einsum(
        "rd,cdk->rck", first_rows, input_weight, preferred_element_type=jnp.float32
    ).reshape(slot_len, 3, head_count, DH)
    query = projected[:, 0]
    key_raw = projected[:, 1]
    query_map = feature(query).astype(jnp.bfloat16)
    key_map = (feature(key_raw) * valid_mask[:, None, None]).astype(jnp.bfloat16)
    values = projected[:, 2].astype(jnp.bfloat16)
    attended, denoms, memory, key_total = attend_forward(query_map, key_map, values, crop_len)
    mixed = attended.reshape(slot_len, local_width).astype(jnp.bfloat16)
    part_rows = mixed
    branch_out = lax.psum_scatter(
        jnp.dot(part_rows, output_weight, preferred_element_type=jnp.float32).astype(jnp.bfloat16),
        "mp",
        scatter_dimension=0,
        tiled=True,
    ).astype(jnp.float32)
    middle = own_rows + branch_out
    second_norm, unit_two, inverse_two = normalise(middle, norm_gain[1], norm_bias[1])
    second_rows = lax.all_gather(second_norm.astype(jnp.bfloat16), "mp", axis=0, tiled=True)
    hidden_in = jnp.dot(second_rows, up_weight, preferred_element_type=jnp.float32)
    hidden = jax.nn.gelu(hidden_in, approximate=True).astype(jnp.bfloat16)
    part_rows = hidden
    mlp_out = lax.psum_scatter(
        jnp.dot(part_rows, down_weight, preferred_element_type=jnp.float32).astype(jnp.bfloat16),
        "mp",
        scatter_dimension=0,
        tiled=True,
    ).astype(jnp.float32)
    block_out = (middle + mlp_out).astype(jnp.bfloat16)[None]
    grad_out = cotangent[0]
    grad_rows = lax.all_gather(grad_out, "mp", axis=0, tiled=True)
    down_grad = jnp.einsum("rf,rd->fd", hidden, grad_rows, preferred_element_type=jnp.float32)
    hidden_grad = jnp.einsum(
        "rd,fd->rf", grad_rows, down_weight, preferred_element_type=jnp.float32
    )
    unused_out, gelu_back = jax.vjp(partial(jax.nn.gelu, approximate=True), hidden_in)
    inner_grad = gelu_back(hidden_grad)[0].astype(jnp.bfloat16)
    up_grad = jnp.einsum("rd,rf->df", second_rows, inner_grad, preferred_element_type=jnp.float32)
    part_rows = inner_grad
    second_grad = lax.psum_scatter(
        jnp.einsum("rf,df->rd", part_rows, up_weight, preferred_element_type=jnp.float32).astype(
            jnp.bfloat16
        ),
        "mp",
        scatter_dimension=0,
        tiled=True,
    ).astype(jnp.float32)
    back_two, gain_two, bias_two = normalise_back(second_grad, unit_two, inverse_two, norm_gain[1])
    middle_grad = grad_out.astype(jnp.float32) + back_two
    middle_low = middle_grad.astype(jnp.bfloat16)
    middle_full = lax.all_gather(middle_low, "mp", axis=0, tiled=True)
    mixed_grad = jnp.einsum(
        "rd,kd->rk", middle_full, output_weight, preferred_element_type=jnp.float32
    ).astype(jnp.bfloat16)
    output_grad = jnp.einsum("rk,rd->kd", mixed, middle_full, preferred_element_type=jnp.float32)
    grad_attn = mixed_grad.astype(jnp.float32).reshape(slot_len, head_count, DH)
    query_grad, key_grad, value_grad = attend_backward(
        grad_attn, attended, denoms, query_map, key_map, values, memory, key_total, crop_len
    )
    query_low = (query_grad * feature_slope(query)).astype(jnp.bfloat16)
    key_low = (key_grad * valid_mask[:, None, None] * feature_slope(key_raw)).astype(jnp.bfloat16)
    value_low = value_grad.astype(jnp.bfloat16)
    qkv_grad = jnp.stack([query_low, key_low, value_low], axis=1).reshape(slot_len, 3, local_width)
    input_grad = jnp.einsum("rd,rck->cdk", first_rows, qkv_grad, preferred_element_type=jnp.float32)
    part_rows = qkv_grad
    first_grad = lax.psum_scatter(
        jnp.einsum(
            "rck,cdk->rd", part_rows, input_weight, preferred_element_type=jnp.float32
        ).astype(jnp.bfloat16),
        "mp",
        scatter_dimension=0,
        tiled=True,
    ).astype(jnp.float32)
    back_one, gain_one, bias_one = normalise_back(first_grad, unit_one, inverse_one, norm_gain[0])
    grad_input = (middle_grad + back_one)[None]
    input_grad, output_grad, up_grad, down_grad = (
        lax.psum(input_grad.astype(jnp.bfloat16), "dp").astype(jnp.float32),
        lax.psum(output_grad.astype(jnp.bfloat16), "dp").astype(jnp.float32),
        lax.psum(up_grad.astype(jnp.bfloat16), "dp").astype(jnp.float32),
        lax.psum(down_grad.astype(jnp.bfloat16), "dp").astype(jnp.float32),
    )
    kept_denoms = jnp.where(valid_mask[:, None] > 0, denoms, 0.0)
    den_total = jnp.sum(kept_denoms)
    den_count = crop_len.astype(jnp.float32) * head_count
    den_peak = jnp.max(kept_denoms)
    gain_grad, bias_grad, den_total, den_count, den_peak = combined_all(
        (
            jnp.stack([gain_one, gain_two]),
            jnp.stack([bias_one, bias_two]),
            den_total,
            den_count,
            den_peak,
        ),
        ("dp", "mp"),
        combine_stats,
    )
    scaling = DH * slot_len
    denominator_stats = jnp.stack([den_peak / scaling, den_total / den_count / scaling])
    return (
        block_out,
        grad_input,
        input_grad,
        output_grad,
        up_grad,
        down_grad,
        gain_grad,
        bias_grad,
        denominator_stats,
    )

MESH = pl.DeviceIdType.MESH
BF = jnp.bfloat16
F32 = jnp.float32
ROWS = 512
CH = 256
PAIR = 128


def dot_nn(a, b):
    return lax.dot_general(a, b, (((1,), (0,)), ((), ())), preferred_element_type=F32)


def dot_nt(a, b):
    return lax.dot_general(a, b, (((1,), (1,)), ((), ())), preferred_element_type=F32)


def dot_tn(a, b):
    return lax.dot_general(a, b, (((0,), (0,)), ((), ())), preferred_element_type=F32)


class Place:
    def __init__(self):
        dp = lax.axis_index("dp")
        mp = lax.axis_index("mp")
        self.dp, self.mp = dp, mp
        self.core = lax.rem(dp, 2)
        chip = dp // 2
        y = lax.rem(chip, 2)
        z = chip // 2
        self.r = z + y * (7 - 2 * z)
        self.across = (dp, 1 - mp)
        self.mate = (dp + 1 - 2 * self.core, mp)
        self.next = self.at(lax.rem(self.r + 1, 8))
        self.prev = self.at(lax.rem(self.r + 7, 8))

    def at(self, r):
        y = r // 4
        z = r + y * (7 - 2 * r)
        return ((z * 2 + y) * 2 + self.core, self.mp)

    def partners(self):
        return [self.across, self.mate, self.next, self.prev]


def greet(partners):
    barrier = pltpu.get_barrier_semaphore()
    for partner in partners:
        pl.semaphore_signal(barrier, inc=1, device_id=partner, device_id_type=MESH)
    pl.semaphore_wait(barrier, len(partners))


def remote(src, dst, send_sem, recv_sem, device):
    return pltpu.make_async_remote_copy(
        src_ref=src, dst_ref=dst, send_sem=send_sem, recv_sem=recv_sem,
        device_id=device, device_id_type=MESH,
    )


def aligned(start, size, unit):
    return pl.ds(pl.multiple_of(start, unit), size)


def lane_head(shape):
    return lax.broadcasted_iota(jnp.int32, shape, len(shape) - 1) < DH


def same_head():
    row = lax.broadcasted_iota(jnp.int32, (PAIR, PAIR), 0) < DH
    lane = lax.broadcasted_iota(jnp.int32, (PAIR, PAIR), 1) < DH
    return row == lane


def causal_tile():
    row = lax.broadcasted_iota(jnp.int32, (CH, CH), 0)
    col = lax.broadcasted_iota(jnp.int32, (CH, CH), 1)
    return row >= col


def unpack_state(packed):
    keep = same_head()
    zero = jnp.zeros_like(packed)
    return jnp.concatenate(
        [jnp.where(keep, packed, zero), jnp.where(keep, pltpu.roll(packed, DH, 1), zero)], axis=1
    )


def split_heads(pair):
    first = lane_head(pair.shape)
    zero = jnp.zeros_like(pair)
    return jnp.where(first, pair, zero), jnp.where(first, zero, pair)


def row_norm(rows):
    centre = jnp.mean(rows, axis=-1, keepdims=True)
    centred = rows - centre
    inverse = lax.rsqrt(jnp.mean(centred * centred, axis=-1, keepdims=True) + EPSILON)
    return centred * inverse, inverse


def front_kernel(
    len_ref, x_hbm, dy_hbm, win_hbm, wo_hbm, wdn_hbm, gain_ref, bias_ref,
    first_o, qkv_o, mix_o, rden_o, state_o, mid_o, sec_o, wino_o, woo_o, dyo_o, hg_o, stat_ref,
    x_v, dy_v, win_v, wino_v, wo_v, woo_v, wdn_v, first_v, qkv_v, num_v, den_v, mix_v, mid_v, sec_v, hg_v,
    local_v, ssend_v, srecv_v, state_v,
    in_sem, out_sem, xs_sem, xr_sem, ring_s, ring_r, mate_s, mate_r,
):
    here = Place()
    loads = [
        (x_hbm, x_v), (win_hbm, win_v), (dy_hbm, dy_v.at[0]), (wdn_hbm, wdn_v), (wo_hbm, wo_v),
    ]
    loads = [pltpu.make_async_copy(a, b, in_sem.at[i]) for i, (a, b) in enumerate(loads)]
    for load in loads:
        load.start()
    greet(here.partners())
    piece = here.r * 2 + here.core
    parts = ((win_hbm, wino_v, 192), (wo_hbm, woo_v, 32))
    cross = []
    for i, (src, dst, rows) in enumerate(parts):
        at = aligned(piece * rows, rows, 32)
        cross.append(remote(src.at[at], dst.at[at], xs_sem.at[i], xr_sem.at[i], here.across))
    cross.append(remote(dy_hbm, dy_v.at[1], xs_sem.at[2], xr_sem.at[2], here.across))
    for copy in cross:
        copy.start()

    gain = gain_ref[0:1, :]
    bias = bias_ref[0:1, :]
    sends = []
    outs = []

    def out(src, dst):
        copy = pltpu.make_async_copy(src, dst, out_sem.at[len(outs)])
        copy.start()
        outs.append(copy)

    def rows_of(array, r, core, half=None):
        rows = parts[array][2]
        start = (r * 2 + core) * rows
        if half is None:
            return aligned(start, rows, 32)
        return aligned(start + half * (rows // 2), rows // 2, 16)

    def to_mate(array, slot, r, half=None):
        at = rows_of(array, r, here.core, half)
        dst = parts[array][1]
        copy = remote(dst.at[at], dst.at[at], mate_s.at[array, slot], mate_r.at[array, slot], here.mate)
        copy.start()
        sends.append(copy)

    def to_ring(array, way, step):
        dst = parts[array][1]
        back = step if way == 0 else 8 - step
        at = rows_of(array, lax.rem(here.r + 8 - back, 8), here.core, way if step == 3 else None)
        copy = remote(
            dst.at[at], dst.at[at], ring_s.at[array, way, step], ring_r.at[array, way, step],
            here.next if way == 0 else here.prev,
        )
        copy.start()
        sends.append(copy)

    def ring_wait(array, way, step):
        dst = parts[array][1]
        back = step + 1 if way == 0 else 7 - step
        owner = lax.rem(here.r + 8 - back, 8)
        half = way if step == 3 else None
        at = rows_of(array, owner, here.core, half)
        remote(
            dst.at[at], dst.at[at], ring_s.at[array, way, step], ring_r.at[array, way, step], here.next
        ).wait_recv()
        return owner, half

    def hop(step):
        for array in (0, 1):
            if step == 0:
                cross[array].wait_recv()
                for way in (0, 1):
                    to_ring(array, way, 0)
                to_mate(array, 0, here.r)
                continue
            for way in (0, 1):
                owner, half = ring_wait(array, way, step - 1)
                if step < 4:
                    to_ring(array, way, step)
                to_mate(array, 1 + 2 * (step - 1) + way, owner, half)

    def mate_wait(array):
        dst = parts[array][1]
        other = 1 - here.core
        for slot in range(9):
            if slot == 0:
                at = rows_of(array, here.r, other)
            else:
                step, way = (slot - 1) // 2, (slot - 1) % 2
                back = step + 1 if way == 0 else 7 - step
                at = rows_of(array, lax.rem(here.r + 8 - back, 8), other, way if step == 3 else None)
            remote(
                dst.at[at], dst.at[at], mate_s.at[array, slot], mate_r.at[array, slot], here.mate
            ).wait_recv()

    loads[0].wait()

    @pl.loop(0, ROWS // 128)
    def _(i):
        at = aligned(i * 128, 128, 128)
        unit, _ = row_norm(x_v[at, :].astype(F32))
        first_v[at, :] = (unit * gain + bias).astype(BF)

    out(first_v, first_o)
    crop_len = len_ref[0]

    def project(half, weights):
        @pl.loop(0, 2)
        def _(c):
            at = aligned(c * CH, CH, CH)
            rows = first_v[at, :]
            for i in range(3):
                raw = dot_nn(rows, weights[pl.ds(i * 1024, 1024), :])
                if i < 2:
                    raw = jnp.where(raw > 0, raw + 1.0, jnp.exp(jnp.minimum(raw, 0.0)))
                if i == 1:
                    place = lax.broadcasted_iota(jnp.int32, raw.shape, 0) + (here.mp * ROWS + c * CH)
                    raw = jnp.where(place < crop_len, raw, 0.0)
                qkv_v[half, i, at, :] = raw.astype(BF)

    def states(half):
        keep = same_head()

        @pl.loop(0, 4)
        def _(p):
            lanes = aligned(p * PAIR, PAIR, PAIR)
            total = None
            for c in range(2):
                keys = qkv_v[half, 1, pl.ds(c * CH, CH), lanes]
                vals = qkv_v[half, 2, pl.ds(c * CH, CH), lanes]
                made = dot_tn(keys, jnp.concatenate([vals, jnp.ones_like(vals)], axis=1))
                packed = jnp.where(keep, made[:, :PAIR], made[:, PAIR:])
                if c == 0:
                    local_v[half, p] = packed
                    total = packed
                else:
                    ssend_v[half, p] = (total + packed).astype(BF)

        copy = remote(
            ssend_v.at[half], srecv_v.at[1 - half], xs_sem.at[3 + half], xr_sem.at[4 - half], here.across
        )
        copy.start()
        sends.append(copy)

    def inside(half):
        mask = causal_tile()

        @pl.loop(0, 8)
        def _(n):
            p = n // 2
            c = lax.rem(n, 2)
            lanes = aligned(p * PAIR, PAIR, PAIR)
            at = aligned(c * CH, CH, CH)
            query = qkv_v[half, 0, at, lanes]
            key = qkv_v[half, 1, at, lanes]
            val = qkv_v[half, 2, at, lanes]
            first = lane_head(val.shape)
            one = jnp.ones_like(val)
            zero = jnp.zeros_like(val)
            sums = None
            for head, part in enumerate(split_heads(query)):
                score = jnp.where(mask, dot_nt(part, key), 0.0).astype(BF)
                mine = first if head == 0 else jnp.logical_not(first)
                right = jnp.concatenate([jnp.where(mine, val, zero), jnp.where(mine, one, zero)], axis=1)
                term = dot_nn(score, right)
                sums = term if sums is None else sums + term
            num_v[at, lanes] = sums[:, :PAIR]
            den_v[half, at, lanes] = sums[:, PAIR:]

    def finish(half):
        flag = here.mp.astype(F32)

        @pl.loop(0, 8)
        def _(n):
            p = n // 2
            c = lax.rem(n, 2)
            lanes = aligned(p * PAIR, PAIR, PAIR)
            at = aligned(c * CH, CH, CH)
            query = qkv_v[half, 0, at, lanes]
            before = srecv_v[half, p].astype(F32) * flag
            state_v[half, p] = before.astype(BF)
            before = before + local_v[half, p] * c.astype(F32)
            term = dot_nn(query, unpack_state(before).astype(BF))
            num = num_v[at, lanes] + term[:, :PAIR]
            den = den_v[half, at, lanes] + term[:, PAIR:]
            inverse = 1.0 / den
            den_v[half, at, lanes] = inverse
            mix_v[half, at, lanes] = (num * inverse).astype(BF)
            place = lax.broadcasted_iota(jnp.int32, den.shape, 0) + (here.mp * ROWS + c * CH)
            kept = jnp.where(place < crop_len, den, 0.0).reshape(CH // 8, 8, PAIR)
            stat_ref[0] = jnp.maximum(stat_ref[0], jnp.max(kept, axis=0))
            stat_ref[1] = stat_ref[1] + jnp.sum(kept, axis=0)

    def hidden_grad(side):
        @pl.loop(0, 2)
        def _(j):
            cols = aligned(j * 1024, 1024, 1024)
            hg_v[pl.ds(side * ROWS, ROWS), cols] = dot_nt(dy_v[side], wdn_v[cols, :]).astype(BF)

    stat_ref[...] = jnp.zeros_like(stat_ref)
    loads[1].wait()
    project(0, win_v)
    hop(0)
    states(0)
    inside_own = inside(0)
    hop(1)
    loads[2].wait()
    loads[3].wait()
    hidden_grad(0)
    hop(2)
    cross[2].wait_recv()
    hop(3)
    hidden_grad(1)
    out(hg_v, hg_o)
    out(dy_v.at[1], dyo_o)
    hop(4)
    mate_wait(0)
    out(wino_v, wino_o)
    mid_v[:, pl.ds(0, 512)] = num_v[...]
    project(1, wino_v)
    states(1)
    inside(1)
    remote(ssend_v.at[0], srecv_v.at[1], xs_sem.at[3], xr_sem.at[4], here.across).wait_recv()
    finish(1)
    num_v[...] = mid_v[:, pl.ds(0, 512)]
    remote(ssend_v.at[1], srecv_v.at[0], xs_sem.at[4], xr_sem.at[3], here.across).wait_recv()
    finish(0)
    out(qkv_v, qkv_o)
    out(den_v, rden_o)
    out(mix_v, mix_o)
    out(state_v, state_o)
    mate_wait(1)
    out(woo_v, woo_o)
    loads[4].wait()
    gain_two = gain_ref[1:2, :]
    bias_two = bias_ref[1:2, :]

    @pl.loop(0, 2)
    def _(c):
        at = aligned(c * CH, CH, CH)
        own = dot_nn(mix_v[0, at, :], wo_v[...]).astype(BF).astype(F32)
        other = dot_nn(mix_v[1, at, :], woo_v[...]).astype(BF).astype(F32)
        middle = x_v[at, :].astype(F32) + (own + other)
        mid_v[at, :] = middle
        unit, _ = row_norm(middle)
        sec_v[at, :] = (unit * gain_two + bias_two).astype(BF)

    out(mid_v, mid_o)
    out(sec_v, sec_o)
    for copy in cross + sends:
        copy.wait_send()
    for copy in outs:
        copy.wait()


def any_spec(count):
    return [pl.BlockSpec(memory_space=pl.ANY)] * count


def front(lengths, x_rows, dy_rows, win, wo, wdn, gain, bias):
    vm = pltpu.VMEM
    shapes = [
        ((512, 1024), BF), ((2, 3, 512, 512), BF), ((2, 512, 512), BF), ((2, 512, 512), F32),
        ((2, 4, PAIR, PAIR), BF), ((512, 1024), F32), ((512, 1024), BF), ((3072, 512), BF),
        ((512, 1024), BF), ((512, 1024), BF), ((1024, 2048), BF), ((2, 8, PAIR), F32),
    ]
    dma = pltpu.SemaphoreType.DMA
    return pl.pallas_call(
        front_kernel,
        out_shape=[jax.ShapeDtypeStruct(s, d) for s, d in shapes],
        in_specs=[pl.BlockSpec(memory_space=pltpu.SMEM)] + any_spec(5)
        + [pl.BlockSpec(memory_space=pltpu.VMEM)] * 2,
        out_specs=any_spec(11) + [pl.BlockSpec(memory_space=pltpu.VMEM)],
        scratch_shapes=[
            vm((512, 1024), BF), vm((2, 512, 1024), BF), vm((3072, 512), BF), vm((3072, 512), BF),
            vm((512, 1024), BF), vm((512, 1024), BF), vm((2048, 1024), BF), vm((512, 1024), BF),
            vm((2, 3, 512, 512), BF), vm((512, 512), F32), vm((2, 512, 512), F32), vm((2, 512, 512), BF),
            vm((512, 1024), F32), vm((512, 1024), BF), vm((1024, 2048), BF),
            vm((2, 4, PAIR, PAIR), F32), vm((2, 4, PAIR, PAIR), BF), vm((2, 4, PAIR, PAIR), BF),
            vm((2, 4, PAIR, PAIR), BF),
            dma((5,)), dma((12,)), dma((5,)), dma((5,)), dma((2, 2, 4)), dma((2, 2, 4)),
            dma((2, 9)), dma((2, 9)),
        ],
        compiler_params=pltpu.CompilerParams(
            collective_id=0, has_side_effects=True, vmem_limit_bytes=58 * 1024 * 1024
        ),
        name="front",
    )(lengths, x_rows, dy_rows, win, wo, wdn, gain, bias)


GELU_A = 0.7978845608028654
GELU_B = 0.044715


def gelu_pair(v):
    square = v * v
    t = jnp.tanh(GELU_A * v * (1.0 + GELU_B * square))
    half = 0.5 * (1.0 + t)
    slope = half + (0.5 * GELU_A) * v * (1.0 - t * t) * (1.0 + (3.0 * GELU_B) * square)
    return v * half, slope


def middle_kernel(
    sec_hbm, dy_hbm, dyo_hbm, hg_hbm, wup_hbm, wdn_hbm,
    part_o, pin_o, mlp_o, dslab_o, uslab_o,
    sec_v, dy_v, hg_v, wup_v, wdn_v, hid_v, part_v, send_v, pin_v, mlp_v,
    dsend_v, drecv_v, dslab_v, usend_v, urecv_v, uslab_v,
    in_sem, out_sem, xs_sem, xr_sem, ms_sem, mr_sem,
):
    here = Place()
    own = pl.ds(0, ROWS)
    other = pl.ds(ROWS, ROWS)
    loads = [
        (sec_hbm, sec_v.at[own]), (wup_hbm, wup_v), (hg_hbm, hg_v), (wdn_hbm, wdn_v),
        (dy_hbm, dy_v.at[own]), (dyo_hbm, dy_v.at[other]),
    ]
    loads = [pltpu.make_async_copy(a, b, in_sem.at[i]) for i, (a, b) in enumerate(loads)]
    for load in loads:
        load.start()
    greet([here.across, here.mate])
    sends = []
    outs = []

    def out(src, dst):
        copy = pltpu.make_async_copy(src, dst, out_sem.at[len(outs)])
        copy.start()
        outs.append(copy)

    def across(src, dst, slot):
        copy = remote(src, dst, xs_sem.at[slot], xr_sem.at[slot], here.across)
        copy.start()
        sends.append(copy)
        return copy

    ahead = [
        across(sec_hbm.at[pl.ds(c * CH, CH)], sec_v.at[pl.ds(ROWS + c * CH, CH)], c) for c in range(2)
    ]

    def up(chunk):
        rows = pl.ds(chunk * CH, CH)

        @pl.loop(0, 4)
        def _(j):
            cols = aligned(j * 512, 512, 512)
            raw = dot_nn(sec_v[rows, :], wup_v[:, cols])
            value, slope = gelu_pair(raw)
            hid_v[rows, cols] = value.astype(BF)
            hg_v[rows, cols] = (hg_v[rows, cols].astype(F32) * slope).astype(BF)

    def back(chunk, dst):
        dst[...] = dot_nt(hg_v[pl.ds(chunk * CH, CH), :], wup_v[...]).astype(BF)

    loads[0].wait()
    loads[1].wait()
    loads[2].wait()
    for c in range(2):
        up(c)
        back(c, part_v.at[pl.ds(c * CH, CH)])
    out(part_v, part_o)
    for c in range(2):
        ahead[c].wait_recv()
        up(2 + c)
        rows = pl.ds(c * CH, CH)
        back(2 + c, send_v.at[rows])
        across(send_v.at[rows], pin_v.at[rows], 2 + c)
    for load in loads[3:]:
        load.wait()
    their = 1 - here.core

    def down_grad(half, dst, plus):
        @pl.loop(0, 2)
        def _(i):
            cols = aligned(half * 1024 + i * 512, 512, 512)
            at = aligned(i * 512, 512, 512)
            made = dot_tn(hid_v[:, cols], dy_v[...])
            if plus is not None:
                made = made + plus[at, :].astype(F32)
            dst[at, :] = made.astype(BF)

    def up_grad(half, dst, plus):
        @pl.loop(0, 2)
        def _(i):
            cols = aligned(half * 512, 512, 512)
            at = aligned(i * 1024, 1024, 1024)
            made = dot_tn(sec_v[:, cols], hg_v[:, at])
            if plus is not None:
                made = made + plus[:, at].astype(F32)
            dst[:, at] = made.astype(BF)

    def to_mate(src, dst, slot):
        copy = remote(src, dst, ms_sem.at[slot], mr_sem.at[slot], here.mate)
        copy.start()
        sends.append(copy)
        return copy

    down_grad(their, dsend_v, None)
    to_d = to_mate(dsend_v, drecv_v, 0)
    up_grad(their, usend_v, None)
    to_u = to_mate(usend_v, urecv_v, 1)

    @pl.loop(0, 2)
    def _(i):
        rows = aligned(i * ROWS, ROWS, ROWS)
        mlp_v[rows, :] = dot_nn(hid_v[rows, :], wdn_v[...]).astype(BF)

    out(mlp_v, mlp_o)
    to_d.wait_recv()
    down_grad(here.core, dslab_v, drecv_v)
    out(dslab_v, dslab_o)
    to_u.wait_recv()
    up_grad(here.core, uslab_v, urecv_v)
    out(uslab_v, uslab_o)
    for c in range(2):
        rows = pl.ds(c * CH, CH)
        remote(send_v.at[rows], pin_v.at[rows], xs_sem.at[2 + c], xr_sem.at[2 + c], here.across).wait_recv()
    out(pin_v, pin_o)
    for copy in sends:
        copy.wait_send()
    for copy in outs:
        copy.wait()


def middle(sec, dy, dyo, hg, wup, wdn):
    vm = pltpu.VMEM
    dma = pltpu.SemaphoreType.DMA
    shapes = [
        ((512, 1024), BF), ((512, 1024), BF), ((1024, 1024), BF), ((1024, 1024), BF), ((512, 2048), BF),
    ]
    return pl.pallas_call(
        middle_kernel,
        out_shape=[jax.ShapeDtypeStruct(s, d) for s, d in shapes],
        in_specs=any_spec(6),
        out_specs=any_spec(5),
        scratch_shapes=[
            vm((1024, 1024), BF), vm((1024, 1024), BF), vm((1024, 2048), BF), vm((1024, 2048), BF),
            vm((2048, 1024), BF), vm((1024, 2048), BF), vm((512, 1024), BF), vm((512, 1024), BF),
            vm((512, 1024), BF), vm((1024, 1024), BF),
            vm((1024, 1024), BF), vm((1024, 1024), BF), vm((1024, 1024), BF),
            vm((512, 2048), BF), vm((512, 2048), BF), vm((512, 2048), BF),
            dma((6,)), dma((5,)), dma((4,)), dma((4,)), dma((2,)), dma((2,)),
        ],
        compiler_params=pltpu.CompilerParams(
            collective_id=1, has_side_effects=True, vmem_limit_bytes=58 * 1024 * 1024
        ),
        name="middle",
    )(sec, dy, dyo, hg, wup, wdn)


class Lane:
    def __init__(self, here, slab, base, rows, way, recv, result, result_base, sems):
        self.here, self.slab, self.base, self.rows, self.way = here, slab, base, rows, way
        self.recv, self.result, self.result_base = recv, result, result_base
        self.rs_s, self.rs_r, self.ag_s, self.ag_r, self.mt_s, self.mt_r, self.local = sems
        self.to = here.next if way == 0 else here.prev
        self.sign = 1 if way == 0 else -1
        self.pending = []

    def chunk(self, offset):
        return lax.rem(self.here.r + 16 + self.sign * offset, 8)

    def slab_at(self, offset):
        return aligned(self.base + self.chunk(offset) * self.rows, self.rows, 16)

    def result_at(self, offset, core):
        return aligned(self.result_base(core) + self.base + self.chunk(offset) * self.rows, self.rows, 16)

    def send(self, src, dst, send_sem, recv_sem, device):
        copy = remote(src, dst, send_sem, recv_sem, device)
        copy.start()
        self.pending.append(copy)

    def hand(self, src, offset, step):
        at = self.result_at(offset, self.here.core)
        if step < 7:
            self.send(src, self.result.at[at], self.ag_s.at[step], self.ag_r.at[step], self.to)
        self.send(src, self.result.at[at], self.mt_s.at[step], self.mt_r.at[step], self.here.mate)

    def tick(self, t):
        here = self.here
        if t == 0:
            self.send(self.slab.at[self.slab_at(0)], self.recv.at[0], self.rs_s.at[0], self.rs_r.at[0], self.to)
        elif t < 8:
            s = t - 1
            slot = self.recv.at[s]
            remote(slot, slot, self.rs_s.at[s], self.rs_r.at[s], self.to).wait_recv()
            mine = self.slab[self.slab_at(-s - 1), :]
            slot[...] = (slot[...].astype(F32) + mine.astype(F32)).astype(BF)
            if s < 6:
                self.send(slot, self.recv.at[s + 1], self.rs_s.at[s + 1], self.rs_r.at[s + 1], self.to)
            else:
                at = self.result_at(1, here.core)
                keep = pltpu.make_async_copy(slot, self.result.at[at], self.local)
                keep.start()
                self.keep = keep
                self.hand(slot, 1, 0)
        else:
            s = t - 8
            got = self.result.at[self.result_at(-s, here.core)]
            remote(got, got, self.ag_s.at[s], self.ag_r.at[s], self.to).wait_recv()
            self.hand(got, -s, s + 1)

    def finish(self):
        for copy in self.pending:
            copy.wait_send()
        self.keep.wait()
        for step in range(8):
            got = self.result.at[self.result_at(1 - step, 1 - self.here.core)]
            remote(got, got, self.mt_s.at[step], self.mt_r.at[step], self.here.mate).wait_recv()


def back_kernel(
    len_ref, gain_ref, bias_ref, stat_ref,
    part_hbm, pin_hbm, mid_hbm, x_hbm, dy_hbm, qkv_hbm, mix_hbm, rden_hbm, state_hbm, first_hbm,
    win_hbm, wino_hbm, wo_hbm, woo_hbm, mlp_hbm, dslab_hbm, uslab_hbm,
    resd_o, resu_o, resi_o, reso_o, out_o, gin_o, small_ref,
    part_v, pin_v, mid_v, x_v, dy_v, qkv_v, mix_v, rden_v, state_v, first_v, win_v, wo_v,
    mlpin_v, mg_v, mgf_v, mixg_v, top_v, bot_v, dqkv_v, local_v, lsend_v, lrecv_v,
    dslab_v, uslab_v, drecv_v, urecv_v, gm_v, gr_v, ga_v, gx_v, om_v, or_v, oa_v, ox_v, irecv_v, orecv_v,
    small_s, small_r, blk_v,
    in_sem, out_sem, xs_sem, xr_sem, ms_sem, mr_sem, bs_sem, br_sem,
    rs_s, rs_r, ag_s, ag_r, mt_s, mt_r, keep_s,
):
    here = Place()
    loads = [
        (part_hbm, part_v), (pin_hbm, pin_v), (mid_hbm, mid_v), (dy_hbm, dy_v), (dslab_hbm, dslab_v),
        (uslab_hbm, uslab_v), (wo_hbm, wo_v.at[0]), (woo_hbm, wo_v.at[1]), (mix_hbm, mix_v),
        (rden_hbm, rden_v), (qkv_hbm, qkv_v), (state_hbm, state_v), (first_hbm, first_v),
        (win_hbm, win_v.at[0]), (wino_hbm, win_v.at[1]), (x_hbm, x_v), (mlp_hbm.at[pl.ds(0, ROWS)], blk_v),
    ]
    loads = [pltpu.make_async_copy(a, b, in_sem.at[i]) for i, (a, b) in enumerate(loads)]
    for load in loads:
        load.start()
    y_mate = (here.dp + 2 - 4 * lax.rem(here.dp // 2, 2), here.mp)
    z_mate = (here.dp + 4 - 8 * lax.rem(here.dp // 4, 2), here.mp)
    z_far = (here.dp + 8 - 16 * (here.dp // 8), here.mp)
    greet(here.partners() + [y_mate, z_mate, z_far])
    sends = []
    outs = []

    def out(src, dst):
        copy = pltpu.make_async_copy(src, dst, out_sem.at[len(outs)])
        copy.start()
        outs.append(copy)

    def across(src, dst, slot):
        copy = remote(src, dst, xs_sem.at[slot], xr_sem.at[slot], here.across)
        copy.start()
        sends.append(copy)
        return copy

    def to_mate(src, dst, slot):
        copy = remote(src, dst, ms_sem.at[slot], mr_sem.at[slot], here.mate)
        copy.start()
        sends.append(copy)
        return copy

    lanes = []

    def add_lane(slab, base, rows, way, recv, result, result_base):
        n = len(lanes)
        sems = (rs_s.at[n], rs_r.at[n], ag_s.at[n], ag_r.at[n], mt_s.at[n], mt_r.at[n], keep_s.at[n])
        lanes.append(Lane(here, slab, base, rows, way, recv, result, result_base, sems))

    for way in (0, 1):
        add_lane(dslab_v, way * 512, 64, way, drecv_v.at[way], resd_o, lambda core: core * 1024)
    for way in (0, 1):
        add_lane(uslab_v, way * 256, 32, way, urecv_v.at[way], resu_o, lambda core: core * 512)
    for way in (0, 1):
        add_lane(ga_v.at[0], way * 768, 96, way, irecv_v.at[way], resi_o, lambda core: core * 1536)
    for way in (0, 1):
        add_lane(oa_v.at[0], way * 128, 16, way, orecv_v.at[way], reso_o, lambda core: core * 256)

    steps = [(lane, t) for t in range(15) for lane in (0, 1, 2, 3)]
    steps.reverse()

    def ring(count):
        for _ in range(count):
            if steps:
                lane, t = steps.pop()
                lanes[lane].tick(t)

    loads[4].wait()
    loads[5].wait()
    ring(4)
    mlp = across(mlp_hbm.at[pl.ds(ROWS, ROWS)], mlpin_v, 0)

    small_s[...] = jnp.zeros_like(small_s)
    for load in loads[0:4]:
        load.wait()
    gain_two = gain_ref[1:2, :]

    @pl.loop(0, ROWS // 128)
    def _(i):
        at = aligned(i * 128, 128, 128)
        grad = part_v[at, :].astype(F32) + pin_v[at, :].astype(F32)
        unit, inverse = row_norm(mid_v[at, :])
        scaled = grad * gain_two
        centre = jnp.mean(scaled, axis=-1, keepdims=True)
        along = jnp.mean(scaled * unit, axis=-1, keepdims=True)
        total = dy_v[at, :].astype(F32) + inverse * (scaled - centre - unit * along)
        mgf_v[at, :] = total
        mg_v[at, :] = total.astype(BF)
        small_s[1:2, :] = small_s[1:2, :] + jnp.sum(grad * unit, axis=0, keepdims=True)
        small_s[3:4, :] = small_s[3:4, :] + jnp.sum(grad, axis=0, keepdims=True)

    for load in loads[6:12]:
        load.wait()
    for half in range(2):
        mixg_v[half] = dot_nt(mg_v[...], wo_v[half]).astype(BF)
    ring(2)
    their = 1 - here.core

    def out_grad(half, side, dst):
        cols = aligned(side * 256, 256, 256)
        dst[...] = dot_tn(mix_v[half, :, cols], mg_v[...]).astype(BF)

    for half in (1, 0):
        out_grad(half, their, om_v.at[half])
        to_mate(om_v.at[half], or_v.at[half], half)
    for half in (1, 0):
        out_grad(half, here.core, oa_v.at[half])
    ring(2)

    keep = same_head()

    def tops(half):
        @pl.loop(0, 4)
        def _(p):
            lanes_at = aligned(p * PAIR, PAIR, PAIR)
            packs = []
            blocks = jnp.where(keep, 1.0, 0.0).astype(BF)
            for c in range(2):
                at = pl.ds(c * CH, CH)
                top = (mixg_v[half, at, lanes_at].astype(F32) * rden_v[half, at, lanes_at]).astype(BF)
                top_v[half, at, lanes_at] = top
                prod = top.astype(F32) * mix_v[half, at, lanes_at].astype(F32)
                high = prod.astype(BF)
                low = (prod - high.astype(F32)).astype(BF)
                bottom = -(dot_nn(high, blocks) + dot_nn(low, blocks))
                high = bottom.astype(BF)
                low = (bottom - high.astype(F32)).astype(BF)
                lane = lax.rem(lax.broadcasted_iota(jnp.int32, bottom.shape, 1), DH)
                bot_v[half, at, lanes_at] = jnp.where(
                    lane == 0, high, jnp.where(lane == 1, low, jnp.zeros_like(high))
                )
                query = qkv_v[half, 0, at, lanes_at]
                made = dot_tn(query, jnp.concatenate([top, high], axis=1))
                packs.append(jnp.where(keep, made[:, :PAIR], pltpu.roll(made[:, PAIR:], DH, 1)))
            local_v[half, p] = packs[1]
            lsend_v[half, p] = (packs[0] + packs[1]).astype(BF)

        across(lsend_v.at[half], lrecv_v.at[1 - half], 1 + half)

    tops(1)
    tops(0)
    ring(2)
    for load in loads[12:15]:
        load.wait()

    def attend_back(half):
        mask = causal_tile()
        earlier = 1.0 - here.mp.astype(F32)
        remote(
            lsend_v.at[1 - half], lrecv_v.at[half], xs_sem.at[2 - half], xr_sem.at[2 - half], here.across
        ).wait_recv()

        def body(p, c):
            lanes_at = aligned(p * PAIR, PAIR, PAIR)
            at = pl.ds(c * CH, CH)
            query = qkv_v[half, 0, at, lanes_at]
            key = qkv_v[half, 1, at, lanes_at]
            val = qkv_v[half, 2, at, lanes_at]
            top = top_v[half, at, lanes_at]
            bot = bot_v[half, at, lanes_at]
            lane = lax.rem(lax.broadcasted_iota(jnp.int32, val.shape, 1), DH)
            one = jnp.ones_like(val)
            zero = jnp.zeros_like(val)
            val_two = jnp.concatenate([val, jnp.where(lane < 2, one, zero)], axis=1)
            val_one = jnp.concatenate([val, jnp.where(lane == 0, one, zero)], axis=1)
            before = state_v[half, p].astype(F32)
            after = lrecv_v[half, p].astype(F32) * earlier
            if c == 1:
                key0 = qkv_v[half, 1, pl.ds(0, CH), lanes_at]
                val0 = qkv_v[half, 2, pl.ds(0, CH), lanes_at]
                made = dot_tn(key0, jnp.concatenate([val0, one], axis=1))
                before = before + jnp.where(keep, made[:, :PAIR], made[:, PAIR:])
            else:
                after = after + local_v[half, p]
            before = unpack_state(before).astype(BF)
            after = unpack_state(after).astype(BF)
            dq = dot_nt(jnp.concatenate([top, bot], axis=1), before)
            dk = dot_nt(val_one, after)
            dv = dot_nn(key, after[:, :PAIR])
            queries, keys, tops_, bots = split_heads(query), split_heads(key), split_heads(top), split_heads(bot)
            for head in range(2):
                score = jnp.where(mask, dot_nt(queries[head], key), 0.0).astype(BF)
                grad = dot_nt(jnp.concatenate([tops_[head], bots[head]], axis=1), val_two)
                grad = jnp.where(mask, grad, 0.0).astype(BF)
                dq = dq + dot_nn(grad, keys[head])
                dk = dk + dot_tn(grad, queries[head])
                dv = dv + dot_tn(score, tops_[head])
            dqkv_v[half, 0, at, lanes_at] = (dq * jnp.minimum(query.astype(F32), 1.0)).astype(BF)
            dqkv_v[half, 1, at, lanes_at] = (dk * jnp.minimum(key.astype(F32), 1.0)).astype(BF)
            dqkv_v[half, 2, at, lanes_at] = dv.astype(BF)

        for part in range(2):
            @pl.loop(part * 2, part * 2 + 2)
            def _(p):
                body(p, 0)
                body(p, 1)

            ring(2)

    def in_grads(half):
        for side, dst in ((their, gm_v), (here.core, ga_v)):
            cols = aligned(side * 512, 512, 512)
            for i in range(3):
                at = pl.ds(i * 512, 512)
                dst[half, at, :] = dot_tn(first_v[:, cols], dqkv_v[half, i]).astype(BF)
            if dst is gm_v:
                to_mate(gm_v.at[half], gr_v.at[half], 2 + half)
        ring(2)

    def add_rows(dst, src, rows, count):
        @pl.loop(0, count)
        def _(i):
            at = aligned(i * rows, rows, rows)
            dst[at, :] = (dst[at, :].astype(F32) + src[at, :].astype(F32)).astype(BF)

    def mate_arrival(half):
        remote(gm_v.at[half], gr_v.at[half], ms_sem.at[2 + half], mr_sem.at[2 + half], here.mate).wait_recv()
        add_rows(ga_v.at[half], gr_v.at[half], 128, 12)

    def mate_arrival_out(half):
        remote(om_v.at[half], or_v.at[half], ms_sem.at[half], mr_sem.at[half], here.mate).wait_recv()
        add_rows(oa_v.at[half], or_v.at[half], 128, 2)

    attend_back(1)
    mate_arrival_out(1)
    cross_o = across(oa_v.at[1], ox_v, 3)
    mate_arrival_out(0)
    in_grads(1)
    mate_arrival(1)
    cross_i = across(ga_v.at[1], gx_v, 4)
    attend_back(0)
    in_grads(0)
    mate_arrival(0)

    loads[15].wait()
    gain_one = gain_ref[0:1, :]

    @pl.loop(0, 4)
    def _(i):
        at = aligned(i * 128, 128, 128)
        grad = None
        for half in range(2):
            term = None
            for j in range(3):
                made = dot_nt(dqkv_v[half, j, at, :], win_v[half, pl.ds(j * 1024, 1024), :])
                term = made if term is None else term + made
            term = term.astype(BF).astype(F32)
            grad = term if grad is None else grad + term
        unit, inverse = row_norm(x_v[at, :].astype(F32))
        scaled = grad * gain_one
        centre = jnp.mean(scaled, axis=-1, keepdims=True)
        along = jnp.mean(scaled * unit, axis=-1, keepdims=True)
        mgf_v[at, :] = mgf_v[at, :] + inverse * (scaled - centre - unit * along)
        small_s[0:1, :] = small_s[0:1, :] + jnp.sum(grad * unit, axis=0, keepdims=True)
        small_s[2:3, :] = small_s[2:3, :] + jnp.sum(grad, axis=0, keepdims=True)

    out(mgf_v, gin_o)
    ring(2)
    small_s[4:5, pl.ds(0, PAIR)] = jnp.sum(stat_ref[1], axis=0, keepdims=True) * (1.0 / DH)
    count = len_ref[0].astype(F32) * (8.0 / 1024.0)
    small_s[5:6, :] = jnp.zeros((1, 1024), F32) + count
    small_s[6:7, pl.ds(0, PAIR)] = jnp.max(stat_ref[0], axis=0, keepdims=True)
    partners = [here.mate, here.across, y_mate, z_mate, z_far]

    def small_send(step):
        src = small_s if step == 0 else small_ref
        copy = remote(src, small_r.at[step], bs_sem.at[step], br_sem.at[step], partners[step])
        copy.start()
        return copy

    def small_step(copy, step):
        copy.wait()
        src = small_s if step == 0 else small_ref
        mine, theirs = src[...], small_r[step]
        row = lax.broadcasted_iota(jnp.int32, mine.shape, 0)
        small_ref[...] = jnp.where(row < 6, mine + theirs, jnp.maximum(mine, theirs))

    loads[16].wait()
    mlp.wait_recv()

    @pl.loop(0, 4)
    def _(i):
        at = aligned(i * 128, 128, 128)
        total = mid_v[at, :] + (blk_v[at, :].astype(F32) + mlpin_v[at, :].astype(F32))
        blk_v[at, :] = total.astype(BF)

    out(blk_v, out_o)
    for step in range(5):
        copy = small_send(step)
        ring(4)
        small_step(copy, step)
    cross_o.wait_recv()
    add_rows(oa_v.at[0], ox_v, 128, 2)
    while len(steps) > 8:
        ring(4)
    cross_i.wait_recv()
    add_rows(ga_v.at[0], gx_v, 128, 12)
    ring(4)
    for lane in (4, 5, 6, 7):
        lanes[lane].tick(0)
    ring(4)
    for t in range(1, 15):
        for lane in (4, 5, 6, 7):
            lanes[lane].tick(t)
    for lane in lanes:
        lane.finish()
    for copy in sends:
        copy.wait_send()
    for copy in outs:
        copy.wait()


def back(lengths, gain, bias, stat, part, pin, mid, x, dy, qkv, mix, rden, state, first, win, wino, wo, woo, mlp, dslab, uslab):
    vm = pltpu.VMEM
    dma = pltpu.SemaphoreType.DMA
    shapes = [
        ((2048, 1024), BF), ((1024, 2048), BF), ((3072, 512), BF), ((512, 1024), BF),
        ((512, 1024), BF), ((512, 1024), F32), ((8, 1024), F32),
    ]
    rows = (512, 1024)
    heads = (2, 512, 512)
    pack = (2, 4, PAIR, PAIR)
    vmem = pl.BlockSpec(memory_space=pltpu.VMEM)
    return pl.pallas_call(
        back_kernel,
        out_shape=[jax.ShapeDtypeStruct(s, d) for s, d in shapes],
        in_specs=[pl.BlockSpec(memory_space=pltpu.SMEM), vmem, vmem, vmem] + any_spec(17),
        out_specs=any_spec(6) + [vmem],
        scratch_shapes=[
            vm(rows, BF), vm(rows, BF), vm(rows, F32), vm(rows, BF), vm(rows, BF),
            vm((2, 3, 512, 512), BF), vm(heads, BF), vm(heads, F32), vm(pack, BF), vm(rows, BF),
            vm((2, 3072, 512), BF), vm((2, 512, 1024), BF),
            vm(rows, BF), vm(rows, BF), vm(rows, F32), vm(heads, BF), vm(heads, BF), vm(heads, BF),
            vm((2, 3, 512, 512), BF), vm(pack, F32), vm(pack, BF), vm(pack, BF),
            vm((1024, 1024), BF), vm((512, 2048), BF), vm((2, 7, 64, 1024), BF), vm((2, 7, 32, 2048), BF),
            vm((2, 1536, 512), BF), vm((2, 1536, 512), BF), vm((2, 1536, 512), BF), vm((1536, 512), BF),
            vm((2, 256, 1024), BF), vm((2, 256, 1024), BF), vm((2, 256, 1024), BF), vm((256, 1024), BF),
            vm((2, 7, 96, 512), BF), vm((2, 7, 16, 1024), BF),
            vm((8, 1024), F32), vm((5, 8, 1024), F32), vm(rows, BF),
            dma((17,)), dma((2,)), dma((5,)), dma((5,)), dma((4,)), dma((4,)), dma((5,)), dma((5,)),
            dma((8, 7)), dma((8, 7)), dma((8, 7)), dma((8, 7)), dma((8, 8)), dma((8, 8)), dma((8,)),
        ],
        compiler_params=pltpu.CompilerParams(
            collective_id=2, has_side_effects=True, vmem_limit_bytes=60 * 1024 * 1024
        ),
        name="back",
    )(lengths, gain, bias, stat, part, pin, mid, x, dy, qkv, mix, rden, state, first, win, wino, wo, woo, mlp, dslab, uslab)


def fast_device(
    block_in, lengths, input_weight, output_weight, up_weight, down_weight, norm_gain, norm_bias, cotangent
):
    x, dy = block_in[0], cotangent[0]
    win = input_weight.reshape(3072, 512)
    first, qkv, mix, rden, state, mid, sec, wino, woo, dyo, hg, stat = front(
        lengths, x, dy, win, output_weight, down_weight, norm_gain, norm_bias
    )
    part, pin, mlp, dslab, uslab = middle(sec, dy, dyo, hg, up_weight, down_weight)
    resd, resu, resi, reso, block_out, grad_in, small = back(
        lengths, norm_gain, norm_bias, stat, part, pin, mid, x, dy, qkv, mix, rden, state, first,
        win, wino, output_weight, woo, mlp, dslab, uslab,
    )
    input_grad = resi.reshape(2, 3, 512, 512).transpose(1, 0, 2, 3).reshape(3, 1024, 512).astype(F32)
    scaling = 1.0 / (DH * 1024)
    total = jnp.sum(small[4])
    count = jnp.sum(small[5])
    stats = jnp.stack([jnp.max(small[6]) * scaling, total / count * scaling])
    return (
        block_out[None], grad_in[None], input_grad, reso.astype(F32), resu.astype(F32), resd.astype(F32),
        small[0:2], small[2:4], stats,
    )


def fits_fast(mesh, block_shape):
    return dict(mesh.shape) == {"dp": 16, "mp": 2} and tuple(block_shape) == (16, 1024, 1024)


def solution(mesh):
    in_specs = (
        P("dp", "mp", None),
        P("dp"),
        P(None, None, "mp"),
        P("mp", None),
        P(None, "mp"),
        P("mp", None),
        P(),
        P(),
        P("dp", "mp", None),
    )
    out_specs = (
        P("dp", "mp", None),
        P("dp", "mp", None),
        P(None, None, "mp"),
        P("mp", None),
        P(None, "mp"),
        P("mp", None),
        P(),
        P(),
        P(),
    )

    def whole(*arrays):
        body = fast_device if fits_fast(mesh, arrays[0].shape) else per_device
        return jax.shard_map(
            body, mesh=mesh, in_specs=in_specs, out_specs=out_specs, check_vma=False
        )(*arrays)

    return whole
```

```python
from functools import partial

import jax
import jax.numpy as jnp
from jax import lax
from jax.experimental import pallas as pl
from jax.experimental.pallas import tpu as pltpu
from jax.sharding import PartitionSpec as P

DH = 64
BLK = 512


EPSILON = 1e-05
PRECISE = lax.Precision.HIGHEST


def combined_all(part, axis, combine):
    gathered = jax.tree.map(lambda a: lax.all_gather(a, axis), part)

    def take(source):
        return jax.tree.map(lambda a: lax.dynamic_index_in_dim(a, source, 0, False), gathered)

    return lax.fori_loop(
        1, lax.axis_size(axis), lambda source, state: combine(state, take(source)), take(0)
    )


def feature(values):
    return jax.nn.elu(values) + 1.0


def feature_slope(values):
    return jnp.where(values > 0, 1.0, jnp.exp(values))


def normalise(inputs, gain_row, bias_row):
    centre = jnp.mean(inputs, axis=-1, keepdims=True)
    centred = inputs - centre
    spread = jnp.mean(centred * centred, axis=-1, keepdims=True)
    inverse = lax.rsqrt(spread + EPSILON)
    unit_rows = centred * inverse
    return (unit_rows * gain_row + bias_row, unit_rows, inverse)


def normalise_back(grad_rows, unit_rows, inverse, gain_row):
    scaled = grad_rows * gain_row
    centre = jnp.mean(scaled, axis=-1, keepdims=True)
    along = jnp.mean(scaled * unit_rows, axis=-1, keepdims=True)
    input_grad = inverse * (scaled - centre - unit_rows * along)
    return (input_grad, jnp.sum(grad_rows * unit_rows, axis=0), jnp.sum(grad_rows, axis=0))


def exclusive(stacked):
    running = jnp.cumsum(stacked, axis=0)
    return jnp.concatenate([jnp.zeros_like(running[:1]), running[:-1]], axis=0)


def later(stacked):
    return exclusive(stacked[::-1])[::-1]


def unchanged(carried):
    return carried


def causal_mask():
    return jnp.tril(jnp.ones((BLK, BLK), jnp.float32))


def attend_forward(query_map, key_map, values, crop_len):
    slot_len, head_count, depth = query_map.shape
    block_count = slot_len // BLK
    block_shape = (block_count, BLK, head_count, depth)
    block_q = query_map.reshape(block_shape)
    block_k = key_map.reshape(block_shape)
    block_v = values.reshape(block_shape)
    memory = exclusive(
        jnp.einsum("nihd,nihe->nhde", block_k, block_v, preferred_element_type=jnp.float32)
    )
    key_total = exclusive(jnp.sum(block_k.astype(jnp.float32), axis=1))
    causal = causal_mask()
    block_starts = jnp.arange(block_count, dtype=jnp.int32) * BLK

    def one_block(block_item):
        query_b, key_b, value_b, memory_b, total_b, start_b = block_item
        query_f = query_b.astype(jnp.float32)
        numerator = jnp.einsum("ihd,hde->ihe", query_f, memory_b, precision=PRECISE)
        denominator = jnp.einsum("ihd,hd->ih", query_f, total_b, precision=PRECISE)

        def inside(partial_sums):
            value_part, weight_part = partial_sums
            scores = (
                jnp.einsum("ihd,jhd->hij", query_b, key_b, preferred_element_type=jnp.float32)
                * causal
            )
            value_part = value_part + jnp.einsum(
                "hij,jhd->ihd",
                scores.astype(jnp.bfloat16),
                value_b,
                preferred_element_type=jnp.float32,
            )
            weight_part = weight_part + jnp.sum(scores, axis=-1).T
            return (value_part, weight_part)

        numerator, denominator = lax.cond(
            start_b < crop_len, inside, unchanged, (numerator, denominator)
        )
        return (numerator / denominator[..., None], denominator)

    attended, denoms = lax.map(
        one_block, (block_q, block_k, block_v, memory, key_total, block_starts)
    )
    return (
        attended.reshape(slot_len, head_count, depth),
        denoms.reshape(slot_len, head_count),
        memory,
        key_total,
    )


def attend_backward(
    grad_attn, attended, denoms, query_map, key_map, values, memory, key_total, crop_len
):
    slot_len, head_count, depth = query_map.shape
    block_count = slot_len // BLK
    block_shape = (block_count, BLK, head_count, depth)
    top_all = (grad_attn / denoms[..., None]).reshape(block_shape)
    bottom_all = (-jnp.sum(grad_attn * attended, axis=-1) / denoms).reshape(
        block_count, BLK, head_count
    )
    query_full = query_map.astype(jnp.float32).reshape(block_shape)
    memory_later = later(jnp.einsum("nihd,nihe->nhde", query_full, top_all, precision=PRECISE))
    total_later = later(jnp.einsum("nihd,nih->nhd", query_full, bottom_all, precision=PRECISE))
    causal = causal_mask()
    block_starts = jnp.arange(block_count, dtype=jnp.int32) * BLK

    def one_block(block_item):
        (
            query_b,
            key_b,
            value_b,
            memory_b,
            total_b,
            later_memory,
            later_total,
            top_grad,
            bottom_grad,
            start_b,
        ) = block_item
        value_f = value_b.astype(jnp.float32)
        key_f = key_b.astype(jnp.float32)
        query_sum = (
            jnp.einsum("ihe,hde->ihd", top_grad, memory_b, precision=PRECISE)
            + bottom_grad[..., None] * total_b[None]
        )
        key_sum = (
            jnp.einsum("jhe,hde->jhd", value_f, later_memory, precision=PRECISE) + later_total[None]
        )
        value_sum = jnp.einsum("jhd,hde->jhe", key_f, later_memory, precision=PRECISE)

        def inside(partial_grads):
            query_acc, key_acc, value_acc = partial_grads
            scores = (
                jnp.einsum("ihd,jhd->hij", query_b, key_b, preferred_element_type=jnp.float32)
                * causal
            )
            score_grad = (
                (
                    jnp.einsum("ihe,jhe->hij", top_grad, value_f, precision=PRECISE)
                    + bottom_grad.T[:, :, None]
                )
                * causal
            ).astype(jnp.bfloat16)
            query_acc = query_acc + jnp.einsum(
                "hij,jhd->ihd", score_grad, key_b, preferred_element_type=jnp.float32
            )
            key_acc = key_acc + jnp.einsum(
                "hij,ihd->jhd", score_grad, query_b, preferred_element_type=jnp.float32
            )
            rounded_scores = scores.astype(jnp.bfloat16).astype(jnp.float32)
            value_acc = value_acc + jnp.einsum(
                "hij,ihe->jhe", rounded_scores, top_grad, precision=PRECISE
            )
            return (query_acc, key_acc, value_acc)

        return lax.cond(start_b < crop_len, inside, unchanged, (query_sum, key_sum, value_sum))

    query_grad, key_grad, value_grad = lax.map(
        one_block,
        (
            query_map.reshape(block_shape),
            key_map.reshape(block_shape),
            values.reshape(block_shape),
            memory,
            key_total,
            memory_later,
            total_later,
            top_all,
            bottom_all,
            block_starts,
        ),
    )
    return (
        query_grad.reshape(slot_len, head_count, depth),
        key_grad.reshape(slot_len, head_count, depth),
        value_grad.reshape(slot_len, head_count, depth),
    )


def combine_stats(first_part, second_part):
    return (
        first_part[0] + second_part[0],
        first_part[1] + second_part[1],
        first_part[2] + second_part[2],
        first_part[3] + second_part[3],
        jnp.maximum(first_part[4], second_part[4]),
    )


def per_device(
    block_in,
    lengths,
    input_weight,
    output_weight,
    up_weight,
    down_weight,
    norm_gain,
    norm_bias,
    cotangent,
):
    group_count = lax.axis_size("mp")
    rows_here = block_in.shape[1]
    slot_len = rows_here * group_count
    local_width = output_weight.shape[0]
    head_count = local_width // DH
    crop_len = lengths[0]
    valid_mask = (jnp.arange(slot_len, dtype=jnp.int32) < crop_len).astype(jnp.float32)
    own_rows = block_in[0].astype(jnp.float32)
    first_norm, unit_one, inverse_one = normalise(own_rows, norm_gain[0], norm_bias[0])
    first_rows = lax.all_gather(first_norm.astype(jnp.bfloat16), "mp", axis=0, tiled=True)
    projected = jnp.einsum(
        "rd,cdk->rck", first_rows, input_weight, preferred_element_type=jnp.float32
    ).reshape(slot_len, 3, head_count, DH)
    query = projected[:, 0]
    key_raw = projected[:, 1]
    query_map = feature(query).astype(jnp.bfloat16)
    key_map = (feature(key_raw) * valid_mask[:, None, None]).astype(jnp.bfloat16)
    values = projected[:, 2].astype(jnp.bfloat16)
    attended, denoms, memory, key_total = attend_forward(query_map, key_map, values, crop_len)
    mixed = attended.reshape(slot_len, local_width).astype(jnp.bfloat16)
    part_rows = mixed
    branch_out = lax.psum_scatter(
        jnp.dot(part_rows, output_weight, preferred_element_type=jnp.float32).astype(jnp.bfloat16),
        "mp",
        scatter_dimension=0,
        tiled=True,
    ).astype(jnp.float32)
    middle = own_rows + branch_out
    second_norm, unit_two, inverse_two = normalise(middle, norm_gain[1], norm_bias[1])
    second_rows = lax.all_gather(second_norm.astype(jnp.bfloat16), "mp", axis=0, tiled=True)
    hidden_in = jnp.dot(second_rows, up_weight, preferred_element_type=jnp.float32)
    hidden = jax.nn.gelu(hidden_in, approximate=True).astype(jnp.bfloat16)
    part_rows = hidden
    mlp_out = lax.psum_scatter(
        jnp.dot(part_rows, down_weight, preferred_element_type=jnp.float32).astype(jnp.bfloat16),
        "mp",
        scatter_dimension=0,
        tiled=True,
    ).astype(jnp.float32)
    block_out = (middle + mlp_out).astype(jnp.bfloat16)[None]
    grad_out = cotangent[0]
    grad_rows = lax.all_gather(grad_out, "mp", axis=0, tiled=True)
    down_grad = jnp.einsum("rf,rd->fd", hidden, grad_rows, preferred_element_type=jnp.float32)
    hidden_grad = jnp.einsum(
        "rd,fd->rf", grad_rows, down_weight, preferred_element_type=jnp.float32
    )
    unused_out, gelu_back = jax.vjp(partial(jax.nn.gelu, approximate=True), hidden_in)
    inner_grad = gelu_back(hidden_grad)[0].astype(jnp.bfloat16)
    up_grad = jnp.einsum("rd,rf->df", second_rows, inner_grad, preferred_element_type=jnp.float32)
    part_rows = inner_grad
    second_grad = lax.psum_scatter(
        jnp.einsum("rf,df->rd", part_rows, up_weight, preferred_element_type=jnp.float32).astype(
            jnp.bfloat16
        ),
        "mp",
        scatter_dimension=0,
        tiled=True,
    ).astype(jnp.float32)
    back_two, gain_two, bias_two = normalise_back(second_grad, unit_two, inverse_two, norm_gain[1])
    middle_grad = grad_out.astype(jnp.float32) + back_two
    middle_low = middle_grad.astype(jnp.bfloat16)
    middle_full = lax.all_gather(middle_low, "mp", axis=0, tiled=True)
    mixed_grad = jnp.einsum(
        "rd,kd->rk", middle_full, output_weight, preferred_element_type=jnp.float32
    ).astype(jnp.bfloat16)
    output_grad = jnp.einsum("rk,rd->kd", mixed, middle_full, preferred_element_type=jnp.float32)
    grad_attn = mixed_grad.astype(jnp.float32).reshape(slot_len, head_count, DH)
    query_grad, key_grad, value_grad = attend_backward(
        grad_attn, attended, denoms, query_map, key_map, values, memory, key_total, crop_len
    )
    query_low = (query_grad * feature_slope(query)).astype(jnp.bfloat16)
    key_low = (key_grad * valid_mask[:, None, None] * feature_slope(key_raw)).astype(jnp.bfloat16)
    value_low = value_grad.astype(jnp.bfloat16)
    qkv_grad = jnp.stack([query_low, key_low, value_low], axis=1).reshape(slot_len, 3, local_width)
    input_grad = jnp.einsum("rd,rck->cdk", first_rows, qkv_grad, preferred_element_type=jnp.float32)
    part_rows = qkv_grad
    first_grad = lax.psum_scatter(
        jnp.einsum(
            "rck,cdk->rd", part_rows, input_weight, preferred_element_type=jnp.float32
        ).astype(jnp.bfloat16),
        "mp",
        scatter_dimension=0,
        tiled=True,
    ).astype(jnp.float32)
    back_one, gain_one, bias_one = normalise_back(first_grad, unit_one, inverse_one, norm_gain[0])
    grad_input = (middle_grad + back_one)[None]
    input_grad, output_grad, up_grad, down_grad = (
        lax.psum(input_grad.astype(jnp.bfloat16), "dp").astype(jnp.float32),
        lax.psum(output_grad.astype(jnp.bfloat16), "dp").astype(jnp.float32),
        lax.psum(up_grad.astype(jnp.bfloat16), "dp").astype(jnp.float32),
        lax.psum(down_grad.astype(jnp.bfloat16), "dp").astype(jnp.float32),
    )
    kept_denoms = jnp.where(valid_mask[:, None] > 0, denoms, 0.0)
    den_total = jnp.sum(kept_denoms)
    den_count = crop_len.astype(jnp.float32) * head_count
    den_peak = jnp.max(kept_denoms)
    gain_grad, bias_grad, den_total, den_count, den_peak = combined_all(
        (
            jnp.stack([gain_one, gain_two]),
            jnp.stack([bias_one, bias_two]),
            den_total,
            den_count,
            den_peak,
        ),
        ("dp", "mp"),
        combine_stats,
    )
    scaling = DH * slot_len
    denominator_stats = jnp.stack([den_peak / scaling, den_total / den_count / scaling])
    return (
        block_out,
        grad_input,
        input_grad,
        output_grad,
        up_grad,
        down_grad,
        gain_grad,
        bias_grad,
        denominator_stats,
    )

MESH = pl.DeviceIdType.MESH
BF = jnp.bfloat16
F32 = jnp.float32
ROWS = 512
CH = 256
PAIR = 128


def dot_nn(a, b):
    return lax.dot_general(a, b, (((1,), (0,)), ((), ())), preferred_element_type=F32)


def dot_nt(a, b):
    return lax.dot_general(a, b, (((1,), (1,)), ((), ())), preferred_element_type=F32)


def dot_tn(a, b):
    return lax.dot_general(a, b, (((0,), (0,)), ((), ())), preferred_element_type=F32)


class Place:
    def __init__(self):
        dp = lax.axis_index("dp")
        mp = lax.axis_index("mp")
        self.dp, self.mp = dp, mp
        self.core = lax.rem(dp, 2)
        chip = dp // 2
        y = lax.rem(chip, 2)
        z = chip // 2
        self.r = z + y * (7 - 2 * z)
        self.across = (dp, 1 - mp)
        self.mate = (dp + 1 - 2 * self.core, mp)
        self.next = self.at(lax.rem(self.r + 1, 8))
        self.prev = self.at(lax.rem(self.r + 7, 8))

    def at(self, r):
        y = r // 4
        z = r + y * (7 - 2 * r)
        return ((z * 2 + y) * 2 + self.core, self.mp)

    def partners(self):
        return [self.across, self.mate, self.next, self.prev]


def greet(partners):
    barrier = pltpu.get_barrier_semaphore()
    for partner in partners:
        pl.semaphore_signal(barrier, inc=1, device_id=partner, device_id_type=MESH)
    pl.semaphore_wait(barrier, len(partners))


def remote(src, dst, send_sem, recv_sem, device):
    return pltpu.make_async_remote_copy(
        src_ref=src, dst_ref=dst, send_sem=send_sem, recv_sem=recv_sem,
        device_id=device, device_id_type=MESH,
    )


def aligned(start, size, unit):
    return pl.ds(pl.multiple_of(start, unit), size)


def lane_head(shape):
    return lax.broadcasted_iota(jnp.int32, shape, len(shape) - 1) < DH


def same_head():
    row = lax.broadcasted_iota(jnp.int32, (PAIR, PAIR), 0) < DH
    lane = lax.broadcasted_iota(jnp.int32, (PAIR, PAIR), 1) < DH
    return row == lane


def causal_tile():
    row = lax.broadcasted_iota(jnp.int32, (CH, CH), 0)
    col = lax.broadcasted_iota(jnp.int32, (CH, CH), 1)
    return row >= col


def unpack_state(packed):
    keep = same_head()
    zero = jnp.zeros_like(packed)
    return jnp.concatenate(
        [jnp.where(keep, packed, zero), jnp.where(keep, pltpu.roll(packed, DH, 1), zero)], axis=1
    )


def split_heads(pair):
    first = lane_head(pair.shape)
    zero = jnp.zeros_like(pair)
    return jnp.where(first, pair, zero), jnp.where(first, zero, pair)


def row_norm(rows):
    centre = jnp.mean(rows, axis=-1, keepdims=True)
    centred = rows - centre
    inverse = lax.rsqrt(jnp.mean(centred * centred, axis=-1, keepdims=True) + EPSILON)
    return centred * inverse, inverse


def front_kernel(
    len_ref, x_hbm, dy_hbm, win_hbm, wo_hbm, wdn_hbm, gain_ref, bias_ref,
    first_o, qkv_o, mix_o, rden_o, state_o, mid_o, sec_o, wino_o, woo_o, dyo_o, hg_o, stat_ref,
    x_v, dy_v, win_v, wino_v, wo_v, woo_v, wdn_v, first_v, qkv_v, num_v, den_v, mix_v, mid_v, sec_v, hg_v,
    local_v, ssend_v, srecv_v, state_v,
    in_sem, out_sem, xs_sem, xr_sem, ring_s, ring_r, mate_s, mate_r,
):
    here = Place()
    loads = [
        (x_hbm, x_v), (win_hbm, win_v), (dy_hbm, dy_v.at[0]), (wdn_hbm, wdn_v), (wo_hbm, wo_v),
    ]
    loads = [pltpu.make_async_copy(a, b, in_sem.at[i]) for i, (a, b) in enumerate(loads)]
    for load in loads:
        load.start()
    greet(here.partners())
    piece = here.r * 2 + here.core
    parts = ((win_hbm, wino_v, 192), (wo_hbm, woo_v, 32))
    cross = []
    for i, (src, dst, rows) in enumerate(parts):
        at = aligned(piece * rows, rows, 32)
        cross.append(remote(src.at[at], dst.at[at], xs_sem.at[i], xr_sem.at[i], here.across))
    cross.append(remote(dy_hbm, dy_v.at[1], xs_sem.at[2], xr_sem.at[2], here.across))
    for copy in cross:
        copy.start()

    gain = gain_ref[0:1, :]
    bias = bias_ref[0:1, :]
    sends = []
    outs = []

    def out(src, dst):
        copy = pltpu.make_async_copy(src, dst, out_sem.at[len(outs)])
        copy.start()
        outs.append(copy)

    def rows_of(array, r, core, half=None):
        rows = parts[array][2]
        start = (r * 2 + core) * rows
        if half is None:
            return aligned(start, rows, 32)
        return aligned(start + half * (rows // 2), rows // 2, 16)

    def to_mate(array, slot, r, half=None):
        at = rows_of(array, r, here.core, half)
        dst = parts[array][1]
        copy = remote(dst.at[at], dst.at[at], mate_s.at[array, slot], mate_r.at[array, slot], here.mate)
        copy.start()
        sends.append(copy)

    def to_ring(array, way, step):
        dst = parts[array][1]
        back = step if way == 0 else 8 - step
        at = rows_of(array, lax.rem(here.r + 8 - back, 8), here.core, way if step == 3 else None)
        copy = remote(
            dst.at[at], dst.at[at], ring_s.at[array, way, step], ring_r.at[array, way, step],
            here.next if way == 0 else here.prev,
        )
        copy.start()
        sends.append(copy)

    def ring_wait(array, way, step):
        dst = parts[array][1]
        back = step + 1 if way == 0 else 7 - step
        owner = lax.rem(here.r + 8 - back, 8)
        half = way if step == 3 else None
        at = rows_of(array, owner, here.core, half)
        remote(
            dst.at[at], dst.at[at], ring_s.at[array, way, step], ring_r.at[array, way, step], here.next
        ).wait_recv()
        return owner, half

    def hop(step):
        for array in (0, 1):
            if step == 0:
                cross[array].wait_recv()
                for way in (0, 1):
                    to_ring(array, way, 0)
                to_mate(array, 0, here.r)
                continue
            for way in (0, 1):
                owner, half = ring_wait(array, way, step - 1)
                if step < 4:
                    to_ring(array, way, step)
                to_mate(array, 1 + 2 * (step - 1) + way, owner, half)

    def mate_wait(array):
        dst = parts[array][1]
        other = 1 - here.core
        for slot in range(9):
            if slot == 0:
                at = rows_of(array, here.r, other)
            else:
                step, way = (slot - 1) // 2, (slot - 1) % 2
                back = step + 1 if way == 0 else 7 - step
                at = rows_of(array, lax.rem(here.r + 8 - back, 8), other, way if step == 3 else None)
            remote(
                dst.at[at], dst.at[at], mate_s.at[array, slot], mate_r.at[array, slot], here.mate
            ).wait_recv()

    loads[0].wait()

    @pl.loop(0, ROWS // 128)
    def _(i):
        at = aligned(i * 128, 128, 128)
        unit, _ = row_norm(x_v[at, :].astype(F32))
        first_v[at, :] = (unit * gain + bias).astype(BF)

    out(first_v, first_o)
    crop_len = len_ref[0]

    def project(half, weights):
        @pl.loop(0, 2)
        def _(c):
            at = aligned(c * CH, CH, CH)
            rows = first_v[at, :]
            for i in range(3):
                raw = dot_nn(rows, weights[pl.ds(i * 1024, 1024), :])
                if i < 2:
                    raw = jnp.where(raw > 0, raw + 1.0, jnp.exp(jnp.minimum(raw, 0.0)))
                if i == 1:
                    place = lax.broadcasted_iota(jnp.int32, raw.shape, 0) + (here.mp * ROWS + c * CH)
                    raw = jnp.where(place < crop_len, raw, 0.0)
                qkv_v[half, i, at, :] = raw.astype(BF)

    def states(half):
        keep = same_head()

        @pl.loop(0, 4)
        def _(p):
            lanes = aligned(p * PAIR, PAIR, PAIR)
            total = None
            for c in range(2):
                keys = qkv_v[half, 1, pl.ds(c * CH, CH), lanes]
                vals = qkv_v[half, 2, pl.ds(c * CH, CH), lanes]
                made = dot_tn(keys, jnp.concatenate([vals, jnp.ones_like(vals)], axis=1))
                packed = jnp.where(keep, made[:, :PAIR], made[:, PAIR:])
                if c == 0:
                    local_v[half, p] = packed
                    total = packed
                else:
                    ssend_v[half, p] = (total + packed).astype(BF)

        copy = remote(
            ssend_v.at[half], srecv_v.at[1 - half], xs_sem.at[3 + half], xr_sem.at[4 - half], here.across
        )
        copy.start()
        sends.append(copy)

    def inside(half):
        mask = causal_tile()

        @pl.loop(0, 8)
        def _(n):
            p = n // 2
            c = lax.rem(n, 2)
            lanes = aligned(p * PAIR, PAIR, PAIR)
            at = aligned(c * CH, CH, CH)
            query = qkv_v[half, 0, at, lanes]
            key = qkv_v[half, 1, at, lanes]
            val = qkv_v[half, 2, at, lanes]
            first = lane_head(val.shape)
            one = jnp.ones_like(val)
            zero = jnp.zeros_like(val)
            sums = None
            for head, part in enumerate(split_heads(query)):
                score = jnp.where(mask, dot_nt(part, key), 0.0).astype(BF)
                mine = first if head == 0 else jnp.logical_not(first)
                right = jnp.concatenate([jnp.where(mine, val, zero), jnp.where(mine, one, zero)], axis=1)
                term = dot_nn(score, right)
                sums = term if sums is None else sums + term
            num_v[at, lanes] = sums[:, :PAIR]
            den_v[half, at, lanes] = sums[:, PAIR:]

    def finish(half):
        flag = here.mp.astype(F32)

        @pl.loop(0, 8)
        def _(n):
            p = n // 2
            c = lax.rem(n, 2)
            lanes = aligned(p * PAIR, PAIR, PAIR)
            at = aligned(c * CH, CH, CH)
            query = qkv_v[half, 0, at, lanes]
            before = srecv_v[half, p].astype(F32) * flag
            state_v[half, p] = before.astype(BF)
            before = before + local_v[half, p] * c.astype(F32)
            term = dot_nn(query, unpack_state(before).astype(BF))
            num = num_v[at, lanes] + term[:, :PAIR]
            den = den_v[half, at, lanes] + term[:, PAIR:]
            inverse = 1.0 / den
            den_v[half, at, lanes] = inverse
            mix_v[half, at, lanes] = (num * inverse).astype(BF)
            place = lax.broadcasted_iota(jnp.int32, den.shape, 0) + (here.mp * ROWS + c * CH)
            kept = jnp.where(place < crop_len, den, 0.0).reshape(CH // 8, 8, PAIR)
            stat_ref[0] = jnp.maximum(stat_ref[0], jnp.max(kept, axis=0))
            stat_ref[1] = stat_ref[1] + jnp.sum(kept, axis=0)

    def hidden_grad(side):
        @pl.loop(0, 2)
        def _(j):
            cols = aligned(j * 1024, 1024, 1024)
            hg_v[pl.ds(side * ROWS, ROWS), cols] = dot_nt(dy_v[side], wdn_v[cols, :]).astype(BF)

    stat_ref[...] = jnp.zeros_like(stat_ref)
    loads[1].wait()
    project(0, win_v)
    hop(0)
    states(0)
    inside_own = inside(0)
    hop(1)
    loads[2].wait()
    loads[3].wait()
    hidden_grad(0)
    hop(2)
    cross[2].wait_recv()
    hop(3)
    hidden_grad(1)
    out(hg_v, hg_o)
    out(dy_v.at[1], dyo_o)
    hop(4)
    mate_wait(0)
    out(wino_v, wino_o)
    mid_v[:, pl.ds(0, 512)] = num_v[...]
    project(1, wino_v)
    states(1)
    inside(1)
    remote(ssend_v.at[0], srecv_v.at[1], xs_sem.at[3], xr_sem.at[4], here.across).wait_recv()
    finish(1)
    num_v[...] = mid_v[:, pl.ds(0, 512)]
    remote(ssend_v.at[1], srecv_v.at[0], xs_sem.at[4], xr_sem.at[3], here.across).wait_recv()
    finish(0)
    out(qkv_v, qkv_o)
    out(den_v, rden_o)
    out(mix_v, mix_o)
    out(state_v, state_o)
    mate_wait(1)
    out(woo_v, woo_o)
    loads[4].wait()
    gain_two = gain_ref[1:2, :]
    bias_two = bias_ref[1:2, :]

    @pl.loop(0, 2)
    def _(c):
        at = aligned(c * CH, CH, CH)
        own = dot_nn(mix_v[0, at, :], wo_v[...]).astype(BF).astype(F32)
        other = dot_nn(mix_v[1, at, :], woo_v[...]).astype(BF).astype(F32)
        middle = x_v[at, :].astype(F32) + (own + other)
        mid_v[at, :] = middle
        unit, _ = row_norm(middle)
        sec_v[at, :] = (unit * gain_two + bias_two).astype(BF)

    out(mid_v, mid_o)
    out(sec_v, sec_o)
    for copy in cross + sends:
        copy.wait_send()
    for copy in outs:
        copy.wait()


def any_spec(count):
    return [pl.BlockSpec(memory_space=pl.ANY)] * count


def front(lengths, x_rows, dy_rows, win, wo, wdn, gain, bias):
    vm = pltpu.VMEM
    shapes = [
        ((512, 1024), BF), ((2, 3, 512, 512), BF), ((2, 512, 512), BF), ((2, 512, 512), F32),
        ((2, 4, PAIR, PAIR), BF), ((512, 1024), F32), ((512, 1024), BF), ((3072, 512), BF),
        ((512, 1024), BF), ((512, 1024), BF), ((1024, 2048), BF), ((2, 8, PAIR), F32),
    ]
    dma = pltpu.SemaphoreType.DMA
    return pl.pallas_call(
        front_kernel,
        out_shape=[jax.ShapeDtypeStruct(s, d) for s, d in shapes],
        in_specs=[pl.BlockSpec(memory_space=pltpu.SMEM)] + any_spec(5)
        + [pl.BlockSpec(memory_space=pltpu.VMEM)] * 2,
        out_specs=any_spec(11) + [pl.BlockSpec(memory_space=pltpu.VMEM)],
        scratch_shapes=[
            vm((512, 1024), BF), vm((2, 512, 1024), BF), vm((3072, 512), BF), vm((3072, 512), BF),
            vm((512, 1024), BF), vm((512, 1024), BF), vm((2048, 1024), BF), vm((512, 1024), BF),
            vm((2, 3, 512, 512), BF), vm((512, 512), F32), vm((2, 512, 512), F32), vm((2, 512, 512), BF),
            vm((512, 1024), F32), vm((512, 1024), BF), vm((1024, 2048), BF),
            vm((2, 4, PAIR, PAIR), F32), vm((2, 4, PAIR, PAIR), BF), vm((2, 4, PAIR, PAIR), BF),
            vm((2, 4, PAIR, PAIR), BF),
            dma((5,)), dma((12,)), dma((5,)), dma((5,)), dma((2, 2, 4)), dma((2, 2, 4)),
            dma((2, 9)), dma((2, 9)),
        ],
        compiler_params=pltpu.CompilerParams(
            collective_id=0, has_side_effects=True, vmem_limit_bytes=58 * 1024 * 1024
        ),
        name="front",
    )(lengths, x_rows, dy_rows, win, wo, wdn, gain, bias)


GELU_A = 0.7978845608028654
GELU_B = 0.044715


def gelu_pair(v):
    square = v * v
    t = jnp.tanh(GELU_A * v * (1.0 + GELU_B * square))
    half = 0.5 * (1.0 + t)
    slope = half + (0.5 * GELU_A) * v * (1.0 - t * t) * (1.0 + (3.0 * GELU_B) * square)
    return v * half, slope


def middle_kernel(
    sec_hbm, dy_hbm, dyo_hbm, hg_hbm, wup_hbm, wdn_hbm,
    part_o, pin_o, mlp_o, dslab_o, uslab_o,
    sec_v, dy_v, hg_v, wup_v, wdn_v, hid_v, part_v, send_v, pin_v, mlp_v,
    dsend_v, drecv_v, dslab_v, usend_v, urecv_v, uslab_v,
    in_sem, out_sem, xs_sem, xr_sem, ms_sem, mr_sem,
):
    here = Place()
    own = pl.ds(0, ROWS)
    other = pl.ds(ROWS, ROWS)
    loads = [
        (sec_hbm, sec_v.at[own]), (wup_hbm, wup_v), (hg_hbm, hg_v), (wdn_hbm, wdn_v),
        (dy_hbm, dy_v.at[own]), (dyo_hbm, dy_v.at[other]),
    ]
    loads = [pltpu.make_async_copy(a, b, in_sem.at[i]) for i, (a, b) in enumerate(loads)]
    for load in loads:
        load.start()
    greet([here.across, here.mate])
    sends = []
    outs = []

    def out(src, dst):
        copy = pltpu.make_async_copy(src, dst, out_sem.at[len(outs)])
        copy.start()
        outs.append(copy)

    def across(src, dst, slot):
        copy = remote(src, dst, xs_sem.at[slot], xr_sem.at[slot], here.across)
        copy.start()
        sends.append(copy)
        return copy

    ahead = [
        across(sec_hbm.at[pl.ds(c * CH, CH)], sec_v.at[pl.ds(ROWS + c * CH, CH)], c) for c in range(2)
    ]

    def up(chunk):
        rows = pl.ds(chunk * CH, CH)

        @pl.loop(0, 4)
        def _(j):
            cols = aligned(j * 512, 512, 512)
            raw = dot_nn(sec_v[rows, :], wup_v[:, cols])
            value, slope = gelu_pair(raw)
            hid_v[rows, cols] = value.astype(BF)
            hg_v[rows, cols] = (hg_v[rows, cols].astype(F32) * slope).astype(BF)

    def back(chunk, dst):
        dst[...] = dot_nt(hg_v[pl.ds(chunk * CH, CH), :], wup_v[...]).astype(BF)

    loads[0].wait()
    loads[1].wait()
    loads[2].wait()
    for c in range(2):
        up(c)
        back(c, part_v.at[pl.ds(c * CH, CH)])
    out(part_v, part_o)
    for c in range(2):
        ahead[c].wait_recv()
        up(2 + c)
        rows = pl.ds(c * CH, CH)
        back(2 + c, send_v.at[rows])
        across(send_v.at[rows], pin_v.at[rows], 2 + c)
    for load in loads[3:]:
        load.wait()
    their = 1 - here.core

    def down_grad(half, dst, plus):
        @pl.loop(0, 2)
        def _(i):
            cols = aligned(half * 1024 + i * 512, 512, 512)
            at = aligned(i * 512, 512, 512)
            made = dot_tn(hid_v[:, cols], dy_v[...])
            if plus is not None:
                made = made + plus[at, :].astype(F32)
            dst[at, :] = made.astype(BF)

    def up_grad(half, dst, plus):
        @pl.loop(0, 2)
        def _(i):
            cols = aligned(half * 512, 512, 512)
            at = aligned(i * 1024, 1024, 1024)
            made = dot_tn(sec_v[:, cols], hg_v[:, at])
            if plus is not None:
                made = made + plus[:, at].astype(F32)
            dst[:, at] = made.astype(BF)

    def to_mate(src, dst, slot):
        copy = remote(src, dst, ms_sem.at[slot], mr_sem.at[slot], here.mate)
        copy.start()
        sends.append(copy)
        return copy

    down_grad(their, dsend_v, None)
    to_d = to_mate(dsend_v, drecv_v, 0)
    up_grad(their, usend_v, None)
    to_u = to_mate(usend_v, urecv_v, 1)

    @pl.loop(0, 2)
    def _(i):
        rows = aligned(i * ROWS, ROWS, ROWS)
        mlp_v[rows, :] = dot_nn(hid_v[rows, :], wdn_v[...]).astype(BF)

    out(mlp_v, mlp_o)
    to_d.wait_recv()
    down_grad(here.core, dslab_v, drecv_v)
    out(dslab_v, dslab_o)
    to_u.wait_recv()
    up_grad(here.core, uslab_v, urecv_v)
    out(uslab_v, uslab_o)
    for c in range(2):
        rows = pl.ds(c * CH, CH)
        remote(send_v.at[rows], pin_v.at[rows], xs_sem.at[2 + c], xr_sem.at[2 + c], here.across).wait_recv()
    out(pin_v, pin_o)
    for copy in sends:
        copy.wait_send()
    for copy in outs:
        copy.wait()


def middle(sec, dy, dyo, hg, wup, wdn):
    vm = pltpu.VMEM
    dma = pltpu.SemaphoreType.DMA
    shapes = [
        ((512, 1024), BF), ((512, 1024), BF), ((1024, 1024), BF), ((1024, 1024), BF), ((512, 2048), BF),
    ]
    return pl.pallas_call(
        middle_kernel,
        out_shape=[jax.ShapeDtypeStruct(s, d) for s, d in shapes],
        in_specs=any_spec(6),
        out_specs=any_spec(5),
        scratch_shapes=[
            vm((1024, 1024), BF), vm((1024, 1024), BF), vm((1024, 2048), BF), vm((1024, 2048), BF),
            vm((2048, 1024), BF), vm((1024, 2048), BF), vm((512, 1024), BF), vm((512, 1024), BF),
            vm((512, 1024), BF), vm((1024, 1024), BF),
            vm((1024, 1024), BF), vm((1024, 1024), BF), vm((1024, 1024), BF),
            vm((512, 2048), BF), vm((512, 2048), BF), vm((512, 2048), BF),
            dma((6,)), dma((5,)), dma((4,)), dma((4,)), dma((2,)), dma((2,)),
        ],
        compiler_params=pltpu.CompilerParams(
            collective_id=1, has_side_effects=True, vmem_limit_bytes=58 * 1024 * 1024
        ),
        name="middle",
    )(sec, dy, dyo, hg, wup, wdn)


PACE = 36


class Arc:
    def __init__(self, here, slab, base, rows, recv, result, result_base, sems):
        self.here, self.slab, self.base, self.rows = here, slab, base, rows
        self.recv, self.result, self.result_base = recv, result, result_base
        self.rs_s, self.rs_r, self.ag_s, self.ag_r, self.mt_s, self.mt_r, self.local = sems
        self.pending = []
        self.t = 0

    def span(self, base, offset, half):
        start = base + lax.rem(self.here.r + 8 + offset, 8) * self.rows
        if half is None:
            return aligned(start, self.rows, 16)
        return aligned(start + half * (self.rows // 2), self.rows // 2, 16)

    def mine(self, offset, half=None):
        return self.span(self.base, offset, half)

    def place(self, offset, core, half=None):
        return self.result.at[self.span(self.result_base(core) + self.base, offset, half)]

    def send(self, src, dst, send_sem, recv_sem, device):
        copy = remote(src, dst, send_sem, recv_sem, device)
        copy.start()
        self.pending.append(copy)

    def to(self, way):
        return self.here.next if way == 0 else self.here.prev

    def sign(self, way):
        return 1 if way == 0 else -1

    def slot(self, way, s):
        if s > 0:
            return self.recv.at[way, s]
        return self.recv.at[way, 0, pl.ds(way * (self.rows // 2), self.rows // 2)]

    def arrived(self, way, s):
        got = self.slot(way, s)
        remote(got, got, self.rs_s.at[way, s], self.rs_r.at[way, s], self.to(way)).wait_recv()

    def gather_step(self, way, s):
        sign = self.sign(way)
        if s == 0:
            src = self.slab.at[self.mine(sign * 4, way)]
        else:
            self.arrived(way, s - 1)
            own = self.slab[self.mine(sign * (4 - s)), :].astype(F32)
            src = self.recv.at[way, s - 1]
            if s == 1:
                half = self.rows // 2
                kept = pl.ds(way * half, half)
                rest = pl.ds((1 - way) * half, half)
                at = slice(way * half, way * half + half)
                src[kept, :] = (src[kept, :].astype(F32) + own[at]).astype(BF)
                at = slice((1 - way) * half, (1 - way) * half + half)
                src[rest, :] = own[at].astype(BF)
            else:
                src[...] = (src[...].astype(F32) + own).astype(BF)
        self.send(src, self.slot(way, s), self.rs_s.at[way, s], self.rs_r.at[way, s], self.to(way))

    def spread(self, src, offset, step, way, half=None):
        dst = self.place(offset, self.here.core, half)
        if step < 4 and not (step == 3 and half is None):
            self.send(src, dst, self.ag_s.at[way, step], self.ag_r.at[way, step], self.to(way))

    def to_mate(self, src, offset, slot, half=None):
        dst = self.place(offset, self.here.core, half)
        self.send(src, dst, self.mt_s.at[slot], self.mt_r.at[slot], self.here.mate)

    def total(self):
        self.arrived(0, 3)
        self.arrived(1, 3)
        sums = self.recv.at[0, 3]
        own = self.slab[self.mine(0), :].astype(F32)
        sums[...] = (sums[...].astype(F32) + self.recv[1, 3].astype(F32) + own).astype(BF)
        for way in (0, 1):
            self.spread(sums, 0, 0, way)
        self.to_mate(sums, 0, 0)
        self.keep = pltpu.make_async_copy(sums, self.place(0, self.here.core), self.local)
        self.keep.start()

    def spread_step(self, way, s):
        sign = self.sign(way)
        half = way if s == 3 else None
        got = self.place(-sign * (s + 1), self.here.core, half)
        remote(got, got, self.ag_s.at[way, s], self.ag_r.at[way, s], self.to(way)).wait_recv()
        if s < 3:
            part = way if s == 2 else None
            src = self.place(-sign * (s + 1), self.here.core, part)
            self.spread(src, -sign * (s + 1), s + 1, way, part)
        self.to_mate(got, -sign * (s + 1), 1 + 2 * s + way, half)

    def tick(self):
        t = self.t
        self.t = t + 1
        if t == 4:
            self.total()
        elif t < 9:
            for way in (0, 1):
                if t < 4:
                    self.gather_step(way, t)
                else:
                    self.spread_step(way, t - 5)

    def finish(self):
        for copy in self.pending:
            copy.wait_send()
        self.keep.wait()
        other = 1 - self.here.core
        for slot in range(9):
            if slot == 0:
                got = self.place(0, other)
            else:
                s, way = (slot - 1) // 2, (slot - 1) % 2
                got = self.place(-self.sign(way) * (s + 1), other, way if s == 3 else None)
            remote(got, got, self.mt_s.at[slot], self.mt_r.at[slot], self.here.mate).wait_recv()


def back_kernel(
    len_ref, gain_ref, bias_ref, stat_ref,
    part_hbm, pin_hbm, mid_hbm, x_hbm, dy_hbm, qkv_hbm, mix_hbm, rden_hbm, state_hbm, first_hbm,
    win_hbm, wino_hbm, wo_hbm, woo_hbm, mlp_hbm, dslab_hbm, uslab_hbm,
    resd_o, resu_o, resi_o, reso_o, out_o, gin_o, small_ref,
    part_v, pin_v, mid_v, dy_v, qkv_v, mix_v, rden_v, state_v, first_v, win_v, wo_v,
    mlpin_v, mg_v, mgf_v, mixg_v, top_v, bot_v, dqkv_v, local_v, lsend_v, lrecv_v,
    dslab_v, uslab_v, drecv_v, urecv_v, gm_v, gr_v, ga_v, gx_v, om_v, or_v, oa_v, ox_v, irecv_v, orecv_v,
    small_s, small_r,
    in_sem, out_sem, xs_sem, xr_sem, ms_sem, mr_sem, bs_sem, br_sem,
    rs_s, rs_r, ag_s, ag_r, mt_s, mt_r, keep_s,
):
    here = Place()
    loads = [
        (part_hbm, part_v), (pin_hbm, pin_v), (mid_hbm, mid_v), (dy_hbm, dy_v), (dslab_hbm, dslab_v),
        (uslab_hbm, uslab_v), (wo_hbm, wo_v.at[0]), (woo_hbm, wo_v.at[1]), (mix_hbm, mix_v),
        (rden_hbm, rden_v), (qkv_hbm, qkv_v), (state_hbm, state_v), (first_hbm, first_v),
        (win_hbm, win_v.at[0]), (wino_hbm, win_v.at[1]), (x_hbm, part_v), (mlp_hbm.at[pl.ds(0, ROWS)], pin_v),
    ]
    loads = [pltpu.make_async_copy(a, b, in_sem.at[i]) for i, (a, b) in enumerate(loads)]
    for load in loads[:15]:
        load.start()
    y_mate = (here.dp + 2 - 4 * lax.rem(here.dp // 2, 2), here.mp)
    z_mate = (here.dp + 4 - 8 * lax.rem(here.dp // 4, 2), here.mp)
    z_far = (here.dp + 8 - 16 * (here.dp // 8), here.mp)
    greet(here.partners() + [y_mate, z_mate, z_far])
    sends = []
    outs = []

    def out(src, dst):
        copy = pltpu.make_async_copy(src, dst, out_sem.at[len(outs)])
        copy.start()
        outs.append(copy)

    def across(src, dst, slot):
        copy = remote(src, dst, xs_sem.at[slot], xr_sem.at[slot], here.across)
        copy.start()
        sends.append(copy)
        return copy

    def to_mate(src, dst, slot):
        copy = remote(src, dst, ms_sem.at[slot], mr_sem.at[slot], here.mate)
        copy.start()
        sends.append(copy)
        return copy

    arcs = []

    def add_arc(slab, base, rows, recv, result, result_base):
        n = len(arcs)
        sems = (rs_s.at[n], rs_r.at[n], ag_s.at[n], ag_r.at[n], mt_s.at[n], mt_r.at[n], keep_s.at[n])
        arcs.append(Arc(here, slab, base, rows, recv, result, result_base, sems))
        return arcs[-1]

    ring_d = add_arc(dslab_v, 0, 128, drecv_v, resd_o, lambda core: core * 1024)
    ring_u = add_arc(uslab_v, 0, 64, urecv_v, resu_o, lambda core: core * 512)
    ring_o = add_arc(oa_v.at[0], 0, 32, orecv_v, reso_o, lambda core: core * 256)
    ring_i = [
        add_arc(ga_v.at[0], i * 512, 64, irecv_v.at[i], resi_o, lambda core: core * 1536) for i in range(3)
    ]

    credit = [0]

    def ring(count):
        credit[0] += count * PACE
        while credit[0] >= 100:
            credit[0] -= 100
            first = ring_d if ring_d.t <= ring_u.t else ring_u
            first.tick()

    def ring_on(arc):
        arc.tick()

    loads[4].wait()
    loads[5].wait()
    ring_d.tick()
    ring_u.tick()

    small_s[...] = jnp.zeros_like(small_s)
    for load in loads[0:4]:
        load.wait()
    gain_two = gain_ref[1:2, :]

    @pl.loop(0, ROWS // 128)
    def _(i):
        at = aligned(i * 128, 128, 128)
        grad = part_v[at, :].astype(F32) + pin_v[at, :].astype(F32)
        unit, inverse = row_norm(mid_v[at, :])
        scaled = grad * gain_two
        centre = jnp.mean(scaled, axis=-1, keepdims=True)
        along = jnp.mean(scaled * unit, axis=-1, keepdims=True)
        total = dy_v[at, :].astype(F32) + inverse * (scaled - centre - unit * along)
        mgf_v[at, :] = total
        mg_v[at, :] = total.astype(BF)
        small_s[1:2, :] = small_s[1:2, :] + jnp.sum(grad * unit, axis=0, keepdims=True)
        small_s[3:4, :] = small_s[3:4, :] + jnp.sum(grad, axis=0, keepdims=True)

    for load in loads[15:]:
        load.start()
    ring(2)
    for load in loads[6:12]:
        load.wait()
    for half in range(2):
        mixg_v[half] = dot_nt(mg_v[...], wo_v[half]).astype(BF)
    ring(1)
    their = 1 - here.core

    def out_grad(half, side, dst):
        cols = aligned(side * 256, 256, 256)
        dst[...] = dot_tn(mix_v[half, :, cols], mg_v[...]).astype(BF)

    keep = same_head()

    def tops(half):
        @pl.loop(0, 4)
        def _(p):
            lanes_at = aligned(p * PAIR, PAIR, PAIR)
            packs = []
            blocks = jnp.where(keep, 1.0, 0.0).astype(BF)
            for c in range(2):
                at = pl.ds(c * CH, CH)
                top = (mixg_v[half, at, lanes_at].astype(F32) * rden_v[half, at, lanes_at]).astype(BF)
                top_v[half, at, lanes_at] = top
                prod = top.astype(F32) * mix_v[half, at, lanes_at].astype(F32)
                high = prod.astype(BF)
                low = (prod - high.astype(F32)).astype(BF)
                bottom = -(dot_nn(high, blocks) + dot_nn(low, blocks))
                high = bottom.astype(BF)
                low = (bottom - high.astype(F32)).astype(BF)
                lane = lax.rem(lax.broadcasted_iota(jnp.int32, bottom.shape, 1), DH)
                bot_v[half, at, lanes_at] = jnp.where(
                    lane == 0, high, jnp.where(lane == 1, low, jnp.zeros_like(high))
                )
                query = qkv_v[half, 0, at, lanes_at]
                made = dot_tn(query, jnp.concatenate([top, high], axis=1))
                packs.append(jnp.where(keep, made[:, :PAIR], pltpu.roll(made[:, PAIR:], DH, 1)))
            local_v[half, p] = packs[1]
            lsend_v[half, p] = (packs[0] + packs[1]).astype(BF)

        across(lsend_v.at[half], lrecv_v.at[1 - half], 1 + half)

    tops(0)
    ring(1)
    tops(1)
    ring(1)
    for half in (1, 0):
        out_grad(half, their, om_v.at[half])
        to_mate(om_v.at[half], or_v.at[half], half)
    ring(1)
    for half in (1, 0):
        out_grad(half, here.core, oa_v.at[half])
    ring(1)
    for load in loads[12:15]:
        load.wait()

    def attend_back(half):
        mask = causal_tile()
        earlier = 1.0 - here.mp.astype(F32)
        remote(
            lsend_v.at[1 - half], lrecv_v.at[half], xs_sem.at[2 - half], xr_sem.at[2 - half], here.across
        ).wait_recv()

        def body(p, c):
            lanes_at = aligned(p * PAIR, PAIR, PAIR)
            at = pl.ds(c * CH, CH)
            query = qkv_v[half, 0, at, lanes_at]
            key = qkv_v[half, 1, at, lanes_at]
            val = qkv_v[half, 2, at, lanes_at]
            top = top_v[half, at, lanes_at]
            bot = bot_v[half, at, lanes_at]
            lane = lax.rem(lax.broadcasted_iota(jnp.int32, val.shape, 1), DH)
            one = jnp.ones_like(val)
            zero = jnp.zeros_like(val)
            val_two = jnp.concatenate([val, jnp.where(lane < 2, one, zero)], axis=1)
            val_one = jnp.concatenate([val, jnp.where(lane == 0, one, zero)], axis=1)
            before = state_v[half, p].astype(F32)
            after = lrecv_v[half, p].astype(F32) * earlier
            if c == 1:
                key0 = qkv_v[half, 1, pl.ds(0, CH), lanes_at]
                val0 = qkv_v[half, 2, pl.ds(0, CH), lanes_at]
                made = dot_tn(key0, jnp.concatenate([val0, one], axis=1))
                before = before + jnp.where(keep, made[:, :PAIR], made[:, PAIR:])
            else:
                after = after + local_v[half, p]
            before = unpack_state(before).astype(BF)
            after = unpack_state(after).astype(BF)
            dq = dot_nt(jnp.concatenate([top, bot], axis=1), before)
            dk = dot_nt(val_one, after)
            dv = dot_nn(key, after[:, :PAIR])
            queries, keys, tops_, bots = split_heads(query), split_heads(key), split_heads(top), split_heads(bot)
            for head in range(2):
                score = jnp.where(mask, dot_nt(queries[head], key), 0.0).astype(BF)
                grad = dot_nt(jnp.concatenate([tops_[head], bots[head]], axis=1), val_two)
                grad = jnp.where(mask, grad, 0.0).astype(BF)
                dq = dq + dot_nn(grad, keys[head])
                dk = dk + dot_tn(grad, queries[head])
                dv = dv + dot_tn(score, tops_[head])
            dqkv_v[half, 0, at, lanes_at] = (dq * jnp.minimum(query.astype(F32), 1.0)).astype(BF)
            dqkv_v[half, 1, at, lanes_at] = (dk * jnp.minimum(key.astype(F32), 1.0)).astype(BF)
            dqkv_v[half, 2, at, lanes_at] = dv.astype(BF)

        for part in range(2):
            @pl.loop(part * 2, part * 2 + 2)
            def _(p):
                body(p, 0)
                body(p, 1)

            ring(2)

    def piece(i):
        return pl.ds(i * 512, 512)

    def in_grads(half):
        for side, dst in ((their, gm_v), (here.core, ga_v)):
            cols = aligned(side * 512, 512, 512)
            for i in range(3):
                at = piece(i)
                dst[half, at, :] = dot_tn(first_v[:, cols], dqkv_v[half, i]).astype(BF)
                if dst is gm_v:
                    to_mate(gm_v.at[half, at], gr_v.at[half, at], 2 + half * 3 + i)
            ring(1)

    def add_rows(dst, src, start, count):
        @pl.loop(0, count)
        def _(i):
            at = aligned(start + i * 128, 128, 128)
            dst[at, :] = (dst[at, :].astype(F32) + src[at, :].astype(F32)).astype(BF)

    def mate_arrival(half, i):
        at = piece(i)
        slot = 2 + half * 3 + i
        remote(gm_v.at[half, at], gr_v.at[half, at], ms_sem.at[slot], mr_sem.at[slot], here.mate).wait_recv()
        add_rows(ga_v.at[half], gr_v.at[half], i * 512, 4)

    def mate_arrival_out(half):
        remote(om_v.at[half], or_v.at[half], ms_sem.at[half], mr_sem.at[half], here.mate).wait_recv()
        add_rows(oa_v.at[half], or_v.at[half], 0, 2)

    attend_back(1)
    mate_arrival_out(1)
    cross_o = across(oa_v.at[1], ox_v, 3)
    in_grads(1)
    cross_i = []
    for i in range(3):
        mate_arrival(1, i)
        cross_i.append(across(ga_v.at[1, piece(i)], gx_v.at[piece(i)], 4 + i))
    mlp = across(mlp_hbm.at[pl.ds(ROWS, ROWS)], mlpin_v, 0)
    ring(2)
    mate_arrival_out(0)
    attend_back(0)
    cross_o.wait_recv()
    add_rows(oa_v.at[0], ox_v, 0, 2)
    ring_on(ring_o)
    in_grads(0)
    for i in range(3):
        mate_arrival(0, i)
    ring(2)
    ring_on(ring_o)

    loads[15].wait()
    gain_one = gain_ref[0:1, :]

    for quarter in range(2):
        at = pl.ds(quarter * CH, CH)
        grad = None
        for half in range(2):
            term = None
            for j in range(3):
                made = dot_nt(dqkv_v[half, j, at, :], win_v[half, pl.ds(j * 1024, 1024), :])
                term = made if term is None else term + made
            term = term.astype(BF).astype(F32)
            grad = term if grad is None else grad + term
        unit, inverse = row_norm(part_v[at, :].astype(F32))
        scaled = grad * gain_one
        centre = jnp.mean(scaled, axis=-1, keepdims=True)
        along = jnp.mean(scaled * unit, axis=-1, keepdims=True)
        mgf_v[at, :] = mgf_v[at, :] + inverse * (scaled - centre - unit * along)
        small_s[0:1, :] = small_s[0:1, :] + jnp.sum(grad * unit, axis=0, keepdims=True)
        small_s[2:3, :] = small_s[2:3, :] + jnp.sum(grad, axis=0, keepdims=True)
        ring(2)
        ring_on(ring_o)

    out(mgf_v, gin_o)
    small_s[4:5, pl.ds(0, PAIR)] = jnp.sum(stat_ref[1], axis=0, keepdims=True) * (1.0 / DH)
    count = len_ref[0].astype(F32) * (8.0 / 1024.0)
    small_s[5:6, :] = jnp.zeros((1, 1024), F32) + count
    small_s[6:7, pl.ds(0, PAIR)] = jnp.max(stat_ref[0], axis=0, keepdims=True)
    partners = [here.mate, y_mate, z_mate, z_far, here.across]

    def small_send(step):
        src = small_s if step == 0 else small_ref
        copy = remote(src, small_r.at[step], bs_sem.at[step], br_sem.at[step], partners[step])
        copy.start()
        return copy

    def small_step(copy, step):
        copy.wait()
        src = small_s if step == 0 else small_ref
        mine, theirs = src[...], small_r[step]
        row = lax.broadcasted_iota(jnp.int32, mine.shape, 0)
        small_ref[...] = jnp.where(row < 6, mine + theirs, jnp.maximum(mine, theirs))

    for i in range(3):
        cross_i[i].wait_recv()
        add_rows(ga_v.at[0], gx_v, i * 512, 4)
        for arc in ring_i[: i + 1]:
            ring_on(arc)
        ring(6)
        ring_on(ring_o)
    copy = small_send(0)
    for step in range(9):
        for arc in ring_i:
            ring_on(arc)
        ring(6)
        ring_on(ring_o)
        if 2 <= step < 7:
            small_step(copy, step - 2)
            if step < 6:
                copy = small_send(step - 1)
    ring(2000)

    loads[16].wait()
    mlp.wait_recv()

    @pl.loop(0, 4)
    def _(i):
        at = aligned(i * 128, 128, 128)
        total = mid_v[at, :] + (pin_v[at, :].astype(F32) + mlpin_v[at, :].astype(F32))
        pin_v[at, :] = total.astype(BF)

    out(pin_v, out_o)
    for arc in arcs:
        arc.finish()
    for copy in sends:
        copy.wait_send()
    for copy in outs:
        copy.wait()


def back(lengths, gain, bias, stat, part, pin, mid, x, dy, qkv, mix, rden, state, first, win, wino, wo, woo, mlp, dslab, uslab):
    vm = pltpu.VMEM
    dma = pltpu.SemaphoreType.DMA
    shapes = [
        ((2048, 1024), BF), ((1024, 2048), BF), ((3072, 512), BF), ((512, 1024), BF),
        ((512, 1024), BF), ((512, 1024), F32), ((8, 1024), F32),
    ]
    rows = (512, 1024)
    heads = (2, 512, 512)
    pack = (2, 4, PAIR, PAIR)
    vmem = pl.BlockSpec(memory_space=pltpu.VMEM)
    return pl.pallas_call(
        back_kernel,
        out_shape=[jax.ShapeDtypeStruct(s, d) for s, d in shapes],
        in_specs=[pl.BlockSpec(memory_space=pltpu.SMEM), vmem, vmem, vmem] + any_spec(17),
        out_specs=any_spec(6) + [vmem],
        scratch_shapes=[
            vm(rows, BF), vm(rows, BF), vm(rows, F32), vm(rows, BF),
            vm((2, 3, 512, 512), BF), vm(heads, BF), vm(heads, F32), vm(pack, BF), vm(rows, BF),
            vm((2, 3072, 512), BF), vm((2, 512, 1024), BF),
            vm(rows, BF), vm(rows, BF), vm(rows, F32), vm(heads, BF), vm(heads, BF), vm(heads, BF),
            vm((2, 3, 512, 512), BF), vm(pack, F32), vm(pack, BF), vm(pack, BF),
            vm((1024, 1024), BF), vm((512, 2048), BF), vm((2, 4, 128, 1024), BF), vm((2, 4, 64, 2048), BF),
            vm((2, 1536, 512), BF), vm((2, 1536, 512), BF), vm((2, 1536, 512), BF), vm((1536, 512), BF),
            vm((2, 256, 1024), BF), vm((2, 256, 1024), BF), vm((2, 256, 1024), BF), vm((256, 1024), BF),
            vm((3, 2, 4, 64, 512), BF), vm((2, 4, 32, 1024), BF),
            vm((8, 1024), F32), vm((5, 8, 1024), F32),
            dma((17,)), dma((2,)), dma((7,)), dma((7,)), dma((8,)), dma((8,)), dma((5,)), dma((5,)),
            dma((6, 2, 4)), dma((6, 2, 4)), dma((6, 2, 4)), dma((6, 2, 4)), dma((6, 9)), dma((6, 9)), dma((6,)),
        ],
        compiler_params=pltpu.CompilerParams(
            collective_id=2, has_side_effects=True, vmem_limit_bytes=60 * 1024 * 1024
        ),
        name="back",
    )(lengths, gain, bias, stat, part, pin, mid, x, dy, qkv, mix, rden, state, first, win, wino, wo, woo, mlp, dslab, uslab)


def fast_device(
    block_in, lengths, input_weight, output_weight, up_weight, down_weight, norm_gain, norm_bias, cotangent
):
    x, dy = block_in[0], cotangent[0]
    win = input_weight.reshape(3072, 512)
    first, qkv, mix, rden, state, mid, sec, wino, woo, dyo, hg, stat = front(
        lengths, x, dy, win, output_weight, down_weight, norm_gain, norm_bias
    )
    part, pin, mlp, dslab, uslab = middle(sec, dy, dyo, hg, up_weight, down_weight)
    resd, resu, resi, reso, block_out, grad_in, small = back(
        lengths, norm_gain, norm_bias, stat, part, pin, mid, x, dy, qkv, mix, rden, state, first,
        win, wino, output_weight, woo, mlp, dslab, uslab,
    )
    input_grad = resi.reshape(2, 3, 512, 512).transpose(1, 0, 2, 3).reshape(3, 1024, 512).astype(F32)
    scaling = 1.0 / (DH * 1024)
    total = jnp.sum(small[4])
    count = jnp.sum(small[5])
    stats = jnp.stack([jnp.max(small[6]) * scaling, total / count * scaling])
    return (
        block_out[None], grad_in[None], input_grad, reso.astype(F32), resu.astype(F32), resd.astype(F32),
        small[0:2], small[2:4], stats,
    )


def fits_fast(mesh, block_shape):
    return dict(mesh.shape) == {"dp": 16, "mp": 2} and tuple(block_shape) == (16, 1024, 1024)


def solution(mesh):
    in_specs = (
        P("dp", "mp", None),
        P("dp"),
        P(None, None, "mp"),
        P("mp", None),
        P(None, "mp"),
        P("mp", None),
        P(),
        P(),
        P("dp", "mp", None),
    )
    out_specs = (
        P("dp", "mp", None),
        P("dp", "mp", None),
        P(None, None, "mp"),
        P("mp", None),
        P(None, "mp"),
        P("mp", None),
        P(),
        P(),
        P(),
    )

    def whole(*arrays):
        body = fast_device if fits_fast(mesh, arrays[0].shape) else per_device
        return jax.shard_map(
            body, mesh=mesh, in_specs=in_specs, out_specs=out_specs, check_vma=False
        )(*arrays)

    return whole
```

```python
from functools import partial

import jax
import jax.numpy as jnp
from jax import lax
from jax.experimental import pallas as pl
from jax.experimental.pallas import tpu as pltpu
from jax.sharding import PartitionSpec as P

DH = 64
BLK = 512


EPSILON = 1e-05
PRECISE = lax.Precision.HIGHEST


def combined_all(part, axis, combine):
    gathered = jax.tree.map(lambda a: lax.all_gather(a, axis), part)

    def take(source):
        return jax.tree.map(lambda a: lax.dynamic_index_in_dim(a, source, 0, False), gathered)

    return lax.fori_loop(
        1, lax.axis_size(axis), lambda source, state: combine(state, take(source)), take(0)
    )


def feature(values):
    return jax.nn.elu(values) + 1.0


def feature_slope(values):
    return jnp.where(values > 0, 1.0, jnp.exp(values))


def normalise(inputs, gain_row, bias_row):
    centre = jnp.mean(inputs, axis=-1, keepdims=True)
    centred = inputs - centre
    spread = jnp.mean(centred * centred, axis=-1, keepdims=True)
    inverse = lax.rsqrt(spread + EPSILON)
    unit_rows = centred * inverse
    return (unit_rows * gain_row + bias_row, unit_rows, inverse)


def normalise_back(grad_rows, unit_rows, inverse, gain_row):
    scaled = grad_rows * gain_row
    centre = jnp.mean(scaled, axis=-1, keepdims=True)
    along = jnp.mean(scaled * unit_rows, axis=-1, keepdims=True)
    input_grad = inverse * (scaled - centre - unit_rows * along)
    return (input_grad, jnp.sum(grad_rows * unit_rows, axis=0), jnp.sum(grad_rows, axis=0))


def exclusive(stacked):
    running = jnp.cumsum(stacked, axis=0)
    return jnp.concatenate([jnp.zeros_like(running[:1]), running[:-1]], axis=0)


def later(stacked):
    return exclusive(stacked[::-1])[::-1]


def unchanged(carried):
    return carried


def causal_mask():
    return jnp.tril(jnp.ones((BLK, BLK), jnp.float32))


def attend_forward(query_map, key_map, values, crop_len):
    slot_len, head_count, depth = query_map.shape
    block_count = slot_len // BLK
    block_shape = (block_count, BLK, head_count, depth)
    block_q = query_map.reshape(block_shape)
    block_k = key_map.reshape(block_shape)
    block_v = values.reshape(block_shape)
    memory = exclusive(
        jnp.einsum("nihd,nihe->nhde", block_k, block_v, preferred_element_type=jnp.float32)
    )
    key_total = exclusive(jnp.sum(block_k.astype(jnp.float32), axis=1))
    causal = causal_mask()
    block_starts = jnp.arange(block_count, dtype=jnp.int32) * BLK

    def one_block(block_item):
        query_b, key_b, value_b, memory_b, total_b, start_b = block_item
        query_f = query_b.astype(jnp.float32)
        numerator = jnp.einsum("ihd,hde->ihe", query_f, memory_b, precision=PRECISE)
        denominator = jnp.einsum("ihd,hd->ih", query_f, total_b, precision=PRECISE)

        def inside(partial_sums):
            value_part, weight_part = partial_sums
            scores = (
                jnp.einsum("ihd,jhd->hij", query_b, key_b, preferred_element_type=jnp.float32)
                * causal
            )
            value_part = value_part + jnp.einsum(
                "hij,jhd->ihd",
                scores.astype(jnp.bfloat16),
                value_b,
                preferred_element_type=jnp.float32,
            )
            weight_part = weight_part + jnp.sum(scores, axis=-1).T
            return (value_part, weight_part)

        numerator, denominator = lax.cond(
            start_b < crop_len, inside, unchanged, (numerator, denominator)
        )
        return (numerator / denominator[..., None], denominator)

    attended, denoms = lax.map(
        one_block, (block_q, block_k, block_v, memory, key_total, block_starts)
    )
    return (
        attended.reshape(slot_len, head_count, depth),
        denoms.reshape(slot_len, head_count),
        memory,
        key_total,
    )


def attend_backward(
    grad_attn, attended, denoms, query_map, key_map, values, memory, key_total, crop_len
):
    slot_len, head_count, depth = query_map.shape
    block_count = slot_len // BLK
    block_shape = (block_count, BLK, head_count, depth)
    top_all = (grad_attn / denoms[..., None]).reshape(block_shape)
    bottom_all = (-jnp.sum(grad_attn * attended, axis=-1) / denoms).reshape(
        block_count, BLK, head_count
    )
    query_full = query_map.astype(jnp.float32).reshape(block_shape)
    memory_later = later(jnp.einsum("nihd,nihe->nhde", query_full, top_all, precision=PRECISE))
    total_later = later(jnp.einsum("nihd,nih->nhd", query_full, bottom_all, precision=PRECISE))
    causal = causal_mask()
    block_starts = jnp.arange(block_count, dtype=jnp.int32) * BLK

    def one_block(block_item):
        (
            query_b,
            key_b,
            value_b,
            memory_b,
            total_b,
            later_memory,
            later_total,
            top_grad,
            bottom_grad,
            start_b,
        ) = block_item
        value_f = value_b.astype(jnp.float32)
        key_f = key_b.astype(jnp.float32)
        query_sum = (
            jnp.einsum("ihe,hde->ihd", top_grad, memory_b, precision=PRECISE)
            + bottom_grad[..., None] * total_b[None]
        )
        key_sum = (
            jnp.einsum("jhe,hde->jhd", value_f, later_memory, precision=PRECISE) + later_total[None]
        )
        value_sum = jnp.einsum("jhd,hde->jhe", key_f, later_memory, precision=PRECISE)

        def inside(partial_grads):
            query_acc, key_acc, value_acc = partial_grads
            scores = (
                jnp.einsum("ihd,jhd->hij", query_b, key_b, preferred_element_type=jnp.float32)
                * causal
            )
            score_grad = (
                (
                    jnp.einsum("ihe,jhe->hij", top_grad, value_f, precision=PRECISE)
                    + bottom_grad.T[:, :, None]
                )
                * causal
            ).astype(jnp.bfloat16)
            query_acc = query_acc + jnp.einsum(
                "hij,jhd->ihd", score_grad, key_b, preferred_element_type=jnp.float32
            )
            key_acc = key_acc + jnp.einsum(
                "hij,ihd->jhd", score_grad, query_b, preferred_element_type=jnp.float32
            )
            rounded_scores = scores.astype(jnp.bfloat16).astype(jnp.float32)
            value_acc = value_acc + jnp.einsum(
                "hij,ihe->jhe", rounded_scores, top_grad, precision=PRECISE
            )
            return (query_acc, key_acc, value_acc)

        return lax.cond(start_b < crop_len, inside, unchanged, (query_sum, key_sum, value_sum))

    query_grad, key_grad, value_grad = lax.map(
        one_block,
        (
            query_map.reshape(block_shape),
            key_map.reshape(block_shape),
            values.reshape(block_shape),
            memory,
            key_total,
            memory_later,
            total_later,
            top_all,
            bottom_all,
            block_starts,
        ),
    )
    return (
        query_grad.reshape(slot_len, head_count, depth),
        key_grad.reshape(slot_len, head_count, depth),
        value_grad.reshape(slot_len, head_count, depth),
    )


def combine_stats(first_part, second_part):
    return (
        first_part[0] + second_part[0],
        first_part[1] + second_part[1],
        first_part[2] + second_part[2],
        first_part[3] + second_part[3],
        jnp.maximum(first_part[4], second_part[4]),
    )


def per_device(
    block_in,
    lengths,
    input_weight,
    output_weight,
    up_weight,
    down_weight,
    norm_gain,
    norm_bias,
    cotangent,
):
    group_count = lax.axis_size("mp")
    rows_here = block_in.shape[1]
    slot_len = rows_here * group_count
    local_width = output_weight.shape[0]
    head_count = local_width // DH
    crop_len = lengths[0]
    valid_mask = (jnp.arange(slot_len, dtype=jnp.int32) < crop_len).astype(jnp.float32)
    own_rows = block_in[0].astype(jnp.float32)
    first_norm, unit_one, inverse_one = normalise(own_rows, norm_gain[0], norm_bias[0])
    first_rows = lax.all_gather(first_norm.astype(jnp.bfloat16), "mp", axis=0, tiled=True)
    projected = jnp.einsum(
        "rd,cdk->rck", first_rows, input_weight, preferred_element_type=jnp.float32
    ).reshape(slot_len, 3, head_count, DH)
    query = projected[:, 0]
    key_raw = projected[:, 1]
    query_map = feature(query).astype(jnp.bfloat16)
    key_map = (feature(key_raw) * valid_mask[:, None, None]).astype(jnp.bfloat16)
    values = projected[:, 2].astype(jnp.bfloat16)
    attended, denoms, memory, key_total = attend_forward(query_map, key_map, values, crop_len)
    mixed = attended.reshape(slot_len, local_width).astype(jnp.bfloat16)
    part_rows = mixed
    branch_out = lax.psum_scatter(
        jnp.dot(part_rows, output_weight, preferred_element_type=jnp.float32).astype(jnp.bfloat16),
        "mp",
        scatter_dimension=0,
        tiled=True,
    ).astype(jnp.float32)
    middle = own_rows + branch_out
    second_norm, unit_two, inverse_two = normalise(middle, norm_gain[1], norm_bias[1])
    second_rows = lax.all_gather(second_norm.astype(jnp.bfloat16), "mp", axis=0, tiled=True)
    hidden_in = jnp.dot(second_rows, up_weight, preferred_element_type=jnp.float32)
    hidden = jax.nn.gelu(hidden_in, approximate=True).astype(jnp.bfloat16)
    part_rows = hidden
    mlp_out = lax.psum_scatter(
        jnp.dot(part_rows, down_weight, preferred_element_type=jnp.float32).astype(jnp.bfloat16),
        "mp",
        scatter_dimension=0,
        tiled=True,
    ).astype(jnp.float32)
    block_out = (middle + mlp_out).astype(jnp.bfloat16)[None]
    grad_out = cotangent[0]
    grad_rows = lax.all_gather(grad_out, "mp", axis=0, tiled=True)
    down_grad = jnp.einsum("rf,rd->fd", hidden, grad_rows, preferred_element_type=jnp.float32)
    hidden_grad = jnp.einsum(
        "rd,fd->rf", grad_rows, down_weight, preferred_element_type=jnp.float32
    )
    unused_out, gelu_back = jax.vjp(partial(jax.nn.gelu, approximate=True), hidden_in)
    inner_grad = gelu_back(hidden_grad)[0].astype(jnp.bfloat16)
    up_grad = jnp.einsum("rd,rf->df", second_rows, inner_grad, preferred_element_type=jnp.float32)
    part_rows = inner_grad
    second_grad = lax.psum_scatter(
        jnp.einsum("rf,df->rd", part_rows, up_weight, preferred_element_type=jnp.float32).astype(
            jnp.bfloat16
        ),
        "mp",
        scatter_dimension=0,
        tiled=True,
    ).astype(jnp.float32)
    back_two, gain_two, bias_two = normalise_back(second_grad, unit_two, inverse_two, norm_gain[1])
    middle_grad = grad_out.astype(jnp.float32) + back_two
    middle_low = middle_grad.astype(jnp.bfloat16)
    middle_full = lax.all_gather(middle_low, "mp", axis=0, tiled=True)
    mixed_grad = jnp.einsum(
        "rd,kd->rk", middle_full, output_weight, preferred_element_type=jnp.float32
    ).astype(jnp.bfloat16)
    output_grad = jnp.einsum("rk,rd->kd", mixed, middle_full, preferred_element_type=jnp.float32)
    grad_attn = mixed_grad.astype(jnp.float32).reshape(slot_len, head_count, DH)
    query_grad, key_grad, value_grad = attend_backward(
        grad_attn, attended, denoms, query_map, key_map, values, memory, key_total, crop_len
    )
    query_low = (query_grad * feature_slope(query)).astype(jnp.bfloat16)
    key_low = (key_grad * valid_mask[:, None, None] * feature_slope(key_raw)).astype(jnp.bfloat16)
    value_low = value_grad.astype(jnp.bfloat16)
    qkv_grad = jnp.stack([query_low, key_low, value_low], axis=1).reshape(slot_len, 3, local_width)
    input_grad = jnp.einsum("rd,rck->cdk", first_rows, qkv_grad, preferred_element_type=jnp.float32)
    part_rows = qkv_grad
    first_grad = lax.psum_scatter(
        jnp.einsum(
            "rck,cdk->rd", part_rows, input_weight, preferred_element_type=jnp.float32
        ).astype(jnp.bfloat16),
        "mp",
        scatter_dimension=0,
        tiled=True,
    ).astype(jnp.float32)
    back_one, gain_one, bias_one = normalise_back(first_grad, unit_one, inverse_one, norm_gain[0])
    grad_input = (middle_grad + back_one)[None]
    input_grad, output_grad, up_grad, down_grad = (
        lax.psum(input_grad.astype(jnp.bfloat16), "dp").astype(jnp.float32),
        lax.psum(output_grad.astype(jnp.bfloat16), "dp").astype(jnp.float32),
        lax.psum(up_grad.astype(jnp.bfloat16), "dp").astype(jnp.float32),
        lax.psum(down_grad.astype(jnp.bfloat16), "dp").astype(jnp.float32),
    )
    kept_denoms = jnp.where(valid_mask[:, None] > 0, denoms, 0.0)
    den_total = jnp.sum(kept_denoms)
    den_count = crop_len.astype(jnp.float32) * head_count
    den_peak = jnp.max(kept_denoms)
    gain_grad, bias_grad, den_total, den_count, den_peak = combined_all(
        (
            jnp.stack([gain_one, gain_two]),
            jnp.stack([bias_one, bias_two]),
            den_total,
            den_count,
            den_peak,
        ),
        ("dp", "mp"),
        combine_stats,
    )
    scaling = DH * slot_len
    denominator_stats = jnp.stack([den_peak / scaling, den_total / den_count / scaling])
    return (
        block_out,
        grad_input,
        input_grad,
        output_grad,
        up_grad,
        down_grad,
        gain_grad,
        bias_grad,
        denominator_stats,
    )

MESH = pl.DeviceIdType.MESH
BF = jnp.bfloat16
F32 = jnp.float32
ROWS = 512
CH = 256
PAIR = 128


def dot_nn(a, b):
    return lax.dot_general(a, b, (((1,), (0,)), ((), ())), preferred_element_type=F32)


def dot_nt(a, b):
    return lax.dot_general(a, b, (((1,), (1,)), ((), ())), preferred_element_type=F32)


def dot_tn(a, b):
    return lax.dot_general(a, b, (((0,), (0,)), ((), ())), preferred_element_type=F32)


class Place:
    def __init__(self):
        dp = lax.axis_index("dp")
        mp = lax.axis_index("mp")
        self.dp, self.mp = dp, mp
        self.core = lax.rem(dp, 2)
        chip = dp // 2
        y = lax.rem(chip, 2)
        z = chip // 2
        self.r = z + y * (7 - 2 * z)
        self.across = (dp, 1 - mp)
        self.mate = (dp + 1 - 2 * self.core, mp)
        self.next = self.at(lax.rem(self.r + 1, 8))
        self.prev = self.at(lax.rem(self.r + 7, 8))

    def at(self, r):
        y = r // 4
        z = r + y * (7 - 2 * r)
        return ((z * 2 + y) * 2 + self.core, self.mp)

    def partners(self):
        return [self.across, self.mate, self.next, self.prev]


def greet(partners):
    barrier = pltpu.get_barrier_semaphore()
    for partner in partners:
        pl.semaphore_signal(barrier, inc=1, device_id=partner, device_id_type=MESH)
    pl.semaphore_wait(barrier, len(partners))


def remote(src, dst, send_sem, recv_sem, device):
    return pltpu.make_async_remote_copy(
        src_ref=src, dst_ref=dst, send_sem=send_sem, recv_sem=recv_sem,
        device_id=device, device_id_type=MESH,
    )


def aligned(start, size, unit):
    return pl.ds(pl.multiple_of(start, unit), size)


def lane_head(shape):
    return lax.broadcasted_iota(jnp.int32, shape, len(shape) - 1) < DH


def same_head():
    row = lax.broadcasted_iota(jnp.int32, (PAIR, PAIR), 0) < DH
    lane = lax.broadcasted_iota(jnp.int32, (PAIR, PAIR), 1) < DH
    return row == lane


def causal_tile():
    row = lax.broadcasted_iota(jnp.int32, (CH, CH), 0)
    col = lax.broadcasted_iota(jnp.int32, (CH, CH), 1)
    return row >= col


def unpack_state(packed):
    keep = same_head()
    zero = jnp.zeros_like(packed)
    return jnp.concatenate(
        [jnp.where(keep, packed, zero), jnp.where(keep, pltpu.roll(packed, DH, 1), zero)], axis=1
    )


def split_heads(pair):
    first = lane_head(pair.shape)
    zero = jnp.zeros_like(pair)
    return jnp.where(first, pair, zero), jnp.where(first, zero, pair)


def row_norm(rows):
    centre = jnp.mean(rows, axis=-1, keepdims=True)
    centred = rows - centre
    inverse = lax.rsqrt(jnp.mean(centred * centred, axis=-1, keepdims=True) + EPSILON)
    return centred * inverse, inverse


def front_kernel(
    len_ref, x_hbm, dy_hbm, win_hbm, wo_hbm, wdn_hbm, gain_ref, bias_ref,
    first_o, qkv_o, mix_o, rden_o, state_o, mid_o, sec_o, wino_o, woo_o, dyo_o, hg_o, stat_ref,
    x_v, dy_v, win_v, wino_v, wo_v, woo_v, wdn_v, first_v, qkv_v, num_v, den_v, mix_v, mid_v, sec_v, hg_v,
    local_v, ssend_v, srecv_v, state_v,
    in_sem, out_sem, xs_sem, xr_sem, ring_s, ring_r, mate_s, mate_r,
):
    here = Place()
    loads = [
        (x_hbm, x_v), (win_hbm, win_v), (dy_hbm, dy_v), (wdn_hbm, wdn_v), (wo_hbm, wo_v),
    ]
    loads = [pltpu.make_async_copy(a, b, in_sem.at[i]) for i, (a, b) in enumerate(loads)]
    for load in loads:
        load.start()
    greet(here.partners())
    parts = ((win_hbm, wino_v, 192), (wo_hbm, woo_v, 32))

    def rows_of(array, offset, core):
        rows = parts[array][2]
        return aligned((lax.rem(here.r + 8 + offset, 8) * 2 + core) * rows, rows, 32)

    cross = []
    for array, (src, dst, _) in enumerate(parts):
        for k in range(2):
            at = rows_of(array, 4 * k, here.core)
            slot = 2 * array + k
            cross.append(remote(src.at[at], dst.at[at], xs_sem.at[slot], xr_sem.at[slot], here.across))
    for copy in cross:
        copy.start()
    gone = []

    def dy_part(count):
        for _ in range(count):
            k = len(gone)
            rows = pl.ds(k * 64, 64)
            copy = remote(dy_hbm.at[rows], dyo_o.at[rows], xs_sem.at[7 + k], xr_sem.at[7 + k], here.across)
            copy.start()
            gone.append(copy)

    dy_part(2)

    gain = gain_ref[0:1, :]
    bias = bias_ref[0:1, :]
    sends = []
    outs = []

    def out(src, dst):
        copy = pltpu.make_async_copy(src, dst, out_sem.at[len(outs)])
        copy.start()
        outs.append(copy)

    FAR = ((-1, 3, -2), (1, 5, 2))

    def to_mate(array, slot, offset):
        at = rows_of(array, offset, here.core)
        dst = parts[array][1]
        copy = remote(dst.at[at], dst.at[at], mate_s.at[array, slot], mate_r.at[array, slot], here.mate)
        copy.start()
        sends.append(copy)

    def to_ring(array, way, k, offset):
        at = rows_of(array, offset, here.core)
        dst = parts[array][1]
        copy = remote(
            dst.at[at], dst.at[at], ring_s.at[array, way, k], ring_r.at[array, way, k],
            here.next if way == 0 else here.prev,
        )
        copy.start()
        sends.append(copy)

    def from_across(array):
        for k in range(2):
            cross[2 * array + k].wait_recv()
            for way in (0, 1):
                to_ring(array, way, k, 4 * k)
            to_mate(array, k, 4 * k)

    def from_ring(array, k):
        for way in (0, 1):
            at = rows_of(array, FAR[way][k], here.core)
            dst = parts[array][1].at[at]
            remote(dst, dst, ring_s.at[array, way, k], ring_r.at[array, way, k], here.next).wait_recv()
            if k == 0:
                to_ring(array, way, 2, FAR[way][0])
            to_mate(array, 2 + 2 * k + way, FAR[way][k])

    def mate_wait(array):
        offsets = [0, 4] + [FAR[way][k] for k in range(3) for way in (0, 1)]
        for slot, offset in enumerate(offsets):
            dst = parts[array][1].at[rows_of(array, offset, 1 - here.core)]
            remote(dst, dst, mate_s.at[array, slot], mate_r.at[array, slot], here.mate).wait_recv()

    loads[0].wait()

    @pl.loop(0, ROWS // 128)
    def _(i):
        at = aligned(i * 128, 128, 128)
        unit, _ = row_norm(x_v[at, :].astype(F32))
        first_v[at, :] = (unit * gain + bias).astype(BF)

    out(first_v, first_o)
    crop_len = len_ref[0]

    def project(half, weights, which):
        @pl.loop(0, 2)
        def _(c):
            at = aligned(c * CH, CH, CH)
            rows = first_v[at, :]
            for i in which:
                raw = dot_nn(rows, weights[pl.ds(i * 1024, 1024), :])
                if i < 2:
                    raw = jnp.where(raw > 0, raw + 1.0, jnp.exp(jnp.minimum(raw, 0.0)))
                if i == 1:
                    place = lax.broadcasted_iota(jnp.int32, raw.shape, 0) + (here.mp * ROWS + c * CH)
                    raw = jnp.where(place < crop_len, raw, 0.0)
                qkv_v[half, i, at, :] = raw.astype(BF)

    def states(half):
        keep = same_head()

        @pl.loop(0, 4)
        def _(p):
            lanes = aligned(p * PAIR, PAIR, PAIR)
            total = None
            for c in range(2):
                keys = qkv_v[half, 1, pl.ds(c * CH, CH), lanes]
                vals = qkv_v[half, 2, pl.ds(c * CH, CH), lanes]
                made = dot_tn(keys, jnp.concatenate([vals, jnp.ones_like(vals)], axis=1))
                packed = jnp.where(keep, made[:, :PAIR], made[:, PAIR:])
                if c == 0:
                    local_v[half, p] = packed
                    total = packed
                else:
                    ssend_v[half, p] = (total + packed).astype(BF)

        copy = remote(
            ssend_v.at[half], srecv_v.at[1 - half], xs_sem.at[5 + half], xr_sem.at[6 - half], here.across
        )
        copy.start()
        sends.append(copy)

    def inside(half):
        mask = causal_tile()

        @pl.loop(0, 8)
        def _(n):
            p = n // 2
            c = lax.rem(n, 2)
            lanes = aligned(p * PAIR, PAIR, PAIR)
            at = aligned(c * CH, CH, CH)
            query = qkv_v[half, 0, at, lanes]
            key = qkv_v[half, 1, at, lanes]
            val = qkv_v[half, 2, at, lanes]
            first = lane_head(val.shape)
            one = jnp.ones_like(val)
            zero = jnp.zeros_like(val)
            sums = None
            for head, part in enumerate(split_heads(query)):
                score = jnp.where(mask, dot_nt(part, key), 0.0).astype(BF)
                mine = first if head == 0 else jnp.logical_not(first)
                right = jnp.concatenate([jnp.where(mine, val, zero), jnp.where(mine, one, zero)], axis=1)
                term = dot_nn(score, right)
                sums = term if sums is None else sums + term
            num_v[at, lanes] = sums[:, :PAIR]
            den_v[half, at, lanes] = sums[:, PAIR:]

    def finish(half):
        flag = here.mp.astype(F32)

        @pl.loop(0, 8)
        def _(n):
            p = n // 2
            c = lax.rem(n, 2)
            lanes = aligned(p * PAIR, PAIR, PAIR)
            at = aligned(c * CH, CH, CH)
            query = qkv_v[half, 0, at, lanes]
            before = srecv_v[half, p].astype(F32) * flag
            state_v[half, p] = before.astype(BF)
            before = before + local_v[half, p] * c.astype(F32)
            term = dot_nn(query, unpack_state(before).astype(BF))
            num = num_v[at, lanes] + term[:, :PAIR]
            den = den_v[half, at, lanes] + term[:, PAIR:]
            inverse = 1.0 / den
            den_v[half, at, lanes] = inverse
            mix_v[half, at, lanes] = (num * inverse).astype(BF)
            place = lax.broadcasted_iota(jnp.int32, den.shape, 0) + (here.mp * ROWS + c * CH)
            kept = jnp.where(place < crop_len, den, 0.0).reshape(CH // 8, 8, PAIR)
            stat_ref[0] = jnp.maximum(stat_ref[0], jnp.max(kept, axis=0))
            stat_ref[1] = stat_ref[1] + jnp.sum(kept, axis=0)

    def hidden_grad():
        @pl.loop(0, 2)
        def _(j):
            cols = aligned(j * 1024, 1024, 1024)
            hg_v[:, cols] = dot_nt(dy_v[...], wdn_v[cols, :]).astype(BF)

    stat_ref[...] = jnp.zeros_like(stat_ref)
    loads[1].wait()
    project(0, win_v, (1, 2))
    states(0)
    dy_part(1)
    project(0, win_v, (0,))
    from_across(0)
    dy_part(1)
    inside(0)
    from_ring(0, 0)
    from_across(1)
    dy_part(2)
    loads[2].wait()
    loads[3].wait()
    hidden_grad()
    from_ring(0, 1)
    from_ring(1, 0)
    from_ring(0, 2)
    mate_wait(0)
    from_ring(1, 1)
    out(wino_v, wino_o)
    mid_v[:, pl.ds(0, 512)] = num_v[...]
    project(1, wino_v, (1, 2))
    states(1)
    dy_part(2)
    project(1, wino_v, (0,))
    from_ring(1, 2)
    inside(1)
    remote(ssend_v.at[0], srecv_v.at[1], xs_sem.at[5], xr_sem.at[6], here.across).wait_recv()
    finish(1)
    out(hg_v, hg_o)
    num_v[...] = mid_v[:, pl.ds(0, 512)]
    mate_wait(1)
    remote(ssend_v.at[1], srecv_v.at[0], xs_sem.at[6], xr_sem.at[5], here.across).wait_recv()
    finish(0)
    out(qkv_v, qkv_o)
    out(den_v, rden_o)
    out(mix_v, mix_o)
    out(state_v, state_o)
    out(woo_v, woo_o)
    loads[4].wait()
    gain_two = gain_ref[1:2, :]
    bias_two = bias_ref[1:2, :]

    @pl.loop(0, 2)
    def _(c):
        at = aligned(c * CH, CH, CH)
        own = dot_nn(mix_v[0, at, :], wo_v[...]).astype(BF).astype(F32)
        other = dot_nn(mix_v[1, at, :], woo_v[...]).astype(BF).astype(F32)
        middle = x_v[at, :].astype(F32) + (own + other)
        mid_v[at, :] = middle
        unit, _ = row_norm(middle)
        sec_v[at, :] = (unit * gain_two + bias_two).astype(BF)

    out(mid_v, mid_o)
    out(sec_v, sec_o)
    for copy in gone:
        copy.wait_recv()
    for copy in cross + gone + sends:
        copy.wait_send()
    for copy in outs:
        copy.wait()


def any_spec(count):
    return [pl.BlockSpec(memory_space=pl.ANY)] * count


def front(lengths, x_rows, dy_rows, win, wo, wdn, gain, bias):
    vm = pltpu.VMEM
    shapes = [
        ((512, 1024), BF), ((2, 3, 512, 512), BF), ((2, 512, 512), BF), ((2, 512, 512), F32),
        ((2, 4, PAIR, PAIR), BF), ((512, 1024), F32), ((512, 1024), BF), ((3072, 512), BF),
        ((512, 1024), BF), ((512, 1024), BF), ((512, 2048), BF), ((2, 8, PAIR), F32),
    ]
    dma = pltpu.SemaphoreType.DMA
    return pl.pallas_call(
        front_kernel,
        out_shape=[jax.ShapeDtypeStruct(s, d) for s, d in shapes],
        in_specs=[pl.BlockSpec(memory_space=pltpu.SMEM)] + any_spec(5)
        + [pl.BlockSpec(memory_space=pltpu.VMEM)] * 2,
        out_specs=any_spec(11) + [pl.BlockSpec(memory_space=pltpu.VMEM)],
        scratch_shapes=[
            vm((512, 1024), BF), vm((512, 1024), BF), vm((3072, 512), BF), vm((3072, 512), BF),
            vm((512, 1024), BF), vm((512, 1024), BF), vm((2048, 1024), BF), vm((512, 1024), BF),
            vm((2, 3, 512, 512), BF), vm((512, 512), F32), vm((2, 512, 512), F32), vm((2, 512, 512), BF),
            vm((512, 1024), F32), vm((512, 1024), BF), vm((512, 2048), BF),
            vm((2, 4, PAIR, PAIR), F32), vm((2, 4, PAIR, PAIR), BF), vm((2, 4, PAIR, PAIR), BF),
            vm((2, 4, PAIR, PAIR), BF),
            dma((5,)), dma((12,)), dma((15,)), dma((15,)), dma((2, 2, 3)), dma((2, 2, 3)),
            dma((2, 8)), dma((2, 8)),
        ],
        compiler_params=pltpu.CompilerParams(
            collective_id=0, has_side_effects=True, vmem_limit_bytes=58 * 1024 * 1024
        ),
        name="front",
    )(lengths, x_rows, dy_rows, win, wo, wdn, gain, bias)


GELU_A = 0.7978845608028654
GELU_B = 0.044715


def gelu_pair(v):
    square = v * v
    t = jnp.tanh(GELU_A * v * (1.0 + GELU_B * square))
    half = 0.5 * (1.0 + t)
    slope = half + (0.5 * GELU_A) * v * (1.0 - t * t) * (1.0 + (3.0 * GELU_B) * square)
    return v * half, slope


def middle_kernel(
    sec_hbm, dy_hbm, dyo_hbm, hg_hbm, wup_hbm, wdn_hbm,
    part_o, pin_o, mlp_o, dslab_o, uslab_o,
    sec_v, dy_v, hg_v, wup_v, wdn_v, hid_v, part_v, send_v, pin_v, mlp_v,
    dsend_v, drecv_v, dslab_v, usend_v, urecv_v, uslab_v,
    in_sem, out_sem, xs_sem, xr_sem, ms_sem, mr_sem,
):
    here = Place()
    own = pl.ds(0, ROWS)
    other = pl.ds(ROWS, ROWS)
    loads = [
        (sec_hbm, sec_v.at[own]), (wup_hbm, wup_v), (hg_hbm, hg_v.at[own]), (wdn_hbm, wdn_v),
        (dy_hbm, dy_v.at[own]), (dyo_hbm, dy_v.at[other]),
    ]
    loads = [pltpu.make_async_copy(a, b, in_sem.at[i]) for i, (a, b) in enumerate(loads)]
    for load in loads:
        load.start()
    greet([here.across, here.mate])
    sends = []
    outs = []

    def out(src, dst):
        copy = pltpu.make_async_copy(src, dst, out_sem.at[len(outs)])
        copy.start()
        outs.append(copy)

    def across(src, dst, slot):
        copy = remote(src, dst, xs_sem.at[slot], xr_sem.at[slot], here.across)
        copy.start()
        sends.append(copy)
        return copy

    ahead = [
        across(sec_hbm.at[pl.ds(c * CH, CH)], sec_v.at[pl.ds(ROWS + c * CH, CH)], c) for c in range(2)
    ]

    def up(chunk):
        rows = pl.ds(chunk * CH, CH)

        @pl.loop(0, 4)
        def _(j):
            cols = aligned(j * 512, 512, 512)
            raw = dot_nn(sec_v[rows, :], wup_v[:, cols])
            value, slope = gelu_pair(raw)
            hid_v[rows, cols] = value.astype(BF)
            hg_v[rows, cols] = (hg_v[rows, cols].astype(F32) * slope).astype(BF)

    def back(chunk, dst):
        dst[...] = dot_nt(hg_v[pl.ds(chunk * CH, CH), :], wup_v[...]).astype(BF)

    loads[0].wait()
    loads[1].wait()
    loads[2].wait()
    for c in range(2):
        up(c)
        back(c, part_v.at[pl.ds(c * CH, CH)])
    out(part_v, part_o)
    for load in loads[3:]:
        load.wait()
    for c in range(2):
        @pl.loop(0, 2)
        def _(j):
            cols = aligned(j * 1024, 1024, 1024)
            rows = pl.ds(ROWS + c * CH, CH)
            hg_v[rows, cols] = dot_nt(dy_v[rows, :], wdn_v[cols, :]).astype(BF)

        ahead[c].wait_recv()
        up(2 + c)
        rows = pl.ds(c * CH, CH)
        back(2 + c, send_v.at[rows])
        across(send_v.at[rows], pin_v.at[rows], 2 + c)
    their = 1 - here.core

    def down_grad(half, dst, plus):
        @pl.loop(0, 2)
        def _(i):
            cols = aligned(half * 1024 + i * 512, 512, 512)
            at = aligned(i * 512, 512, 512)
            made = dot_tn(hid_v[:, cols], dy_v[...])
            if plus is not None:
                made = made + plus[at, :].astype(F32)
            dst[at, :] = made.astype(BF)

    def up_grad(half, dst, plus):
        @pl.loop(0, 2)
        def _(i):
            cols = aligned(half * 512, 512, 512)
            at = aligned(i * 1024, 1024, 1024)
            made = dot_tn(sec_v[:, cols], hg_v[:, at])
            if plus is not None:
                made = made + plus[:, at].astype(F32)
            dst[:, at] = made.astype(BF)

    def to_mate(src, dst, slot):
        copy = remote(src, dst, ms_sem.at[slot], mr_sem.at[slot], here.mate)
        copy.start()
        sends.append(copy)
        return copy

    down_grad(their, dsend_v, None)
    to_d = to_mate(dsend_v, drecv_v, 0)
    up_grad(their, usend_v, None)
    to_u = to_mate(usend_v, urecv_v, 1)

    @pl.loop(0, 2)
    def _(i):
        rows = aligned(i * ROWS, ROWS, ROWS)
        mlp_v[rows, :] = dot_nn(hid_v[rows, :], wdn_v[...]).astype(BF)

    out(mlp_v, mlp_o)
    to_d.wait_recv()
    down_grad(here.core, dslab_v, drecv_v)
    out(dslab_v, dslab_o)
    to_u.wait_recv()
    up_grad(here.core, uslab_v, urecv_v)
    out(uslab_v, uslab_o)
    for c in range(2):
        rows = pl.ds(c * CH, CH)
        remote(send_v.at[rows], pin_v.at[rows], xs_sem.at[2 + c], xr_sem.at[2 + c], here.across).wait_recv()
    out(pin_v, pin_o)
    for copy in sends:
        copy.wait_send()
    for copy in outs:
        copy.wait()


def middle(sec, dy, dyo, hg, wup, wdn):
    vm = pltpu.VMEM
    dma = pltpu.SemaphoreType.DMA
    shapes = [
        ((512, 1024), BF), ((512, 1024), BF), ((1024, 1024), BF), ((1024, 1024), BF), ((512, 2048), BF),
    ]
    return pl.pallas_call(
        middle_kernel,
        out_shape=[jax.ShapeDtypeStruct(s, d) for s, d in shapes],
        in_specs=any_spec(6),
        out_specs=any_spec(5),
        scratch_shapes=[
            vm((1024, 1024), BF), vm((1024, 1024), BF), vm((1024, 2048), BF), vm((1024, 2048), BF),
            vm((2048, 1024), BF), vm((1024, 2048), BF), vm((512, 1024), BF), vm((512, 1024), BF),
            vm((512, 1024), BF), vm((1024, 1024), BF),
            vm((1024, 1024), BF), vm((1024, 1024), BF), vm((1024, 1024), BF),
            vm((512, 2048), BF), vm((512, 2048), BF), vm((512, 2048), BF),
            dma((6,)), dma((5,)), dma((4,)), dma((4,)), dma((2,)), dma((2,)),
        ],
        compiler_params=pltpu.CompilerParams(
            collective_id=1, has_side_effects=True, vmem_limit_bytes=58 * 1024 * 1024
        ),
        name="middle",
    )(sec, dy, dyo, hg, wup, wdn)


PACE = 36


class Arc:
    def __init__(self, here, slab, base, rows, recv, result, result_base, sems):
        self.here, self.slab, self.base, self.rows = here, slab, base, rows
        self.recv, self.result, self.result_base = recv, result, result_base
        self.rs_s, self.rs_r, self.ag_s, self.ag_r, self.mt_s, self.mt_r, self.local = sems
        self.pending = []
        self.t = 0

    def span(self, base, offset, half):
        start = base + lax.rem(self.here.r + 8 + offset, 8) * self.rows
        if half is None:
            return aligned(start, self.rows, 16)
        return aligned(start + half * (self.rows // 2), self.rows // 2, 16)

    def mine(self, offset, half=None):
        return self.span(self.base, offset, half)

    def place(self, offset, core, half=None):
        return self.result.at[self.span(self.result_base(core) + self.base, offset, half)]

    def send(self, src, dst, send_sem, recv_sem, device):
        copy = remote(src, dst, send_sem, recv_sem, device)
        copy.start()
        self.pending.append(copy)

    def to(self, way):
        return self.here.next if way == 0 else self.here.prev

    def sign(self, way):
        return 1 if way == 0 else -1

    def slot(self, way, s):
        if s > 0:
            return self.recv.at[way, s]
        return self.recv.at[way, 0, pl.ds(way * (self.rows // 2), self.rows // 2)]

    def arrived(self, way, s):
        got = self.slot(way, s)
        remote(got, got, self.rs_s.at[way, s], self.rs_r.at[way, s], self.to(way)).wait_recv()

    def gather_step(self, way, s):
        sign = self.sign(way)
        if s == 0:
            src = self.slab.at[self.mine(sign * 4, way)]
        else:
            self.arrived(way, s - 1)
            own = self.slab[self.mine(sign * (4 - s)), :].astype(F32)
            src = self.recv.at[way, s - 1]
            if s == 1:
                half = self.rows // 2
                kept = pl.ds(way * half, half)
                rest = pl.ds((1 - way) * half, half)
                at = slice(way * half, way * half + half)
                src[kept, :] = (src[kept, :].astype(F32) + own[at]).astype(BF)
                at = slice((1 - way) * half, (1 - way) * half + half)
                src[rest, :] = own[at].astype(BF)
            else:
                src[...] = (src[...].astype(F32) + own).astype(BF)
        self.send(src, self.slot(way, s), self.rs_s.at[way, s], self.rs_r.at[way, s], self.to(way))

    def spread(self, src, offset, step, way, half=None):
        dst = self.place(offset, self.here.core, half)
        if step < 4 and not (step == 3 and half is None):
            self.send(src, dst, self.ag_s.at[way, step], self.ag_r.at[way, step], self.to(way))

    def to_mate(self, src, offset, slot, half=None):
        dst = self.place(offset, self.here.core, half)
        self.send(src, dst, self.mt_s.at[slot], self.mt_r.at[slot], self.here.mate)

    def total(self):
        self.arrived(0, 3)
        self.arrived(1, 3)
        sums = self.recv.at[0, 3]
        own = self.slab[self.mine(0), :].astype(F32)
        sums[...] = (sums[...].astype(F32) + self.recv[1, 3].astype(F32) + own).astype(BF)
        for way in (0, 1):
            self.spread(sums, 0, 0, way)
        self.to_mate(sums, 0, 0)
        self.keep = pltpu.make_async_copy(sums, self.place(0, self.here.core), self.local)
        self.keep.start()

    def spread_step(self, way, s):
        sign = self.sign(way)
        half = way if s == 3 else None
        got = self.place(-sign * (s + 1), self.here.core, half)
        remote(got, got, self.ag_s.at[way, s], self.ag_r.at[way, s], self.to(way)).wait_recv()
        if s < 3:
            part = way if s == 2 else None
            src = self.place(-sign * (s + 1), self.here.core, part)
            self.spread(src, -sign * (s + 1), s + 1, way, part)
        self.to_mate(got, -sign * (s + 1), 1 + 2 * s + way, half)

    def tick(self):
        t = self.t
        self.t = t + 1
        if t == 4:
            self.total()
        elif t < 9:
            for way in (0, 1):
                if t < 4:
                    self.gather_step(way, t)
                else:
                    self.spread_step(way, t - 5)

    def finish(self):
        for copy in self.pending:
            copy.wait_send()
        self.keep.wait()
        other = 1 - self.here.core
        for slot in range(9):
            if slot == 0:
                got = self.place(0, other)
            else:
                s, way = (slot - 1) // 2, (slot - 1) % 2
                got = self.place(-self.sign(way) * (s + 1), other, way if s == 3 else None)
            remote(got, got, self.mt_s.at[slot], self.mt_r.at[slot], self.here.mate).wait_recv()


def back_kernel(
    len_ref, gain_ref, bias_ref, stat_ref,
    part_hbm, pin_hbm, mid_hbm, x_hbm, dy_hbm, qkv_hbm, mix_hbm, rden_hbm, state_hbm, first_hbm,
    win_hbm, wino_hbm, wo_hbm, woo_hbm, mlp_hbm, dslab_hbm, uslab_hbm,
    resd_o, resu_o, resi_o, reso_o, out_o, gin_o, small_ref,
    part_v, pin_v, mid_v, dy_v, qkv_v, mix_v, rden_v, state_v, first_v, win_v, wo_v,
    mlpin_v, mg_v, mgf_v, mixg_v, top_v, bot_v, dqkv_v, local_v, lsend_v, lrecv_v,
    dslab_v, uslab_v, drecv_v, urecv_v, gm_v, gr_v, ga_v, gx_v, om_v, or_v, oa_v, ox_v, irecv_v, orecv_v,
    small_s, small_r,
    in_sem, out_sem, xs_sem, xr_sem, ms_sem, mr_sem, bs_sem, br_sem,
    rs_s, rs_r, ag_s, ag_r, mt_s, mt_r, keep_s,
):
    here = Place()
    loads = [
        (part_hbm, part_v), (pin_hbm, pin_v), (mid_hbm, mid_v), (dy_hbm, dy_v), (dslab_hbm, dslab_v),
        (uslab_hbm, uslab_v), (wo_hbm, wo_v.at[0]), (woo_hbm, wo_v.at[1]), (mix_hbm, mix_v),
        (rden_hbm, rden_v), (qkv_hbm, qkv_v), (state_hbm, state_v), (first_hbm, first_v),
        (win_hbm, win_v.at[0]), (wino_hbm, win_v.at[1]), (x_hbm, part_v), (mlp_hbm.at[pl.ds(0, ROWS)], pin_v),
    ]
    loads = [pltpu.make_async_copy(a, b, in_sem.at[i]) for i, (a, b) in enumerate(loads)]
    for load in loads[:15]:
        load.start()
    y_mate = (here.dp + 2 - 4 * lax.rem(here.dp // 2, 2), here.mp)
    z_mate = (here.dp + 4 - 8 * lax.rem(here.dp // 4, 2), here.mp)
    z_far = (here.dp + 8 - 16 * (here.dp // 8), here.mp)
    greet(here.partners() + [y_mate, z_mate, z_far])
    sends = []
    outs = []

    def out(src, dst):
        copy = pltpu.make_async_copy(src, dst, out_sem.at[len(outs)])
        copy.start()
        outs.append(copy)

    def across(src, dst, slot):
        copy = remote(src, dst, xs_sem.at[slot], xr_sem.at[slot], here.across)
        copy.start()
        sends.append(copy)
        return copy

    def to_mate(src, dst, slot):
        copy = remote(src, dst, ms_sem.at[slot], mr_sem.at[slot], here.mate)
        copy.start()
        sends.append(copy)
        return copy

    arcs = []

    def add_arc(slab, base, rows, recv, result, result_base):
        n = len(arcs)
        sems = (rs_s.at[n], rs_r.at[n], ag_s.at[n], ag_r.at[n], mt_s.at[n], mt_r.at[n], keep_s.at[n])
        arcs.append(Arc(here, slab, base, rows, recv, result, result_base, sems))
        return arcs[-1]

    ring_d = add_arc(dslab_v, 0, 128, drecv_v, resd_o, lambda core: core * 1024)
    ring_u = add_arc(uslab_v, 0, 64, urecv_v, resu_o, lambda core: core * 512)
    ring_o = add_arc(oa_v.at[0], 0, 32, orecv_v, reso_o, lambda core: core * 256)
    ring_i = [
        add_arc(ga_v.at[0], i * 512, 64, irecv_v.at[i], resi_o, lambda core: core * 1536) for i in range(3)
    ]

    credit = [0]

    def ring(count):
        credit[0] += count * PACE
        while credit[0] >= 100:
            credit[0] -= 100
            first = ring_d if ring_d.t <= ring_u.t else ring_u
            first.tick()

    def ring_on(arc):
        arc.tick()

    loads[4].wait()
    loads[5].wait()
    ring_d.tick()
    ring_u.tick()

    small_s[...] = jnp.zeros_like(small_s)
    for load in loads[0:4]:
        load.wait()
    gain_two = gain_ref[1:2, :]

    @pl.loop(0, ROWS // 128)
    def _(i):
        at = aligned(i * 128, 128, 128)
        grad = part_v[at, :].astype(F32) + pin_v[at, :].astype(F32)
        unit, inverse = row_norm(mid_v[at, :])
        scaled = grad * gain_two
        centre = jnp.mean(scaled, axis=-1, keepdims=True)
        along = jnp.mean(scaled * unit, axis=-1, keepdims=True)
        total = dy_v[at, :].astype(F32) + inverse * (scaled - centre - unit * along)
        mgf_v[at, :] = total
        mg_v[at, :] = total.astype(BF)
        small_s[1:2, :] = small_s[1:2, :] + jnp.sum(grad * unit, axis=0, keepdims=True)
        small_s[3:4, :] = small_s[3:4, :] + jnp.sum(grad, axis=0, keepdims=True)

    for load in loads[15:]:
        load.start()
    ring(2)
    for load in loads[6:12]:
        load.wait()
    for half in range(2):
        mixg_v[half] = dot_nt(mg_v[...], wo_v[half]).astype(BF)
    ring(1)
    their = 1 - here.core

    def out_grad(half, side, dst):
        cols = aligned(side * 256, 256, 256)
        dst[...] = dot_tn(mix_v[half, :, cols], mg_v[...]).astype(BF)

    keep = same_head()

    def tops(half):
        @pl.loop(0, 4)
        def _(p):
            lanes_at = aligned(p * PAIR, PAIR, PAIR)
            packs = []
            blocks = jnp.where(keep, 1.0, 0.0).astype(BF)
            for c in range(2):
                at = pl.ds(c * CH, CH)
                top = (mixg_v[half, at, lanes_at].astype(F32) * rden_v[half, at, lanes_at]).astype(BF)
                top_v[half, at, lanes_at] = top
                prod = top.astype(F32) * mix_v[half, at, lanes_at].astype(F32)
                high = prod.astype(BF)
                low = (prod - high.astype(F32)).astype(BF)
                bottom = -(dot_nn(high, blocks) + dot_nn(low, blocks))
                high = bottom.astype(BF)
                low = (bottom - high.astype(F32)).astype(BF)
                lane = lax.rem(lax.broadcasted_iota(jnp.int32, bottom.shape, 1), DH)
                bot_v[half, at, lanes_at] = jnp.where(
                    lane == 0, high, jnp.where(lane == 1, low, jnp.zeros_like(high))
                )
                query = qkv_v[half, 0, at, lanes_at]
                made = dot_tn(query, jnp.concatenate([top, high], axis=1))
                packs.append(jnp.where(keep, made[:, :PAIR], pltpu.roll(made[:, PAIR:], DH, 1)))
            local_v[half, p] = packs[1]
            lsend_v[half, p] = (packs[0] + packs[1]).astype(BF)

        across(lsend_v.at[half], lrecv_v.at[1 - half], 1 + half)

    tops(0)
    ring(1)
    tops(1)
    ring(1)
    for half in (1, 0):
        out_grad(half, their, om_v.at[half])
        to_mate(om_v.at[half], or_v.at[half], half)
    ring(1)
    for half in (1, 0):
        out_grad(half, here.core, oa_v.at[half])
    ring(1)
    for load in loads[12:15]:
        load.wait()

    def attend_back(half):
        mask = causal_tile()
        earlier = 1.0 - here.mp.astype(F32)
        remote(
            lsend_v.at[1 - half], lrecv_v.at[half], xs_sem.at[2 - half], xr_sem.at[2 - half], here.across
        ).wait_recv()

        def body(p, c):
            lanes_at = aligned(p * PAIR, PAIR, PAIR)
            at = pl.ds(c * CH, CH)
            query = qkv_v[half, 0, at, lanes_at]
            key = qkv_v[half, 1, at, lanes_at]
            val = qkv_v[half, 2, at, lanes_at]
            top = top_v[half, at, lanes_at]
            bot = bot_v[half, at, lanes_at]
            lane = lax.rem(lax.broadcasted_iota(jnp.int32, val.shape, 1), DH)
            one = jnp.ones_like(val)
            zero = jnp.zeros_like(val)
            val_two = jnp.concatenate([val, jnp.where(lane < 2, one, zero)], axis=1)
            val_one = jnp.concatenate([val, jnp.where(lane == 0, one, zero)], axis=1)
            before = state_v[half, p].astype(F32)
            after = lrecv_v[half, p].astype(F32) * earlier
            if c == 1:
                key0 = qkv_v[half, 1, pl.ds(0, CH), lanes_at]
                val0 = qkv_v[half, 2, pl.ds(0, CH), lanes_at]
                made = dot_tn(key0, jnp.concatenate([val0, one], axis=1))
                before = before + jnp.where(keep, made[:, :PAIR], made[:, PAIR:])
            else:
                after = after + local_v[half, p]
            before = unpack_state(before).astype(BF)
            after = unpack_state(after).astype(BF)
            dq = dot_nt(jnp.concatenate([top, bot], axis=1), before)
            dk = dot_nt(val_one, after)
            dv = dot_nn(key, after[:, :PAIR])
            queries, keys, tops_, bots = split_heads(query), split_heads(key), split_heads(top), split_heads(bot)
            for head in range(2):
                score = jnp.where(mask, dot_nt(queries[head], key), 0.0).astype(BF)
                grad = dot_nt(jnp.concatenate([tops_[head], bots[head]], axis=1), val_two)
                grad = jnp.where(mask, grad, 0.0).astype(BF)
                dq = dq + dot_nn(grad, keys[head])
                dk = dk + dot_tn(grad, queries[head])
                dv = dv + dot_tn(score, tops_[head])
            dqkv_v[half, 0, at, lanes_at] = (dq * jnp.minimum(query.astype(F32), 1.0)).astype(BF)
            dqkv_v[half, 1, at, lanes_at] = (dk * jnp.minimum(key.astype(F32), 1.0)).astype(BF)
            dqkv_v[half, 2, at, lanes_at] = dv.astype(BF)

        for part in range(2):
            @pl.loop(part * 2, part * 2 + 2)
            def _(p):
                body(p, 0)
                body(p, 1)

            ring(2)

    def piece(i):
        return pl.ds(i * 512, 512)

    def in_grads(half):
        for side, dst in ((their, gm_v), (here.core, ga_v)):
            cols = aligned(side * 512, 512, 512)
            for i in range(3):
                at = piece(i)
                dst[half, at, :] = dot_tn(first_v[:, cols], dqkv_v[half, i]).astype(BF)
                if dst is gm_v:
                    to_mate(gm_v.at[half, at], gr_v.at[half, at], 2 + half * 3 + i)
            ring(1)

    def add_rows(dst, src, start, count):
        @pl.loop(0, count)
        def _(i):
            at = aligned(start + i * 128, 128, 128)
            dst[at, :] = (dst[at, :].astype(F32) + src[at, :].astype(F32)).astype(BF)

    def mate_arrival(half, i):
        at = piece(i)
        slot = 2 + half * 3 + i
        remote(gm_v.at[half, at], gr_v.at[half, at], ms_sem.at[slot], mr_sem.at[slot], here.mate).wait_recv()
        add_rows(ga_v.at[half], gr_v.at[half], i * 512, 4)

    def mate_arrival_out(half):
        remote(om_v.at[half], or_v.at[half], ms_sem.at[half], mr_sem.at[half], here.mate).wait_recv()
        add_rows(oa_v.at[half], or_v.at[half], 0, 2)

    attend_back(1)
    mate_arrival_out(1)
    cross_o = across(oa_v.at[1], ox_v, 3)
    in_grads(1)
    cross_i = []
    for i in range(3):
        mate_arrival(1, i)
        cross_i.append(across(ga_v.at[1, piece(i)], gx_v.at[piece(i)], 4 + i))
    mlp = across(mlp_hbm.at[pl.ds(ROWS, ROWS)], mlpin_v, 0)
    ring(2)
    mate_arrival_out(0)
    attend_back(0)
    cross_o.wait_recv()
    add_rows(oa_v.at[0], ox_v, 0, 2)
    ring_on(ring_o)
    in_grads(0)
    for i in range(3):
        mate_arrival(0, i)
    ring(2)
    ring_on(ring_o)

    loads[15].wait()
    gain_one = gain_ref[0:1, :]

    for quarter in range(2):
        at = pl.ds(quarter * CH, CH)
        grad = None
        for half in range(2):
            term = None
            for j in range(3):
                made = dot_nt(dqkv_v[half, j, at, :], win_v[half, pl.ds(j * 1024, 1024), :])
                term = made if term is None else term + made
            term = term.astype(BF).astype(F32)
            grad = term if grad is None else grad + term
        unit, inverse = row_norm(part_v[at, :].astype(F32))
        scaled = grad * gain_one
        centre = jnp.mean(scaled, axis=-1, keepdims=True)
        along = jnp.mean(scaled * unit, axis=-1, keepdims=True)
        mgf_v[at, :] = mgf_v[at, :] + inverse * (scaled - centre - unit * along)
        small_s[0:1, :] = small_s[0:1, :] + jnp.sum(grad * unit, axis=0, keepdims=True)
        small_s[2:3, :] = small_s[2:3, :] + jnp.sum(grad, axis=0, keepdims=True)
        ring(2)
        ring_on(ring_o)

    out(mgf_v, gin_o)
    small_s[4:5, pl.ds(0, PAIR)] = jnp.sum(stat_ref[1], axis=0, keepdims=True) * (1.0 / DH)
    count = len_ref[0].astype(F32) * (8.0 / 1024.0)
    small_s[5:6, :] = jnp.zeros((1, 1024), F32) + count
    small_s[6:7, pl.ds(0, PAIR)] = jnp.max(stat_ref[0], axis=0, keepdims=True)
    partners = [here.mate, y_mate, z_mate, z_far, here.across]

    def small_send(step):
        src = small_s if step == 0 else small_ref
        copy = remote(src, small_r.at[step], bs_sem.at[step], br_sem.at[step], partners[step])
        copy.start()
        return copy

    def small_step(copy, step):
        copy.wait()
        src = small_s if step == 0 else small_ref
        mine, theirs = src[...], small_r[step]
        row = lax.broadcasted_iota(jnp.int32, mine.shape, 0)
        small_ref[...] = jnp.where(row < 6, mine + theirs, jnp.maximum(mine, theirs))

    for i in range(3):
        cross_i[i].wait_recv()
        add_rows(ga_v.at[0], gx_v, i * 512, 4)
        for arc in ring_i[: i + 1]:
            ring_on(arc)
        ring(6)
        ring_on(ring_o)
    copy = small_send(0)
    for step in range(9):
        for arc in ring_i:
            ring_on(arc)
        ring(6)
        ring_on(ring_o)
        if 2 <= step < 7:
            small_step(copy, step - 2)
            if step < 6:
                copy = small_send(step - 1)
    ring(2000)

    loads[16].wait()
    mlp.wait_recv()

    @pl.loop(0, 4)
    def _(i):
        at = aligned(i * 128, 128, 128)
        total = mid_v[at, :] + (pin_v[at, :].astype(F32) + mlpin_v[at, :].astype(F32))
        pin_v[at, :] = total.astype(BF)

    out(pin_v, out_o)
    for arc in arcs:
        arc.finish()
    for copy in sends:
        copy.wait_send()
    for copy in outs:
        copy.wait()


def back(lengths, gain, bias, stat, part, pin, mid, x, dy, qkv, mix, rden, state, first, win, wino, wo, woo, mlp, dslab, uslab):
    vm = pltpu.VMEM
    dma = pltpu.SemaphoreType.DMA
    shapes = [
        ((2048, 1024), BF), ((1024, 2048), BF), ((3072, 512), BF), ((512, 1024), BF),
        ((512, 1024), BF), ((512, 1024), F32), ((8, 1024), F32),
    ]
    rows = (512, 1024)
    heads = (2, 512, 512)
    pack = (2, 4, PAIR, PAIR)
    vmem = pl.BlockSpec(memory_space=pltpu.VMEM)
    return pl.pallas_call(
        back_kernel,
        out_shape=[jax.ShapeDtypeStruct(s, d) for s, d in shapes],
        in_specs=[pl.BlockSpec(memory_space=pltpu.SMEM), vmem, vmem, vmem] + any_spec(17),
        out_specs=any_spec(6) + [vmem],
        scratch_shapes=[
            vm(rows, BF), vm(rows, BF), vm(rows, F32), vm(rows, BF),
            vm((2, 3, 512, 512), BF), vm(heads, BF), vm(heads, F32), vm(pack, BF), vm(rows, BF),
            vm((2, 3072, 512), BF), vm((2, 512, 1024), BF),
            vm(rows, BF), vm(rows, BF), vm(rows, F32), vm(heads, BF), vm(heads, BF), vm(heads, BF),
            vm((2, 3, 512, 512), BF), vm(pack, F32), vm(pack, BF), vm(pack, BF),
            vm((1024, 1024), BF), vm((512, 2048), BF), vm((2, 4, 128, 1024), BF), vm((2, 4, 64, 2048), BF),
            vm((2, 1536, 512), BF), vm((2, 1536, 512), BF), vm((2, 1536, 512), BF), vm((1536, 512), BF),
            vm((2, 256, 1024), BF), vm((2, 256, 1024), BF), vm((2, 256, 1024), BF), vm((256, 1024), BF),
            vm((3, 2, 4, 64, 512), BF), vm((2, 4, 32, 1024), BF),
            vm((8, 1024), F32), vm((5, 8, 1024), F32),
            dma((17,)), dma((2,)), dma((7,)), dma((7,)), dma((8,)), dma((8,)), dma((5,)), dma((5,)),
            dma((6, 2, 4)), dma((6, 2, 4)), dma((6, 2, 4)), dma((6, 2, 4)), dma((6, 9)), dma((6, 9)), dma((6,)),
        ],
        compiler_params=pltpu.CompilerParams(
            collective_id=2, has_side_effects=True, vmem_limit_bytes=60 * 1024 * 1024
        ),
        name="back",
    )(lengths, gain, bias, stat, part, pin, mid, x, dy, qkv, mix, rden, state, first, win, wino, wo, woo, mlp, dslab, uslab)


def widen_kernel(
    d_hbm, u_hbm, i_hbm, o_hbm, gin_hbm, out_hbm, small_ref,
    di_o, ui_o, ii_o, oi_o, gin_o, out_o, gain_ref, bias_ref, stats_ref,
    d_v, u_v, i_v, o_v, df_v, uf_v, if_v, of_v, in_sem, out_sem,
):
    jobs = []
    for k in range(6):
        core, i = k // 3, k % 3
        jobs.append((i_hbm, i_v, k * 512, ii_o, if_v, i * 1024 + core * 512, 512))
    for k in range(2):
        jobs.append((o_hbm, o_v, k * 256, oi_o, of_v, k * 256, 256))
    for k in range(8):
        jobs.append((u_hbm, u_v, k * 128, ui_o, uf_v, k * 128, 128))
    for k in range(8):
        jobs.append((d_hbm, d_v, k * 256, di_o, df_v, k * 256, 256))
    loads, stores = [], []
    for n, (src, held, at, _, _, _, rows) in enumerate(jobs):
        loads.append(pltpu.make_async_copy(src.at[pl.ds(at, rows)], held.at[pl.ds(at, rows)], in_sem.at[n]))
        loads[-1].start()
    for n, (src, dst) in enumerate(((gin_hbm, gin_o), (out_hbm, out_o))):
        stores.append(pltpu.make_async_copy(src, dst, out_sem.at[len(jobs) + n]))
        stores[-1].start()
    for n, (_, held, at, dst, wide, to, rows) in enumerate(jobs):
        loads[n].wait()

        @pl.loop(0, rows // 128)
        def _(k):
            rows_at = aligned(at + k * 128, 128, 128)
            wide[rows_at, :] = held[rows_at, :].astype(F32)

        stores.append(pltpu.make_async_copy(wide.at[pl.ds(at, rows)], dst.at[pl.ds(to, rows)], out_sem.at[n]))
        stores[-1].start()
    gain_ref[...] = small_ref[0:2, :]
    bias_ref[...] = small_ref[2:4, :]
    scaling = 1.0 / (DH * 1024)
    count = jnp.max(small_ref[5:6, :]) * 1024.0
    stats_ref[0] = jnp.max(small_ref[6:7, :]) * scaling
    stats_ref[1] = jnp.sum(small_ref[4:5, :]) / count * scaling
    for copy in stores:
        copy.wait()


def widen(resd, resu, resi, reso, gin, out, small):
    vm = pltpu.VMEM
    vmem = pl.BlockSpec(memory_space=pltpu.VMEM)
    shapes = [
        ((2048, 1024), F32), ((1024, 2048), F32), ((3072, 512), F32), ((512, 1024), F32),
        ((512, 1024), F32), ((512, 1024), BF), ((2, 1024), F32), ((2, 1024), F32), ((2,), F32),
    ]
    return pl.pallas_call(
        widen_kernel,
        out_shape=[jax.ShapeDtypeStruct(s, d) for s, d in shapes],
        in_specs=any_spec(6) + [vmem],
        out_specs=any_spec(6) + [vmem, vmem, pl.BlockSpec(memory_space=pltpu.SMEM)],
        scratch_shapes=[vm(s, BF) for s, _ in shapes[:4]] + [vm(s, F32) for s, _ in shapes[:4]]
        + [pltpu.SemaphoreType.DMA((24,)), pltpu.SemaphoreType.DMA((26,))],
        compiler_params=pltpu.CompilerParams(vmem_limit_bytes=48 * 1024 * 1024),
        name="widen",
    )(resd, resu, resi, reso, gin, out, small)


def fast_device(
    block_in, lengths, input_weight, output_weight, up_weight, down_weight, norm_gain, norm_bias, cotangent
):
    x, dy = block_in[0], cotangent[0]
    win = input_weight.reshape(3072, 512)
    first, qkv, mix, rden, state, mid, sec, wino, woo, dyo, hg, stat = front(
        lengths, x, dy, win, output_weight, down_weight, norm_gain, norm_bias
    )
    part, pin, mlp, dslab, uslab = middle(sec, dy, dyo, hg, up_weight, down_weight)
    resd, resu, resi, reso, block_out, grad_in, small = back(
        lengths, norm_gain, norm_bias, stat, part, pin, mid, x, dy, qkv, mix, rden, state, first,
        win, wino, output_weight, woo, mlp, dslab, uslab,
    )
    down_grad, up_grad, in_grad, out_grad, grad_in, block_out, gain, bias, stats = widen(
        resd, resu, resi, reso, grad_in, block_out, small
    )
    return (
        block_out[None], grad_in[None], in_grad.reshape(3, 1024, 512), out_grad, up_grad, down_grad,
        gain, bias, stats,
    )


def fits_fast(mesh, block_shape):
    return dict(mesh.shape) == {"dp": 16, "mp": 2} and tuple(block_shape) == (16, 1024, 1024)


def solution(mesh):
    in_specs = (
        P("dp", "mp", None),
        P("dp"),
        P(None, None, "mp"),
        P("mp", None),
        P(None, "mp"),
        P("mp", None),
        P(),
        P(),
        P("dp", "mp", None),
    )
    out_specs = (
        P("dp", "mp", None),
        P("dp", "mp", None),
        P(None, None, "mp"),
        P("mp", None),
        P(None, "mp"),
        P("mp", None),
        P(),
        P(),
        P(),
    )

    def whole(*arrays):
        body = fast_device if fits_fast(mesh, arrays[0].shape) else per_device
        return jax.shard_map(
            body, mesh=mesh, in_specs=in_specs, out_specs=out_specs, check_vma=False
        )(*arrays)

    return whole
```

```python
from functools import partial

import jax
import jax.numpy as jnp
from jax import lax
from jax.experimental import pallas as pl
from jax.experimental.pallas import tpu as pltpu
from jax.sharding import PartitionSpec as P

DH = 64
BLK = 512


EPSILON = 1e-05
PRECISE = lax.Precision.HIGHEST


def combined_all(part, axis, combine):
    gathered = jax.tree.map(lambda a: lax.all_gather(a, axis), part)

    def take(source):
        return jax.tree.map(lambda a: lax.dynamic_index_in_dim(a, source, 0, False), gathered)

    return lax.fori_loop(
        1, lax.axis_size(axis), lambda source, state: combine(state, take(source)), take(0)
    )


def feature(values):
    return jax.nn.elu(values) + 1.0


def feature_slope(values):
    return jnp.where(values > 0, 1.0, jnp.exp(values))


def normalise(inputs, gain_row, bias_row):
    centre = jnp.mean(inputs, axis=-1, keepdims=True)
    centred = inputs - centre
    spread = jnp.mean(centred * centred, axis=-1, keepdims=True)
    inverse = lax.rsqrt(spread + EPSILON)
    unit_rows = centred * inverse
    return (unit_rows * gain_row + bias_row, unit_rows, inverse)


def normalise_back(grad_rows, unit_rows, inverse, gain_row):
    scaled = grad_rows * gain_row
    centre = jnp.mean(scaled, axis=-1, keepdims=True)
    along = jnp.mean(scaled * unit_rows, axis=-1, keepdims=True)
    input_grad = inverse * (scaled - centre - unit_rows * along)
    return (input_grad, jnp.sum(grad_rows * unit_rows, axis=0), jnp.sum(grad_rows, axis=0))


def exclusive(stacked):
    running = jnp.cumsum(stacked, axis=0)
    return jnp.concatenate([jnp.zeros_like(running[:1]), running[:-1]], axis=0)


def later(stacked):
    return exclusive(stacked[::-1])[::-1]


def unchanged(carried):
    return carried


def causal_mask():
    return jnp.tril(jnp.ones((BLK, BLK), jnp.float32))


def attend_forward(query_map, key_map, values, crop_len):
    slot_len, head_count, depth = query_map.shape
    block_count = slot_len // BLK
    block_shape = (block_count, BLK, head_count, depth)
    block_q = query_map.reshape(block_shape)
    block_k = key_map.reshape(block_shape)
    block_v = values.reshape(block_shape)
    memory = exclusive(
        jnp.einsum("nihd,nihe->nhde", block_k, block_v, preferred_element_type=jnp.float32)
    )
    key_total = exclusive(jnp.sum(block_k.astype(jnp.float32), axis=1))
    causal = causal_mask()
    block_starts = jnp.arange(block_count, dtype=jnp.int32) * BLK

    def one_block(block_item):
        query_b, key_b, value_b, memory_b, total_b, start_b = block_item
        query_f = query_b.astype(jnp.float32)
        numerator = jnp.einsum("ihd,hde->ihe", query_f, memory_b, precision=PRECISE)
        denominator = jnp.einsum("ihd,hd->ih", query_f, total_b, precision=PRECISE)

        def inside(partial_sums):
            value_part, weight_part = partial_sums
            scores = (
                jnp.einsum("ihd,jhd->hij", query_b, key_b, preferred_element_type=jnp.float32)
                * causal
            )
            value_part = value_part + jnp.einsum(
                "hij,jhd->ihd",
                scores.astype(jnp.bfloat16),
                value_b,
                preferred_element_type=jnp.float32,
            )
            weight_part = weight_part + jnp.sum(scores, axis=-1).T
            return (value_part, weight_part)

        numerator, denominator = lax.cond(
            start_b < crop_len, inside, unchanged, (numerator, denominator)
        )
        return (numerator / denominator[..., None], denominator)

    attended, denoms = lax.map(
        one_block, (block_q, block_k, block_v, memory, key_total, block_starts)
    )
    return (
        attended.reshape(slot_len, head_count, depth),
        denoms.reshape(slot_len, head_count),
        memory,
        key_total,
    )


def attend_backward(
    grad_attn, attended, denoms, query_map, key_map, values, memory, key_total, crop_len
):
    slot_len, head_count, depth = query_map.shape
    block_count = slot_len // BLK
    block_shape = (block_count, BLK, head_count, depth)
    top_all = (grad_attn / denoms[..., None]).reshape(block_shape)
    bottom_all = (-jnp.sum(grad_attn * attended, axis=-1) / denoms).reshape(
        block_count, BLK, head_count
    )
    query_full = query_map.astype(jnp.float32).reshape(block_shape)
    memory_later = later(jnp.einsum("nihd,nihe->nhde", query_full, top_all, precision=PRECISE))
    total_later = later(jnp.einsum("nihd,nih->nhd", query_full, bottom_all, precision=PRECISE))
    causal = causal_mask()
    block_starts = jnp.arange(block_count, dtype=jnp.int32) * BLK

    def one_block(block_item):
        (
            query_b,
            key_b,
            value_b,
            memory_b,
            total_b,
            later_memory,
            later_total,
            top_grad,
            bottom_grad,
            start_b,
        ) = block_item
        value_f = value_b.astype(jnp.float32)
        key_f = key_b.astype(jnp.float32)
        query_sum = (
            jnp.einsum("ihe,hde->ihd", top_grad, memory_b, precision=PRECISE)
            + bottom_grad[..., None] * total_b[None]
        )
        key_sum = (
            jnp.einsum("jhe,hde->jhd", value_f, later_memory, precision=PRECISE) + later_total[None]
        )
        value_sum = jnp.einsum("jhd,hde->jhe", key_f, later_memory, precision=PRECISE)

        def inside(partial_grads):
            query_acc, key_acc, value_acc = partial_grads
            scores = (
                jnp.einsum("ihd,jhd->hij", query_b, key_b, preferred_element_type=jnp.float32)
                * causal
            )
            score_grad = (
                (
                    jnp.einsum("ihe,jhe->hij", top_grad, value_f, precision=PRECISE)
                    + bottom_grad.T[:, :, None]
                )
                * causal
            ).astype(jnp.bfloat16)
            query_acc = query_acc + jnp.einsum(
                "hij,jhd->ihd", score_grad, key_b, preferred_element_type=jnp.float32
            )
            key_acc = key_acc + jnp.einsum(
                "hij,ihd->jhd", score_grad, query_b, preferred_element_type=jnp.float32
            )
            rounded_scores = scores.astype(jnp.bfloat16).astype(jnp.float32)
            value_acc = value_acc + jnp.einsum(
                "hij,ihe->jhe", rounded_scores, top_grad, precision=PRECISE
            )
            return (query_acc, key_acc, value_acc)

        return lax.cond(start_b < crop_len, inside, unchanged, (query_sum, key_sum, value_sum))

    query_grad, key_grad, value_grad = lax.map(
        one_block,
        (
            query_map.reshape(block_shape),
            key_map.reshape(block_shape),
            values.reshape(block_shape),
            memory,
            key_total,
            memory_later,
            total_later,
            top_all,
            bottom_all,
            block_starts,
        ),
    )
    return (
        query_grad.reshape(slot_len, head_count, depth),
        key_grad.reshape(slot_len, head_count, depth),
        value_grad.reshape(slot_len, head_count, depth),
    )


def combine_stats(first_part, second_part):
    return (
        first_part[0] + second_part[0],
        first_part[1] + second_part[1],
        first_part[2] + second_part[2],
        first_part[3] + second_part[3],
        jnp.maximum(first_part[4], second_part[4]),
    )


def per_device(
    block_in,
    lengths,
    input_weight,
    output_weight,
    up_weight,
    down_weight,
    norm_gain,
    norm_bias,
    cotangent,
):
    group_count = lax.axis_size("mp")
    rows_here = block_in.shape[1]
    slot_len = rows_here * group_count
    local_width = output_weight.shape[0]
    head_count = local_width // DH
    crop_len = lengths[0]
    valid_mask = (jnp.arange(slot_len, dtype=jnp.int32) < crop_len).astype(jnp.float32)
    own_rows = block_in[0].astype(jnp.float32)
    first_norm, unit_one, inverse_one = normalise(own_rows, norm_gain[0], norm_bias[0])
    first_rows = lax.all_gather(first_norm.astype(jnp.bfloat16), "mp", axis=0, tiled=True)
    projected = jnp.einsum(
        "rd,cdk->rck", first_rows, input_weight, preferred_element_type=jnp.float32
    ).reshape(slot_len, 3, head_count, DH)
    query = projected[:, 0]
    key_raw = projected[:, 1]
    query_map = feature(query).astype(jnp.bfloat16)
    key_map = (feature(key_raw) * valid_mask[:, None, None]).astype(jnp.bfloat16)
    values = projected[:, 2].astype(jnp.bfloat16)
    attended, denoms, memory, key_total = attend_forward(query_map, key_map, values, crop_len)
    mixed = attended.reshape(slot_len, local_width).astype(jnp.bfloat16)
    part_rows = mixed
    branch_out = lax.psum_scatter(
        jnp.dot(part_rows, output_weight, preferred_element_type=jnp.float32).astype(jnp.bfloat16),
        "mp",
        scatter_dimension=0,
        tiled=True,
    ).astype(jnp.float32)
    middle = own_rows + branch_out
    second_norm, unit_two, inverse_two = normalise(middle, norm_gain[1], norm_bias[1])
    second_rows = lax.all_gather(second_norm.astype(jnp.bfloat16), "mp", axis=0, tiled=True)
    hidden_in = jnp.dot(second_rows, up_weight, preferred_element_type=jnp.float32)
    hidden = jax.nn.gelu(hidden_in, approximate=True).astype(jnp.bfloat16)
    part_rows = hidden
    mlp_out = lax.psum_scatter(
        jnp.dot(part_rows, down_weight, preferred_element_type=jnp.float32).astype(jnp.bfloat16),
        "mp",
        scatter_dimension=0,
        tiled=True,
    ).astype(jnp.float32)
    block_out = (middle + mlp_out).astype(jnp.bfloat16)[None]
    grad_out = cotangent[0]
    grad_rows = lax.all_gather(grad_out, "mp", axis=0, tiled=True)
    down_grad = jnp.einsum("rf,rd->fd", hidden, grad_rows, preferred_element_type=jnp.float32)
    hidden_grad = jnp.einsum(
        "rd,fd->rf", grad_rows, down_weight, preferred_element_type=jnp.float32
    )
    unused_out, gelu_back = jax.vjp(partial(jax.nn.gelu, approximate=True), hidden_in)
    inner_grad = gelu_back(hidden_grad)[0].astype(jnp.bfloat16)
    up_grad = jnp.einsum("rd,rf->df", second_rows, inner_grad, preferred_element_type=jnp.float32)
    part_rows = inner_grad
    second_grad = lax.psum_scatter(
        jnp.einsum("rf,df->rd", part_rows, up_weight, preferred_element_type=jnp.float32).astype(
            jnp.bfloat16
        ),
        "mp",
        scatter_dimension=0,
        tiled=True,
    ).astype(jnp.float32)
    back_two, gain_two, bias_two = normalise_back(second_grad, unit_two, inverse_two, norm_gain[1])
    middle_grad = grad_out.astype(jnp.float32) + back_two
    middle_low = middle_grad.astype(jnp.bfloat16)
    middle_full = lax.all_gather(middle_low, "mp", axis=0, tiled=True)
    mixed_grad = jnp.einsum(
        "rd,kd->rk", middle_full, output_weight, preferred_element_type=jnp.float32
    ).astype(jnp.bfloat16)
    output_grad = jnp.einsum("rk,rd->kd", mixed, middle_full, preferred_element_type=jnp.float32)
    grad_attn = mixed_grad.astype(jnp.float32).reshape(slot_len, head_count, DH)
    query_grad, key_grad, value_grad = attend_backward(
        grad_attn, attended, denoms, query_map, key_map, values, memory, key_total, crop_len
    )
    query_low = (query_grad * feature_slope(query)).astype(jnp.bfloat16)
    key_low = (key_grad * valid_mask[:, None, None] * feature_slope(key_raw)).astype(jnp.bfloat16)
    value_low = value_grad.astype(jnp.bfloat16)
    qkv_grad = jnp.stack([query_low, key_low, value_low], axis=1).reshape(slot_len, 3, local_width)
    input_grad = jnp.einsum("rd,rck->cdk", first_rows, qkv_grad, preferred_element_type=jnp.float32)
    part_rows = qkv_grad
    first_grad = lax.psum_scatter(
        jnp.einsum(
            "rck,cdk->rd", part_rows, input_weight, preferred_element_type=jnp.float32
        ).astype(jnp.bfloat16),
        "mp",
        scatter_dimension=0,
        tiled=True,
    ).astype(jnp.float32)
    back_one, gain_one, bias_one = normalise_back(first_grad, unit_one, inverse_one, norm_gain[0])
    grad_input = (middle_grad + back_one)[None]
    input_grad, output_grad, up_grad, down_grad = (
        lax.psum(input_grad.astype(jnp.bfloat16), "dp").astype(jnp.float32),
        lax.psum(output_grad.astype(jnp.bfloat16), "dp").astype(jnp.float32),
        lax.psum(up_grad.astype(jnp.bfloat16), "dp").astype(jnp.float32),
        lax.psum(down_grad.astype(jnp.bfloat16), "dp").astype(jnp.float32),
    )
    kept_denoms = jnp.where(valid_mask[:, None] > 0, denoms, 0.0)
    den_total = jnp.sum(kept_denoms)
    den_count = crop_len.astype(jnp.float32) * head_count
    den_peak = jnp.max(kept_denoms)
    gain_grad, bias_grad, den_total, den_count, den_peak = combined_all(
        (
            jnp.stack([gain_one, gain_two]),
            jnp.stack([bias_one, bias_two]),
            den_total,
            den_count,
            den_peak,
        ),
        ("dp", "mp"),
        combine_stats,
    )
    scaling = DH * slot_len
    denominator_stats = jnp.stack([den_peak / scaling, den_total / den_count / scaling])
    return (
        block_out,
        grad_input,
        input_grad,
        output_grad,
        up_grad,
        down_grad,
        gain_grad,
        bias_grad,
        denominator_stats,
    )

MESH = pl.DeviceIdType.MESH
BF = jnp.bfloat16
F32 = jnp.float32
ROWS = 512
CH = 256
PAIR = 128


def dot_nn(a, b):
    return lax.dot_general(a, b, (((1,), (0,)), ((), ())), preferred_element_type=F32)


def dot_nt(a, b):
    return lax.dot_general(a, b, (((1,), (1,)), ((), ())), preferred_element_type=F32)


def dot_tn(a, b):
    return lax.dot_general(a, b, (((0,), (0,)), ((), ())), preferred_element_type=F32)


class Place:
    def __init__(self):
        dp = lax.axis_index("dp")
        mp = lax.axis_index("mp")
        self.dp, self.mp = dp, mp
        self.core = lax.rem(dp, 2)
        chip = dp // 2
        y = lax.rem(chip, 2)
        z = chip // 2
        self.r = z + y * (7 - 2 * z)
        self.across = (dp, 1 - mp)
        self.mate = (dp + 1 - 2 * self.core, mp)
        self.next = self.at(lax.rem(self.r + 1, 8))
        self.prev = self.at(lax.rem(self.r + 7, 8))

    def at(self, r):
        y = r // 4
        z = r + y * (7 - 2 * r)
        return ((z * 2 + y) * 2 + self.core, self.mp)

    def partners(self):
        return [self.across, self.mate, self.next, self.prev]


def greet(partners):
    barrier = pltpu.get_barrier_semaphore()
    for partner in partners:
        pl.semaphore_signal(barrier, inc=1, device_id=partner, device_id_type=MESH)
    pl.semaphore_wait(barrier, len(partners))


def remote(src, dst, send_sem, recv_sem, device):
    return pltpu.make_async_remote_copy(
        src_ref=src, dst_ref=dst, send_sem=send_sem, recv_sem=recv_sem,
        device_id=device, device_id_type=MESH,
    )


def aligned(start, size, unit):
    return pl.ds(pl.multiple_of(start, unit), size)


def lane_head(shape):
    return lax.broadcasted_iota(jnp.int32, shape, len(shape) - 1) < DH


def same_head():
    row = lax.broadcasted_iota(jnp.int32, (PAIR, PAIR), 0) < DH
    lane = lax.broadcasted_iota(jnp.int32, (PAIR, PAIR), 1) < DH
    return row == lane


def causal_tile():
    row = lax.broadcasted_iota(jnp.int32, (CH, CH), 0)
    col = lax.broadcasted_iota(jnp.int32, (CH, CH), 1)
    return row >= col


def unpack_state(packed):
    keep = same_head()
    zero = jnp.zeros_like(packed)
    return jnp.concatenate(
        [jnp.where(keep, packed, zero), jnp.where(keep, pltpu.roll(packed, DH, 1), zero)], axis=1
    )


def split_heads(pair):
    first = lane_head(pair.shape)
    zero = jnp.zeros_like(pair)
    return jnp.where(first, pair, zero), jnp.where(first, zero, pair)


def row_norm(rows):
    centre = jnp.mean(rows, axis=-1, keepdims=True)
    centred = rows - centre
    inverse = lax.rsqrt(jnp.mean(centred * centred, axis=-1, keepdims=True) + EPSILON)
    return centred * inverse, inverse


def front_kernel(
    len_ref, x_hbm, dy_hbm, win_hbm, wo_hbm, wdn_hbm, gain_ref, bias_ref,
    first_o, qkv_o, mix_o, rden_o, state_o, mid_o, sec_o, wino_o, woo_o, dyo_o, hg_o, stat_ref,
    x_v, dy_v, win_v, wino_v, wo_v, woo_v, wdn_v, first_v, qkv_v, num_v, den_v, mix_v, mid_v, sec_v, hg_v,
    local_v, ssend_v, srecv_v, state_v,
    in_sem, out_sem, xs_sem, xr_sem, ring_s, ring_r, mate_s, mate_r,
):
    here = Place()
    loads = [
        (x_hbm, x_v), (win_hbm, win_v), (dy_hbm, dy_v), (wdn_hbm, wdn_v), (wo_hbm, wo_v),
    ]
    loads = [pltpu.make_async_copy(a, b, in_sem.at[i]) for i, (a, b) in enumerate(loads)]
    for load in loads:
        load.start()
    greet(here.partners())
    parts = ((win_hbm, wino_v, 192), (wo_hbm, woo_v, 32))

    def rows_of(array, offset, core):
        rows = parts[array][2]
        return aligned((lax.rem(here.r + 8 + offset, 8) * 2 + core) * rows, rows, 32)

    cross = []
    for array, (src, dst, _) in enumerate(parts):
        for k in range(2):
            at = rows_of(array, 4 * k, here.core)
            slot = 2 * array + k
            cross.append(remote(src.at[at], dst.at[at], xs_sem.at[slot], xr_sem.at[slot], here.across))
    for copy in cross:
        copy.start()
    gone = []

    def dy_part(count):
        for _ in range(count):
            k = len(gone)
            rows = pl.ds(k * 64, 64)
            copy = remote(dy_hbm.at[rows], dyo_o.at[rows], xs_sem.at[7 + k], xr_sem.at[7 + k], here.across)
            copy.start()
            gone.append(copy)

    dy_part(2)

    gain = gain_ref[0:1, :]
    bias = bias_ref[0:1, :]
    sends = []
    outs = []

    def out(src, dst):
        copy = pltpu.make_async_copy(src, dst, out_sem.at[len(outs)])
        copy.start()
        outs.append(copy)

    FAR = ((-1, 3, -2), (1, 5, 2))

    def to_mate(array, slot, offset):
        at = rows_of(array, offset, here.core)
        dst = parts[array][1]
        copy = remote(dst.at[at], dst.at[at], mate_s.at[array, slot], mate_r.at[array, slot], here.mate)
        copy.start()
        sends.append(copy)

    def to_ring(array, way, k, offset):
        at = rows_of(array, offset, here.core)
        dst = parts[array][1]
        copy = remote(
            dst.at[at], dst.at[at], ring_s.at[array, way, k], ring_r.at[array, way, k],
            here.next if way == 0 else here.prev,
        )
        copy.start()
        sends.append(copy)

    def from_across(array):
        for k in range(2):
            cross[2 * array + k].wait_recv()
            for way in (0, 1):
                to_ring(array, way, k, 4 * k)
            to_mate(array, k, 4 * k)

    def from_ring(array, k):
        for way in (0, 1):
            at = rows_of(array, FAR[way][k], here.core)
            dst = parts[array][1].at[at]
            remote(dst, dst, ring_s.at[array, way, k], ring_r.at[array, way, k], here.next).wait_recv()
            if k == 0:
                to_ring(array, way, 2, FAR[way][0])
            to_mate(array, 2 + 2 * k + way, FAR[way][k])

    def mate_wait(array):
        offsets = [0, 4] + [FAR[way][k] for k in range(3) for way in (0, 1)]
        for slot, offset in enumerate(offsets):
            dst = parts[array][1].at[rows_of(array, offset, 1 - here.core)]
            remote(dst, dst, mate_s.at[array, slot], mate_r.at[array, slot], here.mate).wait_recv()

    loads[0].wait()

    @pl.loop(0, ROWS // 128)
    def _(i):
        at = aligned(i * 128, 128, 128)
        unit, _ = row_norm(x_v[at, :].astype(F32))
        first_v[at, :] = (unit * gain + bias).astype(BF)

    out(first_v, first_o)
    crop_len = len_ref[0]

    def project(half, weights, which):
        @pl.loop(0, 2)
        def _(c):
            at = aligned(c * CH, CH, CH)
            rows = first_v[at, :]
            for i in which:
                raw = dot_nn(rows, weights[pl.ds(i * 1024, 1024), :])
                if i < 2:
                    raw = jnp.where(raw > 0, raw + 1.0, jnp.exp(jnp.minimum(raw, 0.0)))
                if i == 1:
                    place = lax.broadcasted_iota(jnp.int32, raw.shape, 0) + (here.mp * ROWS + c * CH)
                    raw = jnp.where(place < crop_len, raw, 0.0)
                qkv_v[half, i, at, :] = raw.astype(BF)

    def states(half):
        keep = same_head()

        @pl.loop(0, 4)
        def _(p):
            lanes = aligned(p * PAIR, PAIR, PAIR)
            total = None
            for c in range(2):
                keys = qkv_v[half, 1, pl.ds(c * CH, CH), lanes]
                vals = qkv_v[half, 2, pl.ds(c * CH, CH), lanes]
                made = dot_tn(keys, jnp.concatenate([vals, jnp.ones_like(vals)], axis=1))
                packed = jnp.where(keep, made[:, :PAIR], made[:, PAIR:])
                if c == 0:
                    local_v[half, p] = packed
                    total = packed
                else:
                    ssend_v[half, p] = (total + packed).astype(BF)

        copy = remote(
            ssend_v.at[half], srecv_v.at[1 - half], xs_sem.at[5 + half], xr_sem.at[6 - half], here.across
        )
        copy.start()
        sends.append(copy)

    def inside(half):
        mask = causal_tile()

        @pl.loop(0, 8)
        def _(n):
            p = n // 2
            c = lax.rem(n, 2)
            lanes = aligned(p * PAIR, PAIR, PAIR)
            at = aligned(c * CH, CH, CH)
            query = qkv_v[half, 0, at, lanes]
            key = qkv_v[half, 1, at, lanes]
            val = qkv_v[half, 2, at, lanes]
            first = lane_head(val.shape)
            one = jnp.ones_like(val)
            zero = jnp.zeros_like(val)
            sums = None
            for head, part in enumerate(split_heads(query)):
                score = jnp.where(mask, dot_nt(part, key), 0.0).astype(BF)
                mine = first if head == 0 else jnp.logical_not(first)
                right = jnp.concatenate([jnp.where(mine, val, zero), jnp.where(mine, one, zero)], axis=1)
                term = dot_nn(score, right)
                sums = term if sums is None else sums + term
            num_v[at, lanes] = sums[:, :PAIR]
            den_v[half, at, lanes] = sums[:, PAIR:]

    def finish(half):
        flag = here.mp.astype(F32)

        @pl.loop(0, 8)
        def _(n):
            p = n // 2
            c = lax.rem(n, 2)
            lanes = aligned(p * PAIR, PAIR, PAIR)
            at = aligned(c * CH, CH, CH)
            query = qkv_v[half, 0, at, lanes]
            before = srecv_v[half, p].astype(F32) * flag
            state_v[half, p] = before.astype(BF)
            before = before + local_v[half, p] * c.astype(F32)
            term = dot_nn(query, unpack_state(before).astype(BF))
            num = num_v[at, lanes] + term[:, :PAIR]
            den = den_v[half, at, lanes] + term[:, PAIR:]
            inverse = 1.0 / den
            den_v[half, at, lanes] = inverse
            mix_v[half, at, lanes] = (num * inverse).astype(BF)
            place = lax.broadcasted_iota(jnp.int32, den.shape, 0) + (here.mp * ROWS + c * CH)
            kept = jnp.where(place < crop_len, den, 0.0).reshape(CH // 8, 8, PAIR)
            stat_ref[0] = jnp.maximum(stat_ref[0], jnp.max(kept, axis=0))
            stat_ref[1] = stat_ref[1] + jnp.sum(kept, axis=0)

    def hidden_grad():
        @pl.loop(0, 2)
        def _(j):
            cols = aligned(j * 1024, 1024, 1024)
            hg_v[:, cols] = dot_nt(dy_v[...], wdn_v[cols, :]).astype(BF)

    stat_ref[...] = jnp.zeros_like(stat_ref)
    loads[1].wait()
    project(0, win_v, (1, 2))
    states(0)
    dy_part(1)
    project(0, win_v, (0,))
    from_across(0)
    dy_part(1)
    inside(0)
    from_ring(0, 0)
    from_across(1)
    dy_part(2)
    loads[2].wait()
    loads[3].wait()
    hidden_grad()
    from_ring(0, 1)
    from_ring(1, 0)
    from_ring(0, 2)
    mate_wait(0)
    from_ring(1, 1)
    out(wino_v, wino_o)
    mid_v[:, pl.ds(0, 512)] = num_v[...]
    project(1, wino_v, (1, 2))
    states(1)
    dy_part(2)
    project(1, wino_v, (0,))
    from_ring(1, 2)
    inside(1)
    remote(ssend_v.at[0], srecv_v.at[1], xs_sem.at[5], xr_sem.at[6], here.across).wait_recv()
    finish(1)
    out(hg_v, hg_o)
    num_v[...] = mid_v[:, pl.ds(0, 512)]
    mate_wait(1)
    remote(ssend_v.at[1], srecv_v.at[0], xs_sem.at[6], xr_sem.at[5], here.across).wait_recv()
    finish(0)
    out(qkv_v, qkv_o)
    out(den_v, rden_o)
    out(mix_v, mix_o)
    out(state_v, state_o)
    out(woo_v, woo_o)
    loads[4].wait()
    gain_two = gain_ref[1:2, :]
    bias_two = bias_ref[1:2, :]

    @pl.loop(0, 2)
    def _(c):
        at = aligned(c * CH, CH, CH)
        own = dot_nn(mix_v[0, at, :], wo_v[...]).astype(BF).astype(F32)
        other = dot_nn(mix_v[1, at, :], woo_v[...]).astype(BF).astype(F32)
        middle = x_v[at, :].astype(F32) + (own + other)
        mid_v[at, :] = middle
        unit, _ = row_norm(middle)
        sec_v[at, :] = (unit * gain_two + bias_two).astype(BF)

    out(mid_v, mid_o)
    out(sec_v, sec_o)
    for copy in gone:
        copy.wait_recv()
    for copy in cross + gone + sends:
        copy.wait_send()
    for copy in outs:
        copy.wait()


def any_spec(count):
    return [pl.BlockSpec(memory_space=pl.ANY)] * count


def front(lengths, x_rows, dy_rows, win, wo, wdn, gain, bias):
    vm = pltpu.VMEM
    shapes = [
        ((512, 1024), BF), ((2, 3, 512, 512), BF), ((2, 512, 512), BF), ((2, 512, 512), F32),
        ((2, 4, PAIR, PAIR), BF), ((512, 1024), F32), ((512, 1024), BF), ((3072, 512), BF),
        ((512, 1024), BF), ((512, 1024), BF), ((512, 2048), BF), ((2, 8, PAIR), F32),
    ]
    dma = pltpu.SemaphoreType.DMA
    return pl.pallas_call(
        front_kernel,
        out_shape=[jax.ShapeDtypeStruct(s, d) for s, d in shapes],
        in_specs=[pl.BlockSpec(memory_space=pltpu.SMEM)] + any_spec(5)
        + [pl.BlockSpec(memory_space=pltpu.VMEM)] * 2,
        out_specs=any_spec(11) + [pl.BlockSpec(memory_space=pltpu.VMEM)],
        scratch_shapes=[
            vm((512, 1024), BF), vm((512, 1024), BF), vm((3072, 512), BF), vm((3072, 512), BF),
            vm((512, 1024), BF), vm((512, 1024), BF), vm((2048, 1024), BF), vm((512, 1024), BF),
            vm((2, 3, 512, 512), BF), vm((512, 512), F32), vm((2, 512, 512), F32), vm((2, 512, 512), BF),
            vm((512, 1024), F32), vm((512, 1024), BF), vm((512, 2048), BF),
            vm((2, 4, PAIR, PAIR), F32), vm((2, 4, PAIR, PAIR), BF), vm((2, 4, PAIR, PAIR), BF),
            vm((2, 4, PAIR, PAIR), BF),
            dma((5,)), dma((12,)), dma((15,)), dma((15,)), dma((2, 2, 3)), dma((2, 2, 3)),
            dma((2, 8)), dma((2, 8)),
        ],
        compiler_params=pltpu.CompilerParams(
            collective_id=0, has_side_effects=True, vmem_limit_bytes=58 * 1024 * 1024
        ),
        name="front",
    )(lengths, x_rows, dy_rows, win, wo, wdn, gain, bias)


GELU_A = 0.7978845608028654
GELU_B = 0.044715


def gelu_pair(v):
    square = v * v
    t = jnp.tanh(GELU_A * v * (1.0 + GELU_B * square))
    half = 0.5 * (1.0 + t)
    slope = half + (0.5 * GELU_A) * v * (1.0 - t * t) * (1.0 + (3.0 * GELU_B) * square)
    return v * half, slope


def middle_kernel(
    sec_hbm, dy_hbm, dyo_hbm, hg_hbm, wup_hbm, wdn_hbm,
    part_o, pin_o, mlp_o, dslab_o, uslab_o,
    sec_v, dy_v, hg_v, wup_v, wdn_v, hid_v, part_v, send_v, pin_v, mlp_v,
    dsend_v, drecv_v, dslab_v, usend_v, urecv_v, uslab_v,
    in_sem, out_sem, xs_sem, xr_sem, ms_sem, mr_sem,
):
    here = Place()
    own = pl.ds(0, ROWS)
    other = pl.ds(ROWS, ROWS)
    loads = [
        (sec_hbm, sec_v.at[own]), (wup_hbm, wup_v), (hg_hbm, hg_v.at[own]), (wdn_hbm, wdn_v),
        (dy_hbm, dy_v.at[own]), (dyo_hbm, dy_v.at[other]),
    ]
    loads = [pltpu.make_async_copy(a, b, in_sem.at[i]) for i, (a, b) in enumerate(loads)]
    for load in loads:
        load.start()
    greet([here.across, here.mate])
    sends = []
    outs = []

    def out(src, dst):
        copy = pltpu.make_async_copy(src, dst, out_sem.at[len(outs)])
        copy.start()
        outs.append(copy)

    def across(src, dst, slot):
        copy = remote(src, dst, xs_sem.at[slot], xr_sem.at[slot], here.across)
        copy.start()
        sends.append(copy)
        return copy

    ahead = [
        across(sec_hbm.at[pl.ds(c * CH, CH)], sec_v.at[pl.ds(ROWS + c * CH, CH)], c) for c in range(2)
    ]

    def up(chunk):
        rows = pl.ds(chunk * CH, CH)

        @pl.loop(0, 4)
        def _(j):
            cols = aligned(j * 512, 512, 512)
            raw = dot_nn(sec_v[rows, :], wup_v[:, cols])
            value, slope = gelu_pair(raw)
            hid_v[rows, cols] = value.astype(BF)
            hg_v[rows, cols] = (hg_v[rows, cols].astype(F32) * slope).astype(BF)

    def back(chunk, dst):
        dst[...] = dot_nt(hg_v[pl.ds(chunk * CH, CH), :], wup_v[...]).astype(BF)

    loads[0].wait()
    loads[1].wait()
    loads[2].wait()
    for c in range(2):
        up(c)
        back(c, part_v.at[pl.ds(c * CH, CH)])
    out(part_v, part_o)
    for load in loads[3:]:
        load.wait()
    for c in range(2):
        @pl.loop(0, 2)
        def _(j):
            cols = aligned(j * 1024, 1024, 1024)
            rows = pl.ds(ROWS + c * CH, CH)
            hg_v[rows, cols] = dot_nt(dy_v[rows, :], wdn_v[cols, :]).astype(BF)

        ahead[c].wait_recv()
        up(2 + c)
        rows = pl.ds(c * CH, CH)
        back(2 + c, send_v.at[rows])
        across(send_v.at[rows], pin_v.at[rows], 2 + c)
    their = 1 - here.core

    def down_grad(half, dst, plus):
        @pl.loop(0, 2)
        def _(i):
            cols = aligned(half * 1024 + i * 512, 512, 512)
            at = aligned(i * 512, 512, 512)
            made = dot_tn(hid_v[:, cols], dy_v[...])
            if plus is not None:
                made = made + plus[at, :].astype(F32)
            dst[at, :] = made.astype(BF)

    def up_grad(half, dst, plus):
        @pl.loop(0, 2)
        def _(i):
            cols = aligned(half * 512, 512, 512)
            at = aligned(i * 1024, 1024, 1024)
            made = dot_tn(sec_v[:, cols], hg_v[:, at])
            if plus is not None:
                made = made + plus[:, at].astype(F32)
            dst[:, at] = made.astype(BF)

    def to_mate(src, dst, slot):
        copy = remote(src, dst, ms_sem.at[slot], mr_sem.at[slot], here.mate)
        copy.start()
        sends.append(copy)
        return copy

    down_grad(their, dsend_v, None)
    to_d = to_mate(dsend_v, drecv_v, 0)
    up_grad(their, usend_v, None)
    to_u = to_mate(usend_v, urecv_v, 1)

    @pl.loop(0, 2)
    def _(i):
        rows = aligned(i * ROWS, ROWS, ROWS)
        mlp_v[rows, :] = dot_nn(hid_v[rows, :], wdn_v[...]).astype(BF)

    out(mlp_v, mlp_o)
    to_d.wait_recv()
    down_grad(here.core, dslab_v, drecv_v)
    out(dslab_v, dslab_o)
    to_u.wait_recv()
    up_grad(here.core, uslab_v, urecv_v)
    out(uslab_v, uslab_o)
    for c in range(2):
        rows = pl.ds(c * CH, CH)
        remote(send_v.at[rows], pin_v.at[rows], xs_sem.at[2 + c], xr_sem.at[2 + c], here.across).wait_recv()
    out(pin_v, pin_o)
    for copy in sends:
        copy.wait_send()
    for copy in outs:
        copy.wait()


def middle(sec, dy, dyo, hg, wup, wdn):
    vm = pltpu.VMEM
    dma = pltpu.SemaphoreType.DMA
    shapes = [
        ((512, 1024), BF), ((512, 1024), BF), ((1024, 1024), BF), ((1024, 1024), BF), ((512, 2048), BF),
    ]
    return pl.pallas_call(
        middle_kernel,
        out_shape=[jax.ShapeDtypeStruct(s, d) for s, d in shapes],
        in_specs=any_spec(6),
        out_specs=any_spec(5),
        scratch_shapes=[
            vm((1024, 1024), BF), vm((1024, 1024), BF), vm((1024, 2048), BF), vm((1024, 2048), BF),
            vm((2048, 1024), BF), vm((1024, 2048), BF), vm((512, 1024), BF), vm((512, 1024), BF),
            vm((512, 1024), BF), vm((1024, 1024), BF),
            vm((1024, 1024), BF), vm((1024, 1024), BF), vm((1024, 1024), BF),
            vm((512, 2048), BF), vm((512, 2048), BF), vm((512, 2048), BF),
            dma((6,)), dma((5,)), dma((4,)), dma((4,)), dma((2,)), dma((2,)),
        ],
        compiler_params=pltpu.CompilerParams(
            collective_id=1, has_side_effects=True, vmem_limit_bytes=58 * 1024 * 1024
        ),
        name="middle",
    )(sec, dy, dyo, hg, wup, wdn)


PACE = 36


class Arc:
    def __init__(self, here, slab, base, rows, recv, result, result_base, sems):
        self.here, self.slab, self.base, self.rows = here, slab, base, rows
        self.recv, self.result, self.result_base = recv, result, result_base
        self.rs_s, self.rs_r, self.ag_s, self.ag_r, self.mt_s, self.mt_r, self.local = sems
        self.pending = []
        self.t = 0

    def span(self, base, offset, half):
        start = base + lax.rem(self.here.r + 8 + offset, 8) * self.rows
        if half is None:
            return aligned(start, self.rows, 16)
        return aligned(start + half * (self.rows // 2), self.rows // 2, 16)

    def mine(self, offset, half=None):
        return self.span(self.base, offset, half)

    def place(self, offset, core, half=None):
        return self.result.at[self.span(self.result_base(core) + self.base, offset, half)]

    def send(self, src, dst, send_sem, recv_sem, device):
        copy = remote(src, dst, send_sem, recv_sem, device)
        copy.start()
        self.pending.append(copy)

    def to(self, way):
        return self.here.next if way == 0 else self.here.prev

    def sign(self, way):
        return 1 if way == 0 else -1

    def slot(self, way, s):
        if s > 0:
            return self.recv.at[way, s]
        return self.recv.at[way, 0, pl.ds(way * (self.rows // 2), self.rows // 2)]

    def arrived(self, way, s):
        got = self.slot(way, s)
        remote(got, got, self.rs_s.at[way, s], self.rs_r.at[way, s], self.to(way)).wait_recv()

    def gather_step(self, way, s):
        sign = self.sign(way)
        if s == 0:
            src = self.slab.at[self.mine(sign * 4, way)]
        else:
            self.arrived(way, s - 1)
            own = self.slab[self.mine(sign * (4 - s)), :].astype(F32)
            src = self.recv.at[way, s - 1]
            if s == 1:
                half = self.rows // 2
                kept = pl.ds(way * half, half)
                rest = pl.ds((1 - way) * half, half)
                at = slice(way * half, way * half + half)
                src[kept, :] = (src[kept, :].astype(F32) + own[at]).astype(BF)
                at = slice((1 - way) * half, (1 - way) * half + half)
                src[rest, :] = own[at].astype(BF)
            else:
                src[...] = (src[...].astype(F32) + own).astype(BF)
        self.send(src, self.slot(way, s), self.rs_s.at[way, s], self.rs_r.at[way, s], self.to(way))

    def spread(self, src, offset, step, way, half=None):
        dst = self.place(offset, self.here.core, half)
        if step < 4 and not (step == 3 and half is None):
            self.send(src, dst, self.ag_s.at[way, step], self.ag_r.at[way, step], self.to(way))

    def to_mate(self, src, offset, slot, half=None):
        dst = self.place(offset, self.here.core, half)
        self.send(src, dst, self.mt_s.at[slot], self.mt_r.at[slot], self.here.mate)

    def total(self):
        self.arrived(0, 3)
        self.arrived(1, 3)
        sums = self.recv.at[0, 3]
        own = self.slab[self.mine(0), :].astype(F32)
        sums[...] = (sums[...].astype(F32) + self.recv[1, 3].astype(F32) + own).astype(BF)
        for way in (0, 1):
            self.spread(sums, 0, 0, way)
        self.to_mate(sums, 0, 0)
        self.keep = pltpu.make_async_copy(sums, self.place(0, self.here.core), self.local)
        self.keep.start()

    def spread_step(self, way, s):
        sign = self.sign(way)
        half = way if s == 3 else None
        got = self.place(-sign * (s + 1), self.here.core, half)
        remote(got, got, self.ag_s.at[way, s], self.ag_r.at[way, s], self.to(way)).wait_recv()
        if s < 3:
            part = way if s == 2 else None
            src = self.place(-sign * (s + 1), self.here.core, part)
            self.spread(src, -sign * (s + 1), s + 1, way, part)
        self.to_mate(got, -sign * (s + 1), 1 + 2 * s + way, half)

    def tick(self):
        t = self.t
        self.t = t + 1
        if t == 4:
            self.total()
        elif t < 9:
            for way in (0, 1):
                if t < 4:
                    self.gather_step(way, t)
                else:
                    self.spread_step(way, t - 5)

    def finish(self):
        for copy in self.pending:
            copy.wait_send()
        self.keep.wait()
        other = 1 - self.here.core
        for slot in range(9):
            if slot == 0:
                got = self.place(0, other)
            else:
                s, way = (slot - 1) // 2, (slot - 1) % 2
                got = self.place(-self.sign(way) * (s + 1), other, way if s == 3 else None)
            remote(got, got, self.mt_s.at[slot], self.mt_r.at[slot], self.here.mate).wait_recv()


def back_kernel(
    len_ref, gain_ref, bias_ref, stat_ref,
    part_hbm, pin_hbm, mid_hbm, x_hbm, dy_hbm, qkv_hbm, mix_hbm, rden_hbm, state_hbm, first_hbm,
    win_hbm, wino_hbm, wo_hbm, woo_hbm, mlp_hbm, dslab_hbm, uslab_hbm,
    resd_o, resu_o, resi_o, reso_o, out_o, gin_o, small_ref,
    part_v, pin_v, mid_v, dy_v, qkv_v, mix_v, rden_v, state_v, first_v, win_v, wo_v,
    mlpin_v, mg_v, mgf_v, mixg_v, top_v, bot_v, dqkv_v, local_v, lsend_v, lrecv_v,
    dslab_v, uslab_v, drecv_v, urecv_v, gm_v, gr_v, ga_v, gx_v, om_v, or_v, oa_v, ox_v, irecv_v, orecv_v,
    small_s, small_r,
    in_sem, out_sem, xs_sem, xr_sem, ms_sem, mr_sem, bs_sem, br_sem,
    rs_s, rs_r, ag_s, ag_r, mt_s, mt_r, keep_s,
):
    here = Place()
    loads = [
        (part_hbm, part_v), (pin_hbm, pin_v), (mid_hbm, mid_v), (dy_hbm, dy_v), (dslab_hbm, dslab_v),
        (uslab_hbm, uslab_v), (wo_hbm, wo_v.at[0]), (woo_hbm, wo_v.at[1]), (mix_hbm, mix_v),
        (rden_hbm, rden_v), (qkv_hbm, qkv_v), (state_hbm, state_v), (first_hbm, first_v),
        (win_hbm, win_v.at[0]), (wino_hbm, win_v.at[1]), (x_hbm, part_v), (mlp_hbm.at[pl.ds(0, ROWS)], pin_v),
    ]
    loads = [pltpu.make_async_copy(a, b, in_sem.at[i]) for i, (a, b) in enumerate(loads)]
    for load in loads[:15]:
        load.start()
    y_mate = (here.dp + 2 - 4 * lax.rem(here.dp // 2, 2), here.mp)
    z_mate = (here.dp + 4 - 8 * lax.rem(here.dp // 4, 2), here.mp)
    z_far = (here.dp + 8 - 16 * (here.dp // 8), here.mp)
    greet(here.partners() + [y_mate, z_mate, z_far])
    sends = []
    outs = []

    def out(src, dst):
        copy = pltpu.make_async_copy(src, dst, out_sem.at[len(outs)])
        copy.start()
        outs.append(copy)

    def across(src, dst, slot):
        copy = remote(src, dst, xs_sem.at[slot], xr_sem.at[slot], here.across)
        copy.start()
        sends.append(copy)
        return copy

    def to_mate(src, dst, slot):
        copy = remote(src, dst, ms_sem.at[slot], mr_sem.at[slot], here.mate)
        copy.start()
        sends.append(copy)
        return copy

    arcs = []

    def add_arc(slab, base, rows, recv, result, result_base):
        n = len(arcs)
        sems = (rs_s.at[n], rs_r.at[n], ag_s.at[n], ag_r.at[n], mt_s.at[n], mt_r.at[n], keep_s.at[n])
        arcs.append(Arc(here, slab, base, rows, recv, result, result_base, sems))
        return arcs[-1]

    ring_d = add_arc(dslab_v, 0, 128, drecv_v, resd_o, lambda core: core * 1024)
    ring_u = add_arc(uslab_v, 0, 64, urecv_v, resu_o, lambda core: core * 512)
    ring_o = add_arc(oa_v.at[0], 0, 32, orecv_v, reso_o, lambda core: core * 256)
    ring_i = [
        add_arc(ga_v.at[0], i * 512, 64, irecv_v.at[i], resi_o, lambda core: core * 1536) for i in range(3)
    ]

    credit = [0]

    def ring(count):
        credit[0] += count * PACE
        while credit[0] >= 100:
            credit[0] -= 100
            first = ring_d if ring_d.t <= ring_u.t else ring_u
            first.tick()

    def ring_on(arc):
        arc.tick()

    loads[4].wait()
    loads[5].wait()
    ring_d.tick()
    ring_u.tick()

    small_s[...] = jnp.zeros_like(small_s)
    for load in loads[0:4]:
        load.wait()
    gain_two = gain_ref[1:2, :]

    @pl.loop(0, ROWS // 128)
    def _(i):
        at = aligned(i * 128, 128, 128)
        grad = part_v[at, :].astype(F32) + pin_v[at, :].astype(F32)
        unit, inverse = row_norm(mid_v[at, :])
        scaled = grad * gain_two
        centre = jnp.mean(scaled, axis=-1, keepdims=True)
        along = jnp.mean(scaled * unit, axis=-1, keepdims=True)
        total = dy_v[at, :].astype(F32) + inverse * (scaled - centre - unit * along)
        mgf_v[at, :] = total
        mg_v[at, :] = total.astype(BF)
        small_s[1:2, :] = small_s[1:2, :] + jnp.sum(grad * unit, axis=0, keepdims=True)
        small_s[3:4, :] = small_s[3:4, :] + jnp.sum(grad, axis=0, keepdims=True)

    for load in loads[15:]:
        load.start()
    ring(2)
    for load in loads[6:12]:
        load.wait()
    @pl.loop(0, 2)
    def _(half):
        mixg_v[half] = dot_nt(mg_v[...], wo_v[half]).astype(BF)

    ring(1)
    their = 1 - here.core

    def out_grad(half, side, dst):
        cols = aligned(side * 256, 256, 256)
        dst[...] = dot_tn(mix_v[half, :, cols], mg_v[...]).astype(BF)

    keep = same_head()

    def tops(half):
        @pl.loop(0, 4)
        def _(p):
            lanes_at = aligned(p * PAIR, PAIR, PAIR)
            packs = []
            blocks = jnp.where(keep, 1.0, 0.0).astype(BF)
            for c in range(2):
                at = pl.ds(c * CH, CH)
                top = (mixg_v[half, at, lanes_at].astype(F32) * rden_v[half, at, lanes_at]).astype(BF)
                top_v[half, at, lanes_at] = top
                prod = top.astype(F32) * mix_v[half, at, lanes_at].astype(F32)
                high = prod.astype(BF)
                low = (prod - high.astype(F32)).astype(BF)
                bottom = -(dot_nn(high, blocks) + dot_nn(low, blocks))
                high = bottom.astype(BF)
                low = (bottom - high.astype(F32)).astype(BF)
                lane = lax.rem(lax.broadcasted_iota(jnp.int32, bottom.shape, 1), DH)
                bot_v[half, at, lanes_at] = jnp.where(
                    lane == 0, high, jnp.where(lane == 1, low, jnp.zeros_like(high))
                )
                query = qkv_v[half, 0, at, lanes_at]
                made = dot_tn(query, jnp.concatenate([top, high], axis=1))
                packs.append(jnp.where(keep, made[:, :PAIR], pltpu.roll(made[:, PAIR:], DH, 1)))
            local_v[half, p] = packs[1]
            lsend_v[half, p] = (packs[0] + packs[1]).astype(BF)

        across(lsend_v.at[half], lrecv_v.at[1 - half], 1 + half)

    tops(0)
    ring(1)
    tops(1)
    ring(1)
    for half in (1, 0):
        out_grad(half, their, om_v.at[half])
        to_mate(om_v.at[half], or_v.at[half], half)
    ring(1)
    for half in (1, 0):
        out_grad(half, here.core, oa_v.at[half])
    ring(1)
    for load in loads[12:15]:
        load.wait()

    def attend_back(half):
        mask = causal_tile()
        earlier = 1.0 - here.mp.astype(F32)
        remote(
            lsend_v.at[1 - half], lrecv_v.at[half], xs_sem.at[2 - half], xr_sem.at[2 - half], here.across
        ).wait_recv()

        def body(p, c):
            lanes_at = aligned(p * PAIR, PAIR, PAIR)
            at = aligned(c * CH, CH, CH)
            second = c.astype(F32)
            query = qkv_v[half, 0, at, lanes_at]
            key = qkv_v[half, 1, at, lanes_at]
            val = qkv_v[half, 2, at, lanes_at]
            top = top_v[half, at, lanes_at]
            bot = bot_v[half, at, lanes_at]
            lane = lax.rem(lax.broadcasted_iota(jnp.int32, val.shape, 1), DH)
            one = jnp.ones_like(val)
            zero = jnp.zeros_like(val)
            val_two = jnp.concatenate([val, jnp.where(lane < 2, one, zero)], axis=1)
            val_one = jnp.concatenate([val, jnp.where(lane == 0, one, zero)], axis=1)
            key0 = qkv_v[half, 1, pl.ds(0, CH), lanes_at]
            val0 = qkv_v[half, 2, pl.ds(0, CH), lanes_at]
            made = dot_tn(key0, jnp.concatenate([val0, one], axis=1))
            made = jnp.where(keep, made[:, :PAIR], made[:, PAIR:])
            before = state_v[half, p].astype(F32) + made * second
            after = lrecv_v[half, p].astype(F32) * earlier + local_v[half, p] * (1.0 - second)
            before = unpack_state(before).astype(BF)
            after = unpack_state(after).astype(BF)
            dq = dot_nt(jnp.concatenate([top, bot], axis=1), before)
            dk = dot_nt(val_one, after)
            dv = dot_nn(key, after[:, :PAIR])
            queries, keys, tops_, bots = split_heads(query), split_heads(key), split_heads(top), split_heads(bot)
            for head in range(2):
                score = jnp.where(mask, dot_nt(queries[head], key), 0.0).astype(BF)
                grad = dot_nt(jnp.concatenate([tops_[head], bots[head]], axis=1), val_two)
                grad = jnp.where(mask, grad, 0.0).astype(BF)
                dq = dq + dot_nn(grad, keys[head])
                dk = dk + dot_tn(grad, queries[head])
                dv = dv + dot_tn(score, tops_[head])
            dqkv_v[half, 0, at, lanes_at] = (dq * jnp.minimum(query.astype(F32), 1.0)).astype(BF)
            dqkv_v[half, 1, at, lanes_at] = (dk * jnp.minimum(key.astype(F32), 1.0)).astype(BF)
            dqkv_v[half, 2, at, lanes_at] = dv.astype(BF)

        for part in range(2):
            @pl.loop(part * 4, part * 4 + 4)
            def _(n):
                body(n // 2, lax.rem(n, 2))

            ring(2)

    def piece(i):
        return pl.ds(i * 512, 512)

    def in_grads(half):
        for side, dst in ((their, gm_v), (here.core, ga_v)):
            cols = aligned(side * 512, 512, 512)
            @pl.loop(0, 3)
            def _(i):
                dst[half, aligned(i * 512, 512, 512), :] = dot_tn(first_v[:, cols], dqkv_v[half, i]).astype(BF)

            if dst is gm_v:
                for i in range(3):
                    at = piece(i)
                    to_mate(gm_v.at[half, at], gr_v.at[half, at], 2 + half * 3 + i)
            ring(1)

    def add_rows(dst, src, start, count):
        @pl.loop(0, count)
        def _(i):
            at = aligned(start + i * 128, 128, 128)
            dst[at, :] = (dst[at, :].astype(F32) + src[at, :].astype(F32)).astype(BF)

    def mate_arrival(half, i):
        at = piece(i)
        slot = 2 + half * 3 + i
        remote(gm_v.at[half, at], gr_v.at[half, at], ms_sem.at[slot], mr_sem.at[slot], here.mate).wait_recv()
        add_rows(ga_v.at[half], gr_v.at[half], i * 512, 4)

    def mate_arrival_out(half):
        remote(om_v.at[half], or_v.at[half], ms_sem.at[half], mr_sem.at[half], here.mate).wait_recv()
        add_rows(oa_v.at[half], or_v.at[half], 0, 2)

    attend_back(1)
    mate_arrival_out(1)
    cross_o = across(oa_v.at[1], ox_v, 3)
    in_grads(1)
    cross_i = []
    for i in range(3):
        mate_arrival(1, i)
        cross_i.append(across(ga_v.at[1, piece(i)], gx_v.at[piece(i)], 4 + i))
    mlp = across(mlp_hbm.at[pl.ds(ROWS, ROWS)], mlpin_v, 0)
    ring(2)
    mate_arrival_out(0)
    attend_back(0)
    cross_o.wait_recv()
    add_rows(oa_v.at[0], ox_v, 0, 2)
    ring_on(ring_o)
    in_grads(0)
    for i in range(3):
        mate_arrival(0, i)
    ring(2)
    ring_on(ring_o)

    loads[15].wait()
    gain_one = gain_ref[0:1, :]

    @pl.loop(0, 2)
    def _(quarter):
        at = aligned(quarter * CH, CH, CH)
        grad = None
        for half in range(2):
            term = None
            for j in range(3):
                made = dot_nt(dqkv_v[half, j, at, :], win_v[half, pl.ds(j * 1024, 1024), :])
                term = made if term is None else term + made
            term = term.astype(BF).astype(F32)
            grad = term if grad is None else grad + term
        unit, inverse = row_norm(part_v[at, :].astype(F32))
        scaled = grad * gain_one
        centre = jnp.mean(scaled, axis=-1, keepdims=True)
        along = jnp.mean(scaled * unit, axis=-1, keepdims=True)
        mgf_v[at, :] = mgf_v[at, :] + inverse * (scaled - centre - unit * along)
        small_s[0:1, :] = small_s[0:1, :] + jnp.sum(grad * unit, axis=0, keepdims=True)
        small_s[2:3, :] = small_s[2:3, :] + jnp.sum(grad, axis=0, keepdims=True)

    ring(4)
    ring_on(ring_o)
    out(mgf_v, gin_o)
    small_s[4:5, pl.ds(0, PAIR)] = jnp.sum(stat_ref[1], axis=0, keepdims=True) * (1.0 / DH)
    count = len_ref[0].astype(F32) * (8.0 / 1024.0)
    small_s[5:6, :] = jnp.zeros((1, 1024), F32) + count
    small_s[6:7, pl.ds(0, PAIR)] = jnp.max(stat_ref[0], axis=0, keepdims=True)
    partners = [here.mate, y_mate, z_mate, z_far, here.across]

    def small_send(step):
        src = small_s if step == 0 else small_ref
        copy = remote(src, small_r.at[step], bs_sem.at[step], br_sem.at[step], partners[step])
        copy.start()
        return copy

    def small_step(copy, step):
        copy.wait()
        src = small_s if step == 0 else small_ref
        mine, theirs = src[...], small_r[step]
        row = lax.broadcasted_iota(jnp.int32, mine.shape, 0)
        small_ref[...] = jnp.where(row < 6, mine + theirs, jnp.maximum(mine, theirs))

    for i in range(3):
        cross_i[i].wait_recv()
        add_rows(ga_v.at[0], gx_v, i * 512, 4)
        for arc in ring_i[: i + 1]:
            ring_on(arc)
        ring(6)
        ring_on(ring_o)
    copy = small_send(0)
    for step in range(9):
        for arc in ring_i:
            ring_on(arc)
        ring(6)
        ring_on(ring_o)
        if 2 <= step < 7:
            small_step(copy, step - 2)
            if step < 6:
                copy = small_send(step - 1)
    ring(2000)

    loads[16].wait()
    mlp.wait_recv()

    @pl.loop(0, 4)
    def _(i):
        at = aligned(i * 128, 128, 128)
        total = mid_v[at, :] + (pin_v[at, :].astype(F32) + mlpin_v[at, :].astype(F32))
        pin_v[at, :] = total.astype(BF)

    out(pin_v, out_o)
    for arc in arcs:
        arc.finish()
    for copy in sends:
        copy.wait_send()
    for copy in outs:
        copy.wait()


def back(lengths, gain, bias, stat, part, pin, mid, x, dy, qkv, mix, rden, state, first, win, wino, wo, woo, mlp, dslab, uslab):
    vm = pltpu.VMEM
    dma = pltpu.SemaphoreType.DMA
    shapes = [
        ((2048, 1024), BF), ((1024, 2048), BF), ((3072, 512), BF), ((512, 1024), BF),
        ((512, 1024), BF), ((512, 1024), F32), ((8, 1024), F32),
    ]
    rows = (512, 1024)
    heads = (2, 512, 512)
    pack = (2, 4, PAIR, PAIR)
    vmem = pl.BlockSpec(memory_space=pltpu.VMEM)
    return pl.pallas_call(
        back_kernel,
        out_shape=[jax.ShapeDtypeStruct(s, d) for s, d in shapes],
        in_specs=[pl.BlockSpec(memory_space=pltpu.SMEM), vmem, vmem, vmem] + any_spec(17),
        out_specs=any_spec(6) + [vmem],
        scratch_shapes=[
            vm(rows, BF), vm(rows, BF), vm(rows, F32), vm(rows, BF),
            vm((2, 3, 512, 512), BF), vm(heads, BF), vm(heads, F32), vm(pack, BF), vm(rows, BF),
            vm((2, 3072, 512), BF), vm((2, 512, 1024), BF),
            vm(rows, BF), vm(rows, BF), vm(rows, F32), vm(heads, BF), vm(heads, BF), vm(heads, BF),
            vm((2, 3, 512, 512), BF), vm(pack, F32), vm(pack, BF), vm(pack, BF),
            vm((1024, 1024), BF), vm((512, 2048), BF), vm((2, 4, 128, 1024), BF), vm((2, 4, 64, 2048), BF),
            vm((2, 1536, 512), BF), vm((2, 1536, 512), BF), vm((2, 1536, 512), BF), vm((1536, 512), BF),
            vm((2, 256, 1024), BF), vm((2, 256, 1024), BF), vm((2, 256, 1024), BF), vm((256, 1024), BF),
            vm((3, 2, 4, 64, 512), BF), vm((2, 4, 32, 1024), BF),
            vm((8, 1024), F32), vm((5, 8, 1024), F32),
            dma((17,)), dma((2,)), dma((7,)), dma((7,)), dma((8,)), dma((8,)), dma((5,)), dma((5,)),
            dma((6, 2, 4)), dma((6, 2, 4)), dma((6, 2, 4)), dma((6, 2, 4)), dma((6, 9)), dma((6, 9)), dma((6,)),
        ],
        compiler_params=pltpu.CompilerParams(
            collective_id=2, has_side_effects=True, vmem_limit_bytes=60 * 1024 * 1024
        ),
        name="back",
    )(lengths, gain, bias, stat, part, pin, mid, x, dy, qkv, mix, rden, state, first, win, wino, wo, woo, mlp, dslab, uslab)


def widen_kernel(
    d_hbm, u_hbm, i_hbm, o_hbm, gin_hbm, out_hbm, small_ref,
    di_o, ui_o, ii_o, oi_o, gin_o, out_o, gain_ref, bias_ref, stats_ref,
    d_v, u_v, i_v, o_v, df_v, uf_v, if_v, of_v, in_sem, out_sem,
):
    jobs = []
    for k in range(6):
        core, i = k // 3, k % 3
        jobs.append((i_hbm, i_v, k * 512, ii_o, if_v, i * 1024 + core * 512, 512))
    for k in range(2):
        jobs.append((o_hbm, o_v, k * 256, oi_o, of_v, k * 256, 256))
    for k in range(8):
        jobs.append((u_hbm, u_v, k * 128, ui_o, uf_v, k * 128, 128))
    for k in range(8):
        jobs.append((d_hbm, d_v, k * 256, di_o, df_v, k * 256, 256))
    loads, stores = [], []
    for n, (src, held, at, _, _, _, rows) in enumerate(jobs):
        loads.append(pltpu.make_async_copy(src.at[pl.ds(at, rows)], held.at[pl.ds(at, rows)], in_sem.at[n]))
        loads[-1].start()
    for n, (src, dst) in enumerate(((gin_hbm, gin_o), (out_hbm, out_o))):
        stores.append(pltpu.make_async_copy(src, dst, out_sem.at[len(jobs) + n]))
        stores[-1].start()
    for n, (_, held, at, dst, wide, to, rows) in enumerate(jobs):
        loads[n].wait()

        @pl.loop(0, rows // 128)
        def _(k):
            rows_at = aligned(at + k * 128, 128, 128)
            wide[rows_at, :] = held[rows_at, :].astype(F32)

        stores.append(pltpu.make_async_copy(wide.at[pl.ds(at, rows)], dst.at[pl.ds(to, rows)], out_sem.at[n]))
        stores[-1].start()
    gain_ref[...] = small_ref[0:2, :]
    bias_ref[...] = small_ref[2:4, :]
    scaling = 1.0 / (DH * 1024)
    count = jnp.max(small_ref[5:6, :]) * 1024.0
    stats_ref[0] = jnp.max(small_ref[6:7, :]) * scaling
    stats_ref[1] = jnp.sum(small_ref[4:5, :]) / count * scaling
    for copy in stores:
        copy.wait()


def widen(resd, resu, resi, reso, gin, out, small):
    vm = pltpu.VMEM
    vmem = pl.BlockSpec(memory_space=pltpu.VMEM)
    shapes = [
        ((2048, 1024), F32), ((1024, 2048), F32), ((3072, 512), F32), ((512, 1024), F32),
        ((512, 1024), F32), ((512, 1024), BF), ((2, 1024), F32), ((2, 1024), F32), ((2,), F32),
    ]
    return pl.pallas_call(
        widen_kernel,
        out_shape=[jax.ShapeDtypeStruct(s, d) for s, d in shapes],
        in_specs=any_spec(6) + [vmem],
        out_specs=any_spec(6) + [vmem, vmem, pl.BlockSpec(memory_space=pltpu.SMEM)],
        scratch_shapes=[vm(s, BF) for s, _ in shapes[:4]] + [vm(s, F32) for s, _ in shapes[:4]]
        + [pltpu.SemaphoreType.DMA((24,)), pltpu.SemaphoreType.DMA((26,))],
        compiler_params=pltpu.CompilerParams(vmem_limit_bytes=48 * 1024 * 1024),
        name="widen",
    )(resd, resu, resi, reso, gin, out, small)


def fast_device(
    block_in, lengths, input_weight, output_weight, up_weight, down_weight, norm_gain, norm_bias, cotangent
):
    x, dy = block_in[0], cotangent[0]
    win = input_weight.reshape(3072, 512)
    first, qkv, mix, rden, state, mid, sec, wino, woo, dyo, hg, stat = front(
        lengths, x, dy, win, output_weight, down_weight, norm_gain, norm_bias
    )
    part, pin, mlp, dslab, uslab = middle(sec, dy, dyo, hg, up_weight, down_weight)
    resd, resu, resi, reso, block_out, grad_in, small = back(
        lengths, norm_gain, norm_bias, stat, part, pin, mid, x, dy, qkv, mix, rden, state, first,
        win, wino, output_weight, woo, mlp, dslab, uslab,
    )
    down_grad, up_grad, in_grad, out_grad, grad_in, block_out, gain, bias, stats = widen(
        resd, resu, resi, reso, grad_in, block_out, small
    )
    return (
        block_out[None], grad_in[None], in_grad.reshape(3, 1024, 512), out_grad, up_grad, down_grad,
        gain, bias, stats,
    )


def fits_fast(mesh, block_shape):
    return dict(mesh.shape) == {"dp": 16, "mp": 2} and tuple(block_shape) == (16, 1024, 1024)


def solution(mesh):
    in_specs = (
        P("dp", "mp", None),
        P("dp"),
        P(None, None, "mp"),
        P("mp", None),
        P(None, "mp"),
        P("mp", None),
        P(),
        P(),
        P("dp", "mp", None),
    )
    out_specs = (
        P("dp", "mp", None),
        P("dp", "mp", None),
        P(None, None, "mp"),
        P("mp", None),
        P(None, "mp"),
        P("mp", None),
        P(),
        P(),
        P(),
    )

    def whole(*arrays):
        body = fast_device if fits_fast(mesh, arrays[0].shape) else per_device
        return jax.shard_map(
            body, mesh=mesh, in_specs=in_specs, out_specs=out_specs, check_vma=False
        )(*arrays)

    return whole
```

```python
from functools import partial

import jax
import jax.numpy as jnp
from jax import lax
from jax.experimental import pallas as pl
from jax.experimental.pallas import tpu as pltpu
from jax.sharding import PartitionSpec as P

DH = 64
BLK = 512


EPSILON = 1e-05
PRECISE = lax.Precision.HIGHEST


def combined_all(part, axis, combine):
    gathered = jax.tree.map(lambda a: lax.all_gather(a, axis), part)

    def take(source):
        return jax.tree.map(lambda a: lax.dynamic_index_in_dim(a, source, 0, False), gathered)

    return lax.fori_loop(
        1, lax.axis_size(axis), lambda source, state: combine(state, take(source)), take(0)
    )


def feature(values):
    return jax.nn.elu(values) + 1.0


def feature_slope(values):
    return jnp.where(values > 0, 1.0, jnp.exp(values))


def normalise(inputs, gain_row, bias_row):
    centre = jnp.mean(inputs, axis=-1, keepdims=True)
    centred = inputs - centre
    spread = jnp.mean(centred * centred, axis=-1, keepdims=True)
    inverse = lax.rsqrt(spread + EPSILON)
    unit_rows = centred * inverse
    return (unit_rows * gain_row + bias_row, unit_rows, inverse)


def normalise_back(grad_rows, unit_rows, inverse, gain_row):
    scaled = grad_rows * gain_row
    centre = jnp.mean(scaled, axis=-1, keepdims=True)
    along = jnp.mean(scaled * unit_rows, axis=-1, keepdims=True)
    input_grad = inverse * (scaled - centre - unit_rows * along)
    return (input_grad, jnp.sum(grad_rows * unit_rows, axis=0), jnp.sum(grad_rows, axis=0))


def exclusive(stacked):
    running = jnp.cumsum(stacked, axis=0)
    return jnp.concatenate([jnp.zeros_like(running[:1]), running[:-1]], axis=0)


def later(stacked):
    return exclusive(stacked[::-1])[::-1]


def unchanged(carried):
    return carried


def causal_mask():
    return jnp.tril(jnp.ones((BLK, BLK), jnp.float32))


def attend_forward(query_map, key_map, values, crop_len):
    slot_len, head_count, depth = query_map.shape
    block_count = slot_len // BLK
    block_shape = (block_count, BLK, head_count, depth)
    block_q = query_map.reshape(block_shape)
    block_k = key_map.reshape(block_shape)
    block_v = values.reshape(block_shape)
    memory = exclusive(
        jnp.einsum("nihd,nihe->nhde", block_k, block_v, preferred_element_type=jnp.float32)
    )
    key_total = exclusive(jnp.sum(block_k.astype(jnp.float32), axis=1))
    causal = causal_mask()
    block_starts = jnp.arange(block_count, dtype=jnp.int32) * BLK

    def one_block(block_item):
        query_b, key_b, value_b, memory_b, total_b, start_b = block_item
        query_f = query_b.astype(jnp.float32)
        numerator = jnp.einsum("ihd,hde->ihe", query_f, memory_b, precision=PRECISE)
        denominator = jnp.einsum("ihd,hd->ih", query_f, total_b, precision=PRECISE)

        def inside(partial_sums):
            value_part, weight_part = partial_sums
            scores = (
                jnp.einsum("ihd,jhd->hij", query_b, key_b, preferred_element_type=jnp.float32)
                * causal
            )
            value_part = value_part + jnp.einsum(
                "hij,jhd->ihd",
                scores.astype(jnp.bfloat16),
                value_b,
                preferred_element_type=jnp.float32,
            )
            weight_part = weight_part + jnp.sum(scores, axis=-1).T
            return (value_part, weight_part)

        numerator, denominator = lax.cond(
            start_b < crop_len, inside, unchanged, (numerator, denominator)
        )
        return (numerator / denominator[..., None], denominator)

    attended, denoms = lax.map(
        one_block, (block_q, block_k, block_v, memory, key_total, block_starts)
    )
    return (
        attended.reshape(slot_len, head_count, depth),
        denoms.reshape(slot_len, head_count),
        memory,
        key_total,
    )


def attend_backward(
    grad_attn, attended, denoms, query_map, key_map, values, memory, key_total, crop_len
):
    slot_len, head_count, depth = query_map.shape
    block_count = slot_len // BLK
    block_shape = (block_count, BLK, head_count, depth)
    top_all = (grad_attn / denoms[..., None]).reshape(block_shape)
    bottom_all = (-jnp.sum(grad_attn * attended, axis=-1) / denoms).reshape(
        block_count, BLK, head_count
    )
    query_full = query_map.astype(jnp.float32).reshape(block_shape)
    memory_later = later(jnp.einsum("nihd,nihe->nhde", query_full, top_all, precision=PRECISE))
    total_later = later(jnp.einsum("nihd,nih->nhd", query_full, bottom_all, precision=PRECISE))
    causal = causal_mask()
    block_starts = jnp.arange(block_count, dtype=jnp.int32) * BLK

    def one_block(block_item):
        (
            query_b,
            key_b,
            value_b,
            memory_b,
            total_b,
            later_memory,
            later_total,
            top_grad,
            bottom_grad,
            start_b,
        ) = block_item
        value_f = value_b.astype(jnp.float32)
        key_f = key_b.astype(jnp.float32)
        query_sum = (
            jnp.einsum("ihe,hde->ihd", top_grad, memory_b, precision=PRECISE)
            + bottom_grad[..., None] * total_b[None]
        )
        key_sum = (
            jnp.einsum("jhe,hde->jhd", value_f, later_memory, precision=PRECISE) + later_total[None]
        )
        value_sum = jnp.einsum("jhd,hde->jhe", key_f, later_memory, precision=PRECISE)

        def inside(partial_grads):
            query_acc, key_acc, value_acc = partial_grads
            scores = (
                jnp.einsum("ihd,jhd->hij", query_b, key_b, preferred_element_type=jnp.float32)
                * causal
            )
            score_grad = (
                (
                    jnp.einsum("ihe,jhe->hij", top_grad, value_f, precision=PRECISE)
                    + bottom_grad.T[:, :, None]
                )
                * causal
            ).astype(jnp.bfloat16)
            query_acc = query_acc + jnp.einsum(
                "hij,jhd->ihd", score_grad, key_b, preferred_element_type=jnp.float32
            )
            key_acc = key_acc + jnp.einsum(
                "hij,ihd->jhd", score_grad, query_b, preferred_element_type=jnp.float32
            )
            rounded_scores = scores.astype(jnp.bfloat16).astype(jnp.float32)
            value_acc = value_acc + jnp.einsum(
                "hij,ihe->jhe", rounded_scores, top_grad, precision=PRECISE
            )
            return (query_acc, key_acc, value_acc)

        return lax.cond(start_b < crop_len, inside, unchanged, (query_sum, key_sum, value_sum))

    query_grad, key_grad, value_grad = lax.map(
        one_block,
        (
            query_map.reshape(block_shape),
            key_map.reshape(block_shape),
            values.reshape(block_shape),
            memory,
            key_total,
            memory_later,
            total_later,
            top_all,
            bottom_all,
            block_starts,
        ),
    )
    return (
        query_grad.reshape(slot_len, head_count, depth),
        key_grad.reshape(slot_len, head_count, depth),
        value_grad.reshape(slot_len, head_count, depth),
    )


def combine_stats(first_part, second_part):
    return (
        first_part[0] + second_part[0],
        first_part[1] + second_part[1],
        first_part[2] + second_part[2],
        first_part[3] + second_part[3],
        jnp.maximum(first_part[4], second_part[4]),
    )


def per_device(
    block_in,
    lengths,
    input_weight,
    output_weight,
    up_weight,
    down_weight,
    norm_gain,
    norm_bias,
    cotangent,
):
    group_count = lax.axis_size("mp")
    rows_here = block_in.shape[1]
    slot_len = rows_here * group_count
    local_width = output_weight.shape[0]
    head_count = local_width // DH
    crop_len = lengths[0]
    valid_mask = (jnp.arange(slot_len, dtype=jnp.int32) < crop_len).astype(jnp.float32)
    own_rows = block_in[0].astype(jnp.float32)
    first_norm, unit_one, inverse_one = normalise(own_rows, norm_gain[0], norm_bias[0])
    first_rows = lax.all_gather(first_norm.astype(jnp.bfloat16), "mp", axis=0, tiled=True)
    projected = jnp.einsum(
        "rd,cdk->rck", first_rows, input_weight, preferred_element_type=jnp.float32
    ).reshape(slot_len, 3, head_count, DH)
    query = projected[:, 0]
    key_raw = projected[:, 1]
    query_map = feature(query).astype(jnp.bfloat16)
    key_map = (feature(key_raw) * valid_mask[:, None, None]).astype(jnp.bfloat16)
    values = projected[:, 2].astype(jnp.bfloat16)
    attended, denoms, memory, key_total = attend_forward(query_map, key_map, values, crop_len)
    mixed = attended.reshape(slot_len, local_width).astype(jnp.bfloat16)
    part_rows = mixed
    branch_out = lax.psum_scatter(
        jnp.dot(part_rows, output_weight, preferred_element_type=jnp.float32).astype(jnp.bfloat16),
        "mp",
        scatter_dimension=0,
        tiled=True,
    ).astype(jnp.float32)
    middle = own_rows + branch_out
    second_norm, unit_two, inverse_two = normalise(middle, norm_gain[1], norm_bias[1])
    second_rows = lax.all_gather(second_norm.astype(jnp.bfloat16), "mp", axis=0, tiled=True)
    hidden_in = jnp.dot(second_rows, up_weight, preferred_element_type=jnp.float32)
    hidden = jax.nn.gelu(hidden_in, approximate=True).astype(jnp.bfloat16)
    part_rows = hidden
    mlp_out = lax.psum_scatter(
        jnp.dot(part_rows, down_weight, preferred_element_type=jnp.float32).astype(jnp.bfloat16),
        "mp",
        scatter_dimension=0,
        tiled=True,
    ).astype(jnp.float32)
    block_out = (middle + mlp_out).astype(jnp.bfloat16)[None]
    grad_out = cotangent[0]
    grad_rows = lax.all_gather(grad_out, "mp", axis=0, tiled=True)
    down_grad = jnp.einsum("rf,rd->fd", hidden, grad_rows, preferred_element_type=jnp.float32)
    hidden_grad = jnp.einsum(
        "rd,fd->rf", grad_rows, down_weight, preferred_element_type=jnp.float32
    )
    unused_out, gelu_back = jax.vjp(partial(jax.nn.gelu, approximate=True), hidden_in)
    inner_grad = gelu_back(hidden_grad)[0].astype(jnp.bfloat16)
    up_grad = jnp.einsum("rd,rf->df", second_rows, inner_grad, preferred_element_type=jnp.float32)
    part_rows = inner_grad
    second_grad = lax.psum_scatter(
        jnp.einsum("rf,df->rd", part_rows, up_weight, preferred_element_type=jnp.float32).astype(
            jnp.bfloat16
        ),
        "mp",
        scatter_dimension=0,
        tiled=True,
    ).astype(jnp.float32)
    back_two, gain_two, bias_two = normalise_back(second_grad, unit_two, inverse_two, norm_gain[1])
    middle_grad = grad_out.astype(jnp.float32) + back_two
    middle_low = middle_grad.astype(jnp.bfloat16)
    middle_full = lax.all_gather(middle_low, "mp", axis=0, tiled=True)
    mixed_grad = jnp.einsum(
        "rd,kd->rk", middle_full, output_weight, preferred_element_type=jnp.float32
    ).astype(jnp.bfloat16)
    output_grad = jnp.einsum("rk,rd->kd", mixed, middle_full, preferred_element_type=jnp.float32)
    grad_attn = mixed_grad.astype(jnp.float32).reshape(slot_len, head_count, DH)
    query_grad, key_grad, value_grad = attend_backward(
        grad_attn, attended, denoms, query_map, key_map, values, memory, key_total, crop_len
    )
    query_low = (query_grad * feature_slope(query)).astype(jnp.bfloat16)
    key_low = (key_grad * valid_mask[:, None, None] * feature_slope(key_raw)).astype(jnp.bfloat16)
    value_low = value_grad.astype(jnp.bfloat16)
    qkv_grad = jnp.stack([query_low, key_low, value_low], axis=1).reshape(slot_len, 3, local_width)
    input_grad = jnp.einsum("rd,rck->cdk", first_rows, qkv_grad, preferred_element_type=jnp.float32)
    part_rows = qkv_grad
    first_grad = lax.psum_scatter(
        jnp.einsum(
            "rck,cdk->rd", part_rows, input_weight, preferred_element_type=jnp.float32
        ).astype(jnp.bfloat16),
        "mp",
        scatter_dimension=0,
        tiled=True,
    ).astype(jnp.float32)
    back_one, gain_one, bias_one = normalise_back(first_grad, unit_one, inverse_one, norm_gain[0])
    grad_input = (middle_grad + back_one)[None]
    input_grad, output_grad, up_grad, down_grad = (
        lax.psum(input_grad.astype(jnp.bfloat16), "dp").astype(jnp.float32),
        lax.psum(output_grad.astype(jnp.bfloat16), "dp").astype(jnp.float32),
        lax.psum(up_grad.astype(jnp.bfloat16), "dp").astype(jnp.float32),
        lax.psum(down_grad.astype(jnp.bfloat16), "dp").astype(jnp.float32),
    )
    kept_denoms = jnp.where(valid_mask[:, None] > 0, denoms, 0.0)
    den_total = jnp.sum(kept_denoms)
    den_count = crop_len.astype(jnp.float32) * head_count
    den_peak = jnp.max(kept_denoms)
    gain_grad, bias_grad, den_total, den_count, den_peak = combined_all(
        (
            jnp.stack([gain_one, gain_two]),
            jnp.stack([bias_one, bias_two]),
            den_total,
            den_count,
            den_peak,
        ),
        ("dp", "mp"),
        combine_stats,
    )
    scaling = DH * slot_len
    denominator_stats = jnp.stack([den_peak / scaling, den_total / den_count / scaling])
    return (
        block_out,
        grad_input,
        input_grad,
        output_grad,
        up_grad,
        down_grad,
        gain_grad,
        bias_grad,
        denominator_stats,
    )

MESH = pl.DeviceIdType.MESH
BF = jnp.bfloat16
F32 = jnp.float32
ROWS = 512
CH = 256
PAIR = 128


def dot_nn(a, b):
    return lax.dot_general(a, b, (((1,), (0,)), ((), ())), preferred_element_type=F32)


def dot_nt(a, b):
    return lax.dot_general(a, b, (((1,), (1,)), ((), ())), preferred_element_type=F32)


def dot_tn(a, b):
    return lax.dot_general(a, b, (((0,), (0,)), ((), ())), preferred_element_type=F32)


class Place:
    def __init__(self):
        dp = lax.axis_index("dp")
        mp = lax.axis_index("mp")
        self.dp, self.mp = dp, mp
        self.core = lax.rem(dp, 2)
        chip = dp // 2
        y = lax.rem(chip, 2)
        z = chip // 2
        self.r = z + y * (7 - 2 * z)
        self.across = (dp, 1 - mp)
        self.mate = (dp + 1 - 2 * self.core, mp)
        self.next = self.at(lax.rem(self.r + 1, 8))
        self.prev = self.at(lax.rem(self.r + 7, 8))

    def at(self, r):
        y = r // 4
        z = r + y * (7 - 2 * r)
        return ((z * 2 + y) * 2 + self.core, self.mp)

    def partners(self):
        return [self.across, self.mate, self.next, self.prev]


def greet(partners):
    barrier = pltpu.get_barrier_semaphore()
    for partner in partners:
        pl.semaphore_signal(barrier, inc=1, device_id=partner, device_id_type=MESH)
    pl.semaphore_wait(barrier, len(partners))


def remote(src, dst, send_sem, recv_sem, device):
    return pltpu.make_async_remote_copy(
        src_ref=src, dst_ref=dst, send_sem=send_sem, recv_sem=recv_sem,
        device_id=device, device_id_type=MESH,
    )


def aligned(start, size, unit):
    return pl.ds(pl.multiple_of(start, unit), size)


def lane_head(shape):
    return lax.broadcasted_iota(jnp.int32, shape, len(shape) - 1) < DH


def same_head():
    row = lax.broadcasted_iota(jnp.int32, (PAIR, PAIR), 0) < DH
    lane = lax.broadcasted_iota(jnp.int32, (PAIR, PAIR), 1) < DH
    return row == lane


def causal_tile():
    row = lax.broadcasted_iota(jnp.int32, (CH, CH), 0)
    col = lax.broadcasted_iota(jnp.int32, (CH, CH), 1)
    return row >= col


def unpack_state(packed):
    keep = same_head()
    zero = jnp.zeros_like(packed)
    return jnp.concatenate(
        [jnp.where(keep, packed, zero), jnp.where(keep, pltpu.roll(packed, DH, 1), zero)], axis=1
    )


def split_heads(pair):
    first = lane_head(pair.shape)
    zero = jnp.zeros_like(pair)
    return jnp.where(first, pair, zero), jnp.where(first, zero, pair)


def row_norm(rows):
    centre = jnp.mean(rows, axis=-1, keepdims=True)
    centred = rows - centre
    inverse = lax.rsqrt(jnp.mean(centred * centred, axis=-1, keepdims=True) + EPSILON)
    return centred * inverse, inverse


def front_kernel(
    len_ref, x_hbm, dy_hbm, win_hbm, wo_hbm, wdn_hbm, gain_ref, bias_ref,
    first_o, qkv_o, mix_o, rden_o, state_o, mid_o, sec_o, wino_o, woo_o, dyo_o, hg_o, stat_ref,
    x_v, dy_v, win_v, wino_v, wo_v, woo_v, wdn_v, first_v, qkv_v, num_v, den_v, mix_v, mid_v, sec_v, hg_v,
    local_v, ssend_v, srecv_v, state_v,
    in_sem, out_sem, xs_sem, xr_sem, ring_s, ring_r, mate_s, mate_r,
):
    here = Place()
    loads = [
        (x_hbm, x_v), (win_hbm, win_v), (dy_hbm, dy_v), (wdn_hbm, wdn_v), (wo_hbm, wo_v),
    ]
    loads = [pltpu.make_async_copy(a, b, in_sem.at[i]) for i, (a, b) in enumerate(loads)]
    for load in loads:
        load.start()
    greet(here.partners())
    parts = ((win_hbm, wino_v, 192), (wo_hbm, woo_v, 32))

    def rows_of(array, offset, core):
        rows = parts[array][2]
        return aligned((lax.rem(here.r + 8 + offset, 8) * 2 + core) * rows, rows, 32)

    cross = []
    for array, (src, dst, _) in enumerate(parts):
        for k in range(2):
            at = rows_of(array, 4 * k, here.core)
            slot = 2 * array + k
            cross.append(remote(src.at[at], dst.at[at], xs_sem.at[slot], xr_sem.at[slot], here.across))
    for copy in cross:
        copy.start()
    gone = []

    def dy_part(count):
        for _ in range(count):
            k = len(gone)
            rows = pl.ds(k * 64, 64)
            copy = remote(dy_hbm.at[rows], dyo_o.at[rows], xs_sem.at[7 + k], xr_sem.at[7 + k], here.across)
            copy.start()
            gone.append(copy)

    dy_part(2)

    gain = gain_ref[0:1, :]
    bias = bias_ref[0:1, :]
    sends = []
    outs = []

    def out(src, dst):
        copy = pltpu.make_async_copy(src, dst, out_sem.at[len(outs)])
        copy.start()
        outs.append(copy)

    FAR = ((-1, 3, -2), (1, 5, 2))

    def to_mate(array, slot, offset):
        at = rows_of(array, offset, here.core)
        dst = parts[array][1]
        copy = remote(dst.at[at], dst.at[at], mate_s.at[array, slot], mate_r.at[array, slot], here.mate)
        copy.start()
        sends.append(copy)

    def to_ring(array, way, k, offset):
        at = rows_of(array, offset, here.core)
        dst = parts[array][1]
        copy = remote(
            dst.at[at], dst.at[at], ring_s.at[array, way, k], ring_r.at[array, way, k],
            here.next if way == 0 else here.prev,
        )
        copy.start()
        sends.append(copy)

    def from_across(array):
        for k in range(2):
            cross[2 * array + k].wait_recv()
            for way in (0, 1):
                to_ring(array, way, k, 4 * k)
            to_mate(array, k, 4 * k)

    def from_ring(array, k):
        for way in (0, 1):
            at = rows_of(array, FAR[way][k], here.core)
            dst = parts[array][1].at[at]
            remote(dst, dst, ring_s.at[array, way, k], ring_r.at[array, way, k], here.next).wait_recv()
            if k == 0:
                to_ring(array, way, 2, FAR[way][0])
            to_mate(array, 2 + 2 * k + way, FAR[way][k])

    def mate_wait(array):
        offsets = [0, 4] + [FAR[way][k] for k in range(3) for way in (0, 1)]
        for slot, offset in enumerate(offsets):
            dst = parts[array][1].at[rows_of(array, offset, 1 - here.core)]
            remote(dst, dst, mate_s.at[array, slot], mate_r.at[array, slot], here.mate).wait_recv()

    loads[0].wait()

    @pl.loop(0, ROWS // 128)
    def _(i):
        at = aligned(i * 128, 128, 128)
        unit, _ = row_norm(x_v[at, :].astype(F32))
        first_v[at, :] = (unit * gain + bias).astype(BF)

    out(first_v, first_o)
    crop_len = len_ref[0]

    def project(half, weights, which):
        @pl.loop(0, 2)
        def _(c):
            at = aligned(c * CH, CH, CH)
            rows = first_v[at, :]
            for i in which:
                raw = dot_nn(rows, weights[pl.ds(i * 1024, 1024), :])
                if i < 2:
                    raw = jnp.where(raw > 0, raw + 1.0, jnp.exp(jnp.minimum(raw, 0.0)))
                if i == 1:
                    place = lax.broadcasted_iota(jnp.int32, raw.shape, 0) + (here.mp * ROWS + c * CH)
                    raw = jnp.where(place < crop_len, raw, 0.0)
                qkv_v[half, i, at, :] = raw.astype(BF)

    def states(half):
        keep = same_head()

        @pl.loop(0, 4)
        def _(p):
            lanes = aligned(p * PAIR, PAIR, PAIR)
            total = None
            for c in range(2):
                keys = qkv_v[half, 1, pl.ds(c * CH, CH), lanes]
                vals = qkv_v[half, 2, pl.ds(c * CH, CH), lanes]
                made = dot_tn(keys, jnp.concatenate([vals, jnp.ones_like(vals)], axis=1))
                packed = jnp.where(keep, made[:, :PAIR], made[:, PAIR:])
                if c == 0:
                    local_v[half, p] = packed
                    total = packed
                else:
                    ssend_v[half, p] = (total + packed).astype(BF)

        copy = remote(
            ssend_v.at[half], srecv_v.at[1 - half], xs_sem.at[5 + half], xr_sem.at[6 - half], here.across
        )
        copy.start()
        sends.append(copy)

    def inside(half):
        mask = causal_tile()

        @pl.loop(0, 8)
        def _(n):
            p = n // 2
            c = lax.rem(n, 2)
            lanes = aligned(p * PAIR, PAIR, PAIR)
            at = aligned(c * CH, CH, CH)
            query = qkv_v[half, 0, at, lanes]
            key = qkv_v[half, 1, at, lanes]
            val = qkv_v[half, 2, at, lanes]
            first = lane_head(val.shape)
            one = jnp.ones_like(val)
            zero = jnp.zeros_like(val)
            sums = None
            for head, part in enumerate(split_heads(query)):
                score = jnp.where(mask, dot_nt(part, key), 0.0).astype(BF)
                mine = first if head == 0 else jnp.logical_not(first)
                right = jnp.concatenate([jnp.where(mine, val, zero), jnp.where(mine, one, zero)], axis=1)
                term = dot_nn(score, right)
                sums = term if sums is None else sums + term
            num_v[at, lanes] = sums[:, :PAIR]
            den_v[half, at, lanes] = sums[:, PAIR:]

    def finish(half):
        flag = here.mp.astype(F32)

        @pl.loop(0, 8)
        def _(n):
            p = n // 2
            c = lax.rem(n, 2)
            lanes = aligned(p * PAIR, PAIR, PAIR)
            at = aligned(c * CH, CH, CH)
            query = qkv_v[half, 0, at, lanes]
            before = srecv_v[half, p].astype(F32) * flag
            state_v[half, p] = before.astype(BF)
            before = before + local_v[half, p] * c.astype(F32)
            term = dot_nn(query, unpack_state(before).astype(BF))
            num = num_v[at, lanes] + term[:, :PAIR]
            den = den_v[half, at, lanes] + term[:, PAIR:]
            inverse = 1.0 / den
            den_v[half, at, lanes] = inverse
            mix_v[half, at, lanes] = (num * inverse).astype(BF)
            place = lax.broadcasted_iota(jnp.int32, den.shape, 0) + (here.mp * ROWS + c * CH)
            kept = jnp.where(place < crop_len, den, 0.0).reshape(CH // 8, 8, PAIR)
            stat_ref[0] = jnp.maximum(stat_ref[0], jnp.max(kept, axis=0))
            stat_ref[1] = stat_ref[1] + jnp.sum(kept, axis=0)

    def hidden_grad():
        @pl.loop(0, 2)
        def _(j):
            cols = aligned(j * 1024, 1024, 1024)
            hg_v[:, cols] = dot_nt(dy_v[...], wdn_v[cols, :]).astype(BF)

    stat_ref[...] = jnp.zeros_like(stat_ref)
    loads[1].wait()
    project(0, win_v, (1, 2))
    states(0)
    dy_part(1)
    project(0, win_v, (0,))
    from_across(0)
    dy_part(1)
    inside(0)
    from_ring(0, 0)
    from_across(1)
    dy_part(2)
    loads[2].wait()
    loads[3].wait()
    hidden_grad()
    from_ring(0, 1)
    from_ring(1, 0)
    from_ring(0, 2)
    mate_wait(0)
    from_ring(1, 1)
    out(wino_v, wino_o)
    mid_v[:, pl.ds(0, 512)] = num_v[...]
    project(1, wino_v, (1, 2))
    states(1)
    dy_part(2)
    project(1, wino_v, (0,))
    from_ring(1, 2)
    inside(1)
    remote(ssend_v.at[0], srecv_v.at[1], xs_sem.at[5], xr_sem.at[6], here.across).wait_recv()
    finish(1)
    out(hg_v, hg_o)
    num_v[...] = mid_v[:, pl.ds(0, 512)]
    mate_wait(1)
    remote(ssend_v.at[1], srecv_v.at[0], xs_sem.at[6], xr_sem.at[5], here.across).wait_recv()
    finish(0)
    out(qkv_v, qkv_o)
    out(den_v, rden_o)
    out(mix_v, mix_o)
    out(state_v, state_o)
    out(woo_v, woo_o)
    loads[4].wait()
    gain_two = gain_ref[1:2, :]
    bias_two = bias_ref[1:2, :]

    @pl.loop(0, 2)
    def _(c):
        at = aligned(c * CH, CH, CH)
        own = dot_nn(mix_v[0, at, :], wo_v[...]).astype(BF).astype(F32)
        other = dot_nn(mix_v[1, at, :], woo_v[...]).astype(BF).astype(F32)
        middle = x_v[at, :].astype(F32) + (own + other)
        mid_v[at, :] = middle
        unit, _ = row_norm(middle)
        sec_v[at, :] = (unit * gain_two + bias_two).astype(BF)

    out(mid_v, mid_o)
    out(sec_v, sec_o)
    for copy in gone:
        copy.wait_recv()
    for copy in cross + gone + sends:
        copy.wait_send()
    for copy in outs:
        copy.wait()


def any_spec(count):
    return [pl.BlockSpec(memory_space=pl.ANY)] * count


def front(lengths, x_rows, dy_rows, win, wo, wdn, gain, bias):
    vm = pltpu.VMEM
    shapes = [
        ((512, 1024), BF), ((2, 3, 512, 512), BF), ((2, 512, 512), BF), ((2, 512, 512), F32),
        ((2, 4, PAIR, PAIR), BF), ((512, 1024), F32), ((512, 1024), BF), ((3072, 512), BF),
        ((512, 1024), BF), ((512, 1024), BF), ((512, 2048), BF), ((2, 8, PAIR), F32),
    ]
    dma = pltpu.SemaphoreType.DMA
    return pl.pallas_call(
        front_kernel,
        out_shape=[jax.ShapeDtypeStruct(s, d) for s, d in shapes],
        in_specs=[pl.BlockSpec(memory_space=pltpu.SMEM)] + any_spec(5)
        + [pl.BlockSpec(memory_space=pltpu.VMEM)] * 2,
        out_specs=any_spec(11) + [pl.BlockSpec(memory_space=pltpu.VMEM)],
        scratch_shapes=[
            vm((512, 1024), BF), vm((512, 1024), BF), vm((3072, 512), BF), vm((3072, 512), BF),
            vm((512, 1024), BF), vm((512, 1024), BF), vm((2048, 1024), BF), vm((512, 1024), BF),
            vm((2, 3, 512, 512), BF), vm((512, 512), F32), vm((2, 512, 512), F32), vm((2, 512, 512), BF),
            vm((512, 1024), F32), vm((512, 1024), BF), vm((512, 2048), BF),
            vm((2, 4, PAIR, PAIR), F32), vm((2, 4, PAIR, PAIR), BF), vm((2, 4, PAIR, PAIR), BF),
            vm((2, 4, PAIR, PAIR), BF),
            dma((5,)), dma((12,)), dma((15,)), dma((15,)), dma((2, 2, 3)), dma((2, 2, 3)),
            dma((2, 8)), dma((2, 8)),
        ],
        compiler_params=pltpu.CompilerParams(
            collective_id=0, has_side_effects=True, vmem_limit_bytes=58 * 1024 * 1024
        ),
        name="front",
    )(lengths, x_rows, dy_rows, win, wo, wdn, gain, bias)


GELU_A = 0.7978845608028654
GELU_B = 0.044715


def gelu_pair(v):
    square = v * v
    t = jnp.tanh(GELU_A * v * (1.0 + GELU_B * square))
    half = 0.5 * (1.0 + t)
    slope = half + (0.5 * GELU_A) * v * (1.0 - t * t) * (1.0 + (3.0 * GELU_B) * square)
    return v * half, slope


def middle_kernel(
    sec_hbm, dy_hbm, dyo_hbm, hg_hbm, wup_hbm, wdn_hbm,
    part_o, pin_o, mlp_o, dslab_o, uslab_o,
    sec_v, dy_v, hg_v, wup_v, wdn_v, hid_v, part_v, send_v, pin_v, mlp_v,
    dsend_v, drecv_v, dslab_v, usend_v, urecv_v, uslab_v,
    in_sem, out_sem, xs_sem, xr_sem, ms_sem, mr_sem,
):
    here = Place()
    own = pl.ds(0, ROWS)
    other = pl.ds(ROWS, ROWS)
    loads = [
        (sec_hbm, sec_v.at[own]), (wup_hbm, wup_v), (hg_hbm, hg_v.at[own]), (wdn_hbm, wdn_v),
        (dy_hbm, dy_v.at[own]), (dyo_hbm, dy_v.at[other]),
    ]
    loads = [pltpu.make_async_copy(a, b, in_sem.at[i]) for i, (a, b) in enumerate(loads)]
    for load in loads:
        load.start()
    greet([here.across, here.mate])
    sends = []
    outs = []

    def out(src, dst):
        copy = pltpu.make_async_copy(src, dst, out_sem.at[len(outs)])
        copy.start()
        outs.append(copy)

    def across(src, dst, slot):
        copy = remote(src, dst, xs_sem.at[slot], xr_sem.at[slot], here.across)
        copy.start()
        sends.append(copy)
        return copy

    ahead = [
        across(sec_hbm.at[pl.ds(c * CH, CH)], sec_v.at[pl.ds(ROWS + c * CH, CH)], c) for c in range(2)
    ]

    def up(chunk):
        rows = pl.ds(chunk * CH, CH)

        @pl.loop(0, 4)
        def _(j):
            cols = aligned(j * 512, 512, 512)
            raw = dot_nn(sec_v[rows, :], wup_v[:, cols])
            value, slope = gelu_pair(raw)
            hid_v[rows, cols] = value.astype(BF)
            hg_v[rows, cols] = (hg_v[rows, cols].astype(F32) * slope).astype(BF)

    def back(chunk, dst):
        dst[...] = dot_nt(hg_v[pl.ds(chunk * CH, CH), :], wup_v[...]).astype(BF)

    loads[0].wait()
    loads[1].wait()
    loads[2].wait()
    for c in range(2):
        up(c)
        back(c, part_v.at[pl.ds(c * CH, CH)])
    out(part_v, part_o)
    for load in loads[3:]:
        load.wait()
    for c in range(2):
        @pl.loop(0, 2)
        def _(j):
            cols = aligned(j * 1024, 1024, 1024)
            rows = pl.ds(ROWS + c * CH, CH)
            hg_v[rows, cols] = dot_nt(dy_v[rows, :], wdn_v[cols, :]).astype(BF)

        ahead[c].wait_recv()
        up(2 + c)
        rows = pl.ds(c * CH, CH)
        back(2 + c, send_v.at[rows])
        across(send_v.at[rows], pin_v.at[rows], 2 + c)
    their = 1 - here.core

    def down_grad(half, dst, plus):
        @pl.loop(0, 2)
        def _(i):
            cols = aligned(half * 1024 + i * 512, 512, 512)
            at = aligned(i * 512, 512, 512)
            made = dot_tn(hid_v[:, cols], dy_v[...])
            if plus is not None:
                made = made + plus[at, :].astype(F32)
            dst[at, :] = made.astype(BF)

    def up_grad(half, dst, plus):
        @pl.loop(0, 2)
        def _(i):
            cols = aligned(half * 512, 512, 512)
            at = aligned(i * 1024, 1024, 1024)
            made = dot_tn(sec_v[:, cols], hg_v[:, at])
            if plus is not None:
                made = made + plus[:, at].astype(F32)
            dst[:, at] = made.astype(BF)

    def to_mate(src, dst, slot):
        copy = remote(src, dst, ms_sem.at[slot], mr_sem.at[slot], here.mate)
        copy.start()
        sends.append(copy)
        return copy

    down_grad(their, dsend_v, None)
    to_d = to_mate(dsend_v, drecv_v, 0)
    up_grad(their, usend_v, None)
    to_u = to_mate(usend_v, urecv_v, 1)

    @pl.loop(0, 2)
    def _(i):
        rows = aligned(i * ROWS, ROWS, ROWS)
        mlp_v[rows, :] = dot_nn(hid_v[rows, :], wdn_v[...]).astype(BF)

    out(mlp_v, mlp_o)
    to_d.wait_recv()
    down_grad(here.core, dslab_v, drecv_v)
    out(dslab_v, dslab_o)
    to_u.wait_recv()
    up_grad(here.core, uslab_v, urecv_v)
    out(uslab_v, uslab_o)
    for c in range(2):
        rows = pl.ds(c * CH, CH)
        remote(send_v.at[rows], pin_v.at[rows], xs_sem.at[2 + c], xr_sem.at[2 + c], here.across).wait_recv()
    out(pin_v, pin_o)
    for copy in sends:
        copy.wait_send()
    for copy in outs:
        copy.wait()


def middle(sec, dy, dyo, hg, wup, wdn):
    vm = pltpu.VMEM
    dma = pltpu.SemaphoreType.DMA
    shapes = [
        ((512, 1024), BF), ((512, 1024), BF), ((1024, 1024), BF), ((1024, 1024), BF), ((512, 2048), BF),
    ]
    return pl.pallas_call(
        middle_kernel,
        out_shape=[jax.ShapeDtypeStruct(s, d) for s, d in shapes],
        in_specs=any_spec(6),
        out_specs=any_spec(5),
        scratch_shapes=[
            vm((1024, 1024), BF), vm((1024, 1024), BF), vm((1024, 2048), BF), vm((1024, 2048), BF),
            vm((2048, 1024), BF), vm((1024, 2048), BF), vm((512, 1024), BF), vm((512, 1024), BF),
            vm((512, 1024), BF), vm((1024, 1024), BF),
            vm((1024, 1024), BF), vm((1024, 1024), BF), vm((1024, 1024), BF),
            vm((512, 2048), BF), vm((512, 2048), BF), vm((512, 2048), BF),
            dma((6,)), dma((5,)), dma((4,)), dma((4,)), dma((2,)), dma((2,)),
        ],
        compiler_params=pltpu.CompilerParams(
            collective_id=1, has_side_effects=True, vmem_limit_bytes=58 * 1024 * 1024
        ),
        name="middle",
    )(sec, dy, dyo, hg, wup, wdn)


PACE = 36


class Arc:
    def __init__(self, here, slab, base, rows, recv, result, result_base, sems, source=None):
        self.here, self.slab, self.base, self.rows = here, slab, base, rows
        self.source = slab if source is None else source
        self.recv, self.result, self.result_base = recv, result, result_base
        self.rs_s, self.rs_r, self.ag_s, self.ag_r, self.mt_s, self.mt_r, self.local = sems
        self.pending = []
        self.t = 0

    def span(self, base, offset, half):
        start = base + lax.rem(self.here.r + 8 + offset, 8) * self.rows
        if half is None:
            return aligned(start, self.rows, 16)
        return aligned(start + half * (self.rows // 2), self.rows // 2, 16)

    def mine(self, offset, half=None):
        return self.span(self.base, offset, half)

    def place(self, offset, core, half=None):
        return self.result.at[self.span(self.result_base(core) + self.base, offset, half)]

    def send(self, src, dst, send_sem, recv_sem, device):
        copy = remote(src, dst, send_sem, recv_sem, device)
        copy.start()
        self.pending.append(copy)

    def to(self, way):
        return self.here.next if way == 0 else self.here.prev

    def sign(self, way):
        return 1 if way == 0 else -1

    def slot(self, way, s):
        if s > 0:
            return self.recv.at[way, s]
        return self.recv.at[way, 0, pl.ds(way * (self.rows // 2), self.rows // 2)]

    def arrived(self, way, s):
        got = self.slot(way, s)
        remote(got, got, self.rs_s.at[way, s], self.rs_r.at[way, s], self.to(way)).wait_recv()

    def gather_step(self, way, s):
        sign = self.sign(way)
        if s == 0:
            src = self.source.at[self.mine(sign * 4, way)]
        else:
            self.arrived(way, s - 1)
            own = self.slab[self.mine(sign * (4 - s)), :].astype(F32)
            src = self.recv.at[way, s - 1]
            if s == 1:
                half = self.rows // 2
                kept = pl.ds(way * half, half)
                rest = pl.ds((1 - way) * half, half)
                at = slice(way * half, way * half + half)
                src[kept, :] = (src[kept, :].astype(F32) + own[at]).astype(BF)
                at = slice((1 - way) * half, (1 - way) * half + half)
                src[rest, :] = own[at].astype(BF)
            else:
                src[...] = (src[...].astype(F32) + own).astype(BF)
        self.send(src, self.slot(way, s), self.rs_s.at[way, s], self.rs_r.at[way, s], self.to(way))

    def spread(self, src, offset, step, way, half=None):
        dst = self.place(offset, self.here.core, half)
        if step < 4 and not (step == 3 and half is None):
            self.send(src, dst, self.ag_s.at[way, step], self.ag_r.at[way, step], self.to(way))

    def to_mate(self, src, offset, slot, half=None):
        dst = self.place(offset, self.here.core, half)
        self.send(src, dst, self.mt_s.at[slot], self.mt_r.at[slot], self.here.mate)

    def total(self):
        self.arrived(0, 3)
        self.arrived(1, 3)
        sums = self.recv.at[0, 3]
        own = self.slab[self.mine(0), :].astype(F32)
        sums[...] = (sums[...].astype(F32) + self.recv[1, 3].astype(F32) + own).astype(BF)
        for way in (0, 1):
            self.spread(sums, 0, 0, way)
        self.to_mate(sums, 0, 0)
        self.keep = pltpu.make_async_copy(sums, self.place(0, self.here.core), self.local)
        self.keep.start()

    def spread_step(self, way, s):
        sign = self.sign(way)
        half = way if s == 3 else None
        got = self.place(-sign * (s + 1), self.here.core, half)
        remote(got, got, self.ag_s.at[way, s], self.ag_r.at[way, s], self.to(way)).wait_recv()
        if s < 3:
            part = way if s == 2 else None
            src = self.place(-sign * (s + 1), self.here.core, part)
            self.spread(src, -sign * (s + 1), s + 1, way, part)
        self.to_mate(got, -sign * (s + 1), 1 + 2 * s + way, half)

    def tick(self):
        t = self.t
        self.t = t + 1
        if t == 4:
            self.total()
        elif t < 9:
            for way in (0, 1):
                if t < 4:
                    self.gather_step(way, t)
                else:
                    self.spread_step(way, t - 5)

    def finish(self):
        for copy in self.pending:
            copy.wait_send()
        self.keep.wait()
        other = 1 - self.here.core
        for slot in range(9):
            if slot == 0:
                got = self.place(0, other)
            else:
                s, way = (slot - 1) // 2, (slot - 1) % 2
                got = self.place(-self.sign(way) * (s + 1), other, way if s == 3 else None)
            remote(got, got, self.mt_s.at[slot], self.mt_r.at[slot], self.here.mate).wait_recv()


def back_kernel(
    len_ref, gain_ref, bias_ref, stat_ref,
    part_hbm, pin_hbm, mid_hbm, x_hbm, dy_hbm, qkv_hbm, mix_hbm, rden_hbm, state_hbm, first_hbm,
    win_hbm, wino_hbm, wo_hbm, woo_hbm, mlp_hbm, dslab_hbm, uslab_hbm,
    resd_o, resu_o, resi_o, reso_o, out_o, gin_o, small_ref,
    part_v, pin_v, mid_v, dy_v, qkv_v, mix_v, rden_v, state_v, first_v, win_v, wo_v,
    mlpin_v, mg_v, mgf_v, mixg_v, top_v, bot_v, dqkv_v, local_v, lsend_v, lrecv_v,
    dslab_v, uslab_v, drecv_v, urecv_v, gm_v, gr_v, ga_v, gx_v, om_v, or_v, oa_v, ox_v, irecv_v, orecv_v,
    small_s, small_r,
    in_sem, out_sem, xs_sem, xr_sem, ms_sem, mr_sem, bs_sem, br_sem,
    rs_s, rs_r, ag_s, ag_r, mt_s, mt_r, keep_s,
):
    here = Place()
    loads = [
        (part_hbm, part_v), (pin_hbm, pin_v), (mid_hbm, mid_v), (dy_hbm, dy_v), (dslab_hbm, dslab_v),
        (uslab_hbm, uslab_v), (wo_hbm, wo_v.at[0]), (woo_hbm, wo_v.at[1]), (mix_hbm, mix_v),
        (rden_hbm, rden_v), (qkv_hbm, qkv_v), (state_hbm, state_v), (first_hbm, first_v),
        (win_hbm, win_v.at[0]), (wino_hbm, win_v.at[1]), (x_hbm, part_v), (mlp_hbm.at[pl.ds(0, ROWS)], pin_v),
    ]
    loads = [pltpu.make_async_copy(a, b, in_sem.at[i]) for i, (a, b) in enumerate(loads)]
    for load in loads[:15]:
        load.start()
    y_mate = (here.dp + 2 - 4 * lax.rem(here.dp // 2, 2), here.mp)
    z_mate = (here.dp + 4 - 8 * lax.rem(here.dp // 4, 2), here.mp)
    z_far = (here.dp + 8 - 16 * (here.dp // 8), here.mp)
    greet(here.partners() + [y_mate, z_mate, z_far])
    sends = []
    outs = []

    def out(src, dst):
        copy = pltpu.make_async_copy(src, dst, out_sem.at[len(outs)])
        copy.start()
        outs.append(copy)

    def across(src, dst, slot):
        copy = remote(src, dst, xs_sem.at[slot], xr_sem.at[slot], here.across)
        copy.start()
        sends.append(copy)
        return copy

    def to_mate(src, dst, slot):
        copy = remote(src, dst, ms_sem.at[slot], mr_sem.at[slot], here.mate)
        copy.start()
        sends.append(copy)
        return copy

    arcs = []

    def add_arc(slab, base, rows, recv, result, result_base, source=None):
        n = len(arcs)
        sems = (rs_s.at[n], rs_r.at[n], ag_s.at[n], ag_r.at[n], mt_s.at[n], mt_r.at[n], keep_s.at[n])
        arcs.append(Arc(here, slab, base, rows, recv, result, result_base, sems, source))
        return arcs[-1]

    ring_d = add_arc(dslab_v, 0, 128, drecv_v, resd_o, lambda core: core * 1024, dslab_hbm)
    ring_u = add_arc(uslab_v, 0, 64, urecv_v, resu_o, lambda core: core * 512, uslab_hbm)
    ring_o = add_arc(oa_v.at[0], 0, 32, orecv_v, reso_o, lambda core: core * 256)
    ring_i = [
        add_arc(ga_v.at[0], i * 512, 64, irecv_v.at[i], resi_o, lambda core: core * 1536) for i in range(3)
    ]

    credit = [0]

    def ring(count):
        credit[0] += count * PACE
        while credit[0] >= 100:
            credit[0] -= 100
            first = ring_d if ring_d.t <= ring_u.t else ring_u
            first.tick()

    def ring_on(arc):
        arc.tick()

    ring_d.tick()
    ring_u.tick()

    small_s[...] = jnp.zeros_like(small_s)
    for load in loads[0:6]:
        load.wait()
    gain_two = gain_ref[1:2, :]

    @pl.loop(0, ROWS // 128)
    def _(i):
        at = aligned(i * 128, 128, 128)
        grad = part_v[at, :].astype(F32) + pin_v[at, :].astype(F32)
        unit, inverse = row_norm(mid_v[at, :])
        scaled = grad * gain_two
        centre = jnp.mean(scaled, axis=-1, keepdims=True)
        along = jnp.mean(scaled * unit, axis=-1, keepdims=True)
        total = dy_v[at, :].astype(F32) + inverse * (scaled - centre - unit * along)
        mgf_v[at, :] = total
        mg_v[at, :] = total.astype(BF)
        small_s[1:2, :] = small_s[1:2, :] + jnp.sum(grad * unit, axis=0, keepdims=True)
        small_s[3:4, :] = small_s[3:4, :] + jnp.sum(grad, axis=0, keepdims=True)

    for load in loads[15:]:
        load.start()
    ring(2)
    for load in loads[6:12]:
        load.wait()
    @pl.loop(0, 2)
    def _(half):
        mixg_v[half] = dot_nt(mg_v[...], wo_v[half]).astype(BF)

    ring(1)
    their = 1 - here.core

    def out_grad(half, side, dst):
        cols = aligned(side * 256, 256, 256)
        dst[...] = dot_tn(mix_v[half, :, cols], mg_v[...]).astype(BF)

    keep = same_head()

    def tops(half):
        @pl.loop(0, 4)
        def _(p):
            lanes_at = aligned(p * PAIR, PAIR, PAIR)
            packs = []
            blocks = jnp.where(keep, 1.0, 0.0).astype(BF)
            for c in range(2):
                at = pl.ds(c * CH, CH)
                top = (mixg_v[half, at, lanes_at].astype(F32) * rden_v[half, at, lanes_at]).astype(BF)
                top_v[half, at, lanes_at] = top
                prod = top.astype(F32) * mix_v[half, at, lanes_at].astype(F32)
                high = prod.astype(BF)
                low = (prod - high.astype(F32)).astype(BF)
                bottom = -(dot_nn(high, blocks) + dot_nn(low, blocks))
                high = bottom.astype(BF)
                low = (bottom - high.astype(F32)).astype(BF)
                lane = lax.rem(lax.broadcasted_iota(jnp.int32, bottom.shape, 1), DH)
                bot_v[half, at, lanes_at] = jnp.where(
                    lane == 0, high, jnp.where(lane == 1, low, jnp.zeros_like(high))
                )
                query = qkv_v[half, 0, at, lanes_at]
                made = dot_tn(query, jnp.concatenate([top, high], axis=1))
                packs.append(jnp.where(keep, made[:, :PAIR], pltpu.roll(made[:, PAIR:], DH, 1)))
            local_v[half, p] = packs[1]
            lsend_v[half, p] = (packs[0] + packs[1]).astype(BF)

        across(lsend_v.at[half], lrecv_v.at[1 - half], 1 + half)

    tops(0)
    ring(1)
    tops(1)
    ring(1)
    for half in (1, 0):
        out_grad(half, their, om_v.at[half])
        to_mate(om_v.at[half], or_v.at[half], half)
    ring(1)
    for half in (1, 0):
        out_grad(half, here.core, oa_v.at[half])
    ring(1)
    for load in loads[12:15]:
        load.wait()

    def attend_back(half):
        mask = causal_tile()
        earlier = 1.0 - here.mp.astype(F32)
        remote(
            lsend_v.at[1 - half], lrecv_v.at[half], xs_sem.at[2 - half], xr_sem.at[2 - half], here.across
        ).wait_recv()

        def body(p, c):
            lanes_at = aligned(p * PAIR, PAIR, PAIR)
            at = aligned(c * CH, CH, CH)
            second = c.astype(F32)
            query = qkv_v[half, 0, at, lanes_at]
            key = qkv_v[half, 1, at, lanes_at]
            val = qkv_v[half, 2, at, lanes_at]
            top = top_v[half, at, lanes_at]
            bot = bot_v[half, at, lanes_at]
            lane = lax.rem(lax.broadcasted_iota(jnp.int32, val.shape, 1), DH)
            one = jnp.ones_like(val)
            zero = jnp.zeros_like(val)
            val_two = jnp.concatenate([val, jnp.where(lane < 2, one, zero)], axis=1)
            val_one = jnp.concatenate([val, jnp.where(lane == 0, one, zero)], axis=1)
            key0 = qkv_v[half, 1, pl.ds(0, CH), lanes_at]
            val0 = qkv_v[half, 2, pl.ds(0, CH), lanes_at]
            made = dot_tn(key0, jnp.concatenate([val0, one], axis=1))
            made = jnp.where(keep, made[:, :PAIR], made[:, PAIR:])
            before = state_v[half, p].astype(F32) + made * second
            after = lrecv_v[half, p].astype(F32) * earlier + local_v[half, p] * (1.0 - second)
            before = unpack_state(before).astype(BF)
            after = unpack_state(after).astype(BF)
            dq = dot_nt(jnp.concatenate([top, bot], axis=1), before)
            dk = dot_nt(val_one, after)
            dv = dot_nn(key, after[:, :PAIR])
            queries, keys, tops_, bots = split_heads(query), split_heads(key), split_heads(top), split_heads(bot)
            for head in range(2):
                score = jnp.where(mask, dot_nt(queries[head], key), 0.0).astype(BF)
                grad = dot_nt(jnp.concatenate([tops_[head], bots[head]], axis=1), val_two)
                grad = jnp.where(mask, grad, 0.0).astype(BF)
                dq = dq + dot_nn(grad, keys[head])
                dk = dk + dot_tn(grad, queries[head])
                dv = dv + dot_tn(score, tops_[head])
            dqkv_v[half, 0, at, lanes_at] = (dq * jnp.minimum(query.astype(F32), 1.0)).astype(BF)
            dqkv_v[half, 1, at, lanes_at] = (dk * jnp.minimum(key.astype(F32), 1.0)).astype(BF)
            dqkv_v[half, 2, at, lanes_at] = dv.astype(BF)

        for part in range(2):
            @pl.loop(part * 4, part * 4 + 4)
            def _(n):
                body(n // 2, lax.rem(n, 2))

            ring(2)

    def piece(i):
        return pl.ds(i * 512, 512)

    def in_grads(half):
        for side, dst in ((their, gm_v), (here.core, ga_v)):
            cols = aligned(side * 512, 512, 512)
            @pl.loop(0, 3)
            def _(i):
                dst[half, aligned(i * 512, 512, 512), :] = dot_tn(first_v[:, cols], dqkv_v[half, i]).astype(BF)

            if dst is gm_v:
                for i in range(3):
                    at = piece(i)
                    to_mate(gm_v.at[half, at], gr_v.at[half, at], 2 + half * 3 + i)
            ring(1)

    def add_rows(dst, src, start, count):
        @pl.loop(0, count)
        def _(i):
            at = aligned(start + i * 128, 128, 128)
            dst[at, :] = (dst[at, :].astype(F32) + src[at, :].astype(F32)).astype(BF)

    def mate_arrival(half, i):
        at = piece(i)
        slot = 2 + half * 3 + i
        remote(gm_v.at[half, at], gr_v.at[half, at], ms_sem.at[slot], mr_sem.at[slot], here.mate).wait_recv()
        add_rows(ga_v.at[half], gr_v.at[half], i * 512, 4)

    def mate_arrival_out(half):
        remote(om_v.at[half], or_v.at[half], ms_sem.at[half], mr_sem.at[half], here.mate).wait_recv()
        add_rows(oa_v.at[half], or_v.at[half], 0, 2)

    attend_back(1)
    mate_arrival_out(1)
    cross_o = across(oa_v.at[1], ox_v, 3)
    in_grads(1)
    cross_i = []
    for i in range(3):
        mate_arrival(1, i)
        cross_i.append(across(ga_v.at[1, piece(i)], gx_v.at[piece(i)], 4 + i))
    mlp = across(mlp_hbm.at[pl.ds(ROWS, ROWS)], mlpin_v, 0)
    ring(2)
    mate_arrival_out(0)
    attend_back(0)
    cross_o.wait_recv()
    add_rows(oa_v.at[0], ox_v, 0, 2)
    ring_on(ring_o)
    in_grads(0)
    for i in range(3):
        mate_arrival(0, i)
    ring(2)
    ring_on(ring_o)

    loads[15].wait()
    gain_one = gain_ref[0:1, :]

    @pl.loop(0, 2)
    def _(quarter):
        at = aligned(quarter * CH, CH, CH)
        grad = None
        for half in range(2):
            term = None
            for j in range(3):
                made = dot_nt(dqkv_v[half, j, at, :], win_v[half, pl.ds(j * 1024, 1024), :])
                term = made if term is None else term + made
            term = term.astype(BF).astype(F32)
            grad = term if grad is None else grad + term
        unit, inverse = row_norm(part_v[at, :].astype(F32))
        scaled = grad * gain_one
        centre = jnp.mean(scaled, axis=-1, keepdims=True)
        along = jnp.mean(scaled * unit, axis=-1, keepdims=True)
        mgf_v[at, :] = mgf_v[at, :] + inverse * (scaled - centre - unit * along)
        small_s[0:1, :] = small_s[0:1, :] + jnp.sum(grad * unit, axis=0, keepdims=True)
        small_s[2:3, :] = small_s[2:3, :] + jnp.sum(grad, axis=0, keepdims=True)

    ring(4)
    ring_on(ring_o)
    out(mgf_v, gin_o)
    small_s[4:5, pl.ds(0, PAIR)] = jnp.sum(stat_ref[1], axis=0, keepdims=True) * (1.0 / DH)
    count = len_ref[0].astype(F32) * (8.0 / 1024.0)
    small_s[5:6, :] = jnp.zeros((1, 1024), F32) + count
    small_s[6:7, pl.ds(0, PAIR)] = jnp.max(stat_ref[0], axis=0, keepdims=True)
    partners = [here.mate, y_mate, z_mate, z_far, here.across]

    def small_send(step):
        src = small_s if step == 0 else small_ref
        copy = remote(src, small_r.at[step], bs_sem.at[step], br_sem.at[step], partners[step])
        copy.start()
        return copy

    def small_step(copy, step):
        copy.wait()
        src = small_s if step == 0 else small_ref
        mine, theirs = src[...], small_r[step]
        row = lax.broadcasted_iota(jnp.int32, mine.shape, 0)
        small_ref[...] = jnp.where(row < 6, mine + theirs, jnp.maximum(mine, theirs))

    for i in range(3):
        cross_i[i].wait_recv()
        add_rows(ga_v.at[0], gx_v, i * 512, 4)
        for arc in ring_i[: i + 1]:
            ring_on(arc)
        ring(6)
        ring_on(ring_o)
    copy = small_send(0)
    for step in range(9):
        for arc in ring_i:
            ring_on(arc)
        ring(6)
        ring_on(ring_o)
        if 2 <= step < 7:
            small_step(copy, step - 2)
            if step < 6:
                copy = small_send(step - 1)
    ring(2000)

    loads[16].wait()
    mlp.wait_recv()

    @pl.loop(0, 4)
    def _(i):
        at = aligned(i * 128, 128, 128)
        total = mid_v[at, :] + (pin_v[at, :].astype(F32) + mlpin_v[at, :].astype(F32))
        pin_v[at, :] = total.astype(BF)

    out(pin_v, out_o)
    for arc in arcs:
        arc.finish()
    for copy in sends:
        copy.wait_send()
    for copy in outs:
        copy.wait()


def back(lengths, gain, bias, stat, part, pin, mid, x, dy, qkv, mix, rden, state, first, win, wino, wo, woo, mlp, dslab, uslab):
    vm = pltpu.VMEM
    dma = pltpu.SemaphoreType.DMA
    shapes = [
        ((2048, 1024), BF), ((1024, 2048), BF), ((3072, 512), BF), ((512, 1024), BF),
        ((512, 1024), BF), ((512, 1024), F32), ((8, 1024), F32),
    ]
    rows = (512, 1024)
    heads = (2, 512, 512)
    pack = (2, 4, PAIR, PAIR)
    vmem = pl.BlockSpec(memory_space=pltpu.VMEM)
    return pl.pallas_call(
        back_kernel,
        out_shape=[jax.ShapeDtypeStruct(s, d) for s, d in shapes],
        in_specs=[pl.BlockSpec(memory_space=pltpu.SMEM), vmem, vmem, vmem] + any_spec(17),
        out_specs=any_spec(6) + [vmem],
        scratch_shapes=[
            vm(rows, BF), vm(rows, BF), vm(rows, F32), vm(rows, BF),
            vm((2, 3, 512, 512), BF), vm(heads, BF), vm(heads, F32), vm(pack, BF), vm(rows, BF),
            vm((2, 3072, 512), BF), vm((2, 512, 1024), BF),
            vm(rows, BF), vm(rows, BF), vm(rows, F32), vm(heads, BF), vm(heads, BF), vm(heads, BF),
            vm((2, 3, 512, 512), BF), vm(pack, F32), vm(pack, BF), vm(pack, BF),
            vm((1024, 1024), BF), vm((512, 2048), BF), vm((2, 4, 128, 1024), BF), vm((2, 4, 64, 2048), BF),
            vm((2, 1536, 512), BF), vm((2, 1536, 512), BF), vm((2, 1536, 512), BF), vm((1536, 512), BF),
            vm((2, 256, 1024), BF), vm((2, 256, 1024), BF), vm((2, 256, 1024), BF), vm((256, 1024), BF),
            vm((3, 2, 4, 64, 512), BF), vm((2, 4, 32, 1024), BF),
            vm((8, 1024), F32), vm((5, 8, 1024), F32),
            dma((17,)), dma((2,)), dma((7,)), dma((7,)), dma((8,)), dma((8,)), dma((5,)), dma((5,)),
            dma((6, 2, 4)), dma((6, 2, 4)), dma((6, 2, 4)), dma((6, 2, 4)), dma((6, 9)), dma((6, 9)), dma((6,)),
        ],
        compiler_params=pltpu.CompilerParams(
            collective_id=2, has_side_effects=True, vmem_limit_bytes=60 * 1024 * 1024
        ),
        name="back",
    )(lengths, gain, bias, stat, part, pin, mid, x, dy, qkv, mix, rden, state, first, win, wino, wo, woo, mlp, dslab, uslab)


def widen_kernel(
    d_hbm, u_hbm, i_hbm, o_hbm, gin_hbm, out_hbm, small_ref,
    di_o, ui_o, ii_o, oi_o, gin_o, out_o, gain_ref, bias_ref, stats_ref,
    d_v, u_v, i_v, o_v, df_v, uf_v, if_v, of_v, gin_v, out_v, in_sem, out_sem,
):
    jobs = []
    for k in range(6):
        core, i = k // 3, k % 3
        jobs.append((i_hbm, i_v, k * 512, ii_o, if_v, i * 1024 + core * 512, 512))
    for k in range(2):
        jobs.append((o_hbm, o_v, k * 256, oi_o, of_v, k * 256, 256))
    for k in range(8):
        jobs.append((u_hbm, u_v, k * 128, ui_o, uf_v, k * 128, 128))
    for k in range(8):
        jobs.append((d_hbm, d_v, k * 256, di_o, df_v, k * 256, 256))
    loads, stores = [], []
    for n, (src, held, at, _, _, _, rows) in enumerate(jobs):
        loads.append(pltpu.make_async_copy(src.at[pl.ds(at, rows)], held.at[pl.ds(at, rows)], in_sem.at[n]))
        loads[-1].start()
    passed = ((gin_hbm, gin_v, gin_o), (out_hbm, out_v, out_o))
    for n, (src, held, _) in enumerate(passed):
        loads.append(pltpu.make_async_copy(src, held, in_sem.at[len(jobs) + n]))
        loads[-1].start()
    for n, (_, held, at, dst, wide, to, rows) in enumerate(jobs):
        loads[n].wait()

        @pl.loop(0, rows // 128)
        def _(k):
            rows_at = aligned(at + k * 128, 128, 128)
            wide[rows_at, :] = held[rows_at, :].astype(F32)

        stores.append(pltpu.make_async_copy(wide.at[pl.ds(at, rows)], dst.at[pl.ds(to, rows)], out_sem.at[n]))
        stores[-1].start()
    for n, (_, held, dst) in enumerate(passed):
        loads[len(jobs) + n].wait()
        stores.append(pltpu.make_async_copy(held, dst, out_sem.at[len(jobs) + n]))
        stores[-1].start()
    gain_ref[...] = small_ref[0:2, :]
    bias_ref[...] = small_ref[2:4, :]
    scaling = 1.0 / (DH * 1024)
    count = jnp.max(small_ref[5:6, :]) * 1024.0
    stats_ref[0] = jnp.max(small_ref[6:7, :]) * scaling
    stats_ref[1] = jnp.sum(small_ref[4:5, :]) / count * scaling
    for copy in stores:
        copy.wait()


def widen(resd, resu, resi, reso, gin, out, small):
    vm = pltpu.VMEM
    vmem = pl.BlockSpec(memory_space=pltpu.VMEM)
    shapes = [
        ((2048, 1024), F32), ((1024, 2048), F32), ((3072, 512), F32), ((512, 1024), F32),
        ((512, 1024), F32), ((512, 1024), BF), ((2, 1024), F32), ((2, 1024), F32), ((2,), F32),
    ]
    return pl.pallas_call(
        widen_kernel,
        out_shape=[jax.ShapeDtypeStruct(s, d) for s, d in shapes],
        in_specs=any_spec(6) + [vmem],
        out_specs=any_spec(6) + [vmem, vmem, pl.BlockSpec(memory_space=pltpu.SMEM)],
        scratch_shapes=[vm(s, BF) for s, _ in shapes[:4]] + [vm(s, F32) for s, _ in shapes[:4]]
        + [vm((512, 1024), F32), vm((512, 1024), BF)]
        + [pltpu.SemaphoreType.DMA((26,)), pltpu.SemaphoreType.DMA((26,))],
        compiler_params=pltpu.CompilerParams(vmem_limit_bytes=60 * 1024 * 1024),
        name="widen",
    )(resd, resu, resi, reso, gin, out, small)


def fast_device(
    block_in, lengths, input_weight, output_weight, up_weight, down_weight, norm_gain, norm_bias, cotangent
):
    x, dy = block_in[0], cotangent[0]
    win = input_weight.reshape(3072, 512)
    first, qkv, mix, rden, state, mid, sec, wino, woo, dyo, hg, stat = front(
        lengths, x, dy, win, output_weight, down_weight, norm_gain, norm_bias
    )
    part, pin, mlp, dslab, uslab = middle(sec, dy, dyo, hg, up_weight, down_weight)
    resd, resu, resi, reso, block_out, grad_in, small = back(
        lengths, norm_gain, norm_bias, stat, part, pin, mid, x, dy, qkv, mix, rden, state, first,
        win, wino, output_weight, woo, mlp, dslab, uslab,
    )
    down_grad, up_grad, in_grad, out_grad, grad_in, block_out, gain, bias, stats = widen(
        resd, resu, resi, reso, grad_in, block_out, small
    )
    return (
        block_out[None], grad_in[None], in_grad.reshape(3, 1024, 512), out_grad, up_grad, down_grad,
        gain, bias, stats,
    )


def fits_fast(mesh, block_shape):
    return dict(mesh.shape) == {"dp": 16, "mp": 2} and tuple(block_shape) == (16, 1024, 1024)


def solution(mesh):
    in_specs = (
        P("dp", "mp", None),
        P("dp"),
        P(None, None, "mp"),
        P("mp", None),
        P(None, "mp"),
        P("mp", None),
        P(),
        P(),
        P("dp", "mp", None),
    )
    out_specs = (
        P("dp", "mp", None),
        P("dp", "mp", None),
        P(None, None, "mp"),
        P("mp", None),
        P(None, "mp"),
        P("mp", None),
        P(),
        P(),
        P(),
    )

    def whole(*arrays):
        body = fast_device if fits_fast(mesh, arrays[0].shape) else per_device
        return jax.shard_map(
            body, mesh=mesh, in_specs=in_specs, out_specs=out_specs, check_vma=False
        )(*arrays)

    return whole
```

```python
from functools import partial

import jax
import jax.numpy as jnp
from jax import lax
from jax.experimental import pallas as pl
from jax.experimental.pallas import tpu as pltpu
from jax.sharding import PartitionSpec as P

DH = 64
BLK = 512


EPSILON = 1e-05
PRECISE = lax.Precision.HIGHEST


def combined_all(part, axis, combine):
    gathered = jax.tree.map(lambda a: lax.all_gather(a, axis), part)

    def take(source):
        return jax.tree.map(lambda a: lax.dynamic_index_in_dim(a, source, 0, False), gathered)

    return lax.fori_loop(
        1, lax.axis_size(axis), lambda source, state: combine(state, take(source)), take(0)
    )


def feature(values):
    return jax.nn.elu(values) + 1.0


def feature_slope(values):
    return jnp.where(values > 0, 1.0, jnp.exp(values))


def normalise(inputs, gain_row, bias_row):
    centre = jnp.mean(inputs, axis=-1, keepdims=True)
    centred = inputs - centre
    spread = jnp.mean(centred * centred, axis=-1, keepdims=True)
    inverse = lax.rsqrt(spread + EPSILON)
    unit_rows = centred * inverse
    return (unit_rows * gain_row + bias_row, unit_rows, inverse)


def normalise_back(grad_rows, unit_rows, inverse, gain_row):
    scaled = grad_rows * gain_row
    centre = jnp.mean(scaled, axis=-1, keepdims=True)
    along = jnp.mean(scaled * unit_rows, axis=-1, keepdims=True)
    input_grad = inverse * (scaled - centre - unit_rows * along)
    return (input_grad, jnp.sum(grad_rows * unit_rows, axis=0), jnp.sum(grad_rows, axis=0))


def exclusive(stacked):
    running = jnp.cumsum(stacked, axis=0)
    return jnp.concatenate([jnp.zeros_like(running[:1]), running[:-1]], axis=0)


def later(stacked):
    return exclusive(stacked[::-1])[::-1]


def unchanged(carried):
    return carried


def causal_mask():
    return jnp.tril(jnp.ones((BLK, BLK), jnp.float32))


def attend_forward(query_map, key_map, values, crop_len):
    slot_len, head_count, depth = query_map.shape
    block_count = slot_len // BLK
    block_shape = (block_count, BLK, head_count, depth)
    block_q = query_map.reshape(block_shape)
    block_k = key_map.reshape(block_shape)
    block_v = values.reshape(block_shape)
    memory = exclusive(
        jnp.einsum("nihd,nihe->nhde", block_k, block_v, preferred_element_type=jnp.float32)
    )
    key_total = exclusive(jnp.sum(block_k.astype(jnp.float32), axis=1))
    causal = causal_mask()
    block_starts = jnp.arange(block_count, dtype=jnp.int32) * BLK

    def one_block(block_item):
        query_b, key_b, value_b, memory_b, total_b, start_b = block_item
        query_f = query_b.astype(jnp.float32)
        numerator = jnp.einsum("ihd,hde->ihe", query_f, memory_b, precision=PRECISE)
        denominator = jnp.einsum("ihd,hd->ih", query_f, total_b, precision=PRECISE)

        def inside(partial_sums):
            value_part, weight_part = partial_sums
            scores = (
                jnp.einsum("ihd,jhd->hij", query_b, key_b, preferred_element_type=jnp.float32)
                * causal
            )
            value_part = value_part + jnp.einsum(
                "hij,jhd->ihd",
                scores.astype(jnp.bfloat16),
                value_b,
                preferred_element_type=jnp.float32,
            )
            weight_part = weight_part + jnp.sum(scores, axis=-1).T
            return (value_part, weight_part)

        numerator, denominator = lax.cond(
            start_b < crop_len, inside, unchanged, (numerator, denominator)
        )
        return (numerator / denominator[..., None], denominator)

    attended, denoms = lax.map(
        one_block, (block_q, block_k, block_v, memory, key_total, block_starts)
    )
    return (
        attended.reshape(slot_len, head_count, depth),
        denoms.reshape(slot_len, head_count),
        memory,
        key_total,
    )


def attend_backward(
    grad_attn, attended, denoms, query_map, key_map, values, memory, key_total, crop_len
):
    slot_len, head_count, depth = query_map.shape
    block_count = slot_len // BLK
    block_shape = (block_count, BLK, head_count, depth)
    top_all = (grad_attn / denoms[..., None]).reshape(block_shape)
    bottom_all = (-jnp.sum(grad_attn * attended, axis=-1) / denoms).reshape(
        block_count, BLK, head_count
    )
    query_full = query_map.astype(jnp.float32).reshape(block_shape)
    memory_later = later(jnp.einsum("nihd,nihe->nhde", query_full, top_all, precision=PRECISE))
    total_later = later(jnp.einsum("nihd,nih->nhd", query_full, bottom_all, precision=PRECISE))
    causal = causal_mask()
    block_starts = jnp.arange(block_count, dtype=jnp.int32) * BLK

    def one_block(block_item):
        (
            query_b,
            key_b,
            value_b,
            memory_b,
            total_b,
            later_memory,
            later_total,
            top_grad,
            bottom_grad,
            start_b,
        ) = block_item
        value_f = value_b.astype(jnp.float32)
        key_f = key_b.astype(jnp.float32)
        query_sum = (
            jnp.einsum("ihe,hde->ihd", top_grad, memory_b, precision=PRECISE)
            + bottom_grad[..., None] * total_b[None]
        )
        key_sum = (
            jnp.einsum("jhe,hde->jhd", value_f, later_memory, precision=PRECISE) + later_total[None]
        )
        value_sum = jnp.einsum("jhd,hde->jhe", key_f, later_memory, precision=PRECISE)

        def inside(partial_grads):
            query_acc, key_acc, value_acc = partial_grads
            scores = (
                jnp.einsum("ihd,jhd->hij", query_b, key_b, preferred_element_type=jnp.float32)
                * causal
            )
            score_grad = (
                (
                    jnp.einsum("ihe,jhe->hij", top_grad, value_f, precision=PRECISE)
                    + bottom_grad.T[:, :, None]
                )
                * causal
            ).astype(jnp.bfloat16)
            query_acc = query_acc + jnp.einsum(
                "hij,jhd->ihd", score_grad, key_b, preferred_element_type=jnp.float32
            )
            key_acc = key_acc + jnp.einsum(
                "hij,ihd->jhd", score_grad, query_b, preferred_element_type=jnp.float32
            )
            rounded_scores = scores.astype(jnp.bfloat16).astype(jnp.float32)
            value_acc = value_acc + jnp.einsum(
                "hij,ihe->jhe", rounded_scores, top_grad, precision=PRECISE
            )
            return (query_acc, key_acc, value_acc)

        return lax.cond(start_b < crop_len, inside, unchanged, (query_sum, key_sum, value_sum))

    query_grad, key_grad, value_grad = lax.map(
        one_block,
        (
            query_map.reshape(block_shape),
            key_map.reshape(block_shape),
            values.reshape(block_shape),
            memory,
            key_total,
            memory_later,
            total_later,
            top_all,
            bottom_all,
            block_starts,
        ),
    )
    return (
        query_grad.reshape(slot_len, head_count, depth),
        key_grad.reshape(slot_len, head_count, depth),
        value_grad.reshape(slot_len, head_count, depth),
    )


def combine_stats(first_part, second_part):
    return (
        first_part[0] + second_part[0],
        first_part[1] + second_part[1],
        first_part[2] + second_part[2],
        first_part[3] + second_part[3],
        jnp.maximum(first_part[4], second_part[4]),
    )


def per_device(
    block_in,
    lengths,
    input_weight,
    output_weight,
    up_weight,
    down_weight,
    norm_gain,
    norm_bias,
    cotangent,
):
    group_count = lax.axis_size("mp")
    rows_here = block_in.shape[1]
    slot_len = rows_here * group_count
    local_width = output_weight.shape[0]
    head_count = local_width // DH
    crop_len = lengths[0]
    valid_mask = (jnp.arange(slot_len, dtype=jnp.int32) < crop_len).astype(jnp.float32)
    own_rows = block_in[0].astype(jnp.float32)
    first_norm, unit_one, inverse_one = normalise(own_rows, norm_gain[0], norm_bias[0])
    first_rows = lax.all_gather(first_norm.astype(jnp.bfloat16), "mp", axis=0, tiled=True)
    projected = jnp.einsum(
        "rd,cdk->rck", first_rows, input_weight, preferred_element_type=jnp.float32
    ).reshape(slot_len, 3, head_count, DH)
    query = projected[:, 0]
    key_raw = projected[:, 1]
    query_map = feature(query).astype(jnp.bfloat16)
    key_map = (feature(key_raw) * valid_mask[:, None, None]).astype(jnp.bfloat16)
    values = projected[:, 2].astype(jnp.bfloat16)
    attended, denoms, memory, key_total = attend_forward(query_map, key_map, values, crop_len)
    mixed = attended.reshape(slot_len, local_width).astype(jnp.bfloat16)
    part_rows = mixed
    branch_out = lax.psum_scatter(
        jnp.dot(part_rows, output_weight, preferred_element_type=jnp.float32).astype(jnp.bfloat16),
        "mp",
        scatter_dimension=0,
        tiled=True,
    ).astype(jnp.float32)
    middle = own_rows + branch_out
    second_norm, unit_two, inverse_two = normalise(middle, norm_gain[1], norm_bias[1])
    second_rows = lax.all_gather(second_norm.astype(jnp.bfloat16), "mp", axis=0, tiled=True)
    hidden_in = jnp.dot(second_rows, up_weight, preferred_element_type=jnp.float32)
    hidden = jax.nn.gelu(hidden_in, approximate=True).astype(jnp.bfloat16)
    part_rows = hidden
    mlp_out = lax.psum_scatter(
        jnp.dot(part_rows, down_weight, preferred_element_type=jnp.float32).astype(jnp.bfloat16),
        "mp",
        scatter_dimension=0,
        tiled=True,
    ).astype(jnp.float32)
    block_out = (middle + mlp_out).astype(jnp.bfloat16)[None]
    grad_out = cotangent[0]
    grad_rows = lax.all_gather(grad_out, "mp", axis=0, tiled=True)
    down_grad = jnp.einsum("rf,rd->fd", hidden, grad_rows, preferred_element_type=jnp.float32)
    hidden_grad = jnp.einsum(
        "rd,fd->rf", grad_rows, down_weight, preferred_element_type=jnp.float32
    )
    unused_out, gelu_back = jax.vjp(partial(jax.nn.gelu, approximate=True), hidden_in)
    inner_grad = gelu_back(hidden_grad)[0].astype(jnp.bfloat16)
    up_grad = jnp.einsum("rd,rf->df", second_rows, inner_grad, preferred_element_type=jnp.float32)
    part_rows = inner_grad
    second_grad = lax.psum_scatter(
        jnp.einsum("rf,df->rd", part_rows, up_weight, preferred_element_type=jnp.float32).astype(
            jnp.bfloat16
        ),
        "mp",
        scatter_dimension=0,
        tiled=True,
    ).astype(jnp.float32)
    back_two, gain_two, bias_two = normalise_back(second_grad, unit_two, inverse_two, norm_gain[1])
    middle_grad = grad_out.astype(jnp.float32) + back_two
    middle_low = middle_grad.astype(jnp.bfloat16)
    middle_full = lax.all_gather(middle_low, "mp", axis=0, tiled=True)
    mixed_grad = jnp.einsum(
        "rd,kd->rk", middle_full, output_weight, preferred_element_type=jnp.float32
    ).astype(jnp.bfloat16)
    output_grad = jnp.einsum("rk,rd->kd", mixed, middle_full, preferred_element_type=jnp.float32)
    grad_attn = mixed_grad.astype(jnp.float32).reshape(slot_len, head_count, DH)
    query_grad, key_grad, value_grad = attend_backward(
        grad_attn, attended, denoms, query_map, key_map, values, memory, key_total, crop_len
    )
    query_low = (query_grad * feature_slope(query)).astype(jnp.bfloat16)
    key_low = (key_grad * valid_mask[:, None, None] * feature_slope(key_raw)).astype(jnp.bfloat16)
    value_low = value_grad.astype(jnp.bfloat16)
    qkv_grad = jnp.stack([query_low, key_low, value_low], axis=1).reshape(slot_len, 3, local_width)
    input_grad = jnp.einsum("rd,rck->cdk", first_rows, qkv_grad, preferred_element_type=jnp.float32)
    part_rows = qkv_grad
    first_grad = lax.psum_scatter(
        jnp.einsum(
            "rck,cdk->rd", part_rows, input_weight, preferred_element_type=jnp.float32
        ).astype(jnp.bfloat16),
        "mp",
        scatter_dimension=0,
        tiled=True,
    ).astype(jnp.float32)
    back_one, gain_one, bias_one = normalise_back(first_grad, unit_one, inverse_one, norm_gain[0])
    grad_input = (middle_grad + back_one)[None]
    input_grad, output_grad, up_grad, down_grad = (
        lax.psum(input_grad.astype(jnp.bfloat16), "dp").astype(jnp.float32),
        lax.psum(output_grad.astype(jnp.bfloat16), "dp").astype(jnp.float32),
        lax.psum(up_grad.astype(jnp.bfloat16), "dp").astype(jnp.float32),
        lax.psum(down_grad.astype(jnp.bfloat16), "dp").astype(jnp.float32),
    )
    kept_denoms = jnp.where(valid_mask[:, None] > 0, denoms, 0.0)
    den_total = jnp.sum(kept_denoms)
    den_count = crop_len.astype(jnp.float32) * head_count
    den_peak = jnp.max(kept_denoms)
    gain_grad, bias_grad, den_total, den_count, den_peak = combined_all(
        (
            jnp.stack([gain_one, gain_two]),
            jnp.stack([bias_one, bias_two]),
            den_total,
            den_count,
            den_peak,
        ),
        ("dp", "mp"),
        combine_stats,
    )
    scaling = DH * slot_len
    denominator_stats = jnp.stack([den_peak / scaling, den_total / den_count / scaling])
    return (
        block_out,
        grad_input,
        input_grad,
        output_grad,
        up_grad,
        down_grad,
        gain_grad,
        bias_grad,
        denominator_stats,
    )

MESH = pl.DeviceIdType.MESH
BF = jnp.bfloat16
F32 = jnp.float32
ROWS = 512
CH = 256
PAIR = 128


def dot_nn(a, b):
    return lax.dot_general(a, b, (((1,), (0,)), ((), ())), preferred_element_type=F32)


def dot_nt(a, b):
    return lax.dot_general(a, b, (((1,), (1,)), ((), ())), preferred_element_type=F32)


def dot_tn(a, b):
    return lax.dot_general(a, b, (((0,), (0,)), ((), ())), preferred_element_type=F32)


class Place:
    def __init__(self):
        dp = lax.axis_index("dp")
        mp = lax.axis_index("mp")
        self.dp, self.mp = dp, mp
        self.core = lax.rem(dp, 2)
        chip = dp // 2
        y = lax.rem(chip, 2)
        z = chip // 2
        self.r = z + y * (7 - 2 * z)
        self.across = (dp, 1 - mp)
        self.mate = (dp + 1 - 2 * self.core, mp)
        self.next = self.at(lax.rem(self.r + 1, 8))
        self.prev = self.at(lax.rem(self.r + 7, 8))

    def at(self, r):
        y = r // 4
        z = r + y * (7 - 2 * r)
        return ((z * 2 + y) * 2 + self.core, self.mp)

    def partners(self):
        return [self.across, self.mate, self.next, self.prev]


def greet(partners):
    barrier = pltpu.get_barrier_semaphore()
    for partner in partners:
        pl.semaphore_signal(barrier, inc=1, device_id=partner, device_id_type=MESH)
    pl.semaphore_wait(barrier, len(partners))


def remote(src, dst, send_sem, recv_sem, device):
    return pltpu.make_async_remote_copy(
        src_ref=src, dst_ref=dst, send_sem=send_sem, recv_sem=recv_sem,
        device_id=device, device_id_type=MESH,
    )


def aligned(start, size, unit):
    return pl.ds(pl.multiple_of(start, unit), size)


def lane_head(shape):
    return lax.broadcasted_iota(jnp.int32, shape, len(shape) - 1) < DH


def same_head():
    row = lax.broadcasted_iota(jnp.int32, (PAIR, PAIR), 0) < DH
    lane = lax.broadcasted_iota(jnp.int32, (PAIR, PAIR), 1) < DH
    return row == lane


def causal_tile():
    row = lax.broadcasted_iota(jnp.int32, (CH, CH), 0)
    col = lax.broadcasted_iota(jnp.int32, (CH, CH), 1)
    return row >= col


def unpack_state(packed):
    keep = same_head()
    zero = jnp.zeros_like(packed)
    return jnp.concatenate(
        [jnp.where(keep, packed, zero), jnp.where(keep, pltpu.roll(packed, DH, 1), zero)], axis=1
    )


def split_heads(pair):
    first = lane_head(pair.shape)
    zero = jnp.zeros_like(pair)
    return jnp.where(first, pair, zero), jnp.where(first, zero, pair)


def row_norm(rows):
    centre = jnp.mean(rows, axis=-1, keepdims=True)
    centred = rows - centre
    inverse = lax.rsqrt(jnp.mean(centred * centred, axis=-1, keepdims=True) + EPSILON)
    return centred * inverse, inverse


def front_kernel(
    len_ref, x_hbm, dy_hbm, win_hbm, wo_hbm, wdn_hbm, gain_ref, bias_ref,
    first_o, qkv_o, mix_o, rden_o, state_o, mid_o, sec_o, wino_o, woo_o, dyo_o, hg_o, stat_ref,
    x_v, dy_v, win_v, wino_v, wo_v, woo_v, wdn_v, first_v, qkv_v, num_v, den_v, mix_v, mid_v, sec_v, hg_v,
    local_v, ssend_v, srecv_v, state_v,
    in_sem, out_sem, xs_sem, xr_sem, ring_s, ring_r, mate_s, mate_r,
):
    here = Place()
    loads = [
        (x_hbm, x_v), (win_hbm, win_v), (dy_hbm, dy_v), (wdn_hbm, wdn_v), (wo_hbm, wo_v),
    ]
    loads = [pltpu.make_async_copy(a, b, in_sem.at[i]) for i, (a, b) in enumerate(loads)]
    for load in loads:
        load.start()
    greet(here.partners())
    parts = ((win_hbm, wino_v, 192), (wo_hbm, woo_v, 32))

    def rows_of(array, offset, core):
        rows = parts[array][2]
        return aligned((lax.rem(here.r + 8 + offset, 8) * 2 + core) * rows, rows, 32)

    cross = []
    for array, (src, dst, _) in enumerate(parts):
        for k in range(2):
            at = rows_of(array, 4 * k, here.core)
            slot = 2 * array + k
            cross.append(remote(src.at[at], dst.at[at], xs_sem.at[slot], xr_sem.at[slot], here.across))
    for copy in cross:
        copy.start()
    gone = []

    def dy_part(count):
        for _ in range(count):
            k = len(gone)
            rows = pl.ds(k * 64, 64)
            copy = remote(dy_hbm.at[rows], dyo_o.at[rows], xs_sem.at[7 + k], xr_sem.at[7 + k], here.across)
            copy.start()
            gone.append(copy)

    dy_part(2)

    gain = gain_ref[0:1, :]
    bias = bias_ref[0:1, :]
    sends = []
    outs = []

    def out(src, dst):
        copy = pltpu.make_async_copy(src, dst, out_sem.at[len(outs)])
        copy.start()
        outs.append(copy)

    FAR = ((-1, 3, -2), (1, 5, 2))

    def to_mate(array, slot, offset):
        at = rows_of(array, offset, here.core)
        dst = parts[array][1]
        copy = remote(dst.at[at], dst.at[at], mate_s.at[array, slot], mate_r.at[array, slot], here.mate)
        copy.start()
        sends.append(copy)

    def to_ring(array, way, k, offset):
        at = rows_of(array, offset, here.core)
        dst = parts[array][1]
        copy = remote(
            dst.at[at], dst.at[at], ring_s.at[array, way, k], ring_r.at[array, way, k],
            here.next if way == 0 else here.prev,
        )
        copy.start()
        sends.append(copy)

    def from_across(array):
        for k in range(2):
            cross[2 * array + k].wait_recv()
            for way in (0, 1):
                to_ring(array, way, k, 4 * k)
            to_mate(array, k, 4 * k)

    def from_ring(array, k):
        for way in (0, 1):
            at = rows_of(array, FAR[way][k], here.core)
            dst = parts[array][1].at[at]
            remote(dst, dst, ring_s.at[array, way, k], ring_r.at[array, way, k], here.next).wait_recv()
            if k == 0:
                to_ring(array, way, 2, FAR[way][0])
            to_mate(array, 2 + 2 * k + way, FAR[way][k])

    def mate_wait(array):
        offsets = [0, 4] + [FAR[way][k] for k in range(3) for way in (0, 1)]
        for slot, offset in enumerate(offsets):
            dst = parts[array][1].at[rows_of(array, offset, 1 - here.core)]
            remote(dst, dst, mate_s.at[array, slot], mate_r.at[array, slot], here.mate).wait_recv()

    loads[0].wait()

    @pl.loop(0, ROWS // 128)
    def _(i):
        at = aligned(i * 128, 128, 128)
        unit, _ = row_norm(x_v[at, :].astype(F32))
        first_v[at, :] = (unit * gain + bias).astype(BF)

    out(first_v, first_o)
    crop_len = len_ref[0]

    def project(half, weights, which):
        @pl.loop(0, 2)
        def _(c):
            at = aligned(c * CH, CH, CH)
            rows = first_v[at, :]
            for i in which:
                raw = dot_nn(rows, weights[pl.ds(i * 1024, 1024), :])
                if i < 2:
                    raw = jnp.where(raw > 0, raw + 1.0, jnp.exp(jnp.minimum(raw, 0.0)))
                if i == 1:
                    place = lax.broadcasted_iota(jnp.int32, raw.shape, 0) + (here.mp * ROWS + c * CH)
                    raw = jnp.where(place < crop_len, raw, 0.0)
                qkv_v[half, i, at, :] = raw.astype(BF)

    def states(half):
        keep = same_head()

        @pl.loop(0, 4)
        def _(p):
            lanes = aligned(p * PAIR, PAIR, PAIR)
            total = None
            for c in range(2):
                keys = qkv_v[half, 1, pl.ds(c * CH, CH), lanes]
                vals = qkv_v[half, 2, pl.ds(c * CH, CH), lanes]
                made = dot_tn(keys, jnp.concatenate([vals, jnp.ones_like(vals)], axis=1))
                packed = jnp.where(keep, made[:, :PAIR], made[:, PAIR:])
                if c == 0:
                    local_v[half, p] = packed
                    total = packed
                else:
                    ssend_v[half, p] = (total + packed).astype(BF)

        copy = remote(
            ssend_v.at[half], srecv_v.at[1 - half], xs_sem.at[5 + half], xr_sem.at[6 - half], here.across
        )
        copy.start()
        sends.append(copy)

    def inside(half):
        mask = causal_tile()

        @pl.loop(0, 8)
        def _(n):
            p = n // 2
            c = lax.rem(n, 2)
            lanes = aligned(p * PAIR, PAIR, PAIR)
            at = aligned(c * CH, CH, CH)
            query = qkv_v[half, 0, at, lanes]
            key = qkv_v[half, 1, at, lanes]
            val = qkv_v[half, 2, at, lanes]
            first = lane_head(val.shape)
            one = jnp.ones_like(val)
            zero = jnp.zeros_like(val)
            sums = None
            for head, part in enumerate(split_heads(query)):
                score = jnp.where(mask, dot_nt(part, key), 0.0).astype(BF)
                mine = first if head == 0 else jnp.logical_not(first)
                right = jnp.concatenate([jnp.where(mine, val, zero), jnp.where(mine, one, zero)], axis=1)
                term = dot_nn(score, right)
                sums = term if sums is None else sums + term
            num_v[at, lanes] = sums[:, :PAIR]
            den_v[half, at, lanes] = sums[:, PAIR:]

    def finish(half):
        flag = here.mp.astype(F32)

        @pl.loop(0, 8)
        def _(n):
            p = n // 2
            c = lax.rem(n, 2)
            lanes = aligned(p * PAIR, PAIR, PAIR)
            at = aligned(c * CH, CH, CH)
            query = qkv_v[half, 0, at, lanes]
            before = srecv_v[half, p].astype(F32) * flag
            state_v[half, p] = before.astype(BF)
            before = before + local_v[half, p] * c.astype(F32)
            term = dot_nn(query, unpack_state(before).astype(BF))
            num = num_v[at, lanes] + term[:, :PAIR]
            den = den_v[half, at, lanes] + term[:, PAIR:]
            inverse = 1.0 / den
            den_v[half, at, lanes] = inverse
            mix_v[half, at, lanes] = (num * inverse).astype(BF)
            place = lax.broadcasted_iota(jnp.int32, den.shape, 0) + (here.mp * ROWS + c * CH)
            kept = jnp.where(place < crop_len, den, 0.0).reshape(CH // 8, 8, PAIR)
            stat_ref[0] = jnp.maximum(stat_ref[0], jnp.max(kept, axis=0))
            stat_ref[1] = stat_ref[1] + jnp.sum(kept, axis=0)

    def hidden_grad():
        @pl.loop(0, 2)
        def _(j):
            cols = aligned(j * 1024, 1024, 1024)
            hg_v[:, cols] = dot_nt(dy_v[...], wdn_v[cols, :]).astype(BF)

    stat_ref[...] = jnp.zeros_like(stat_ref)
    loads[1].wait()
    project(0, win_v, (1, 2))
    states(0)
    dy_part(1)
    project(0, win_v, (0,))
    from_across(0)
    dy_part(1)
    inside(0)
    from_ring(0, 0)
    from_across(1)
    dy_part(2)
    loads[2].wait()
    loads[3].wait()
    hidden_grad()
    from_ring(0, 1)
    from_ring(1, 0)
    from_ring(0, 2)
    mate_wait(0)
    from_ring(1, 1)
    out(wino_v, wino_o)
    mid_v[:, pl.ds(0, 512)] = num_v[...]
    project(1, wino_v, (1, 2))
    states(1)
    dy_part(2)
    project(1, wino_v, (0,))
    from_ring(1, 2)
    inside(1)
    remote(ssend_v.at[0], srecv_v.at[1], xs_sem.at[5], xr_sem.at[6], here.across).wait_recv()
    finish(1)
    out(hg_v, hg_o)
    num_v[...] = mid_v[:, pl.ds(0, 512)]
    mate_wait(1)
    remote(ssend_v.at[1], srecv_v.at[0], xs_sem.at[6], xr_sem.at[5], here.across).wait_recv()
    finish(0)
    out(qkv_v, qkv_o)
    out(den_v, rden_o)
    out(mix_v, mix_o)
    out(state_v, state_o)
    out(woo_v, woo_o)
    loads[4].wait()
    gain_two = gain_ref[1:2, :]
    bias_two = bias_ref[1:2, :]

    @pl.loop(0, 2)
    def _(c):
        at = aligned(c * CH, CH, CH)
        own = dot_nn(mix_v[0, at, :], wo_v[...]).astype(BF).astype(F32)
        other = dot_nn(mix_v[1, at, :], woo_v[...]).astype(BF).astype(F32)
        middle = x_v[at, :].astype(F32) + (own + other)
        mid_v[at, :] = middle
        unit, _ = row_norm(middle)
        sec_v[at, :] = (unit * gain_two + bias_two).astype(BF)

    out(mid_v, mid_o)
    out(sec_v, sec_o)
    for copy in gone:
        copy.wait_recv()
    for copy in cross + gone + sends:
        copy.wait_send()
    for copy in outs:
        copy.wait()


def any_spec(count):
    return [pl.BlockSpec(memory_space=pl.ANY)] * count


def front(lengths, x_rows, dy_rows, win, wo, wdn, gain, bias):
    vm = pltpu.VMEM
    shapes = [
        ((512, 1024), BF), ((2, 3, 512, 512), BF), ((2, 512, 512), BF), ((2, 512, 512), F32),
        ((2, 4, PAIR, PAIR), BF), ((512, 1024), F32), ((512, 1024), BF), ((3072, 512), BF),
        ((512, 1024), BF), ((512, 1024), BF), ((512, 2048), BF), ((2, 8, PAIR), F32),
    ]
    dma = pltpu.SemaphoreType.DMA
    return pl.pallas_call(
        front_kernel,
        out_shape=[jax.ShapeDtypeStruct(s, d) for s, d in shapes],
        in_specs=[pl.BlockSpec(memory_space=pltpu.SMEM)] + any_spec(5)
        + [pl.BlockSpec(memory_space=pltpu.VMEM)] * 2,
        out_specs=any_spec(11) + [pl.BlockSpec(memory_space=pltpu.VMEM)],
        scratch_shapes=[
            vm((512, 1024), BF), vm((512, 1024), BF), vm((3072, 512), BF), vm((3072, 512), BF),
            vm((512, 1024), BF), vm((512, 1024), BF), vm((2048, 1024), BF), vm((512, 1024), BF),
            vm((2, 3, 512, 512), BF), vm((512, 512), F32), vm((2, 512, 512), F32), vm((2, 512, 512), BF),
            vm((512, 1024), F32), vm((512, 1024), BF), vm((512, 2048), BF),
            vm((2, 4, PAIR, PAIR), F32), vm((2, 4, PAIR, PAIR), BF), vm((2, 4, PAIR, PAIR), BF),
            vm((2, 4, PAIR, PAIR), BF),
            dma((5,)), dma((12,)), dma((15,)), dma((15,)), dma((2, 2, 3)), dma((2, 2, 3)),
            dma((2, 8)), dma((2, 8)),
        ],
        compiler_params=pltpu.CompilerParams(
            collective_id=0, has_side_effects=True, vmem_limit_bytes=58 * 1024 * 1024
        ),
        name="front",
    )(lengths, x_rows, dy_rows, win, wo, wdn, gain, bias)


GELU_A = 0.7978845608028654
GELU_B = 0.044715


def gelu_pair(v):
    square = v * v
    t = jnp.tanh(GELU_A * v * (1.0 + GELU_B * square))
    half = 0.5 * (1.0 + t)
    slope = half + (0.5 * GELU_A) * v * (1.0 - t * t) * (1.0 + (3.0 * GELU_B) * square)
    return v * half, slope


def middle_kernel(
    sec_hbm, dy_hbm, dyo_hbm, hg_hbm, wup_hbm, wdn_hbm,
    part_o, pin_o, mlp_o, dslab_o, uslab_o, dring_o,
    sec_v, dy_v, hg_v, wup_v, wdn_v, hid_v, part_v, send_v, pin_v, mlp_v,
    dsend_v, drecv_v, dslab_v, usend_v, urecv_v, uslab_v, dring_v,
    in_sem, out_sem, xs_sem, xr_sem, ms_sem, mr_sem, rs_s, rs_r,
):
    here = Place()
    own = pl.ds(0, ROWS)
    other = pl.ds(ROWS, ROWS)
    loads = [
        (sec_hbm, sec_v.at[own]), (wup_hbm, wup_v), (hg_hbm, hg_v.at[own]), (wdn_hbm, wdn_v),
        (dy_hbm, dy_v.at[own]), (dyo_hbm, dy_v.at[other]),
    ]
    loads = [pltpu.make_async_copy(a, b, in_sem.at[i]) for i, (a, b) in enumerate(loads)]
    for load in loads:
        load.start()
    greet(here.partners())
    ring_d = Arc(here, dslab_v, 0, 128, dring_v, None, None, (rs_s, rs_r, None, None, None, None, None))
    sends = []
    outs = []

    def out(src, dst):
        copy = pltpu.make_async_copy(src, dst, out_sem.at[len(outs)])
        copy.start()
        outs.append(copy)

    def across(src, dst, slot):
        copy = remote(src, dst, xs_sem.at[slot], xr_sem.at[slot], here.across)
        copy.start()
        sends.append(copy)
        return copy

    ahead = [
        across(sec_hbm.at[pl.ds(c * CH, CH)], sec_v.at[pl.ds(ROWS + c * CH, CH)], c) for c in range(2)
    ]

    def up(chunk):
        rows = pl.ds(chunk * CH, CH)

        @pl.loop(0, 4)
        def _(j):
            cols = aligned(j * 512, 512, 512)
            raw = dot_nn(sec_v[rows, :], wup_v[:, cols])
            value, slope = gelu_pair(raw)
            hid_v[rows, cols] = value.astype(BF)
            hg_v[rows, cols] = (hg_v[rows, cols].astype(F32) * slope).astype(BF)

    def back(chunk, dst):
        dst[...] = dot_nt(hg_v[pl.ds(chunk * CH, CH), :], wup_v[...]).astype(BF)

    loads[0].wait()
    loads[1].wait()
    loads[2].wait()
    for c in range(2):
        up(c)
        back(c, part_v.at[pl.ds(c * CH, CH)])
    out(part_v, part_o)
    for load in loads[3:]:
        load.wait()
    for c in range(2):
        @pl.loop(0, 2)
        def _(j):
            cols = aligned(j * 1024, 1024, 1024)
            rows = pl.ds(ROWS + c * CH, CH)
            hg_v[rows, cols] = dot_nt(dy_v[rows, :], wdn_v[cols, :]).astype(BF)

        ahead[c].wait_recv()
        up(2 + c)
        rows = pl.ds(c * CH, CH)
        back(2 + c, send_v.at[rows])
        across(send_v.at[rows], pin_v.at[rows], 2 + c)
    their = 1 - here.core

    def down_grad(half, dst, plus):
        @pl.loop(0, 2)
        def _(i):
            cols = aligned(half * 1024 + i * 512, 512, 512)
            at = aligned(i * 512, 512, 512)
            made = dot_tn(hid_v[:, cols], dy_v[...])
            if plus is not None:
                made = made + plus[at, :].astype(F32)
            dst[at, :] = made.astype(BF)

    def up_grad(half, dst, plus):
        @pl.loop(0, 2)
        def _(i):
            cols = aligned(half * 512, 512, 512)
            at = aligned(i * 1024, 1024, 1024)
            made = dot_tn(sec_v[:, cols], hg_v[:, at])
            if plus is not None:
                made = made + plus[:, at].astype(F32)
            dst[:, at] = made.astype(BF)

    def to_mate(src, dst, slot):
        copy = remote(src, dst, ms_sem.at[slot], mr_sem.at[slot], here.mate)
        copy.start()
        sends.append(copy)
        return copy

    down_grad(their, dsend_v, None)
    to_d = to_mate(dsend_v, drecv_v, 0)
    down_grad(here.core, dslab_v, None)
    to_d.wait_recv()

    @pl.loop(0, 8)
    def _(i):
        at = aligned(i * 128, 128, 128)
        dslab_v[at, :] = (dslab_v[at, :].astype(F32) + drecv_v[at, :].astype(F32)).astype(BF)

    for way in (0, 1):
        ring_d.gather_step(way, 0)
    out(dslab_v, dslab_o)
    up_grad(their, usend_v, None)
    to_u = to_mate(usend_v, urecv_v, 1)

    def mlp_rows(i):
        rows = pl.ds(i * ROWS, ROWS)
        mlp_v[rows, :] = dot_nn(hid_v[rows, :], wdn_v[...]).astype(BF)

    mlp_rows(0)
    for way in (0, 1):
        ring_d.gather_step(way, 1)
    mlp_rows(1)
    out(mlp_v, mlp_o)
    to_u.wait_recv()
    up_grad(here.core, uslab_v, urecv_v)
    out(uslab_v, uslab_o)
    for c in range(2):
        rows = pl.ds(c * CH, CH)
        remote(send_v.at[rows], pin_v.at[rows], xs_sem.at[2 + c], xr_sem.at[2 + c], here.across).wait_recv()
    out(pin_v, pin_o)
    for way in (0, 1):
        ring_d.arrived(way, 1)
        out(dring_v.at[way, 1], dring_o.at[way])
    for copy in sends + ring_d.pending:
        copy.wait_send()
    for copy in outs:
        copy.wait()


def middle(sec, dy, dyo, hg, wup, wdn):
    vm = pltpu.VMEM
    dma = pltpu.SemaphoreType.DMA
    shapes = [
        ((512, 1024), BF), ((512, 1024), BF), ((1024, 1024), BF), ((1024, 1024), BF), ((512, 2048), BF),
        ((2, 128, 1024), BF),
    ]
    return pl.pallas_call(
        middle_kernel,
        out_shape=[jax.ShapeDtypeStruct(s, d) for s, d in shapes],
        in_specs=any_spec(6),
        out_specs=any_spec(6),
        scratch_shapes=[
            vm((1024, 1024), BF), vm((1024, 1024), BF), vm((1024, 2048), BF), vm((1024, 2048), BF),
            vm((2048, 1024), BF), vm((1024, 2048), BF), vm((512, 1024), BF), vm((512, 1024), BF),
            vm((512, 1024), BF), vm((1024, 1024), BF),
            vm((1024, 1024), BF), vm((1024, 1024), BF), vm((1024, 1024), BF),
            vm((512, 2048), BF), vm((512, 2048), BF), vm((512, 2048), BF), vm((2, 2, 128, 1024), BF),
            dma((6,)), dma((7,)), dma((4,)), dma((4,)), dma((2,)), dma((2,)), dma((2, 2)), dma((2, 2)),
        ],
        compiler_params=pltpu.CompilerParams(
            collective_id=1, has_side_effects=True, vmem_limit_bytes=58 * 1024 * 1024
        ),
        name="middle",
    )(sec, dy, dyo, hg, wup, wdn)


PACE = 36


class Arc:
    def __init__(self, here, slab, base, rows, recv, result, result_base, sems, source=None, begun=0):
        self.here, self.slab, self.base, self.rows = here, slab, base, rows
        self.source = slab if source is None else source
        self.recv, self.result, self.result_base = recv, result, result_base
        self.rs_s, self.rs_r, self.ag_s, self.ag_r, self.mt_s, self.mt_r, self.local = sems
        self.pending = []
        self.t = self.begun = begun

    def span(self, base, offset, half):
        start = base + lax.rem(self.here.r + 8 + offset, 8) * self.rows
        if half is None:
            return aligned(start, self.rows, 16)
        return aligned(start + half * (self.rows // 2), self.rows // 2, 16)

    def mine(self, offset, half=None):
        return self.span(self.base, offset, half)

    def place(self, offset, core, half=None):
        return self.result.at[self.span(self.result_base(core) + self.base, offset, half)]

    def send(self, src, dst, send_sem, recv_sem, device):
        copy = remote(src, dst, send_sem, recv_sem, device)
        copy.start()
        self.pending.append(copy)

    def to(self, way):
        return self.here.next if way == 0 else self.here.prev

    def sign(self, way):
        return 1 if way == 0 else -1

    def slot(self, way, s):
        if s > 0:
            return self.recv.at[way, s]
        return self.recv.at[way, 0, pl.ds(way * (self.rows // 2), self.rows // 2)]

    def arrived(self, way, s):
        got = self.slot(way, s)
        remote(got, got, self.rs_s.at[way, s], self.rs_r.at[way, s], self.to(way)).wait_recv()

    def gather_step(self, way, s):
        sign = self.sign(way)
        if s == 0:
            src = self.source.at[self.mine(sign * 4, way)]
        else:
            if s > self.begun or s == 1:
                self.arrived(way, s - 1)
            own = self.slab[self.mine(sign * (4 - s)), :].astype(F32)
            src = self.recv.at[way, s - 1]
            if s == 1:
                half = self.rows // 2
                kept = pl.ds(way * half, half)
                rest = pl.ds((1 - way) * half, half)
                at = slice(way * half, way * half + half)
                src[kept, :] = (src[kept, :].astype(F32) + own[at]).astype(BF)
                at = slice((1 - way) * half, (1 - way) * half + half)
                src[rest, :] = own[at].astype(BF)
            else:
                src[...] = (src[...].astype(F32) + own).astype(BF)
        self.send(src, self.slot(way, s), self.rs_s.at[way, s], self.rs_r.at[way, s], self.to(way))

    def spread(self, src, offset, step, way, half=None):
        dst = self.place(offset, self.here.core, half)
        if step < 4 and not (step == 3 and half is None):
            self.send(src, dst, self.ag_s.at[way, step], self.ag_r.at[way, step], self.to(way))

    def to_mate(self, src, offset, slot, half=None):
        dst = self.place(offset, self.here.core, half)
        self.send(src, dst, self.mt_s.at[slot], self.mt_r.at[slot], self.here.mate)

    def total(self):
        self.arrived(0, 3)
        self.arrived(1, 3)
        sums = self.recv.at[0, 3]
        own = self.slab[self.mine(0), :].astype(F32)
        sums[...] = (sums[...].astype(F32) + self.recv[1, 3].astype(F32) + own).astype(BF)
        for way in (0, 1):
            self.spread(sums, 0, 0, way)
        self.to_mate(sums, 0, 0)
        self.keep = pltpu.make_async_copy(sums, self.place(0, self.here.core), self.local)
        self.keep.start()

    def spread_step(self, way, s):
        sign = self.sign(way)
        half = way if s == 3 else None
        got = self.place(-sign * (s + 1), self.here.core, half)
        remote(got, got, self.ag_s.at[way, s], self.ag_r.at[way, s], self.to(way)).wait_recv()
        if s < 3:
            part = way if s == 2 else None
            src = self.place(-sign * (s + 1), self.here.core, part)
            self.spread(src, -sign * (s + 1), s + 1, way, part)
        self.to_mate(got, -sign * (s + 1), 1 + 2 * s + way, half)

    def tick(self):
        t = self.t
        self.t = t + 1
        if t == 4:
            self.total()
        elif t < 9:
            for way in (0, 1):
                if t < 4:
                    self.gather_step(way, t)
                else:
                    self.spread_step(way, t - 5)

    def finish(self):
        for copy in self.pending:
            copy.wait_send()
        self.keep.wait()
        other = 1 - self.here.core
        for slot in range(9):
            if slot == 0:
                got = self.place(0, other)
            else:
                s, way = (slot - 1) // 2, (slot - 1) % 2
                got = self.place(-self.sign(way) * (s + 1), other, way if s == 3 else None)
            remote(got, got, self.mt_s.at[slot], self.mt_r.at[slot], self.here.mate).wait_recv()


def back_kernel(
    len_ref, gain_ref, bias_ref, stat_ref,
    part_hbm, pin_hbm, mid_hbm, x_hbm, dy_hbm, qkv_hbm, mix_hbm, rden_hbm, state_hbm, first_hbm,
    win_hbm, wino_hbm, wo_hbm, woo_hbm, mlp_hbm, dslab_hbm, uslab_hbm, dring_hbm,
    resd_o, resu_o, resi_o, reso_o, out_o, gin_o, small_ref,
    part_v, pin_v, mid_v, dy_v, qkv_v, mix_v, rden_v, state_v, first_v, win_v, wo_v,
    mlpin_v, mg_v, mgf_v, mixg_v, top_v, bot_v, dqkv_v, local_v, lsend_v, lrecv_v,
    dslab_v, uslab_v, drecv_v, urecv_v, gm_v, gr_v, ga_v, gx_v, om_v, or_v, oa_v, ox_v, irecv_v, orecv_v,
    small_s, small_r,
    in_sem, out_sem, xs_sem, xr_sem, ms_sem, mr_sem, bs_sem, br_sem,
    rs_s, rs_r, ag_s, ag_r, mt_s, mt_r, keep_s,
):
    here = Place()
    loads = [
        (part_hbm, part_v), (pin_hbm, pin_v), (mid_hbm, mid_v), (dy_hbm, dy_v), (dslab_hbm, dslab_v),
        (uslab_hbm, uslab_v), (wo_hbm, wo_v.at[0]), (woo_hbm, wo_v.at[1]), (mix_hbm, mix_v),
        (rden_hbm, rden_v), (qkv_hbm, qkv_v), (state_hbm, state_v), (first_hbm, first_v),
        (win_hbm, win_v.at[0]), (wino_hbm, win_v.at[1]), (x_hbm, part_v), (mlp_hbm.at[pl.ds(0, ROWS)], pin_v),
        (dring_hbm.at[0], drecv_v.at[0, 1]), (dring_hbm.at[1], drecv_v.at[1, 1]),
    ]
    loads = [pltpu.make_async_copy(a, b, in_sem.at[i]) for i, (a, b) in enumerate(loads)]
    begun = [loads[17], loads[18], loads[4]]
    for load in begun + [load for load in loads[:15] if load is not loads[4]]:
        load.start()
    y_mate = (here.dp + 2 - 4 * lax.rem(here.dp // 2, 2), here.mp)
    z_mate = (here.dp + 4 - 8 * lax.rem(here.dp // 4, 2), here.mp)
    z_far = (here.dp + 8 - 16 * (here.dp // 8), here.mp)
    greet(here.partners() + [y_mate, z_mate, z_far])
    sends = []
    outs = []

    def out(src, dst):
        copy = pltpu.make_async_copy(src, dst, out_sem.at[len(outs)])
        copy.start()
        outs.append(copy)

    def across(src, dst, slot):
        copy = remote(src, dst, xs_sem.at[slot], xr_sem.at[slot], here.across)
        copy.start()
        sends.append(copy)
        return copy

    def to_mate(src, dst, slot):
        copy = remote(src, dst, ms_sem.at[slot], mr_sem.at[slot], here.mate)
        copy.start()
        sends.append(copy)
        return copy

    arcs = []

    def add_arc(slab, base, rows, recv, result, result_base, source=None, begun=0):
        n = len(arcs)
        sems = (rs_s.at[n], rs_r.at[n], ag_s.at[n], ag_r.at[n], mt_s.at[n], mt_r.at[n], keep_s.at[n])
        arcs.append(Arc(here, slab, base, rows, recv, result, result_base, sems, source, begun))
        return arcs[-1]

    ring_d = add_arc(dslab_v, 0, 128, drecv_v, resd_o, lambda core: core * 1024, None, 2)
    ring_u = add_arc(uslab_v, 0, 64, urecv_v, resu_o, lambda core: core * 512, uslab_hbm)
    ring_o = add_arc(oa_v.at[0], 0, 32, orecv_v, reso_o, lambda core: core * 256)
    ring_i = [
        add_arc(ga_v.at[0], i * 512, 64, irecv_v.at[i], resi_o, lambda core: core * 1536) for i in range(3)
    ]

    credit = [0]

    def ring(count):
        credit[0] += count * PACE
        while credit[0] >= 100:
            credit[0] -= 100
            first = ring_d if ring_d.t <= ring_u.t else ring_u
            first.tick()

    def ring_on(arc):
        arc.tick()

    ring_u.tick()
    for load in begun:
        load.wait()
    ring_d.tick()

    small_s[...] = jnp.zeros_like(small_s)
    for load in loads[0:4] + loads[5:6]:
        load.wait()
    gain_two = gain_ref[1:2, :]

    @pl.loop(0, ROWS // 128)
    def _(i):
        at = aligned(i * 128, 128, 128)
        grad = part_v[at, :].astype(F32) + pin_v[at, :].astype(F32)
        unit, inverse = row_norm(mid_v[at, :])
        scaled = grad * gain_two
        centre = jnp.mean(scaled, axis=-1, keepdims=True)
        along = jnp.mean(scaled * unit, axis=-1, keepdims=True)
        total = dy_v[at, :].astype(F32) + inverse * (scaled - centre - unit * along)
        mgf_v[at, :] = total
        mg_v[at, :] = total.astype(BF)
        small_s[1:2, :] = small_s[1:2, :] + jnp.sum(grad * unit, axis=0, keepdims=True)
        small_s[3:4, :] = small_s[3:4, :] + jnp.sum(grad, axis=0, keepdims=True)

    for load in loads[15:17]:
        load.start()
    ring(2)
    for load in loads[6:12]:
        load.wait()
    @pl.loop(0, 2)
    def _(half):
        mixg_v[half] = dot_nt(mg_v[...], wo_v[half]).astype(BF)

    ring(1)
    their = 1 - here.core

    def out_grad(half, side, dst):
        cols = aligned(side * 256, 256, 256)
        dst[...] = dot_tn(mix_v[half, :, cols], mg_v[...]).astype(BF)

    keep = same_head()

    def tops(half):
        @pl.loop(0, 4)
        def _(p):
            lanes_at = aligned(p * PAIR, PAIR, PAIR)
            packs = []
            blocks = jnp.where(keep, 1.0, 0.0).astype(BF)
            for c in range(2):
                at = pl.ds(c * CH, CH)
                top = (mixg_v[half, at, lanes_at].astype(F32) * rden_v[half, at, lanes_at]).astype(BF)
                top_v[half, at, lanes_at] = top
                prod = top.astype(F32) * mix_v[half, at, lanes_at].astype(F32)
                high = prod.astype(BF)
                low = (prod - high.astype(F32)).astype(BF)
                bottom = -(dot_nn(high, blocks) + dot_nn(low, blocks))
                high = bottom.astype(BF)
                low = (bottom - high.astype(F32)).astype(BF)
                lane = lax.rem(lax.broadcasted_iota(jnp.int32, bottom.shape, 1), DH)
                bot_v[half, at, lanes_at] = jnp.where(
                    lane == 0, high, jnp.where(lane == 1, low, jnp.zeros_like(high))
                )
                query = qkv_v[half, 0, at, lanes_at]
                made = dot_tn(query, jnp.concatenate([top, high], axis=1))
                packs.append(jnp.where(keep, made[:, :PAIR], pltpu.roll(made[:, PAIR:], DH, 1)))
            local_v[half, p] = packs[1]
            lsend_v[half, p] = (packs[0] + packs[1]).astype(BF)

        across(lsend_v.at[half], lrecv_v.at[1 - half], 1 + half)

    tops(0)
    ring(1)
    tops(1)
    ring(1)
    for half in (1, 0):
        out_grad(half, their, om_v.at[half])
        to_mate(om_v.at[half], or_v.at[half], half)
    ring(1)
    for half in (1, 0):
        out_grad(half, here.core, oa_v.at[half])
    ring(1)
    for load in loads[12:15]:
        load.wait()

    def attend_back(half):
        mask = causal_tile()
        earlier = 1.0 - here.mp.astype(F32)
        remote(
            lsend_v.at[1 - half], lrecv_v.at[half], xs_sem.at[2 - half], xr_sem.at[2 - half], here.across
        ).wait_recv()

        def body(p, c):
            lanes_at = aligned(p * PAIR, PAIR, PAIR)
            at = aligned(c * CH, CH, CH)
            second = c.astype(F32)
            query = qkv_v[half, 0, at, lanes_at]
            key = qkv_v[half, 1, at, lanes_at]
            val = qkv_v[half, 2, at, lanes_at]
            top = top_v[half, at, lanes_at]
            bot = bot_v[half, at, lanes_at]
            lane = lax.rem(lax.broadcasted_iota(jnp.int32, val.shape, 1), DH)
            one = jnp.ones_like(val)
            zero = jnp.zeros_like(val)
            val_two = jnp.concatenate([val, jnp.where(lane < 2, one, zero)], axis=1)
            val_one = jnp.concatenate([val, jnp.where(lane == 0, one, zero)], axis=1)
            key0 = qkv_v[half, 1, pl.ds(0, CH), lanes_at]
            val0 = qkv_v[half, 2, pl.ds(0, CH), lanes_at]
            made = dot_tn(key0, jnp.concatenate([val0, one], axis=1))
            made = jnp.where(keep, made[:, :PAIR], made[:, PAIR:])
            before = state_v[half, p].astype(F32) + made * second
            after = lrecv_v[half, p].astype(F32) * earlier + local_v[half, p] * (1.0 - second)
            before = unpack_state(before).astype(BF)
            after = unpack_state(after).astype(BF)
            dq = dot_nt(jnp.concatenate([top, bot], axis=1), before)
            dk = dot_nt(val_one, after)
            dv = dot_nn(key, after[:, :PAIR])
            queries, keys, tops_, bots = split_heads(query), split_heads(key), split_heads(top), split_heads(bot)
            for head in range(2):
                score = jnp.where(mask, dot_nt(queries[head], key), 0.0).astype(BF)
                grad = dot_nt(jnp.concatenate([tops_[head], bots[head]], axis=1), val_two)
                grad = jnp.where(mask, grad, 0.0).astype(BF)
                dq = dq + dot_nn(grad, keys[head])
                dk = dk + dot_tn(grad, queries[head])
                dv = dv + dot_tn(score, tops_[head])
            dqkv_v[half, 0, at, lanes_at] = (dq * jnp.minimum(query.astype(F32), 1.0)).astype(BF)
            dqkv_v[half, 1, at, lanes_at] = (dk * jnp.minimum(key.astype(F32), 1.0)).astype(BF)
            dqkv_v[half, 2, at, lanes_at] = dv.astype(BF)

        for part in range(2):
            @pl.loop(part * 4, part * 4 + 4)
            def _(n):
                body(n // 2, lax.rem(n, 2))

            ring(2)

    def piece(i):
        return pl.ds(i * 512, 512)

    def in_grads(half):
        for side, dst in ((their, gm_v), (here.core, ga_v)):
            cols = aligned(side * 512, 512, 512)
            @pl.loop(0, 3)
            def _(i):
                dst[half, aligned(i * 512, 512, 512), :] = dot_tn(first_v[:, cols], dqkv_v[half, i]).astype(BF)

            if dst is gm_v:
                for i in range(3):
                    at = piece(i)
                    to_mate(gm_v.at[half, at], gr_v.at[half, at], 2 + half * 3 + i)
            ring(1)

    def add_rows(dst, src, start, count):
        @pl.loop(0, count)
        def _(i):
            at = aligned(start + i * 128, 128, 128)
            dst[at, :] = (dst[at, :].astype(F32) + src[at, :].astype(F32)).astype(BF)

    def mate_arrival(half, i):
        at = piece(i)
        slot = 2 + half * 3 + i
        remote(gm_v.at[half, at], gr_v.at[half, at], ms_sem.at[slot], mr_sem.at[slot], here.mate).wait_recv()
        add_rows(ga_v.at[half], gr_v.at[half], i * 512, 4)

    def mate_arrival_out(half):
        remote(om_v.at[half], or_v.at[half], ms_sem.at[half], mr_sem.at[half], here.mate).wait_recv()
        add_rows(oa_v.at[half], or_v.at[half], 0, 2)

    attend_back(1)
    mate_arrival_out(1)
    cross_o = across(oa_v.at[1], ox_v, 3)
    in_grads(1)
    cross_i = []
    for i in range(3):
        mate_arrival(1, i)
        cross_i.append(across(ga_v.at[1, piece(i)], gx_v.at[piece(i)], 4 + i))
    mlp = across(mlp_hbm.at[pl.ds(ROWS, ROWS)], mlpin_v, 0)
    ring(2)
    mate_arrival_out(0)
    attend_back(0)
    cross_o.wait_recv()
    add_rows(oa_v.at[0], ox_v, 0, 2)
    ring_on(ring_o)
    in_grads(0)
    for i in range(3):
        mate_arrival(0, i)
    ring(2)
    ring_on(ring_o)

    loads[15].wait()
    gain_one = gain_ref[0:1, :]

    @pl.loop(0, 2)
    def _(quarter):
        at = aligned(quarter * CH, CH, CH)
        grad = None
        for half in range(2):
            term = None
            for j in range(3):
                made = dot_nt(dqkv_v[half, j, at, :], win_v[half, pl.ds(j * 1024, 1024), :])
                term = made if term is None else term + made
            term = term.astype(BF).astype(F32)
            grad = term if grad is None else grad + term
        unit, inverse = row_norm(part_v[at, :].astype(F32))
        scaled = grad * gain_one
        centre = jnp.mean(scaled, axis=-1, keepdims=True)
        along = jnp.mean(scaled * unit, axis=-1, keepdims=True)
        mgf_v[at, :] = mgf_v[at, :] + inverse * (scaled - centre - unit * along)
        small_s[0:1, :] = small_s[0:1, :] + jnp.sum(grad * unit, axis=0, keepdims=True)
        small_s[2:3, :] = small_s[2:3, :] + jnp.sum(grad, axis=0, keepdims=True)

    ring(4)
    ring_on(ring_o)
    out(mgf_v, gin_o)
    small_s[4:5, pl.ds(0, PAIR)] = jnp.sum(stat_ref[1], axis=0, keepdims=True) * (1.0 / DH)
    count = len_ref[0].astype(F32) * (8.0 / 1024.0)
    small_s[5:6, :] = jnp.zeros((1, 1024), F32) + count
    small_s[6:7, pl.ds(0, PAIR)] = jnp.max(stat_ref[0], axis=0, keepdims=True)
    partners = [here.mate, y_mate, z_mate, z_far, here.across]

    def small_send(step):
        src = small_s if step == 0 else small_ref
        copy = remote(src, small_r.at[step], bs_sem.at[step], br_sem.at[step], partners[step])
        copy.start()
        return copy

    def small_step(copy, step):
        copy.wait()
        src = small_s if step == 0 else small_ref
        mine, theirs = src[...], small_r[step]
        row = lax.broadcasted_iota(jnp.int32, mine.shape, 0)
        small_ref[...] = jnp.where(row < 6, mine + theirs, jnp.maximum(mine, theirs))

    for i in range(3):
        cross_i[i].wait_recv()
        add_rows(ga_v.at[0], gx_v, i * 512, 4)
        for arc in ring_i[: i + 1]:
            ring_on(arc)
        ring(6)
        ring_on(ring_o)
    copy = small_send(0)
    for step in range(9):
        for arc in ring_i:
            ring_on(arc)
        ring(6)
        ring_on(ring_o)
        if 2 <= step < 7:
            small_step(copy, step - 2)
            if step < 6:
                copy = small_send(step - 1)
    ring(2000)

    loads[16].wait()
    mlp.wait_recv()

    @pl.loop(0, 4)
    def _(i):
        at = aligned(i * 128, 128, 128)
        total = mid_v[at, :] + (pin_v[at, :].astype(F32) + mlpin_v[at, :].astype(F32))
        pin_v[at, :] = total.astype(BF)

    out(pin_v, out_o)
    for arc in arcs:
        arc.finish()
    for copy in sends:
        copy.wait_send()
    for copy in outs:
        copy.wait()


def back(lengths, gain, bias, stat, part, pin, mid, x, dy, qkv, mix, rden, state, first, win, wino, wo, woo, mlp, dslab, uslab, dring):
    vm = pltpu.VMEM
    dma = pltpu.SemaphoreType.DMA
    shapes = [
        ((2048, 1024), BF), ((1024, 2048), BF), ((3072, 512), BF), ((512, 1024), BF),
        ((512, 1024), BF), ((512, 1024), F32), ((8, 1024), F32),
    ]
    rows = (512, 1024)
    heads = (2, 512, 512)
    pack = (2, 4, PAIR, PAIR)
    vmem = pl.BlockSpec(memory_space=pltpu.VMEM)
    return pl.pallas_call(
        back_kernel,
        out_shape=[jax.ShapeDtypeStruct(s, d) for s, d in shapes],
        in_specs=[pl.BlockSpec(memory_space=pltpu.SMEM), vmem, vmem, vmem] + any_spec(18),
        out_specs=any_spec(6) + [vmem],
        scratch_shapes=[
            vm(rows, BF), vm(rows, BF), vm(rows, F32), vm(rows, BF),
            vm((2, 3, 512, 512), BF), vm(heads, BF), vm(heads, F32), vm(pack, BF), vm(rows, BF),
            vm((2, 3072, 512), BF), vm((2, 512, 1024), BF),
            vm(rows, BF), vm(rows, BF), vm(rows, F32), vm(heads, BF), vm(heads, BF), vm(heads, BF),
            vm((2, 3, 512, 512), BF), vm(pack, F32), vm(pack, BF), vm(pack, BF),
            vm((1024, 1024), BF), vm((512, 2048), BF), vm((2, 4, 128, 1024), BF), vm((2, 4, 64, 2048), BF),
            vm((2, 1536, 512), BF), vm((2, 1536, 512), BF), vm((2, 1536, 512), BF), vm((1536, 512), BF),
            vm((2, 256, 1024), BF), vm((2, 256, 1024), BF), vm((2, 256, 1024), BF), vm((256, 1024), BF),
            vm((3, 2, 4, 64, 512), BF), vm((2, 4, 32, 1024), BF),
            vm((8, 1024), F32), vm((5, 8, 1024), F32),
            dma((19,)), dma((2,)), dma((7,)), dma((7,)), dma((8,)), dma((8,)), dma((5,)), dma((5,)),
            dma((6, 2, 4)), dma((6, 2, 4)), dma((6, 2, 4)), dma((6, 2, 4)), dma((6, 9)), dma((6, 9)), dma((6,)),
        ],
        compiler_params=pltpu.CompilerParams(
            collective_id=2, has_side_effects=True, vmem_limit_bytes=60 * 1024 * 1024
        ),
        name="back",
    )(lengths, gain, bias, stat, part, pin, mid, x, dy, qkv, mix, rden, state, first, win, wino, wo, woo, mlp, dslab, uslab, dring)


def widen_kernel(
    d_hbm, u_hbm, i_hbm, o_hbm, gin_hbm, out_hbm, small_ref,
    di_o, ui_o, ii_o, oi_o, gin_o, out_o, gain_ref, bias_ref, stats_ref,
    d_v, u_v, i_v, o_v, df_v, uf_v, if_v, of_v, gin_v, out_v, in_sem, out_sem,
):
    jobs = []
    for k in range(6):
        core, i = k // 3, k % 3
        jobs.append((i_hbm, i_v, k * 512, ii_o, if_v, i * 1024 + core * 512, 512))
    for k in range(2):
        jobs.append((o_hbm, o_v, k * 256, oi_o, of_v, k * 256, 256))
    for k in range(8):
        jobs.append((u_hbm, u_v, k * 128, ui_o, uf_v, k * 128, 128))
    for k in range(8):
        jobs.append((d_hbm, d_v, k * 256, di_o, df_v, k * 256, 256))
    loads, stores = [], []
    for n, (src, held, at, _, _, _, rows) in enumerate(jobs):
        loads.append(pltpu.make_async_copy(src.at[pl.ds(at, rows)], held.at[pl.ds(at, rows)], in_sem.at[n]))
        loads[-1].start()
    passed = ((gin_hbm, gin_v, gin_o), (out_hbm, out_v, out_o))
    for n, (src, held, _) in enumerate(passed):
        loads.append(pltpu.make_async_copy(src, held, in_sem.at[len(jobs) + n]))
        loads[-1].start()
    for n, (_, held, at, dst, wide, to, rows) in enumerate(jobs):
        loads[n].wait()

        @pl.loop(0, rows // 128)
        def _(k):
            rows_at = aligned(at + k * 128, 128, 128)
            wide[rows_at, :] = held[rows_at, :].astype(F32)

        stores.append(pltpu.make_async_copy(wide.at[pl.ds(at, rows)], dst.at[pl.ds(to, rows)], out_sem.at[n]))
        stores[-1].start()
    for n, (_, held, dst) in enumerate(passed):
        loads[len(jobs) + n].wait()
        stores.append(pltpu.make_async_copy(held, dst, out_sem.at[len(jobs) + n]))
        stores[-1].start()
    gain_ref[...] = small_ref[0:2, :]
    bias_ref[...] = small_ref[2:4, :]
    scaling = 1.0 / (DH * 1024)
    count = jnp.max(small_ref[5:6, :]) * 1024.0
    stats_ref[0] = jnp.max(small_ref[6:7, :]) * scaling
    stats_ref[1] = jnp.sum(small_ref[4:5, :]) / count * scaling
    for copy in stores:
        copy.wait()


def widen(resd, resu, resi, reso, gin, out, small):
    vm = pltpu.VMEM
    vmem = pl.BlockSpec(memory_space=pltpu.VMEM)
    shapes = [
        ((2048, 1024), F32), ((1024, 2048), F32), ((3072, 512), F32), ((512, 1024), F32),
        ((512, 1024), F32), ((512, 1024), BF), ((2, 1024), F32), ((2, 1024), F32), ((2,), F32),
    ]
    return pl.pallas_call(
        widen_kernel,
        out_shape=[jax.ShapeDtypeStruct(s, d) for s, d in shapes],
        in_specs=any_spec(6) + [vmem],
        out_specs=any_spec(6) + [vmem, vmem, pl.BlockSpec(memory_space=pltpu.SMEM)],
        scratch_shapes=[vm(s, BF) for s, _ in shapes[:4]] + [vm(s, F32) for s, _ in shapes[:4]]
        + [vm((512, 1024), F32), vm((512, 1024), BF)]
        + [pltpu.SemaphoreType.DMA((26,)), pltpu.SemaphoreType.DMA((26,))],
        compiler_params=pltpu.CompilerParams(vmem_limit_bytes=60 * 1024 * 1024),
        name="widen",
    )(resd, resu, resi, reso, gin, out, small)


def fast_device(
    block_in, lengths, input_weight, output_weight, up_weight, down_weight, norm_gain, norm_bias, cotangent
):
    x, dy = block_in[0], cotangent[0]
    win = input_weight.reshape(3072, 512)
    first, qkv, mix, rden, state, mid, sec, wino, woo, dyo, hg, stat = front(
        lengths, x, dy, win, output_weight, down_weight, norm_gain, norm_bias
    )
    part, pin, mlp, dslab, uslab, dring = middle(sec, dy, dyo, hg, up_weight, down_weight)
    resd, resu, resi, reso, block_out, grad_in, small = back(
        lengths, norm_gain, norm_bias, stat, part, pin, mid, x, dy, qkv, mix, rden, state, first,
        win, wino, output_weight, woo, mlp, dslab, uslab, dring,
    )
    down_grad, up_grad, in_grad, out_grad, grad_in, block_out, gain, bias, stats = widen(
        resd, resu, resi, reso, grad_in, block_out, small
    )
    return (
        block_out[None], grad_in[None], in_grad.reshape(3, 1024, 512), out_grad, up_grad, down_grad,
        gain, bias, stats,
    )


def fits_fast(mesh, block_shape):
    return dict(mesh.shape) == {"dp": 16, "mp": 2} and tuple(block_shape) == (16, 1024, 1024)


def solution(mesh):
    in_specs = (
        P("dp", "mp", None),
        P("dp"),
        P(None, None, "mp"),
        P("mp", None),
        P(None, "mp"),
        P("mp", None),
        P(),
        P(),
        P("dp", "mp", None),
    )
    out_specs = (
        P("dp", "mp", None),
        P("dp", "mp", None),
        P(None, None, "mp"),
        P("mp", None),
        P(None, "mp"),
        P("mp", None),
        P(),
        P(),
        P(),
    )

    def whole(*arrays):
        body = fast_device if fits_fast(mesh, arrays[0].shape) else per_device
        return jax.shard_map(
            body, mesh=mesh, in_specs=in_specs, out_specs=out_specs, check_vma=False
        )(*arrays)

    return whole
```

```python
from functools import partial

import jax
import jax.numpy as jnp
from jax import lax
from jax.experimental import pallas as pl
from jax.experimental.pallas import tpu as pltpu
from jax.sharding import PartitionSpec as P

DH = 64
BLK = 512


EPSILON = 1e-05
PRECISE = lax.Precision.HIGHEST


def combined_all(part, axis, combine):
    gathered = jax.tree.map(lambda a: lax.all_gather(a, axis), part)

    def take(source):
        return jax.tree.map(lambda a: lax.dynamic_index_in_dim(a, source, 0, False), gathered)

    return lax.fori_loop(
        1, lax.axis_size(axis), lambda source, state: combine(state, take(source)), take(0)
    )


def feature(values):
    return jax.nn.elu(values) + 1.0


def feature_slope(values):
    return jnp.where(values > 0, 1.0, jnp.exp(values))


def normalise(inputs, gain_row, bias_row):
    centre = jnp.mean(inputs, axis=-1, keepdims=True)
    centred = inputs - centre
    spread = jnp.mean(centred * centred, axis=-1, keepdims=True)
    inverse = lax.rsqrt(spread + EPSILON)
    unit_rows = centred * inverse
    return (unit_rows * gain_row + bias_row, unit_rows, inverse)


def normalise_back(grad_rows, unit_rows, inverse, gain_row):
    scaled = grad_rows * gain_row
    centre = jnp.mean(scaled, axis=-1, keepdims=True)
    along = jnp.mean(scaled * unit_rows, axis=-1, keepdims=True)
    input_grad = inverse * (scaled - centre - unit_rows * along)
    return (input_grad, jnp.sum(grad_rows * unit_rows, axis=0), jnp.sum(grad_rows, axis=0))


def exclusive(stacked):
    running = jnp.cumsum(stacked, axis=0)
    return jnp.concatenate([jnp.zeros_like(running[:1]), running[:-1]], axis=0)


def later(stacked):
    return exclusive(stacked[::-1])[::-1]


def unchanged(carried):
    return carried


def causal_mask():
    return jnp.tril(jnp.ones((BLK, BLK), jnp.float32))


def attend_forward(query_map, key_map, values, crop_len):
    slot_len, head_count, depth = query_map.shape
    block_count = slot_len // BLK
    block_shape = (block_count, BLK, head_count, depth)
    block_q = query_map.reshape(block_shape)
    block_k = key_map.reshape(block_shape)
    block_v = values.reshape(block_shape)
    memory = exclusive(
        jnp.einsum("nihd,nihe->nhde", block_k, block_v, preferred_element_type=jnp.float32)
    )
    key_total = exclusive(jnp.sum(block_k.astype(jnp.float32), axis=1))
    causal = causal_mask()
    block_starts = jnp.arange(block_count, dtype=jnp.int32) * BLK

    def one_block(block_item):
        query_b, key_b, value_b, memory_b, total_b, start_b = block_item
        query_f = query_b.astype(jnp.float32)
        numerator = jnp.einsum("ihd,hde->ihe", query_f, memory_b, precision=PRECISE)
        denominator = jnp.einsum("ihd,hd->ih", query_f, total_b, precision=PRECISE)

        def inside(partial_sums):
            value_part, weight_part = partial_sums
            scores = (
                jnp.einsum("ihd,jhd->hij", query_b, key_b, preferred_element_type=jnp.float32)
                * causal
            )
            value_part = value_part + jnp.einsum(
                "hij,jhd->ihd",
                scores.astype(jnp.bfloat16),
                value_b,
                preferred_element_type=jnp.float32,
            )
            weight_part = weight_part + jnp.sum(scores, axis=-1).T
            return (value_part, weight_part)

        numerator, denominator = lax.cond(
            start_b < crop_len, inside, unchanged, (numerator, denominator)
        )
        return (numerator / denominator[..., None], denominator)

    attended, denoms = lax.map(
        one_block, (block_q, block_k, block_v, memory, key_total, block_starts)
    )
    return (
        attended.reshape(slot_len, head_count, depth),
        denoms.reshape(slot_len, head_count),
        memory,
        key_total,
    )


def attend_backward(
    grad_attn, attended, denoms, query_map, key_map, values, memory, key_total, crop_len
):
    slot_len, head_count, depth = query_map.shape
    block_count = slot_len // BLK
    block_shape = (block_count, BLK, head_count, depth)
    top_all = (grad_attn / denoms[..., None]).reshape(block_shape)
    bottom_all = (-jnp.sum(grad_attn * attended, axis=-1) / denoms).reshape(
        block_count, BLK, head_count
    )
    query_full = query_map.astype(jnp.float32).reshape(block_shape)
    memory_later = later(jnp.einsum("nihd,nihe->nhde", query_full, top_all, precision=PRECISE))
    total_later = later(jnp.einsum("nihd,nih->nhd", query_full, bottom_all, precision=PRECISE))
    causal = causal_mask()
    block_starts = jnp.arange(block_count, dtype=jnp.int32) * BLK

    def one_block(block_item):
        (
            query_b,
            key_b,
            value_b,
            memory_b,
            total_b,
            later_memory,
            later_total,
            top_grad,
            bottom_grad,
            start_b,
        ) = block_item
        value_f = value_b.astype(jnp.float32)
        key_f = key_b.astype(jnp.float32)
        query_sum = (
            jnp.einsum("ihe,hde->ihd", top_grad, memory_b, precision=PRECISE)
            + bottom_grad[..., None] * total_b[None]
        )
        key_sum = (
            jnp.einsum("jhe,hde->jhd", value_f, later_memory, precision=PRECISE) + later_total[None]
        )
        value_sum = jnp.einsum("jhd,hde->jhe", key_f, later_memory, precision=PRECISE)

        def inside(partial_grads):
            query_acc, key_acc, value_acc = partial_grads
            scores = (
                jnp.einsum("ihd,jhd->hij", query_b, key_b, preferred_element_type=jnp.float32)
                * causal
            )
            score_grad = (
                (
                    jnp.einsum("ihe,jhe->hij", top_grad, value_f, precision=PRECISE)
                    + bottom_grad.T[:, :, None]
                )
                * causal
            ).astype(jnp.bfloat16)
            query_acc = query_acc + jnp.einsum(
                "hij,jhd->ihd", score_grad, key_b, preferred_element_type=jnp.float32
            )
            key_acc = key_acc + jnp.einsum(
                "hij,ihd->jhd", score_grad, query_b, preferred_element_type=jnp.float32
            )
            rounded_scores = scores.astype(jnp.bfloat16).astype(jnp.float32)
            value_acc = value_acc + jnp.einsum(
                "hij,ihe->jhe", rounded_scores, top_grad, precision=PRECISE
            )
            return (query_acc, key_acc, value_acc)

        return lax.cond(start_b < crop_len, inside, unchanged, (query_sum, key_sum, value_sum))

    query_grad, key_grad, value_grad = lax.map(
        one_block,
        (
            query_map.reshape(block_shape),
            key_map.reshape(block_shape),
            values.reshape(block_shape),
            memory,
            key_total,
            memory_later,
            total_later,
            top_all,
            bottom_all,
            block_starts,
        ),
    )
    return (
        query_grad.reshape(slot_len, head_count, depth),
        key_grad.reshape(slot_len, head_count, depth),
        value_grad.reshape(slot_len, head_count, depth),
    )


def combine_stats(first_part, second_part):
    return (
        first_part[0] + second_part[0],
        first_part[1] + second_part[1],
        first_part[2] + second_part[2],
        first_part[3] + second_part[3],
        jnp.maximum(first_part[4], second_part[4]),
    )


def per_device(
    block_in,
    lengths,
    input_weight,
    output_weight,
    up_weight,
    down_weight,
    norm_gain,
    norm_bias,
    cotangent,
):
    group_count = lax.axis_size("mp")
    rows_here = block_in.shape[1]
    slot_len = rows_here * group_count
    local_width = output_weight.shape[0]
    head_count = local_width // DH
    crop_len = lengths[0]
    valid_mask = (jnp.arange(slot_len, dtype=jnp.int32) < crop_len).astype(jnp.float32)
    own_rows = block_in[0].astype(jnp.float32)
    first_norm, unit_one, inverse_one = normalise(own_rows, norm_gain[0], norm_bias[0])
    first_rows = lax.all_gather(first_norm.astype(jnp.bfloat16), "mp", axis=0, tiled=True)
    projected = jnp.einsum(
        "rd,cdk->rck", first_rows, input_weight, preferred_element_type=jnp.float32
    ).reshape(slot_len, 3, head_count, DH)
    query = projected[:, 0]
    key_raw = projected[:, 1]
    query_map = feature(query).astype(jnp.bfloat16)
    key_map = (feature(key_raw) * valid_mask[:, None, None]).astype(jnp.bfloat16)
    values = projected[:, 2].astype(jnp.bfloat16)
    attended, denoms, memory, key_total = attend_forward(query_map, key_map, values, crop_len)
    mixed = attended.reshape(slot_len, local_width).astype(jnp.bfloat16)
    part_rows = mixed
    branch_out = lax.psum_scatter(
        jnp.dot(part_rows, output_weight, preferred_element_type=jnp.float32).astype(jnp.bfloat16),
        "mp",
        scatter_dimension=0,
        tiled=True,
    ).astype(jnp.float32)
    middle = own_rows + branch_out
    second_norm, unit_two, inverse_two = normalise(middle, norm_gain[1], norm_bias[1])
    second_rows = lax.all_gather(second_norm.astype(jnp.bfloat16), "mp", axis=0, tiled=True)
    hidden_in = jnp.dot(second_rows, up_weight, preferred_element_type=jnp.float32)
    hidden = jax.nn.gelu(hidden_in, approximate=True).astype(jnp.bfloat16)
    part_rows = hidden
    mlp_out = lax.psum_scatter(
        jnp.dot(part_rows, down_weight, preferred_element_type=jnp.float32).astype(jnp.bfloat16),
        "mp",
        scatter_dimension=0,
        tiled=True,
    ).astype(jnp.float32)
    block_out = (middle + mlp_out).astype(jnp.bfloat16)[None]
    grad_out = cotangent[0]
    grad_rows = lax.all_gather(grad_out, "mp", axis=0, tiled=True)
    down_grad = jnp.einsum("rf,rd->fd", hidden, grad_rows, preferred_element_type=jnp.float32)
    hidden_grad = jnp.einsum(
        "rd,fd->rf", grad_rows, down_weight, preferred_element_type=jnp.float32
    )
    unused_out, gelu_back = jax.vjp(partial(jax.nn.gelu, approximate=True), hidden_in)
    inner_grad = gelu_back(hidden_grad)[0].astype(jnp.bfloat16)
    up_grad = jnp.einsum("rd,rf->df", second_rows, inner_grad, preferred_element_type=jnp.float32)
    part_rows = inner_grad
    second_grad = lax.psum_scatter(
        jnp.einsum("rf,df->rd", part_rows, up_weight, preferred_element_type=jnp.float32).astype(
            jnp.bfloat16
        ),
        "mp",
        scatter_dimension=0,
        tiled=True,
    ).astype(jnp.float32)
    back_two, gain_two, bias_two = normalise_back(second_grad, unit_two, inverse_two, norm_gain[1])
    middle_grad = grad_out.astype(jnp.float32) + back_two
    middle_low = middle_grad.astype(jnp.bfloat16)
    middle_full = lax.all_gather(middle_low, "mp", axis=0, tiled=True)
    mixed_grad = jnp.einsum(
        "rd,kd->rk", middle_full, output_weight, preferred_element_type=jnp.float32
    ).astype(jnp.bfloat16)
    output_grad = jnp.einsum("rk,rd->kd", mixed, middle_full, preferred_element_type=jnp.float32)
    grad_attn = mixed_grad.astype(jnp.float32).reshape(slot_len, head_count, DH)
    query_grad, key_grad, value_grad = attend_backward(
        grad_attn, attended, denoms, query_map, key_map, values, memory, key_total, crop_len
    )
    query_low = (query_grad * feature_slope(query)).astype(jnp.bfloat16)
    key_low = (key_grad * valid_mask[:, None, None] * feature_slope(key_raw)).astype(jnp.bfloat16)
    value_low = value_grad.astype(jnp.bfloat16)
    qkv_grad = jnp.stack([query_low, key_low, value_low], axis=1).reshape(slot_len, 3, local_width)
    input_grad = jnp.einsum("rd,rck->cdk", first_rows, qkv_grad, preferred_element_type=jnp.float32)
    part_rows = qkv_grad
    first_grad = lax.psum_scatter(
        jnp.einsum(
            "rck,cdk->rd", part_rows, input_weight, preferred_element_type=jnp.float32
        ).astype(jnp.bfloat16),
        "mp",
        scatter_dimension=0,
        tiled=True,
    ).astype(jnp.float32)
    back_one, gain_one, bias_one = normalise_back(first_grad, unit_one, inverse_one, norm_gain[0])
    grad_input = (middle_grad + back_one)[None]
    input_grad, output_grad, up_grad, down_grad = (
        lax.psum(input_grad.astype(jnp.bfloat16), "dp").astype(jnp.float32),
        lax.psum(output_grad.astype(jnp.bfloat16), "dp").astype(jnp.float32),
        lax.psum(up_grad.astype(jnp.bfloat16), "dp").astype(jnp.float32),
        lax.psum(down_grad.astype(jnp.bfloat16), "dp").astype(jnp.float32),
    )
    kept_denoms = jnp.where(valid_mask[:, None] > 0, denoms, 0.0)
    den_total = jnp.sum(kept_denoms)
    den_count = crop_len.astype(jnp.float32) * head_count
    den_peak = jnp.max(kept_denoms)
    gain_grad, bias_grad, den_total, den_count, den_peak = combined_all(
        (
            jnp.stack([gain_one, gain_two]),
            jnp.stack([bias_one, bias_two]),
            den_total,
            den_count,
            den_peak,
        ),
        ("dp", "mp"),
        combine_stats,
    )
    scaling = DH * slot_len
    denominator_stats = jnp.stack([den_peak / scaling, den_total / den_count / scaling])
    return (
        block_out,
        grad_input,
        input_grad,
        output_grad,
        up_grad,
        down_grad,
        gain_grad,
        bias_grad,
        denominator_stats,
    )

MESH = pl.DeviceIdType.MESH
BF = jnp.bfloat16
F32 = jnp.float32
ROWS = 512
CH = 256
PAIR = 128


def dot_nn(a, b):
    return lax.dot_general(a, b, (((1,), (0,)), ((), ())), preferred_element_type=F32)


def dot_nt(a, b):
    return lax.dot_general(a, b, (((1,), (1,)), ((), ())), preferred_element_type=F32)


def dot_tn(a, b):
    return lax.dot_general(a, b, (((0,), (0,)), ((), ())), preferred_element_type=F32)


class Place:
    def __init__(self):
        dp = lax.axis_index("dp")
        mp = lax.axis_index("mp")
        self.dp, self.mp = dp, mp
        self.core = lax.rem(dp, 2)
        chip = dp // 2
        y = lax.rem(chip, 2)
        z = chip // 2
        self.r = z + y * (7 - 2 * z)
        self.across = (dp, 1 - mp)
        self.mate = (dp + 1 - 2 * self.core, mp)
        self.next = self.at(lax.rem(self.r + 1, 8))
        self.prev = self.at(lax.rem(self.r + 7, 8))

    def at(self, r):
        y = r // 4
        z = r + y * (7 - 2 * r)
        return ((z * 2 + y) * 2 + self.core, self.mp)

    def partners(self):
        return [self.across, self.mate, self.next, self.prev]


def greet(partners):
    barrier = pltpu.get_barrier_semaphore()
    for partner in partners:
        pl.semaphore_signal(barrier, inc=1, device_id=partner, device_id_type=MESH)
    pl.semaphore_wait(barrier, len(partners))


def remote(src, dst, send_sem, recv_sem, device):
    return pltpu.make_async_remote_copy(
        src_ref=src, dst_ref=dst, send_sem=send_sem, recv_sem=recv_sem,
        device_id=device, device_id_type=MESH,
    )


def aligned(start, size, unit):
    return pl.ds(pl.multiple_of(start, unit), size)


def lane_head(shape):
    return lax.broadcasted_iota(jnp.int32, shape, len(shape) - 1) < DH


def same_head():
    row = lax.broadcasted_iota(jnp.int32, (PAIR, PAIR), 0) < DH
    lane = lax.broadcasted_iota(jnp.int32, (PAIR, PAIR), 1) < DH
    return row == lane


def causal_tile():
    row = lax.broadcasted_iota(jnp.int32, (CH, CH), 0)
    col = lax.broadcasted_iota(jnp.int32, (CH, CH), 1)
    return row >= col


def unpack_state(packed):
    keep = same_head()
    zero = jnp.zeros_like(packed)
    return jnp.concatenate(
        [jnp.where(keep, packed, zero), jnp.where(keep, pltpu.roll(packed, DH, 1), zero)], axis=1
    )


def split_heads(pair):
    first = lane_head(pair.shape)
    zero = jnp.zeros_like(pair)
    return jnp.where(first, pair, zero), jnp.where(first, zero, pair)


def row_norm(rows):
    centre = jnp.mean(rows, axis=-1, keepdims=True)
    centred = rows - centre
    inverse = lax.rsqrt(jnp.mean(centred * centred, axis=-1, keepdims=True) + EPSILON)
    return centred * inverse, inverse


def front_kernel(
    len_ref, x_hbm, dy_hbm, win_hbm, wo_hbm, wdn_hbm, gain_ref, bias_ref,
    first_o, qkv_o, mix_o, rden_o, state_o, mid_o, sec_o, wino_o, woo_o, dyo_o, hg_o, stat_ref,
    x_v, dy_v, win_v, wino_v, wo_v, woo_v, wdn_v, first_v, qkv_v, num_v, den_v, mix_v, mid_v, sec_v, hg_v,
    local_v, ssend_v, srecv_v, state_v,
    in_sem, out_sem, xs_sem, xr_sem, ring_s, ring_r, mate_s, mate_r,
):
    here = Place()
    loads = [
        (x_hbm, x_v), (win_hbm, win_v), (dy_hbm, dy_v), (wdn_hbm, wdn_v), (wo_hbm, wo_v),
    ]
    loads = [pltpu.make_async_copy(a, b, in_sem.at[i]) for i, (a, b) in enumerate(loads)]
    for load in loads:
        load.start()
    greet(here.partners())
    parts = ((win_hbm, wino_v, 192), (wo_hbm, woo_v, 32))

    def rows_of(array, offset, core):
        rows = parts[array][2]
        return aligned((lax.rem(here.r + 8 + offset, 8) * 2 + core) * rows, rows, 32)

    cross = []
    for array, (src, dst, _) in enumerate(parts):
        for k in range(2):
            at = rows_of(array, 4 * k, here.core)
            slot = 2 * array + k
            cross.append(remote(src.at[at], dst.at[at], xs_sem.at[slot], xr_sem.at[slot], here.across))
    for copy in cross:
        copy.start()
    gone = []

    def dy_part(count):
        for _ in range(count):
            k = len(gone)
            rows = pl.ds(k * 64, 64)
            copy = remote(dy_hbm.at[rows], dyo_o.at[rows], xs_sem.at[7 + k], xr_sem.at[7 + k], here.across)
            copy.start()
            gone.append(copy)

    dy_part(2)

    gain = gain_ref[0:1, :]
    bias = bias_ref[0:1, :]
    sends = []
    outs = []

    def out(src, dst):
        copy = pltpu.make_async_copy(src, dst, out_sem.at[len(outs)])
        copy.start()
        outs.append(copy)

    FAR = ((-1, 3, -2), (1, 5, 2))

    def to_mate(array, slot, offset):
        at = rows_of(array, offset, here.core)
        dst = parts[array][1]
        copy = remote(dst.at[at], dst.at[at], mate_s.at[array, slot], mate_r.at[array, slot], here.mate)
        copy.start()
        sends.append(copy)

    def to_ring(array, way, k, offset):
        at = rows_of(array, offset, here.core)
        dst = parts[array][1]
        copy = remote(
            dst.at[at], dst.at[at], ring_s.at[array, way, k], ring_r.at[array, way, k],
            here.next if way == 0 else here.prev,
        )
        copy.start()
        sends.append(copy)

    def from_across(array):
        for k in range(2):
            cross[2 * array + k].wait_recv()
            for way in (0, 1):
                to_ring(array, way, k, 4 * k)
            to_mate(array, k, 4 * k)

    def from_ring(array, k):
        for way in (0, 1):
            at = rows_of(array, FAR[way][k], here.core)
            dst = parts[array][1].at[at]
            remote(dst, dst, ring_s.at[array, way, k], ring_r.at[array, way, k], here.next).wait_recv()
            if k == 0:
                to_ring(array, way, 2, FAR[way][0])
            to_mate(array, 2 + 2 * k + way, FAR[way][k])

    def mate_wait(array):
        offsets = [0, 4] + [FAR[way][k] for k in range(3) for way in (0, 1)]
        for slot, offset in enumerate(offsets):
            dst = parts[array][1].at[rows_of(array, offset, 1 - here.core)]
            remote(dst, dst, mate_s.at[array, slot], mate_r.at[array, slot], here.mate).wait_recv()

    loads[0].wait()

    @pl.loop(0, ROWS // 128)
    def _(i):
        at = aligned(i * 128, 128, 128)
        unit, _ = row_norm(x_v[at, :].astype(F32))
        first_v[at, :] = (unit * gain + bias).astype(BF)

    out(first_v, first_o)
    crop_len = len_ref[0]

    def project(half, weights, which):
        @pl.loop(0, 2)
        def _(c):
            at = aligned(c * CH, CH, CH)
            rows = first_v[at, :]
            for i in which:
                raw = dot_nn(rows, weights[pl.ds(i * 1024, 1024), :])
                if i < 2:
                    raw = jnp.where(raw > 0, raw + 1.0, jnp.exp(jnp.minimum(raw, 0.0)))
                if i == 1:
                    place = lax.broadcasted_iota(jnp.int32, raw.shape, 0) + (here.mp * ROWS + c * CH)
                    raw = jnp.where(place < crop_len, raw, 0.0)
                qkv_v[half, i, at, :] = raw.astype(BF)

    def states(half):
        keep = same_head()

        @pl.loop(0, 4)
        def _(p):
            lanes = aligned(p * PAIR, PAIR, PAIR)
            total = None
            for c in range(2):
                keys = qkv_v[half, 1, pl.ds(c * CH, CH), lanes]
                vals = qkv_v[half, 2, pl.ds(c * CH, CH), lanes]
                made = dot_tn(keys, jnp.concatenate([vals, jnp.ones_like(vals)], axis=1))
                packed = jnp.where(keep, made[:, :PAIR], made[:, PAIR:])
                if c == 0:
                    local_v[half, p] = packed
                    total = packed
                else:
                    ssend_v[half, p] = (total + packed).astype(BF)

        copy = remote(
            ssend_v.at[half], srecv_v.at[1 - half], xs_sem.at[5 + half], xr_sem.at[6 - half], here.across
        )
        copy.start()
        sends.append(copy)

    def inside(half):
        mask = causal_tile()

        @pl.loop(0, 8)
        def _(n):
            p = n // 2
            c = lax.rem(n, 2)
            lanes = aligned(p * PAIR, PAIR, PAIR)
            at = aligned(c * CH, CH, CH)
            query = qkv_v[half, 0, at, lanes]
            key = qkv_v[half, 1, at, lanes]
            val = qkv_v[half, 2, at, lanes]
            first = lane_head(val.shape)
            one = jnp.ones_like(val)
            zero = jnp.zeros_like(val)
            sums = None
            for head, part in enumerate(split_heads(query)):
                score = jnp.where(mask, dot_nt(part, key), 0.0).astype(BF)
                mine = first if head == 0 else jnp.logical_not(first)
                right = jnp.concatenate([jnp.where(mine, val, zero), jnp.where(mine, one, zero)], axis=1)
                term = dot_nn(score, right)
                sums = term if sums is None else sums + term
            num_v[at, lanes] = sums[:, :PAIR]
            den_v[half, at, lanes] = sums[:, PAIR:]

    def finish(half):
        flag = here.mp.astype(F32)

        @pl.loop(0, 8)
        def _(n):
            p = n // 2
            c = lax.rem(n, 2)
            lanes = aligned(p * PAIR, PAIR, PAIR)
            at = aligned(c * CH, CH, CH)
            query = qkv_v[half, 0, at, lanes]
            before = srecv_v[half, p].astype(F32) * flag
            state_v[half, p] = before.astype(BF)
            before = before + local_v[half, p] * c.astype(F32)
            term = dot_nn(query, unpack_state(before).astype(BF))
            num = num_v[at, lanes] + term[:, :PAIR]
            den = den_v[half, at, lanes] + term[:, PAIR:]
            inverse = 1.0 / den
            den_v[half, at, lanes] = inverse
            mix_v[half, at, lanes] = (num * inverse).astype(BF)
            place = lax.broadcasted_iota(jnp.int32, den.shape, 0) + (here.mp * ROWS + c * CH)
            kept = jnp.where(place < crop_len, den, 0.0).reshape(CH // 8, 8, PAIR)
            stat_ref[0] = jnp.maximum(stat_ref[0], jnp.max(kept, axis=0))
            stat_ref[1] = stat_ref[1] + jnp.sum(kept, axis=0)

    def hidden_grad():
        @pl.loop(0, 2)
        def _(j):
            cols = aligned(j * 1024, 1024, 1024)
            hg_v[:, cols] = dot_nt(dy_v[...], wdn_v[cols, :]).astype(BF)

    stat_ref[...] = jnp.zeros_like(stat_ref)
    loads[1].wait()
    project(0, win_v, (1, 2))
    states(0)
    dy_part(1)
    project(0, win_v, (0,))
    from_across(0)
    dy_part(1)
    inside(0)
    from_ring(0, 0)
    from_across(1)
    dy_part(1)
    loads[2].wait()
    loads[3].wait()
    hidden_grad()
    from_ring(0, 1)
    from_ring(1, 0)
    from_ring(0, 2)
    mate_wait(0)
    from_ring(1, 1)
    out(wino_v, wino_o)
    mid_v[:, pl.ds(0, 512)] = num_v[...]
    project(1, wino_v, (1, 2))
    states(1)
    dy_part(3)
    project(1, wino_v, (0,))
    from_ring(1, 2)
    inside(1)
    remote(ssend_v.at[0], srecv_v.at[1], xs_sem.at[5], xr_sem.at[6], here.across).wait_recv()
    finish(1)
    out(hg_v, hg_o)
    num_v[...] = mid_v[:, pl.ds(0, 512)]
    mate_wait(1)
    remote(ssend_v.at[1], srecv_v.at[0], xs_sem.at[6], xr_sem.at[5], here.across).wait_recv()
    finish(0)
    out(qkv_v, qkv_o)
    out(den_v, rden_o)
    out(mix_v, mix_o)
    out(state_v, state_o)
    out(woo_v, woo_o)
    loads[4].wait()
    gain_two = gain_ref[1:2, :]
    bias_two = bias_ref[1:2, :]

    @pl.loop(0, 2)
    def _(c):
        at = aligned(c * CH, CH, CH)
        own = dot_nn(mix_v[0, at, :], wo_v[...]).astype(BF).astype(F32)
        other = dot_nn(mix_v[1, at, :], woo_v[...]).astype(BF).astype(F32)
        middle = x_v[at, :].astype(F32) + (own + other)
        mid_v[at, :] = middle
        unit, _ = row_norm(middle)
        sec_v[at, :] = (unit * gain_two + bias_two).astype(BF)

    out(mid_v, mid_o)
    out(sec_v, sec_o)
    for copy in gone:
        copy.wait_recv()
    for copy in cross + gone + sends:
        copy.wait_send()
    for copy in outs:
        copy.wait()


def any_spec(count):
    return [pl.BlockSpec(memory_space=pl.ANY)] * count


def front(lengths, x_rows, dy_rows, win, wo, wdn, gain, bias):
    vm = pltpu.VMEM
    shapes = [
        ((512, 1024), BF), ((2, 3, 512, 512), BF), ((2, 512, 512), BF), ((2, 512, 512), F32),
        ((2, 4, PAIR, PAIR), BF), ((512, 1024), F32), ((512, 1024), BF), ((3072, 512), BF),
        ((512, 1024), BF), ((512, 1024), BF), ((512, 2048), BF), ((2, 8, PAIR), F32),
    ]
    dma = pltpu.SemaphoreType.DMA
    return pl.pallas_call(
        front_kernel,
        out_shape=[jax.ShapeDtypeStruct(s, d) for s, d in shapes],
        in_specs=[pl.BlockSpec(memory_space=pltpu.SMEM)] + any_spec(5)
        + [pl.BlockSpec(memory_space=pltpu.VMEM)] * 2,
        out_specs=any_spec(11) + [pl.BlockSpec(memory_space=pltpu.VMEM)],
        scratch_shapes=[
            vm((512, 1024), BF), vm((512, 1024), BF), vm((3072, 512), BF), vm((3072, 512), BF),
            vm((512, 1024), BF), vm((512, 1024), BF), vm((2048, 1024), BF), vm((512, 1024), BF),
            vm((2, 3, 512, 512), BF), vm((512, 512), F32), vm((2, 512, 512), F32), vm((2, 512, 512), BF),
            vm((512, 1024), F32), vm((512, 1024), BF), vm((512, 2048), BF),
            vm((2, 4, PAIR, PAIR), F32), vm((2, 4, PAIR, PAIR), BF), vm((2, 4, PAIR, PAIR), BF),
            vm((2, 4, PAIR, PAIR), BF),
            dma((5,)), dma((12,)), dma((15,)), dma((15,)), dma((2, 2, 3)), dma((2, 2, 3)),
            dma((2, 8)), dma((2, 8)),
        ],
        compiler_params=pltpu.CompilerParams(
            collective_id=0, has_side_effects=True, vmem_limit_bytes=58 * 1024 * 1024
        ),
        name="front",
    )(lengths, x_rows, dy_rows, win, wo, wdn, gain, bias)


GELU_A = 0.7978845608028654
GELU_B = 0.044715


def gelu_pair(v):
    square = v * v
    t = jnp.tanh(GELU_A * v * (1.0 + GELU_B * square))
    half = 0.5 * (1.0 + t)
    slope = half + (0.5 * GELU_A) * v * (1.0 - t * t) * (1.0 + (3.0 * GELU_B) * square)
    return v * half, slope


def middle_kernel(
    sec_hbm, dy_hbm, dyo_hbm, hg_hbm, wup_hbm, wdn_hbm,
    part_o, pin_o, mlp_o, dslab_o, uslab_o, dring_o,
    sec_v, dy_v, hg_v, wup_v, wdn_v, hid_v, part_v, send_v, pin_v, mlp_v,
    dsend_v, drecv_v, dslab_v, usend_v, urecv_v, uslab_v, dring_v,
    in_sem, out_sem, xs_sem, xr_sem, ms_sem, mr_sem, rs_s, rs_r,
):
    here = Place()
    own = pl.ds(0, ROWS)
    other = pl.ds(ROWS, ROWS)
    loads = [
        (sec_hbm, sec_v.at[own]), (wup_hbm, wup_v), (hg_hbm, hg_v.at[own]), (wdn_hbm, wdn_v),
        (dy_hbm, dy_v.at[own]), (dyo_hbm, dy_v.at[other]),
    ]
    loads = [pltpu.make_async_copy(a, b, in_sem.at[i]) for i, (a, b) in enumerate(loads)]
    for load in loads:
        load.start()
    greet(here.partners())
    ring_d = Arc(here, dslab_v, 0, 128, dring_v, None, None, (rs_s, rs_r, None, None, None, None, None))
    sends = []
    outs = []

    def out(src, dst):
        copy = pltpu.make_async_copy(src, dst, out_sem.at[len(outs)])
        copy.start()
        outs.append(copy)

    def across(src, dst, slot):
        copy = remote(src, dst, xs_sem.at[slot], xr_sem.at[slot], here.across)
        copy.start()
        sends.append(copy)
        return copy

    ahead = [
        across(sec_hbm.at[pl.ds(c * CH, CH)], sec_v.at[pl.ds(ROWS + c * CH, CH)], c) for c in range(2)
    ]

    def up(chunk):
        rows = pl.ds(chunk * CH, CH)

        @pl.loop(0, 4)
        def _(j):
            cols = aligned(j * 512, 512, 512)
            raw = dot_nn(sec_v[rows, :], wup_v[:, cols])
            value, slope = gelu_pair(raw)
            hid_v[rows, cols] = value.astype(BF)
            hg_v[rows, cols] = (hg_v[rows, cols].astype(F32) * slope).astype(BF)

    def back(chunk, dst):
        dst[...] = dot_nt(hg_v[pl.ds(chunk * CH, CH), :], wup_v[...]).astype(BF)

    loads[0].wait()
    loads[1].wait()
    loads[2].wait()
    for c in range(2):
        up(c)
        back(c, part_v.at[pl.ds(c * CH, CH)])
    out(part_v, part_o)
    for load in loads[3:]:
        load.wait()
    for c in range(2):
        @pl.loop(0, 2)
        def _(j):
            cols = aligned(j * 1024, 1024, 1024)
            rows = pl.ds(ROWS + c * CH, CH)
            hg_v[rows, cols] = dot_nt(dy_v[rows, :], wdn_v[cols, :]).astype(BF)

        ahead[c].wait_recv()
        up(2 + c)
        rows = pl.ds(c * CH, CH)
        back(2 + c, send_v.at[rows])
        across(send_v.at[rows], pin_v.at[rows], 2 + c)
    their = 1 - here.core

    def down_grad(half, dst, plus):
        @pl.loop(0, 2)
        def _(i):
            cols = aligned(half * 1024 + i * 512, 512, 512)
            at = aligned(i * 512, 512, 512)
            made = dot_tn(hid_v[:, cols], dy_v[...])
            if plus is not None:
                made = made + plus[at, :].astype(F32)
            dst[at, :] = made.astype(BF)

    def up_grad(half, dst, plus):
        @pl.loop(0, 2)
        def _(i):
            cols = aligned(half * 512, 512, 512)
            at = aligned(i * 1024, 1024, 1024)
            made = dot_tn(sec_v[:, cols], hg_v[:, at])
            if plus is not None:
                made = made + plus[:, at].astype(F32)
            dst[:, at] = made.astype(BF)

    def to_mate(src, dst, slot):
        copy = remote(src, dst, ms_sem.at[slot], mr_sem.at[slot], here.mate)
        copy.start()
        sends.append(copy)
        return copy

    down_grad(their, dsend_v, None)
    to_d = to_mate(dsend_v, drecv_v, 0)
    down_grad(here.core, dslab_v, None)
    to_d.wait_recv()

    @pl.loop(0, 8)
    def _(i):
        at = aligned(i * 128, 128, 128)
        dslab_v[at, :] = (dslab_v[at, :].astype(F32) + drecv_v[at, :].astype(F32)).astype(BF)

    for way in (0, 1):
        ring_d.gather_step(way, 0)
    out(dslab_v, dslab_o)
    up_grad(their, usend_v, None)
    to_u = to_mate(usend_v, urecv_v, 1)

    def mlp_rows(i):
        rows = pl.ds(i * ROWS, ROWS)
        mlp_v[rows, :] = dot_nn(hid_v[rows, :], wdn_v[...]).astype(BF)

    mlp_rows(0)
    for way in (0, 1):
        ring_d.gather_step(way, 1)
    mlp_rows(1)
    out(mlp_v, mlp_o)
    to_u.wait_recv()
    up_grad(here.core, uslab_v, urecv_v)
    out(uslab_v, uslab_o)
    for c in range(2):
        rows = pl.ds(c * CH, CH)
        remote(send_v.at[rows], pin_v.at[rows], xs_sem.at[2 + c], xr_sem.at[2 + c], here.across).wait_recv()
    out(pin_v, pin_o)
    for way in (0, 1):
        ring_d.arrived(way, 1)
        out(dring_v.at[way, 1], dring_o.at[way])
    for copy in sends + ring_d.pending:
        copy.wait_send()
    for copy in outs:
        copy.wait()


def middle(sec, dy, dyo, hg, wup, wdn):
    vm = pltpu.VMEM
    dma = pltpu.SemaphoreType.DMA
    shapes = [
        ((512, 1024), BF), ((512, 1024), BF), ((1024, 1024), BF), ((1024, 1024), BF), ((512, 2048), BF),
        ((2, 128, 1024), BF),
    ]
    return pl.pallas_call(
        middle_kernel,
        out_shape=[jax.ShapeDtypeStruct(s, d) for s, d in shapes],
        in_specs=any_spec(6),
        out_specs=any_spec(6),
        scratch_shapes=[
            vm((1024, 1024), BF), vm((1024, 1024), BF), vm((1024, 2048), BF), vm((1024, 2048), BF),
            vm((2048, 1024), BF), vm((1024, 2048), BF), vm((512, 1024), BF), vm((512, 1024), BF),
            vm((512, 1024), BF), vm((1024, 1024), BF),
            vm((1024, 1024), BF), vm((1024, 1024), BF), vm((1024, 1024), BF),
            vm((512, 2048), BF), vm((512, 2048), BF), vm((512, 2048), BF), vm((2, 2, 128, 1024), BF),
            dma((6,)), dma((7,)), dma((4,)), dma((4,)), dma((2,)), dma((2,)), dma((2, 2)), dma((2, 2)),
        ],
        compiler_params=pltpu.CompilerParams(
            collective_id=1, has_side_effects=True, vmem_limit_bytes=58 * 1024 * 1024
        ),
        name="middle",
    )(sec, dy, dyo, hg, wup, wdn)


PACE = 36


class Arc:
    def __init__(self, here, slab, base, rows, recv, result, result_base, sems, source=None, begun=0):
        self.here, self.slab, self.base, self.rows = here, slab, base, rows
        self.source = slab if source is None else source
        self.recv, self.result, self.result_base = recv, result, result_base
        self.rs_s, self.rs_r, self.ag_s, self.ag_r, self.mt_s, self.mt_r, self.local = sems
        self.pending = []
        self.t = self.begun = begun

    def span(self, base, offset, half):
        start = base + lax.rem(self.here.r + 8 + offset, 8) * self.rows
        if half is None:
            return aligned(start, self.rows, 16)
        return aligned(start + half * (self.rows // 2), self.rows // 2, 16)

    def mine(self, offset, half=None):
        return self.span(self.base, offset, half)

    def place(self, offset, core, half=None):
        return self.result.at[self.span(self.result_base(core) + self.base, offset, half)]

    def send(self, src, dst, send_sem, recv_sem, device):
        copy = remote(src, dst, send_sem, recv_sem, device)
        copy.start()
        self.pending.append(copy)

    def to(self, way):
        return self.here.next if way == 0 else self.here.prev

    def sign(self, way):
        return 1 if way == 0 else -1

    def slot(self, way, s):
        if s > 0:
            return self.recv.at[way, s]
        return self.recv.at[way, 0, pl.ds(way * (self.rows // 2), self.rows // 2)]

    def arrived(self, way, s):
        got = self.slot(way, s)
        remote(got, got, self.rs_s.at[way, s], self.rs_r.at[way, s], self.to(way)).wait_recv()

    def gather_step(self, way, s):
        sign = self.sign(way)
        if s == 0:
            src = self.source.at[self.mine(sign * 4, way)]
        else:
            if s > self.begun or s == 1:
                self.arrived(way, s - 1)
            own = self.slab[self.mine(sign * (4 - s)), :].astype(F32)
            src = self.recv.at[way, s - 1]
            if s == 1:
                half = self.rows // 2
                kept = pl.ds(way * half, half)
                rest = pl.ds((1 - way) * half, half)
                at = slice(way * half, way * half + half)
                src[kept, :] = (src[kept, :].astype(F32) + own[at]).astype(BF)
                at = slice((1 - way) * half, (1 - way) * half + half)
                src[rest, :] = own[at].astype(BF)
            else:
                src[...] = (src[...].astype(F32) + own).astype(BF)
        self.send(src, self.slot(way, s), self.rs_s.at[way, s], self.rs_r.at[way, s], self.to(way))

    def spread(self, src, offset, step, way, half=None):
        dst = self.place(offset, self.here.core, half)
        if step < 4 and not (step == 3 and half is None):
            self.send(src, dst, self.ag_s.at[way, step], self.ag_r.at[way, step], self.to(way))

    def to_mate(self, src, offset, slot, half=None):
        dst = self.place(offset, self.here.core, half)
        self.send(src, dst, self.mt_s.at[slot], self.mt_r.at[slot], self.here.mate)

    def total(self):
        self.arrived(0, 3)
        self.arrived(1, 3)
        sums = self.recv.at[0, 3]
        own = self.slab[self.mine(0), :].astype(F32)
        sums[...] = (sums[...].astype(F32) + self.recv[1, 3].astype(F32) + own).astype(BF)
        for way in (0, 1):
            self.spread(sums, 0, 0, way)
        self.to_mate(sums, 0, 0)
        self.keep = pltpu.make_async_copy(sums, self.place(0, self.here.core), self.local)
        self.keep.start()

    def spread_step(self, way, s):
        sign = self.sign(way)
        half = way if s == 3 else None
        got = self.place(-sign * (s + 1), self.here.core, half)
        remote(got, got, self.ag_s.at[way, s], self.ag_r.at[way, s], self.to(way)).wait_recv()
        if s < 3:
            part = way if s == 2 else None
            src = self.place(-sign * (s + 1), self.here.core, part)
            self.spread(src, -sign * (s + 1), s + 1, way, part)
        self.to_mate(got, -sign * (s + 1), 1 + 2 * s + way, half)

    def tick(self):
        t = self.t
        self.t = t + 1
        if t == 4:
            self.total()
        elif t < 9:
            for way in (0, 1):
                if t < 4:
                    self.gather_step(way, t)
                else:
                    self.spread_step(way, t - 5)

    def finish(self):
        for copy in self.pending:
            copy.wait_send()
        self.keep.wait()
        other = 1 - self.here.core
        for slot in range(9):
            if slot == 0:
                got = self.place(0, other)
            else:
                s, way = (slot - 1) // 2, (slot - 1) % 2
                got = self.place(-self.sign(way) * (s + 1), other, way if s == 3 else None)
            remote(got, got, self.mt_s.at[slot], self.mt_r.at[slot], self.here.mate).wait_recv()


def back_kernel(
    len_ref, gain_ref, bias_ref, stat_ref,
    part_hbm, pin_hbm, mid_hbm, x_hbm, dy_hbm, qkv_hbm, mix_hbm, rden_hbm, state_hbm, first_hbm,
    win_hbm, wino_hbm, wo_hbm, woo_hbm, mlp_hbm, dslab_hbm, uslab_hbm, dring_hbm,
    resd_o, resu_o, resi_o, reso_o, out_o, gin_o, small_ref,
    part_v, pin_v, mid_v, dy_v, qkv_v, mix_v, rden_v, state_v, first_v, win_v, wo_v,
    mlpin_v, mg_v, mgf_v, mixg_v, top_v, bot_v, dqkv_v, local_v, lsend_v, lrecv_v,
    dslab_v, uslab_v, drecv_v, urecv_v, gm_v, gr_v, ga_v, gx_v, om_v, or_v, oa_v, ox_v, irecv_v, orecv_v,
    small_s, small_r,
    in_sem, out_sem, xs_sem, xr_sem, ms_sem, mr_sem, bs_sem, br_sem,
    rs_s, rs_r, ag_s, ag_r, mt_s, mt_r, keep_s,
):
    here = Place()
    loads = [
        (part_hbm, part_v), (pin_hbm, pin_v), (mid_hbm, mid_v), (dy_hbm, dy_v), (dslab_hbm, dslab_v),
        (uslab_hbm, uslab_v), (wo_hbm, wo_v.at[0]), (woo_hbm, wo_v.at[1]), (mix_hbm, mix_v),
        (rden_hbm, rden_v), (qkv_hbm, qkv_v), (state_hbm, state_v), (first_hbm, first_v),
        (win_hbm, win_v.at[0]), (wino_hbm, win_v.at[1]), (x_hbm, part_v), (mlp_hbm.at[pl.ds(0, ROWS)], pin_v),
        (dring_hbm.at[0], drecv_v.at[0, 1]), (dring_hbm.at[1], drecv_v.at[1, 1]),
    ]
    loads = [pltpu.make_async_copy(a, b, in_sem.at[i]) for i, (a, b) in enumerate(loads)]
    begun = [loads[17], loads[18], loads[4]]
    for load in begun + [load for load in loads[:15] if load is not loads[4]]:
        load.start()
    y_mate = (here.dp + 2 - 4 * lax.rem(here.dp // 2, 2), here.mp)
    z_mate = (here.dp + 4 - 8 * lax.rem(here.dp // 4, 2), here.mp)
    z_far = (here.dp + 8 - 16 * (here.dp // 8), here.mp)
    greet(here.partners() + [y_mate, z_mate, z_far])
    sends = []
    outs = []

    def out(src, dst):
        copy = pltpu.make_async_copy(src, dst, out_sem.at[len(outs)])
        copy.start()
        outs.append(copy)

    def across(src, dst, slot):
        copy = remote(src, dst, xs_sem.at[slot], xr_sem.at[slot], here.across)
        copy.start()
        sends.append(copy)
        return copy

    def to_mate(src, dst, slot):
        copy = remote(src, dst, ms_sem.at[slot], mr_sem.at[slot], here.mate)
        copy.start()
        sends.append(copy)
        return copy

    arcs = []

    def add_arc(slab, base, rows, recv, result, result_base, source=None, begun=0):
        n = len(arcs)
        sems = (rs_s.at[n], rs_r.at[n], ag_s.at[n], ag_r.at[n], mt_s.at[n], mt_r.at[n], keep_s.at[n])
        arcs.append(Arc(here, slab, base, rows, recv, result, result_base, sems, source, begun))
        return arcs[-1]

    ring_d = add_arc(dslab_v, 0, 128, drecv_v, resd_o, lambda core: core * 1024, None, 2)
    ring_u = add_arc(uslab_v, 0, 64, urecv_v, resu_o, lambda core: core * 512, uslab_hbm)
    ring_o = add_arc(oa_v.at[0], 0, 32, orecv_v, reso_o, lambda core: core * 256)
    ring_i = [
        add_arc(ga_v.at[0], i * 512, 64, irecv_v.at[i], resi_o, lambda core: core * 1536) for i in range(3)
    ]

    credit = [0]

    def ring(count):
        credit[0] += count * PACE
        while credit[0] >= 100:
            credit[0] -= 100
            first = ring_d if ring_d.t <= ring_u.t else ring_u
            first.tick()

    def ring_on(arc):
        arc.tick()

    ring_u.tick()
    for load in begun:
        load.wait()
    ring_d.tick()

    small_s[...] = jnp.zeros_like(small_s)
    for load in loads[0:4] + loads[5:6]:
        load.wait()
    gain_two = gain_ref[1:2, :]

    @pl.loop(0, ROWS // 128)
    def _(i):
        at = aligned(i * 128, 128, 128)
        grad = part_v[at, :].astype(F32) + pin_v[at, :].astype(F32)
        unit, inverse = row_norm(mid_v[at, :])
        scaled = grad * gain_two
        centre = jnp.mean(scaled, axis=-1, keepdims=True)
        along = jnp.mean(scaled * unit, axis=-1, keepdims=True)
        total = dy_v[at, :].astype(F32) + inverse * (scaled - centre - unit * along)
        mgf_v[at, :] = total
        mg_v[at, :] = total.astype(BF)
        small_s[1:2, :] = small_s[1:2, :] + jnp.sum(grad * unit, axis=0, keepdims=True)
        small_s[3:4, :] = small_s[3:4, :] + jnp.sum(grad, axis=0, keepdims=True)

    for load in loads[15:17]:
        load.start()
    ring(2)
    for load in loads[6:12]:
        load.wait()
    @pl.loop(0, 2)
    def _(half):
        mixg_v[half] = dot_nt(mg_v[...], wo_v[half]).astype(BF)

    ring(1)
    their = 1 - here.core

    def out_grad(half, side, dst):
        cols = aligned(side * 256, 256, 256)
        dst[...] = dot_tn(mix_v[half, :, cols], mg_v[...]).astype(BF)

    keep = same_head()

    def tops(half):
        @pl.loop(0, 4)
        def _(p):
            lanes_at = aligned(p * PAIR, PAIR, PAIR)
            packs = []
            blocks = jnp.where(keep, 1.0, 0.0).astype(BF)
            for c in range(2):
                at = pl.ds(c * CH, CH)
                top = (mixg_v[half, at, lanes_at].astype(F32) * rden_v[half, at, lanes_at]).astype(BF)
                top_v[half, at, lanes_at] = top
                prod = top.astype(F32) * mix_v[half, at, lanes_at].astype(F32)
                high = prod.astype(BF)
                low = (prod - high.astype(F32)).astype(BF)
                bottom = -(dot_nn(high, blocks) + dot_nn(low, blocks))
                high = bottom.astype(BF)
                low = (bottom - high.astype(F32)).astype(BF)
                lane = lax.rem(lax.broadcasted_iota(jnp.int32, bottom.shape, 1), DH)
                bot_v[half, at, lanes_at] = jnp.where(
                    lane == 0, high, jnp.where(lane == 1, low, jnp.zeros_like(high))
                )
                query = qkv_v[half, 0, at, lanes_at]
                made = dot_tn(query, jnp.concatenate([top, high], axis=1))
                packs.append(jnp.where(keep, made[:, :PAIR], pltpu.roll(made[:, PAIR:], DH, 1)))
            local_v[half, p] = packs[1]
            lsend_v[half, p] = (packs[0] + packs[1]).astype(BF)

        across(lsend_v.at[half], lrecv_v.at[1 - half], 1 + half)

    tops(0)
    ring(1)
    tops(1)
    ring(1)
    for half in (1, 0):
        out_grad(half, their, om_v.at[half])
        to_mate(om_v.at[half], or_v.at[half], half)
    ring(1)
    for half in (1, 0):
        out_grad(half, here.core, oa_v.at[half])
    ring(1)
    for load in loads[12:15]:
        load.wait()

    def attend_back(half):
        mask = causal_tile()
        earlier = 1.0 - here.mp.astype(F32)
        remote(
            lsend_v.at[1 - half], lrecv_v.at[half], xs_sem.at[2 - half], xr_sem.at[2 - half], here.across
        ).wait_recv()

        def body(p, c):
            lanes_at = aligned(p * PAIR, PAIR, PAIR)
            at = aligned(c * CH, CH, CH)
            second = c.astype(F32)
            query = qkv_v[half, 0, at, lanes_at]
            key = qkv_v[half, 1, at, lanes_at]
            val = qkv_v[half, 2, at, lanes_at]
            top = top_v[half, at, lanes_at]
            bot = bot_v[half, at, lanes_at]
            lane = lax.rem(lax.broadcasted_iota(jnp.int32, val.shape, 1), DH)
            one = jnp.ones_like(val)
            zero = jnp.zeros_like(val)
            val_two = jnp.concatenate([val, jnp.where(lane < 2, one, zero)], axis=1)
            val_one = jnp.concatenate([val, jnp.where(lane == 0, one, zero)], axis=1)
            key0 = qkv_v[half, 1, pl.ds(0, CH), lanes_at]
            val0 = qkv_v[half, 2, pl.ds(0, CH), lanes_at]
            made = dot_tn(key0, jnp.concatenate([val0, one], axis=1))
            made = jnp.where(keep, made[:, :PAIR], made[:, PAIR:])
            before = state_v[half, p].astype(F32) + made * second
            after = lrecv_v[half, p].astype(F32) * earlier + local_v[half, p] * (1.0 - second)
            before = unpack_state(before).astype(BF)
            after = unpack_state(after).astype(BF)
            dq = dot_nt(jnp.concatenate([top, bot], axis=1), before)
            dk = dot_nt(val_one, after)
            dv = dot_nn(key, after[:, :PAIR])
            queries, keys, tops_, bots = split_heads(query), split_heads(key), split_heads(top), split_heads(bot)
            for head in range(2):
                score = jnp.where(mask, dot_nt(queries[head], key), 0.0).astype(BF)
                grad = dot_nt(jnp.concatenate([tops_[head], bots[head]], axis=1), val_two)
                grad = jnp.where(mask, grad, 0.0).astype(BF)
                dq = dq + dot_nn(grad, keys[head])
                dk = dk + dot_tn(grad, queries[head])
                dv = dv + dot_tn(score, tops_[head])
            dqkv_v[half, 0, at, lanes_at] = (dq * jnp.minimum(query.astype(F32), 1.0)).astype(BF)
            dqkv_v[half, 1, at, lanes_at] = (dk * jnp.minimum(key.astype(F32), 1.0)).astype(BF)
            dqkv_v[half, 2, at, lanes_at] = dv.astype(BF)

        for part in range(2):
            @pl.loop(part * 4, part * 4 + 4)
            def _(n):
                body(n // 2, lax.rem(n, 2))

            ring(2)

    def piece(i):
        return pl.ds(i * 512, 512)

    def in_grads(half):
        for side, dst in ((their, gm_v), (here.core, ga_v)):
            cols = aligned(side * 512, 512, 512)
            @pl.loop(0, 3)
            def _(i):
                dst[half, aligned(i * 512, 512, 512), :] = dot_tn(first_v[:, cols], dqkv_v[half, i]).astype(BF)

            if dst is gm_v:
                for i in range(3):
                    at = piece(i)
                    to_mate(gm_v.at[half, at], gr_v.at[half, at], 2 + half * 3 + i)
            ring(1)

    def add_rows(dst, src, start, count):
        @pl.loop(0, count)
        def _(i):
            at = aligned(start + i * 128, 128, 128)
            dst[at, :] = (dst[at, :].astype(F32) + src[at, :].astype(F32)).astype(BF)

    def mate_arrival(half, i):
        at = piece(i)
        slot = 2 + half * 3 + i
        remote(gm_v.at[half, at], gr_v.at[half, at], ms_sem.at[slot], mr_sem.at[slot], here.mate).wait_recv()
        add_rows(ga_v.at[half], gr_v.at[half], i * 512, 4)

    def mate_arrival_out(half):
        remote(om_v.at[half], or_v.at[half], ms_sem.at[half], mr_sem.at[half], here.mate).wait_recv()
        add_rows(oa_v.at[half], or_v.at[half], 0, 2)

    attend_back(1)
    mate_arrival_out(1)
    cross_o = across(oa_v.at[1], ox_v, 3)
    in_grads(1)
    cross_i = []
    for i in range(3):
        mate_arrival(1, i)
        cross_i.append(across(ga_v.at[1, piece(i)], gx_v.at[piece(i)], 4 + i))
    mlp = across(mlp_hbm.at[pl.ds(ROWS, ROWS)], mlpin_v, 0)
    ring(2)
    mate_arrival_out(0)
    attend_back(0)
    cross_o.wait_recv()
    add_rows(oa_v.at[0], ox_v, 0, 2)
    ring_on(ring_o)
    in_grads(0)
    for i in range(3):
        mate_arrival(0, i)
    ring(2)
    ring_on(ring_o)

    loads[15].wait()
    gain_one = gain_ref[0:1, :]

    @pl.loop(0, 2)
    def _(quarter):
        at = aligned(quarter * CH, CH, CH)
        grad = None
        for half in range(2):
            term = None
            for j in range(3):
                made = dot_nt(dqkv_v[half, j, at, :], win_v[half, pl.ds(j * 1024, 1024), :])
                term = made if term is None else term + made
            term = term.astype(BF).astype(F32)
            grad = term if grad is None else grad + term
        unit, inverse = row_norm(part_v[at, :].astype(F32))
        scaled = grad * gain_one
        centre = jnp.mean(scaled, axis=-1, keepdims=True)
        along = jnp.mean(scaled * unit, axis=-1, keepdims=True)
        mgf_v[at, :] = mgf_v[at, :] + inverse * (scaled - centre - unit * along)
        small_s[0:1, :] = small_s[0:1, :] + jnp.sum(grad * unit, axis=0, keepdims=True)
        small_s[2:3, :] = small_s[2:3, :] + jnp.sum(grad, axis=0, keepdims=True)

    ring(4)
    ring_on(ring_o)
    out(mgf_v, gin_o)
    small_s[4:5, pl.ds(0, PAIR)] = jnp.sum(stat_ref[1], axis=0, keepdims=True) * (1.0 / DH)
    count = len_ref[0].astype(F32) * (8.0 / 1024.0)
    small_s[5:6, :] = jnp.zeros((1, 1024), F32) + count
    small_s[6:7, pl.ds(0, PAIR)] = jnp.max(stat_ref[0], axis=0, keepdims=True)
    partners = [here.mate, y_mate, z_mate, z_far, here.across]

    def small_send(step):
        src = small_s if step == 0 else small_ref
        copy = remote(src, small_r.at[step], bs_sem.at[step], br_sem.at[step], partners[step])
        copy.start()
        return copy

    def small_step(copy, step):
        copy.wait()
        src = small_s if step == 0 else small_ref
        mine, theirs = src[...], small_r[step]
        row = lax.broadcasted_iota(jnp.int32, mine.shape, 0)
        small_ref[...] = jnp.where(row < 6, mine + theirs, jnp.maximum(mine, theirs))

    for i in range(3):
        cross_i[i].wait_recv()
        add_rows(ga_v.at[0], gx_v, i * 512, 4)
        for arc in ring_i[: i + 1]:
            ring_on(arc)
        ring(6)
        ring_on(ring_o)
    copy = small_send(0)
    for step in range(9):
        for arc in ring_i:
            ring_on(arc)
        ring(6)
        ring_on(ring_o)
        if 2 <= step < 7:
            small_step(copy, step - 2)
            if step < 6:
                copy = small_send(step - 1)
    ring(2000)

    loads[16].wait()
    mlp.wait_recv()

    @pl.loop(0, 4)
    def _(i):
        at = aligned(i * 128, 128, 128)
        total = mid_v[at, :] + (pin_v[at, :].astype(F32) + mlpin_v[at, :].astype(F32))
        pin_v[at, :] = total.astype(BF)

    out(pin_v, out_o)
    for arc in arcs:
        arc.finish()
    for copy in sends:
        copy.wait_send()
    for copy in outs:
        copy.wait()


def back(lengths, gain, bias, stat, part, pin, mid, x, dy, qkv, mix, rden, state, first, win, wino, wo, woo, mlp, dslab, uslab, dring):
    vm = pltpu.VMEM
    dma = pltpu.SemaphoreType.DMA
    shapes = [
        ((2048, 1024), BF), ((1024, 2048), BF), ((3072, 512), BF), ((512, 1024), BF),
        ((512, 1024), BF), ((512, 1024), F32), ((8, 1024), F32),
    ]
    rows = (512, 1024)
    heads = (2, 512, 512)
    pack = (2, 4, PAIR, PAIR)
    vmem = pl.BlockSpec(memory_space=pltpu.VMEM)
    return pl.pallas_call(
        back_kernel,
        out_shape=[jax.ShapeDtypeStruct(s, d) for s, d in shapes],
        in_specs=[pl.BlockSpec(memory_space=pltpu.SMEM), vmem, vmem, vmem] + any_spec(18),
        out_specs=any_spec(6) + [vmem],
        scratch_shapes=[
            vm(rows, BF), vm(rows, BF), vm(rows, F32), vm(rows, BF),
            vm((2, 3, 512, 512), BF), vm(heads, BF), vm(heads, F32), vm(pack, BF), vm(rows, BF),
            vm((2, 3072, 512), BF), vm((2, 512, 1024), BF),
            vm(rows, BF), vm(rows, BF), vm(rows, F32), vm(heads, BF), vm(heads, BF), vm(heads, BF),
            vm((2, 3, 512, 512), BF), vm(pack, F32), vm(pack, BF), vm(pack, BF),
            vm((1024, 1024), BF), vm((512, 2048), BF), vm((2, 4, 128, 1024), BF), vm((2, 4, 64, 2048), BF),
            vm((2, 1536, 512), BF), vm((2, 1536, 512), BF), vm((2, 1536, 512), BF), vm((1536, 512), BF),
            vm((2, 256, 1024), BF), vm((2, 256, 1024), BF), vm((2, 256, 1024), BF), vm((256, 1024), BF),
            vm((3, 2, 4, 64, 512), BF), vm((2, 4, 32, 1024), BF),
            vm((8, 1024), F32), vm((5, 8, 1024), F32),
            dma((19,)), dma((2,)), dma((7,)), dma((7,)), dma((8,)), dma((8,)), dma((5,)), dma((5,)),
            dma((6, 2, 4)), dma((6, 2, 4)), dma((6, 2, 4)), dma((6, 2, 4)), dma((6, 9)), dma((6, 9)), dma((6,)),
        ],
        compiler_params=pltpu.CompilerParams(
            collective_id=2, has_side_effects=True, vmem_limit_bytes=60 * 1024 * 1024
        ),
        name="back",
    )(lengths, gain, bias, stat, part, pin, mid, x, dy, qkv, mix, rden, state, first, win, wino, wo, woo, mlp, dslab, uslab, dring)


def widen_kernel(
    d_hbm, u_hbm, i_hbm, o_hbm, gin_hbm, out_hbm, small_ref,
    di_o, ui_o, ii_o, oi_o, gin_o, out_o, gain_ref, bias_ref, stats_ref,
    d_v, u_v, i_v, o_v, df_v, uf_v, if_v, of_v, gin_v, out_v, in_sem, out_sem,
):
    jobs = []
    for k in range(6):
        core, i = k // 3, k % 3
        jobs.append((i_hbm, i_v, k * 512, ii_o, if_v, i * 1024 + core * 512, 512))
    for k in range(2):
        jobs.append((o_hbm, o_v, k * 256, oi_o, of_v, k * 256, 256))
    for k in range(8):
        jobs.append((u_hbm, u_v, k * 128, ui_o, uf_v, k * 128, 128))
    for k in range(8):
        jobs.append((d_hbm, d_v, k * 256, di_o, df_v, k * 256, 256))
    loads, stores = [], []
    for n, (src, held, at, _, _, _, rows) in enumerate(jobs):
        loads.append(pltpu.make_async_copy(src.at[pl.ds(at, rows)], held.at[pl.ds(at, rows)], in_sem.at[n]))
        loads[-1].start()
    passed = ((gin_hbm, gin_v, gin_o), (out_hbm, out_v, out_o))
    for n, (src, held, _) in enumerate(passed):
        loads.append(pltpu.make_async_copy(src, held, in_sem.at[len(jobs) + n]))
        loads[-1].start()
    for n, (_, held, at, dst, wide, to, rows) in enumerate(jobs):
        loads[n].wait()

        @pl.loop(0, rows // 128)
        def _(k):
            rows_at = aligned(at + k * 128, 128, 128)
            wide[rows_at, :] = held[rows_at, :].astype(F32)

        stores.append(pltpu.make_async_copy(wide.at[pl.ds(at, rows)], dst.at[pl.ds(to, rows)], out_sem.at[n]))
        stores[-1].start()
    for n, (_, held, dst) in enumerate(passed):
        loads[len(jobs) + n].wait()
        stores.append(pltpu.make_async_copy(held, dst, out_sem.at[len(jobs) + n]))
        stores[-1].start()
    gain_ref[...] = small_ref[0:2, :]
    bias_ref[...] = small_ref[2:4, :]
    scaling = 1.0 / (DH * 1024)
    count = jnp.max(small_ref[5:6, :]) * 1024.0
    stats_ref[0] = jnp.max(small_ref[6:7, :]) * scaling
    stats_ref[1] = jnp.sum(small_ref[4:5, :]) / count * scaling
    for copy in stores:
        copy.wait()


def widen(resd, resu, resi, reso, gin, out, small):
    vm = pltpu.VMEM
    vmem = pl.BlockSpec(memory_space=pltpu.VMEM)
    shapes = [
        ((2048, 1024), F32), ((1024, 2048), F32), ((3072, 512), F32), ((512, 1024), F32),
        ((512, 1024), F32), ((512, 1024), BF), ((2, 1024), F32), ((2, 1024), F32), ((2,), F32),
    ]
    return pl.pallas_call(
        widen_kernel,
        out_shape=[jax.ShapeDtypeStruct(s, d) for s, d in shapes],
        in_specs=any_spec(6) + [vmem],
        out_specs=any_spec(6) + [vmem, vmem, pl.BlockSpec(memory_space=pltpu.SMEM)],
        scratch_shapes=[vm(s, BF) for s, _ in shapes[:4]] + [vm(s, F32) for s, _ in shapes[:4]]
        + [vm((512, 1024), F32), vm((512, 1024), BF)]
        + [pltpu.SemaphoreType.DMA((26,)), pltpu.SemaphoreType.DMA((26,))],
        compiler_params=pltpu.CompilerParams(vmem_limit_bytes=60 * 1024 * 1024),
        name="widen",
    )(resd, resu, resi, reso, gin, out, small)


def fast_device(
    block_in, lengths, input_weight, output_weight, up_weight, down_weight, norm_gain, norm_bias, cotangent
):
    x, dy = block_in[0], cotangent[0]
    win = input_weight.reshape(3072, 512)
    first, qkv, mix, rden, state, mid, sec, wino, woo, dyo, hg, stat = front(
        lengths, x, dy, win, output_weight, down_weight, norm_gain, norm_bias
    )
    part, pin, mlp, dslab, uslab, dring = middle(sec, dy, dyo, hg, up_weight, down_weight)
    resd, resu, resi, reso, block_out, grad_in, small = back(
        lengths, norm_gain, norm_bias, stat, part, pin, mid, x, dy, qkv, mix, rden, state, first,
        win, wino, output_weight, woo, mlp, dslab, uslab, dring,
    )
    down_grad, up_grad, in_grad, out_grad, grad_in, block_out, gain, bias, stats = widen(
        resd, resu, resi, reso, grad_in, block_out, small
    )
    return (
        block_out[None], grad_in[None], in_grad.reshape(3, 1024, 512), out_grad, up_grad, down_grad,
        gain, bias, stats,
    )


def fits_fast(mesh, block_shape):
    return dict(mesh.shape) == {"dp": 16, "mp": 2} and tuple(block_shape) == (16, 1024, 1024)


def solution(mesh):
    in_specs = (
        P("dp", "mp", None),
        P("dp"),
        P(None, None, "mp"),
        P("mp", None),
        P(None, "mp"),
        P("mp", None),
        P(),
        P(),
        P("dp", "mp", None),
    )
    out_specs = (
        P("dp", "mp", None),
        P("dp", "mp", None),
        P(None, None, "mp"),
        P("mp", None),
        P(None, "mp"),
        P("mp", None),
        P(),
        P(),
        P(),
    )

    def whole(*arrays):
        body = fast_device if fits_fast(mesh, arrays[0].shape) else per_device
        return jax.shard_map(
            body, mesh=mesh, in_specs=in_specs, out_specs=out_specs, check_vma=False
        )(*arrays)

    return whole
```
